32 devices in a mesh: dp: 8 (over z, x), tensor: 4 (over y, core).
Axes of the slice: x: 2, y: 2, z: 4, core: 2. Of those that a mesh axis runs over, the one named last changes fastest.
Arguments:
- tokens: bfloat16 [8192, 1024], P(('dp', 'tensor')), may hold values from -6 to 6
- segments: int32 [8, 1024], P('dp'), may hold values from 0 to 3, never falling along the last dimension, each value on 1 to 512 neighbouring positions
- cotangent: bfloat16 [8192, 1024], P(('dp', 'tensor')), may hold values from -6 to 6
- project_weight: bfloat16 [1024, 3, 1024], P('dp', None, 'tensor'), may hold values from -0.1875 to 0.1875
- output_weight: bfloat16 [1024, 1024], P('tensor', 'dp'), may hold values from -1.5 to 1.5
- up_weight: bfloat16 [1024, 4096], P('dp', 'tensor'), may hold values from -0.1875 to 0.1875
- down_weight: bfloat16 [4096, 1024], P('tensor', 'dp'), may hold values from -0.09375 to 0.09375
- norm_gains: float32 [2, 1024], replicated, may hold values from 0.5 to 1.5
- bias_rows: float32 [6, 1024], replicated, may hold values from -3 to 3
- hidden_bias: float32 [4096], replicated, may hold values from -3 to 3
Outputs:
- layer_out: bfloat16 [8192, 1024], P(('dp', 'tensor'))
- grad_tokens: float32 [8192, 1024], P(('dp', 'tensor'))
- grad_project: float32 [1024, 3, 1024], P('dp', None, 'tensor')
- grad_output: float32 [1024, 1024], P('tensor', 'dp')
- grad_up: float32 [1024, 4096], P('dp', 'tensor')
- grad_down: float32 [4096, 1024], P('tensor', 'dp')
- grad_gains: float32 [2, 1024], replicated
- grad_bias_rows: float32 [6, 1024], replicated
- grad_hidden_bias: float32 [4096], replicated
The draws below stay inside these ranges and needn't reach their ends.
Inputs may be any that keep to these rules, and one draw needn't show every extreme that they name: `segments`: within each sequence the numbers never fall; a document is a run of equal numbers of at most 512 tokens, and every sequence has one document of exactly that length.
All inputs are finite; a program needn't handle non-finite values.
Results may differ from the reference program's by a relative error of at most 0.015.
The reference program's roundings to bfloat16 on the way count: a program that leaves them out, or rounds other values in their place, can miss the bound.
Values may be sent and summed in bfloat16 or wider, within the bound.
A program may use at most 128 MiB of HBM per device.

```python
import math
import jax
import jax.numpy as jnp
import numpy as np
from jax import lax

D = 1024
HEAD = 64
FF = 4096
LEN = 1024
SEQUENCES = 8
TOKENS = 8192


def with_spikes(array, rng, source, target, blocks, factor):
    owner, partner = [(jnp.arange(array.shape[axis_at]) // (array.shape[axis_at] // blocks)).reshape([-1 if axis == axis_at else 1 for axis in range(array.ndim)]) for axis_at in (source, target)]
    chosen = jax.random.permutation(rng, blocks)[partner]
    strong = (owner == chosen) | (owner == (partner + blocks // 2) % blocks)
    return jnp.where(strong, factor * array, array)


def level_of(stream_key, shape, cuts, smallest, largest):
    def one(axis_at, shards_of):
        heights = jax.random.uniform(jax.random.fold_in(jax.random.fold_in(stream_key, 6), axis_at), (shards_of,), jnp.float32, smallest / len(cuts), largest / len(cuts))
        return jnp.repeat(jnp.exp(heights), shape[axis_at] // shards_of).reshape((-1,) + (1,) * (len(shape) - axis_at - 1))

    level = one(*cuts[0])
    for cut in cuts[1:]:
        level = level * one(*cut)
    return level


def length_profile(number_of, total, bound, skew):
    loads = [(1 << 20) // math.isqrt(grade ** skew) + 1 for grade in range(2, number_of + 1)]
    surplus, counts = total - bound - (number_of - 1), [1] * (number_of - 1)
    while surplus > 0:
        movable = [i for i in range(number_of - 1) if counts[i] < bound]
        mass, left = sum([loads[i] for i in movable]), surplus
        for i in movable:
            addition = min(bound - counts[i], max(1, left * loads[i] // mass), surplus)
            counts[i] = counts[i] + addition
            surplus = surplus - addition
    return np.array([bound] + counts)


def ragged_sizes(stream_key, amount, total, bound, lean):
    if amount == 2:
        one = jax.random.randint(stream_key, (), max(1, total - bound), min(bound, total - 1) + 1)
        return jnp.stack([one, total - one])
    lengths = jnp.asarray(length_profile(amount, total, bound, lean), jnp.int32)
    twos = (amount - 1) // 2
    source_of, sink = lengths[1:1 + 2 * twos:2], lengths[2:2 + 2 * twos:2]
    slack = jnp.minimum(source_of - 1, bound - sink)
    moved = jax.random.randint(jax.random.fold_in(stream_key, 1), (twos,), 0, 1 << 20) % (slack + 1)
    lengths = lengths.at[1:1 + 2 * twos:2].set(source_of - moved).at[2:2 + 2 * twos:2].set(sink + moved)
    return lengths[jax.random.permutation(jax.random.fold_in(stream_key, 2), amount)]


def normal_values(own_key, dims, spread, most, shards=(), kind=jnp.bfloat16):
    factor_of = level_of(own_key, dims, shards, -0.22, 0.18) if shards else 1.0
    values = jax.random.normal(own_key, dims, jnp.float32) * spread * factor_of
    return jnp.minimum(jnp.maximum(values, -most), most).astype(kind)


def bell_draw_with(rng, dims, spread, reach, cuts, heavy, kind=jnp.bfloat16):
    result = spread * jax.random.normal(rng, dims, jnp.float32)
    if cuts:
        result = result * level_of(rng, dims, cuts, -0.22, 0.18)
    return jnp.clip(with_spikes(result, jax.random.fold_in(rng, 3), *heavy), -reach, reach).astype(kind)


def setup_inputs(seed: int = 0) -> dict:
    splits = jax.random.split(jax.random.key(seed), 11)
    return {
        "tokens": bell_draw_with(splits[0], (TOKENS, D), 1.0, 6.0, ((0, 32),), (0, 1, 32, 2.75)),
        "segments": jax.vmap(lambda own: jnp.searchsorted(jnp.cumsum(ragged_sizes(own, 4, LEN, LEN // 2, 0)), jnp.arange(LEN), side="right"))(jax.random.split(splits[1], SEQUENCES)).reshape((SEQUENCES, LEN)).astype(jnp.int32),
        "cotangent": normal_values(splits[2], (TOKENS, D), 1.0, 6.0, ((0, 32),)),
        "project_weight": normal_values(splits[3], (D, 3, D), D ** -0.5, 0.1875, ((0, 8), (2, 4))),
        "output_weight": normal_values(splits[4], (D, D), (D // 64) ** -0.5, 1.5, ((0, 4), (1, 8))),
        "up_weight": normal_values(splits[5], (D, FF), D ** -0.5, 0.1875, ((0, 8), (1, 4))),
        "down_weight": normal_values(splits[6], (FF, D), FF ** -0.5, 0.09375, ((0, 4), (1, 8))),
        "norm_gains": jnp.clip(1.0 + 0.1 * jax.random.normal(splits[7], (2, D), jnp.float32), 0.5, 1.5),
        "bias_rows": normal_values(splits[8], (6, D), 0.5, 3.0, (), jnp.float32),
        "hidden_bias": normal_values(splits[9], (FF,), 0.5, 3.0, (), jnp.float32),
    }


@jax.custom_vjp
def low(v):
    return lax.optimization_barrier(v.astype(jnp.bfloat16)).astype(jnp.float32)

@jax.custom_vjp
def low_back(v):
    return v

def low_keep(v):
    return (low(v), None)

def low_pass(kept, grad):
    return (grad,)

def back_keep(v):
    return (v, None)

def back_low(kept, grad):
    return (low(grad),)
low.defvjp(low_keep, low_pass)
low_back.defvjp(back_keep, back_low)
EPSILON = 1e-05
HIGHEST = lax.Precision.HIGHEST

def layer_norm(token_rows, gain, shift):
    average = lax.optimization_barrier(jnp.mean(token_rows, axis=-1, keepdims=True))
    centred = token_rows - average
    variance = lax.optimization_barrier(jnp.mean(centred * centred, axis=-1, keepdims=True))
    return centred * lax.rsqrt(variance + EPSILON) * gain + shift

def attend(queries, key_rows, value_rows, segment):
    length_here = queries.shape[0]
    head_count = queries.shape[1] // HEAD
    query_heads = queries.reshape(length_here, head_count, HEAD)
    key_heads = key_rows.reshape(length_here, head_count, HEAD)
    value_heads = value_rows.reshape(length_here, head_count, HEAD)
    scores = low_back(jnp.einsum('qhd,khd->hqk', query_heads, key_heads, precision=HIGHEST) * HEAD ** (-0.5))
    same_doc = segment[:, None] == segment[None, :]
    scores = jnp.where(same_doc[None], scores, -1e+30)
    weights_low = low(jax.nn.softmax(scores, axis=-1))
    mixed_heads = jnp.einsum('hqk,khd->qhd', weights_low, value_heads, precision=HIGHEST)
    return mixed_heads.reshape(length_here, head_count * HEAD)

def forward(token_rows, segment_block, project_weight, output_weight, up_weight, down_weight, norm_gains, bias_rows, hidden_bias):
    row_total = token_rows.shape[0]
    seq_here = segment_block.shape[0]
    projected = jnp.dot(token_rows, project_weight.reshape(D, 3 * D), precision=HIGHEST).reshape(row_total, 3, D)
    queries = low_back(low(projected[:, 0] + bias_rows[0]))
    key_rows = low_back(low(projected[:, 1]))
    value_rows = low_back(low(projected[:, 2] + bias_rows[1]))
    mixed_rows = jax.vmap(attend)(queries.reshape(seq_here, LEN, D), key_rows.reshape(seq_here, LEN, D), value_rows.reshape(seq_here, LEN, D), segment_block)
    mixed_rows = low_back(low(mixed_rows.reshape(row_total, D)))
    branch_out = low_back(jnp.dot(mixed_rows, output_weight, precision=HIGHEST) + bias_rows[2])
    first_out = layer_norm(token_rows + branch_out, norm_gains[0], bias_rows[3])
    upper_rows = low_back(jnp.dot(low(first_out), up_weight, precision=HIGHEST) + hidden_bias)
    hidden_rows = low(jax.nn.gelu(upper_rows, approximate=False))
    second_out = low_back(jnp.dot(hidden_rows, down_weight, precision=HIGHEST) + bias_rows[4])
    return layer_norm(first_out + second_out, norm_gains[1], bias_rows[5])

def reference(tokens, segments, cotangent, project_weight, output_weight, up_weight, down_weight, norm_gains, bias_rows, hidden_bias):
    per_block = math.gcd(SEQUENCES, 4)
    block_count = SEQUENCES // per_block
    rows_all = tokens.astype(jnp.float32).reshape(block_count, per_block * LEN, D)
    cotangent_all = cotangent.astype(jnp.float32).reshape(block_count, per_block * LEN, D)
    segment_all = segments.reshape(block_count, per_block, LEN)
    params = (project_weight.astype(jnp.float32), output_weight.astype(jnp.float32), up_weight.astype(jnp.float32), down_weight.astype(jnp.float32), norm_gains, bias_rows, hidden_bias)

    def one_block(totals, item):
        token_rows, segment_block, cotangent_rows = item

        def local_forward(rows_in, weight_one, weight_two, weight_three, weight_four, gain_in, bias_in, hidden_in):
            return forward(rows_in, segment_block, weight_one, weight_two, weight_three, weight_four, gain_in, bias_in, hidden_in)
        layer_rows, pullback = jax.vjp(local_forward, token_rows, *params)
        grads = pullback(cotangent_rows)
        new_totals = tuple((total + grad for total, grad in zip(totals, grads[1:])))
        return (new_totals, (layer_rows.astype(jnp.bfloat16), grads[0]))
    zeros = tuple((jnp.zeros_like(parameter) for parameter in params))
    totals, (layer_rows, grad_rows) = lax.scan(one_block, zeros, (rows_all, segment_all, cotangent_all))
    return (layer_rows.reshape(TOKENS, D), grad_rows.reshape(TOKENS, D), totals[0], totals[1], totals[2], totals[3], totals[4], totals[5], totals[6])
```

```python
import jax
import jax.numpy as jnp
from jax import lax
from jax.sharding import PartitionSpec as P

HEAD = 64


EPSILON = 1e-05
NEGATIVE = -1e30


def gelu_exact(values):
    return jax.nn.gelu(values, approximate=False)


def layer_norm(token_rows, gain, shift):
    average = jnp.mean(token_rows, axis=-1, keepdims=True)
    centred = token_rows - average
    variance = jnp.mean(centred * centred, axis=-1, keepdims=True)
    inverse = lax.rsqrt(variance + EPSILON)
    normed = centred * inverse
    return (normed * gain + shift, (normed, inverse))


def norm_back(grad_rows, saved, gain):
    normed, inverse = saved
    grad_gain = jnp.sum(grad_rows * normed, axis=0)
    grad_shift = jnp.sum(grad_rows, axis=0)
    grad_normed = grad_rows * gain
    grad_input = inverse * (
        grad_normed
        - jnp.mean(grad_normed, axis=-1, keepdims=True)
        - normed * jnp.mean(grad_normed * normed, axis=-1, keepdims=True)
    )
    return (grad_input, grad_gain, grad_shift)


def split_heads(token_rows):
    return token_rows.reshape(token_rows.shape[0], token_rows.shape[1] // HEAD, HEAD)


def scatter_sum(partial_sum, axis_name, dimension):
    return lax.psum_scatter(
        partial_sum.astype(jnp.bfloat16), axis_name, scatter_dimension=dimension, tiled=True
    ).astype(jnp.float32)


def place_columns(partial_sum, column_block, total_width):
    full_rows = jnp.zeros(partial_sum.shape[:-1] + (total_width,), jnp.float32)
    return lax.dynamic_update_slice_in_dim(
        full_rows, partial_sum, column_block * partial_sum.shape[-1], partial_sum.ndim - 1
    )


def per_device(
    tokens,
    segments,
    cotangent,
    project_weight,
    output_weight,
    up_weight,
    down_weight,
    norm_gains,
    bias_rows,
    hidden_bias,
):
    tensor_rank = lax.axis_index("tensor")
    local_rows, model_width = tokens.shape
    seq_count, seq_length = segments.shape
    group_rows = seq_count * seq_length
    local_width = project_weight.shape[2]
    score_scale = HEAD ** (-0.5)
    block_rows = min(512, seq_length)
    per_sequence = seq_length // block_rows
    count_blocks = group_rows // block_rows
    block_ids = jnp.arange(count_blocks, dtype=jnp.int32)
    triple_full, output_full, upward_full, downward_full = (
        lax.all_gather(project_weight, "dp", axis=0, tiled=True),
        lax.all_gather(output_weight, "dp", axis=1, tiled=True),
        lax.all_gather(up_weight, "dp", axis=0, tiled=True),
        lax.all_gather(down_weight, "dp", axis=1, tiled=True),
    )
    local_hidden = upward_full.shape[1]
    triple_matrix = triple_full.reshape(model_width, 3 * local_width)
    gathered = lax.all_gather(tokens, "tensor", axis=0, tiled=True)
    head_bias = lax.dynamic_slice_in_dim(bias_rows, tensor_rank * local_width, local_width, 1)
    projected = jnp.dot(gathered, triple_matrix, preferred_element_type=jnp.float32).reshape(
        group_rows, 3, local_width
    )
    queries = (projected[:, 0] + head_bias[0]).astype(jnp.bfloat16)
    key_rows = projected[:, 1].astype(jnp.bfloat16)
    value_rows = (projected[:, 2] + head_bias[1]).astype(jnp.bfloat16)

    def block_parts(block_index):
        sequence = block_index // per_sequence
        row_start = block_index * block_rows
        seq_start = sequence * seq_length
        query_block = split_heads(lax.dynamic_slice_in_dim(queries, row_start, block_rows, 0))
        key_block = split_heads(key_rows)
        value_block = split_heads(value_rows)
        seq_ids = lax.dynamic_index_in_dim(segments, sequence, 0, keepdims=False)
        query_ids = lax.dynamic_slice_in_dim(seq_ids, row_start - seq_start, block_rows, 0)
        products = (
            jnp.einsum("qhd,khd->hqk", query_block, key_block, preferred_element_type=jnp.float32)
            * score_scale
        )
        scores = jnp.where((query_ids[:, None] == seq_ids[None, :])[None], products, NEGATIVE)
        return (row_start, query_block, key_block, value_block, scores)

    def forward_block(block_index):
        row_start, query_block, key_block, value_block, scores = block_parts(block_index)
        row_max = jnp.max(scores, axis=-1, keepdims=True)
        exponent = jnp.exp(scores - row_max)
        row_sum = jnp.sum(exponent, axis=-1, keepdims=True)
        weights_low = (exponent / row_sum).astype(jnp.bfloat16)
        mixed_block = jnp.einsum(
            "hqk,khd->qhd", weights_low, value_block, preferred_element_type=jnp.float32
        )
        log_total = row_max[:, :, 0] + jnp.log(row_sum[:, :, 0])
        return (mixed_block.reshape(block_rows, local_width).astype(jnp.bfloat16), log_total)

    mixed_blocks, log_totals = lax.map(forward_block, block_ids)
    mixed_rows = mixed_blocks.reshape(group_rows, local_width)
    branch_out = (
        scatter_sum(
            jnp.dot(mixed_rows, output_full, preferred_element_type=jnp.float32), "tensor", 0
        )
        + bias_rows[2]
    )
    first_out, first_saved = layer_norm(
        tokens.astype(jnp.float32) + branch_out, norm_gains[0], bias_rows[3]
    )
    first_gathered = lax.all_gather(first_out.astype(jnp.bfloat16), "tensor", axis=0, tiled=True)
    local_bias = lax.dynamic_slice_in_dim(hidden_bias, tensor_rank * local_hidden, local_hidden, 0)
    upper_rows = (
        jnp.dot(first_gathered, upward_full, preferred_element_type=jnp.float32) + local_bias
    )
    hidden_full, gelu_back = jax.vjp(gelu_exact, upper_rows)
    hidden_rows = hidden_full.astype(jnp.bfloat16)
    second_out = (
        scatter_sum(
            jnp.dot(hidden_rows, downward_full, preferred_element_type=jnp.float32), "tensor", 0
        )
        + bias_rows[4]
    )
    layer_out, second_saved = layer_norm(first_out + second_out, norm_gains[1], bias_rows[5])
    reloaded = (
        lax.all_gather(project_weight, "dp", axis=0, tiled=True),
        lax.all_gather(output_weight, "dp", axis=1, tiled=True),
        lax.all_gather(up_weight, "dp", axis=0, tiled=True),
        lax.all_gather(down_weight, "dp", axis=1, tiled=True),
    )
    back_triple = reloaded[0].reshape(model_width, 3 * local_width)
    back_output, back_upward, back_downward = (reloaded[1], reloaded[2], reloaded[3])
    grad_layer = cotangent.astype(jnp.float32)
    grad_second_in, grad_gain_two, grad_shift_two = norm_back(
        grad_layer, second_saved, norm_gains[1]
    )
    grad_second = grad_second_in.astype(jnp.bfloat16)
    grad_second_all = lax.all_gather(grad_second, "tensor", axis=0, tiled=True)
    grad_down_part = jnp.einsum(
        "tf,td->fd", hidden_rows, grad_second_all, preferred_element_type=jnp.float32
    )
    grad_hidden = jnp.einsum(
        "td,fd->tf", grad_second_all, back_downward, preferred_element_type=jnp.float32
    )
    grad_upper = gelu_back(grad_hidden)[0].astype(jnp.bfloat16)
    grad_up_part = jnp.einsum(
        "td,tf->df", first_gathered, grad_upper, preferred_element_type=jnp.float32
    )
    grad_first = (
        scatter_sum(
            jnp.einsum("tf,df->td", grad_upper, back_upward, preferred_element_type=jnp.float32),
            "tensor",
            0,
        )
        + grad_second_in
    )
    grad_first_in, grad_gain_one, grad_shift_one = norm_back(grad_first, first_saved, norm_gains[0])
    grad_branch = grad_first_in.astype(jnp.bfloat16)
    grad_branch_all = lax.all_gather(grad_branch, "tensor", axis=0, tiled=True)
    grad_output_part = jnp.einsum(
        "tc,td->cd", mixed_rows, grad_branch_all, preferred_element_type=jnp.float32
    )
    grad_mixed = jnp.einsum(
        "td,cd->tc", grad_branch_all, back_output, preferred_element_type=jnp.float32
    ).astype(jnp.bfloat16)

    def backward_block(block_index):
        row_start, query_block, key_block, value_block, scores = block_parts(block_index)
        weights_full = jnp.exp(scores - log_totals[block_index][:, :, None])
        grad_mixed_block = split_heads(
            lax.dynamic_slice_in_dim(grad_mixed, row_start, block_rows, 0)
        )
        grad_weights = jnp.einsum(
            "qhd,khd->hqk", grad_mixed_block, value_block, preferred_element_type=jnp.float32
        )
        row_dot = jnp.sum(weights_full * grad_weights, axis=-1, keepdims=True)
        grad_scores = (weights_full * (grad_weights - row_dot)).astype(jnp.bfloat16)
        grad_query = (
            jnp.einsum("hqk,khd->qhd", grad_scores, key_block, preferred_element_type=jnp.float32)
            * score_scale
        )
        grad_key = (
            jnp.einsum("hqk,qhd->khd", grad_scores, query_block, preferred_element_type=jnp.float32)
            * score_scale
        )
        grad_value = jnp.einsum(
            "hqk,qhd->khd",
            weights_full.astype(jnp.bfloat16),
            grad_mixed_block,
            preferred_element_type=jnp.float32,
        )
        return (
            grad_query.reshape(block_rows, local_width),
            grad_key.reshape(seq_length, local_width),
            grad_value.reshape(seq_length, local_width),
        )

    query_blocks, key_blocks, value_blocks = lax.map(backward_block, block_ids)
    grad_queries = query_blocks.reshape(group_rows, local_width)
    grad_keys = (
        key_blocks.reshape(seq_count, per_sequence, seq_length, local_width)
        .sum(axis=1)
        .reshape(group_rows, local_width)
    )
    grad_values = (
        value_blocks.reshape(seq_count, per_sequence, seq_length, local_width)
        .sum(axis=1)
        .reshape(group_rows, local_width)
    )
    grad_projected = jnp.stack((grad_queries, grad_keys, grad_values), axis=1).astype(jnp.bfloat16)
    grad_project_part = jnp.einsum(
        "te,tsc->esc", gathered, grad_projected, preferred_element_type=jnp.float32
    )
    grad_matrix = grad_projected.reshape(group_rows, 3 * local_width)
    grad_tokens = (
        lax.psum_scatter(
            jnp.einsum(
                "tc,ec->te", grad_matrix, back_triple, preferred_element_type=jnp.float32
            ).astype(jnp.bfloat16),
            "tensor",
            scatter_dimension=0,
            tiled=True,
        ).astype(jnp.float32)
        + grad_first_in
    )
    grad_project, grad_output, grad_up, grad_down = (
        scatter_sum(grad_project_part, "dp", 0),
        scatter_sum(grad_output_part, "dp", 1),
        scatter_sum(grad_up_part, "dp", 0),
        scatter_sum(grad_down_part, "dp", 1),
    )
    head_terms = place_columns(
        jnp.stack(
            (
                jnp.sum(grad_projected[:, 0], axis=0, dtype=jnp.float32),
                jnp.sum(grad_projected[:, 2], axis=0, dtype=jnp.float32),
            )
        ),
        tensor_rank,
        model_width,
    )
    shared_terms = jnp.stack(
        (
            jnp.sum(grad_branch, axis=0, dtype=jnp.float32),
            grad_shift_one,
            jnp.sum(grad_second, axis=0, dtype=jnp.float32),
            grad_shift_two,
        )
    )
    bias_terms = jnp.concatenate((head_terms, shared_terms), axis=0)
    gain_terms = jnp.stack((grad_gain_one, grad_gain_two))
    hidden_terms = place_columns(
        jnp.sum(grad_upper, axis=0, dtype=jnp.float32), tensor_rank, hidden_bias.shape[0]
    )
    grad_gains, grad_bias_rows, grad_hidden_bias = lax.psum(
        (gain_terms, bias_terms, hidden_terms), ("dp", "tensor")
    )
    return (
        layer_out.astype(jnp.bfloat16),
        grad_tokens,
        grad_project,
        grad_output,
        grad_up,
        grad_down,
        grad_gains,
        grad_bias_rows,
        grad_hidden_bias,
    )


def solution(mesh):
    placed = (
        P(("dp", "tensor"), None),
        P("dp", None),
        P(("dp", "tensor"), None),
        P("dp", None, "tensor"),
        P("tensor", "dp"),
        P("dp", "tensor"),
        P("tensor", "dp"),
        P(),
        P(),
        P(),
    )
    return jax.shard_map(
        per_device,
        mesh=mesh,
        in_specs=placed,
        out_specs=(
            P(("dp", "tensor"), None),
            P(("dp", "tensor"), None),
            P("dp", None, "tensor"),
            P("tensor", "dp"),
            P("dp", "tensor"),
            P("tensor", "dp"),
            P(),
            P(),
            P(),
        ),
        check_vma=False,
    )
```

```python
import functools

import jax
import jax.numpy as jnp
from jax import lax
from jax.experimental import pallas as pl
from jax.experimental.pallas import tpu as pltpu
from jax.sharding import PartitionSpec as P

HEAD = 64
EPSILON = 1e-05
NEGATIVE = -1e30
MESH = pl.DeviceIdType.MESH
LINES = 4
CORE, ACROSS, FAR = 1, 2, 3
HALVES = 2
VMEM_BYTES = 60 << 20


def remote(src, dst, send_sem, recv_sem, target):
    return pltpu.make_async_remote_copy(
        src_ref=src,
        dst_ref=dst,
        send_sem=send_sem,
        recv_sem=recv_sem,
        device_id=target,
        device_id_type=MESH,
    )


def position():
    return lax.axis_index("dp"), lax.axis_index("tensor")


def greet(with_line):
    dp, tensor = position()
    barrier = pltpu.get_barrier_semaphore()

    def signal(target):
        pl.semaphore_signal(barrier, inc=1, device_id=target, device_id_type=MESH)

    signal((dp, tensor ^ CORE))
    signal((dp, tensor ^ ACROSS))
    count = 2
    if with_line:
        signal((dp ^ 1, tensor))
        line = dp // 2

        @pl.when(line > 0)
        def _():
            signal((dp - 2, tensor))

        @pl.when(line < LINES - 1)
        def _():
            signal((dp + 2, tensor))

        ends = jnp.where(line > 0, 1, 0) + jnp.where(line < LINES - 1, 1, 0)
        count = 3 + ends
    pl.semaphore_wait(barrier, count)


def row_piece(ref, index, size):
    return ref.at[pl.ds(pl.multiple_of(index * size, size), size), :]


def column_piece(ref, index, size):
    return ref.at[:, pl.ds(pl.multiple_of(index * size, size), size)]


class LineGather:
    def __init__(self, own, full, piece, send_sem, recv_sem, local_sem):
        self.own, self.full, self.piece = own, full, piece
        self.send_sem, self.recv_sem, self.local_sem = send_sem, recv_sem, local_sem
        self.dp, self.tensor = position()
        self.line, self.side = self.dp // 2, self.dp % 2
        self.targets = (
            (self.dp + 2, self.tensor),
            (self.dp - 2, self.tensor),
            (self.dp ^ 1, self.tensor),
        )

    def copy(self, index, way, src=None):
        view = self.piece(self.full, index)
        return remote(
            view if src is None else src,
            view,
            self.send_sem.at[way * LINES + index // 2],
            self.recv_sem.at[index],
            self.targets[way],
        )

    def local(self):
        return pltpu.make_async_copy(self.own, self.piece(self.full, self.dp), self.local_sem)

    def start(self):
        self.local().start()

        @pl.when(self.line < LINES - 1)
        def _():
            self.copy(self.dp, 0, self.own).start()

        @pl.when(self.line > 0)
        def _():
            self.copy(self.dp, 1, self.own).start()

        self.copy(self.dp, 2, self.own).start()

    def step(self, distance):
        @pl.when(self.line >= distance)
        def _():
            index = self.dp - 2 * distance
            self.copy(index, 0).wait_recv()

            @pl.when(self.line < LINES - 1)
            def _():
                self.copy(index, 0).start()

            self.copy(index, 2).start()

        @pl.when(self.line + distance < LINES)
        def _():
            index = self.dp + 2 * distance
            self.copy(index, 1).wait_recv()

            @pl.when(self.line > 0)
            def _():
                self.copy(index, 1).start()

            self.copy(index, 2).start()

    def arrive(self):
        self.local().wait()
        for line in range(LINES):
            self.copy(2 * line + 1 - self.side, 2).wait_recv()

    def finish(self):
        for line in range(LINES):
            index = 2 * line + self.side
            self.copy(index, 2).wait_send()

            @pl.when((self.line < LINES - 1) & (line <= self.line))
            def _():
                self.copy(index, 0).wait_send()

            @pl.when((self.line > 0) & (line >= self.line))
            def _():
                self.copy(index, 1).wait_send()


class RowGather:
    def __init__(self, full, rows, send_sem, recv_sem):
        self.full, self.rows = full, rows
        self.send_sem, self.recv_sem = send_sem, recv_sem
        self.dp, self.tensor = position()

    def view(self, rank, half=None):
        if half is None:
            return row_piece(self.full, rank, self.rows)
        return row_piece(self.full, rank * HALVES + half, self.rows // HALVES)

    def near(self, rank):
        view = self.view(rank)
        target = (self.dp, self.tensor ^ CORE)
        return remote(view, view, self.send_sem.at[0], self.recv_sem.at[0], target)

    def across(self, rank, half):
        view, slot = self.view(rank, half), 1 + half
        target = (self.dp, self.tensor ^ ACROSS)
        return remote(view, view, self.send_sem.at[slot], self.recv_sem.at[slot], target)

    def far(self, rank, half):
        view, slot = self.view(rank, half), 1 + HALVES + half
        target = (self.dp, self.tensor ^ CORE)
        return remote(view, view, self.send_sem.at[slot], self.recv_sem.at[slot], target)

    def start(self):
        for half in range(HALVES):
            self.across(self.tensor, half).start()
        self.near(self.tensor).start()

    def wait_near(self):
        self.near(self.tensor ^ CORE).wait_recv()

    def wait_across(self, half):
        self.across(self.tensor ^ ACROSS, half).wait_recv()
        self.far(self.tensor ^ ACROSS, half).start()

    def wait_far(self, half):
        self.far(self.tensor ^ FAR, half).wait_recv()

    def finish(self):
        self.near(self.tensor).wait_send()
        for half in range(HALVES):
            self.across(self.tensor, half).wait_send()
            self.far(self.tensor ^ ACROSS, half).wait_send()


GATHER_SEMS = [pltpu.SemaphoreType.DMA((1 + 2 * HALVES,))] * 2


class RowScatter:
    def __init__(self, near_out, near_in, across_out, across_in, send_sem, recv_sem):
        self.near_out, self.near_in = near_out, near_in
        self.across_out, self.across_in = across_out, across_in
        self.send_sem, self.recv_sem = send_sem, recv_sem
        self.dp, self.tensor = position()

    def near(self, slot):
        return remote(
            self.near_out.at[slot],
            self.near_in.at[slot],
            self.send_sem.at[slot],
            self.recv_sem.at[slot],
            (self.dp, self.tensor ^ CORE),
        )

    def across(self, half):
        rows = self.across_in.shape[0] // HALVES
        return remote(
            row_piece(self.across_out, half, rows),
            row_piece(self.across_in, half, rows),
            self.send_sem.at[2 * HALVES + half],
            self.recv_sem.at[2 * HALVES + half],
            (self.dp, self.tensor ^ ACROSS),
        )

    def give_far(self, half, partial):
        self.near_out[half] = partial.astype(jnp.bfloat16)
        self.near(half).start()

    def give_across(self, half, partial):
        self.near(half).wait_recv()
        rows = partial.shape[0]
        total = partial + self.near_in[half].astype(jnp.float32)
        self.across_out[half * rows : (half + 1) * rows, :] = total.astype(jnp.bfloat16)
        self.across(half).start()

    def give_near(self, half, partial):
        self.near_out[HALVES + half] = partial.astype(jnp.bfloat16)
        self.near(HALVES + half).start()

    def take(self, half, partial):
        self.near(HALVES + half).wait_recv()
        rows = partial.shape[0]
        total = partial + self.near_in[HALVES + half].astype(jnp.float32)
        self.across(half).wait_recv()
        return total + self.across_in[half * rows : (half + 1) * rows, :].astype(jnp.float32)

    def finish(self):
        for slot in range(2 * HALVES):
            self.near(slot).wait_send()
        for half in range(HALVES):
            self.across(half).wait_send()


def scatter_scratch(rows, width):
    half = rows // HALVES
    return [
        pltpu.VMEM((2 * HALVES, half, width), jnp.bfloat16),
        pltpu.VMEM((2 * HALVES, half, width), jnp.bfloat16),
        pltpu.VMEM((rows, width), jnp.bfloat16),
        pltpu.VMEM((rows, width), jnp.bfloat16),
        pltpu.SemaphoreType.DMA((3 * HALVES,)),
        pltpu.SemaphoreType.DMA((3 * HALVES,)),
    ]


def dot(left, right):
    return jnp.dot(left, right, preferred_element_type=jnp.float32)


def dot_nt(left, right):
    return lax.dot_general(left, right, (((1,), (1,)), ((), ())), preferred_element_type=jnp.float32)


def dot_tn(left, right):
    return lax.dot_general(left, right, (((0,), (0,)), ((), ())), preferred_element_type=jnp.float32)


def normalize(rows):
    centred = rows - jnp.mean(rows, axis=-1, keepdims=True)
    inverse = lax.rsqrt(jnp.mean(centred * centred, axis=-1, keepdims=True) + EPSILON)
    return centred * inverse, inverse


def block_rows(ref, rank, rows):
    return ref[pl.ds(pl.multiple_of(rank * rows, rows), rows), :]


def attend_kernel(
    rows,
    tokens,
    triple_own,
    output_own,
    up_own,
    down_own,
    segment_column,
    segment_row,
    bias_rows,
    norm_gains,
    gathered_out,
    triple_out,
    output_out,
    up_full,
    down_full,
    queries,
    key_rows,
    value_rows,
    mixed,
    log_totals,
    normed_out,
    inverse_out,
    first_low,
    gathered,
    triple,
    output,
    line_send,
    line_recv,
    line_local,
    row_send,
    row_recv,
    near_out,
    near_in,
    across_out,
    across_in,
    sum_send,
    sum_recv,
    save_sem,
):
    dp, tensor = position()
    local = queries.shape[1]
    gather = RowGather(gathered, rows, row_send, row_recv)
    scatter = RowScatter(near_out, near_in, across_out, across_in, sum_send, sum_recv)
    piece = triple_own.shape[0]

    def of_rows(ref, index):
        return row_piece(ref, index, piece)

    def of_columns(ref, index):
        return column_piece(ref, index, piece)

    def line(at, own, full, view):
        return LineGather(own, full, view, line_send.at[at], line_recv.at[at], line_local.at[at])

    triple_line = line(0, triple_own, triple, of_rows)
    output_line = line(1, output_own, output, of_columns)
    up_line = line(2, up_own, up_full, of_rows)
    down_line = line(3, down_own, down_full, of_columns)
    greet(True)
    place = pltpu.make_async_copy(tokens, gather.view(tensor), save_sem.at[0])
    place.start()
    triple_line.start()
    place.wait()
    gather.start()
    triple_line.step(1)
    triple_line.step(2)
    gather.wait_near()
    for half in range(HALVES):
        gather.wait_across(half)
    triple_line.step(3)
    output_line.start()
    up_line.start()
    for half in range(HALVES):
        gather.wait_far(half)
    triple_line.arrive()
    saves = [
        pltpu.make_async_copy(gathered, gathered_out, save_sem.at[0]),
        pltpu.make_async_copy(triple, triple_out, save_sem.at[1]),
    ]
    for save in saves:
        save.start()
    columns = pl.ds(pl.multiple_of(tensor * local, local), local)
    query_bias = bias_rows[0:1, columns]
    value_bias = bias_rows[1:2, columns]

    @pl.loop(0, 4)
    def _(block):
        here = pl.ds(pl.multiple_of(block * rows, rows), rows)
        left = gathered[here, :]
        query = (dot(left, triple[:, :local]) + query_bias).astype(jnp.bfloat16)
        queries[here, :] = query * jnp.bfloat16(HEAD**-0.5)
        key_rows[here, :] = dot(left, triple[:, local : 2 * local]).astype(jnp.bfloat16)
        value = dot(left, triple[:, 2 * local :]) + value_bias
        value_rows[here, :] = value.astype(jnp.bfloat16)

    output_line.step(1)
    up_line.step(1)

    def attend(rank):
        here = pl.ds(pl.multiple_of(rank * rows, rows), rows)

        @pl.loop(0, local // (2 * HEAD))
        def _(pair):
            lanes = pl.ds(pl.multiple_of(pair * 2 * HEAD, 2 * HEAD), 2 * HEAD)
            query = queries[here, lanes]
            keys = key_rows[:, lanes]
            values = value_rows[:, lanes]
            same = segment_column[here, :] == segment_row[...]
            lane = lax.broadcasted_iota(jnp.int32, (rows, 2 * HEAD), 1)
            outs = []
            for side in range(2):
                mine = lane // HEAD == side
                scores = dot_nt(jnp.where(mine, query, jnp.bfloat16(0)), keys)
                scores = jnp.where(same, scores, NEGATIVE)
                top = jnp.max(scores, axis=-1, keepdims=True)
                exponent = jnp.exp(scores - top)
                total = jnp.sum(exponent, axis=-1, keepdims=True)
                weights = (exponent * (1.0 / total)).astype(jnp.bfloat16)
                outs.append(dot(weights, values))
                log_totals[pair * 2 + side, here, :] = top + jnp.log(total)
            mixed[here, lanes] = jnp.where(lane < HEAD, outs[0], outs[1]).astype(jnp.bfloat16)

        return mixed[here, :]

    def halves_of(partial):
        half = rows // HALVES
        return [partial[at * half : (at + 1) * half] for at in range(HALVES)]

    far = attend(tensor ^ FAR)
    output_line.step(2)
    output_line.step(3)
    up_line.step(2)
    output_line.arrive()
    save = pltpu.make_async_copy(output, output_out, save_sem.at[2])
    save.start()
    saves.append(save)
    for half, partial in enumerate(halves_of(dot(far, output[...]))):
        scatter.give_far(half, partial)
    other = attend(tensor ^ ACROSS)
    for half, partial in enumerate(halves_of(dot(other, output[...]))):
        scatter.give_across(half, partial)
    up_line.step(3)
    down_line.start()
    near = attend(tensor ^ CORE)
    for half, partial in enumerate(halves_of(dot(near, output[...]))):
        scatter.give_near(half, partial)
    down_line.step(1)
    mine = attend(tensor)
    for half, partial in enumerate(halves_of(dot(mine, output[...]))):
        part = slice(half * rows // HALVES, (half + 1) * rows // HALVES)
        total = scatter.take(half, partial) + bias_rows[2:3, :]
        own_rows = row_piece(gathered, tensor * HALVES + half, rows // HALVES)
        normed, inverse = normalize(own_rows[...].astype(jnp.float32) + total)
        normed_out[part, :] = normed
        inverse_out[part, :] = inverse
        first_low[part, :] = (normed * norm_gains[0:1, :] + bias_rows[3:4, :]).astype(jnp.bfloat16)
    scatter.finish()
    gather.finish()
    down_line.step(2)
    down_line.step(3)
    for each in (up_line, down_line):
        each.arrive()
    for each in (triple_line, output_line, up_line, down_line):
        each.finish()
    for save in saves:
        save.wait()


def attend_forward(tokens, triple_own, output_own, up_own, down_own, segments, bias_rows, norm_gains):
    rows, width = tokens.shape
    length = segments.shape[1]
    local = triple_own.shape[1] // 3
    heads = local // HEAD
    pieces = 2 * LINES
    bf16, f32 = jnp.bfloat16, jnp.float32
    vmem, hbm = pl.BlockSpec(memory_space=pltpu.VMEM), pl.BlockSpec(memory_space=pltpu.HBM)
    hidden = up_own.shape[1]
    return pl.pallas_call(
        functools.partial(attend_kernel, rows),
        out_shape=[
            jax.ShapeDtypeStruct((length, width), bf16),
            jax.ShapeDtypeStruct((width, 3 * local), bf16),
            jax.ShapeDtypeStruct((local, width), bf16),
            jax.ShapeDtypeStruct((width, hidden), bf16),
            jax.ShapeDtypeStruct((hidden, width), bf16),
            jax.ShapeDtypeStruct((length, local), bf16),
            jax.ShapeDtypeStruct((length, local), bf16),
            jax.ShapeDtypeStruct((length, local), bf16),
            jax.ShapeDtypeStruct((length, local), bf16),
            jax.ShapeDtypeStruct((heads, length, 1), f32),
            jax.ShapeDtypeStruct((rows, width), f32),
            jax.ShapeDtypeStruct((rows, 1), f32),
            jax.ShapeDtypeStruct((rows, width), bf16),
        ],
        in_specs=[hbm] * 5 + [vmem] * 4,
        out_specs=[hbm] * 5 + [vmem] * 8,
        scratch_shapes=[
            pltpu.VMEM((length, width), bf16),
            pltpu.VMEM((width, 3 * local), bf16),
            pltpu.VMEM((local, width), bf16),
            pltpu.SemaphoreType.DMA((4, 3 * LINES)),
            pltpu.SemaphoreType.DMA((4, pieces)),
            pltpu.SemaphoreType.DMA((4,)),
        ]
        + GATHER_SEMS
        + scatter_scratch(rows, width)
        + [pltpu.SemaphoreType.DMA((3,))],
        compiler_params=pltpu.CompilerParams(
            collective_id=0, has_side_effects=True, vmem_limit_bytes=VMEM_BYTES
        ),
        name="attend_forward",
    )(
        tokens,
        triple_own,
        output_own,
        up_own,
        down_own,
        segments.reshape(length, 1),
        segments.reshape(1, length),
        bias_rows,
        norm_gains,
    )


def gelu_exact(values):
    return jax.nn.gelu(values, approximate=False)


def layer_norm(token_rows, gain, shift):
    average = jnp.mean(token_rows, axis=-1, keepdims=True)
    centred = token_rows - average
    variance = jnp.mean(centred * centred, axis=-1, keepdims=True)
    inverse = lax.rsqrt(variance + EPSILON)
    normed = centred * inverse
    return (normed * gain + shift, (normed, inverse))


def norm_back(grad_rows, saved, gain):
    normed, inverse = saved
    grad_gain = jnp.sum(grad_rows * normed, axis=0)
    grad_shift = jnp.sum(grad_rows, axis=0)
    grad_normed = grad_rows * gain
    grad_input = inverse * (
        grad_normed
        - jnp.mean(grad_normed, axis=-1, keepdims=True)
        - normed * jnp.mean(grad_normed * normed, axis=-1, keepdims=True)
    )
    return (grad_input, grad_gain, grad_shift)


def split_heads(token_rows):
    return token_rows.reshape(token_rows.shape[0], token_rows.shape[1] // HEAD, HEAD)


def scatter_sum(partial_sum, axis_name, dimension):
    return lax.psum_scatter(
        partial_sum.astype(jnp.bfloat16), axis_name, scatter_dimension=dimension, tiled=True
    ).astype(jnp.float32)


def place_columns(partial_sum, column_block, total_width):
    full_rows = jnp.zeros(partial_sum.shape[:-1] + (total_width,), jnp.float32)
    return lax.dynamic_update_slice_in_dim(
        full_rows, partial_sum, column_block * partial_sum.shape[-1], partial_sum.ndim - 1
    )


def per_device(
    tokens,
    segments,
    cotangent,
    project_weight,
    output_weight,
    up_weight,
    down_weight,
    norm_gains,
    bias_rows,
    hidden_bias,
):
    tensor_rank = lax.axis_index("tensor")
    local_rows, model_width = tokens.shape
    seq_count, seq_length = segments.shape
    group_rows = seq_count * seq_length
    local_width = project_weight.shape[2]
    score_scale = HEAD ** (-0.5)
    block_rows = min(512, seq_length)
    per_sequence = seq_length // block_rows
    count_blocks = group_rows // block_rows
    block_ids = jnp.arange(count_blocks, dtype=jnp.int32)
    triple_full, output_full, upward_full, downward_full = (
        lax.all_gather(project_weight, "dp", axis=0, tiled=True),
        lax.all_gather(output_weight, "dp", axis=1, tiled=True),
        lax.all_gather(up_weight, "dp", axis=0, tiled=True),
        lax.all_gather(down_weight, "dp", axis=1, tiled=True),
    )
    local_hidden = upward_full.shape[1]
    triple_matrix = triple_full.reshape(model_width, 3 * local_width)
    gathered = lax.all_gather(tokens, "tensor", axis=0, tiled=True)
    head_bias = lax.dynamic_slice_in_dim(bias_rows, tensor_rank * local_width, local_width, 1)
    projected = jnp.dot(gathered, triple_matrix, preferred_element_type=jnp.float32).reshape(
        group_rows, 3, local_width
    )
    queries = (projected[:, 0] + head_bias[0]).astype(jnp.bfloat16)
    key_rows = projected[:, 1].astype(jnp.bfloat16)
    value_rows = (projected[:, 2] + head_bias[1]).astype(jnp.bfloat16)

    def block_parts(block_index):
        sequence = block_index // per_sequence
        row_start = block_index * block_rows
        seq_start = sequence * seq_length
        query_block = split_heads(lax.dynamic_slice_in_dim(queries, row_start, block_rows, 0))
        key_block = split_heads(key_rows)
        value_block = split_heads(value_rows)
        seq_ids = lax.dynamic_index_in_dim(segments, sequence, 0, keepdims=False)
        query_ids = lax.dynamic_slice_in_dim(seq_ids, row_start - seq_start, block_rows, 0)
        products = (
            jnp.einsum("qhd,khd->hqk", query_block, key_block, preferred_element_type=jnp.float32)
            * score_scale
        )
        scores = jnp.where((query_ids[:, None] == seq_ids[None, :])[None], products, NEGATIVE)
        return (row_start, query_block, key_block, value_block, scores)

    def forward_block(block_index):
        row_start, query_block, key_block, value_block, scores = block_parts(block_index)
        row_max = jnp.max(scores, axis=-1, keepdims=True)
        exponent = jnp.exp(scores - row_max)
        row_sum = jnp.sum(exponent, axis=-1, keepdims=True)
        weights_low = (exponent / row_sum).astype(jnp.bfloat16)
        mixed_block = jnp.einsum(
            "hqk,khd->qhd", weights_low, value_block, preferred_element_type=jnp.float32
        )
        log_total = row_max[:, :, 0] + jnp.log(row_sum[:, :, 0])
        return (mixed_block.reshape(block_rows, local_width).astype(jnp.bfloat16), log_total)

    mixed_blocks, log_totals = lax.map(forward_block, block_ids)
    mixed_rows = mixed_blocks.reshape(group_rows, local_width)
    branch_out = (
        scatter_sum(
            jnp.dot(mixed_rows, output_full, preferred_element_type=jnp.float32), "tensor", 0
        )
        + bias_rows[2]
    )
    first_out, first_saved = layer_norm(
        tokens.astype(jnp.float32) + branch_out, norm_gains[0], bias_rows[3]
    )
    first_gathered = lax.all_gather(first_out.astype(jnp.bfloat16), "tensor", axis=0, tiled=True)
    local_bias = lax.dynamic_slice_in_dim(hidden_bias, tensor_rank * local_hidden, local_hidden, 0)
    upper_rows = (
        jnp.dot(first_gathered, upward_full, preferred_element_type=jnp.float32) + local_bias
    )
    hidden_full, gelu_back = jax.vjp(gelu_exact, upper_rows)
    hidden_rows = hidden_full.astype(jnp.bfloat16)
    second_out = (
        scatter_sum(
            jnp.dot(hidden_rows, downward_full, preferred_element_type=jnp.float32), "tensor", 0
        )
        + bias_rows[4]
    )
    layer_out, second_saved = layer_norm(first_out + second_out, norm_gains[1], bias_rows[5])
    reloaded = (
        lax.all_gather(project_weight, "dp", axis=0, tiled=True),
        lax.all_gather(output_weight, "dp", axis=1, tiled=True),
        lax.all_gather(up_weight, "dp", axis=0, tiled=True),
        lax.all_gather(down_weight, "dp", axis=1, tiled=True),
    )
    back_triple = reloaded[0].reshape(model_width, 3 * local_width)
    back_output, back_upward, back_downward = (reloaded[1], reloaded[2], reloaded[3])
    grad_layer = cotangent.astype(jnp.float32)
    grad_second_in, grad_gain_two, grad_shift_two = norm_back(
        grad_layer, second_saved, norm_gains[1]
    )
    grad_second = grad_second_in.astype(jnp.bfloat16)
    grad_second_all = lax.all_gather(grad_second, "tensor", axis=0, tiled=True)
    grad_down_part = jnp.einsum(
        "tf,td->fd", hidden_rows, grad_second_all, preferred_element_type=jnp.float32
    )
    grad_hidden = jnp.einsum(
        "td,fd->tf", grad_second_all, back_downward, preferred_element_type=jnp.float32
    )
    grad_upper = gelu_back(grad_hidden)[0].astype(jnp.bfloat16)
    grad_up_part = jnp.einsum(
        "td,tf->df", first_gathered, grad_upper, preferred_element_type=jnp.float32
    )
    grad_first = (
        scatter_sum(
            jnp.einsum("tf,df->td", grad_upper, back_upward, preferred_element_type=jnp.float32),
            "tensor",
            0,
        )
        + grad_second_in
    )
    grad_first_in, grad_gain_one, grad_shift_one = norm_back(grad_first, first_saved, norm_gains[0])
    grad_branch = grad_first_in.astype(jnp.bfloat16)
    grad_branch_all = lax.all_gather(grad_branch, "tensor", axis=0, tiled=True)
    grad_output_part = jnp.einsum(
        "tc,td->cd", mixed_rows, grad_branch_all, preferred_element_type=jnp.float32
    )
    grad_mixed = jnp.einsum(
        "td,cd->tc", grad_branch_all, back_output, preferred_element_type=jnp.float32
    ).astype(jnp.bfloat16)

    def backward_block(block_index):
        row_start, query_block, key_block, value_block, scores = block_parts(block_index)
        weights_full = jnp.exp(scores - log_totals[block_index][:, :, None])
        grad_mixed_block = split_heads(
            lax.dynamic_slice_in_dim(grad_mixed, row_start, block_rows, 0)
        )
        grad_weights = jnp.einsum(
            "qhd,khd->hqk", grad_mixed_block, value_block, preferred_element_type=jnp.float32
        )
        row_dot = jnp.sum(weights_full * grad_weights, axis=-1, keepdims=True)
        grad_scores = (weights_full * (grad_weights - row_dot)).astype(jnp.bfloat16)
        grad_query = (
            jnp.einsum("hqk,khd->qhd", grad_scores, key_block, preferred_element_type=jnp.float32)
            * score_scale
        )
        grad_key = (
            jnp.einsum("hqk,qhd->khd", grad_scores, query_block, preferred_element_type=jnp.float32)
            * score_scale
        )
        grad_value = jnp.einsum(
            "hqk,qhd->khd",
            weights_full.astype(jnp.bfloat16),
            grad_mixed_block,
            preferred_element_type=jnp.float32,
        )
        return (
            grad_query.reshape(block_rows, local_width),
            grad_key.reshape(seq_length, local_width),
            grad_value.reshape(seq_length, local_width),
        )

    query_blocks, key_blocks, value_blocks = lax.map(backward_block, block_ids)
    grad_queries = query_blocks.reshape(group_rows, local_width)
    grad_keys = (
        key_blocks.reshape(seq_count, per_sequence, seq_length, local_width)
        .sum(axis=1)
        .reshape(group_rows, local_width)
    )
    grad_values = (
        value_blocks.reshape(seq_count, per_sequence, seq_length, local_width)
        .sum(axis=1)
        .reshape(group_rows, local_width)
    )
    grad_projected = jnp.stack((grad_queries, grad_keys, grad_values), axis=1).astype(jnp.bfloat16)
    grad_project_part = jnp.einsum(
        "te,tsc->esc", gathered, grad_projected, preferred_element_type=jnp.float32
    )
    grad_matrix = grad_projected.reshape(group_rows, 3 * local_width)
    grad_tokens = (
        lax.psum_scatter(
            jnp.einsum(
                "tc,ec->te", grad_matrix, back_triple, preferred_element_type=jnp.float32
            ).astype(jnp.bfloat16),
            "tensor",
            scatter_dimension=0,
            tiled=True,
        ).astype(jnp.float32)
        + grad_first_in
    )
    grad_project, grad_output, grad_up, grad_down = (
        scatter_sum(grad_project_part, "dp", 0),
        scatter_sum(grad_output_part, "dp", 1),
        scatter_sum(grad_up_part, "dp", 0),
        scatter_sum(grad_down_part, "dp", 1),
    )
    head_terms = place_columns(
        jnp.stack(
            (
                jnp.sum(grad_projected[:, 0], axis=0, dtype=jnp.float32),
                jnp.sum(grad_projected[:, 2], axis=0, dtype=jnp.float32),
            )
        ),
        tensor_rank,
        model_width,
    )
    shared_terms = jnp.stack(
        (
            jnp.sum(grad_branch, axis=0, dtype=jnp.float32),
            grad_shift_one,
            jnp.sum(grad_second, axis=0, dtype=jnp.float32),
            grad_shift_two,
        )
    )
    bias_terms = jnp.concatenate((head_terms, shared_terms), axis=0)
    gain_terms = jnp.stack((grad_gain_one, grad_gain_two))
    hidden_terms = place_columns(
        jnp.sum(grad_upper, axis=0, dtype=jnp.float32), tensor_rank, hidden_bias.shape[0]
    )
    grad_gains, grad_bias_rows, grad_hidden_bias = lax.psum(
        (gain_terms, bias_terms, hidden_terms), ("dp", "tensor")
    )
    return (
        layer_out.astype(jnp.bfloat16),
        grad_tokens,
        grad_project,
        grad_output,
        grad_up,
        grad_down,
        grad_gains,
        grad_bias_rows,
        grad_hidden_bias,
    )


def per_device_kernels(
    tokens,
    segments,
    cotangent,
    project_weight,
    output_weight,
    up_weight,
    down_weight,
    norm_gains,
    bias_rows,
    hidden_bias,
):
    tensor_rank = lax.axis_index("tensor")
    local_rows, model_width = tokens.shape
    seq_count, seq_length = segments.shape
    group_rows = seq_count * seq_length
    local_width = project_weight.shape[2]
    score_scale = HEAD ** (-0.5)
    block_rows = min(512, seq_length)
    per_sequence = seq_length // block_rows
    count_blocks = group_rows // block_rows
    block_ids = jnp.arange(count_blocks, dtype=jnp.int32)
    (
        gathered,
        triple_matrix,
        output_full,
        upward_full,
        downward_full,
        queries,
        key_rows,
        value_rows,
        mixed_rows,
        log_totals,
        normed_one,
        inverse_one,
        first_low,
    ) = attend_forward(
        tokens,
        project_weight.reshape(project_weight.shape[0], -1),
        output_weight,
        up_weight,
        down_weight,
        segments,
        bias_rows,
        norm_gains,
    )
    first_out = normed_one * norm_gains[0] + bias_rows[3]
    first_saved = (normed_one, inverse_one)
    queries = queries * jnp.bfloat16(8)
    log_totals = jnp.stack(
        [log_totals[:, i * block_rows : (i + 1) * block_rows, 0] for i in range(count_blocks)]
    )
    local_hidden = upward_full.shape[1]
    def block_parts(block_index):
        sequence = block_index // per_sequence
        row_start = block_index * block_rows
        seq_start = sequence * seq_length
        query_block = split_heads(lax.dynamic_slice_in_dim(queries, row_start, block_rows, 0))
        key_block = split_heads(key_rows)
        value_block = split_heads(value_rows)
        seq_ids = lax.dynamic_index_in_dim(segments, sequence, 0, keepdims=False)
        query_ids = lax.dynamic_slice_in_dim(seq_ids, row_start - seq_start, block_rows, 0)
        products = (
            jnp.einsum("qhd,khd->hqk", query_block, key_block, preferred_element_type=jnp.float32)
            * score_scale
        )
        scores = jnp.where((query_ids[:, None] == seq_ids[None, :])[None], products, NEGATIVE)
        return (row_start, query_block, key_block, value_block, scores)

    first_gathered = lax.all_gather(first_low, "tensor", axis=0, tiled=True)
    local_bias = lax.dynamic_slice_in_dim(hidden_bias, tensor_rank * local_hidden, local_hidden, 0)
    upper_rows = (
        jnp.dot(first_gathered, upward_full, preferred_element_type=jnp.float32) + local_bias
    )
    hidden_full, gelu_back = jax.vjp(gelu_exact, upper_rows)
    hidden_rows = hidden_full.astype(jnp.bfloat16)
    second_out = (
        scatter_sum(
            jnp.dot(hidden_rows, downward_full, preferred_element_type=jnp.float32), "tensor", 0
        )
        + bias_rows[4]
    )
    layer_out, second_saved = layer_norm(first_out + second_out, norm_gains[1], bias_rows[5])
    reloaded = (triple_matrix, output_full, upward_full, downward_full)
    back_triple = triple_matrix.reshape(model_width, 3 * local_width)
    back_output, back_upward, back_downward = (reloaded[1], reloaded[2], reloaded[3])
    grad_layer = cotangent.astype(jnp.float32)
    grad_second_in, grad_gain_two, grad_shift_two = norm_back(
        grad_layer, second_saved, norm_gains[1]
    )
    grad_second = grad_second_in.astype(jnp.bfloat16)
    grad_second_all = lax.all_gather(grad_second, "tensor", axis=0, tiled=True)
    grad_down_part = jnp.einsum(
        "tf,td->fd", hidden_rows, grad_second_all, preferred_element_type=jnp.float32
    )
    grad_hidden = jnp.einsum(
        "td,fd->tf", grad_second_all, back_downward, preferred_element_type=jnp.float32
    )
    grad_upper = gelu_back(grad_hidden)[0].astype(jnp.bfloat16)
    grad_up_part = jnp.einsum(
        "td,tf->df", first_gathered, grad_upper, preferred_element_type=jnp.float32
    )
    grad_first = (
        scatter_sum(
            jnp.einsum("tf,df->td", grad_upper, back_upward, preferred_element_type=jnp.float32),
            "tensor",
            0,
        )
        + grad_second_in
    )
    grad_first_in, grad_gain_one, grad_shift_one = norm_back(grad_first, first_saved, norm_gains[0])
    grad_branch = grad_first_in.astype(jnp.bfloat16)
    grad_branch_all = lax.all_gather(grad_branch, "tensor", axis=0, tiled=True)
    grad_output_part = jnp.einsum(
        "tc,td->cd", mixed_rows, grad_branch_all, preferred_element_type=jnp.float32
    )
    grad_mixed = jnp.einsum(
        "td,cd->tc", grad_branch_all, back_output, preferred_element_type=jnp.float32
    ).astype(jnp.bfloat16)

    def backward_block(block_index):
        row_start, query_block, key_block, value_block, scores = block_parts(block_index)
        weights_full = jnp.exp(scores - log_totals[block_index][:, :, None])
        grad_mixed_block = split_heads(
            lax.dynamic_slice_in_dim(grad_mixed, row_start, block_rows, 0)
        )
        grad_weights = jnp.einsum(
            "qhd,khd->hqk", grad_mixed_block, value_block, preferred_element_type=jnp.float32
        )
        row_dot = jnp.sum(weights_full * grad_weights, axis=-1, keepdims=True)
        grad_scores = (weights_full * (grad_weights - row_dot)).astype(jnp.bfloat16)
        grad_query = (
            jnp.einsum("hqk,khd->qhd", grad_scores, key_block, preferred_element_type=jnp.float32)
            * score_scale
        )
        grad_key = (
            jnp.einsum("hqk,qhd->khd", grad_scores, query_block, preferred_element_type=jnp.float32)
            * score_scale
        )
        grad_value = jnp.einsum(
            "hqk,qhd->khd",
            weights_full.astype(jnp.bfloat16),
            grad_mixed_block,
            preferred_element_type=jnp.float32,
        )
        return (
            grad_query.reshape(block_rows, local_width),
            grad_key.reshape(seq_length, local_width),
            grad_value.reshape(seq_length, local_width),
        )

    query_blocks, key_blocks, value_blocks = lax.map(backward_block, block_ids)
    grad_queries = query_blocks.reshape(group_rows, local_width)
    grad_keys = (
        key_blocks.reshape(seq_count, per_sequence, seq_length, local_width)
        .sum(axis=1)
        .reshape(group_rows, local_width)
    )
    grad_values = (
        value_blocks.reshape(seq_count, per_sequence, seq_length, local_width)
        .sum(axis=1)
        .reshape(group_rows, local_width)
    )
    grad_projected = jnp.stack((grad_queries, grad_keys, grad_values), axis=1).astype(jnp.bfloat16)
    grad_project_part = jnp.einsum(
        "te,tsc->esc", gathered, grad_projected, preferred_element_type=jnp.float32
    )
    grad_matrix = grad_projected.reshape(group_rows, 3 * local_width)
    grad_tokens = (
        lax.psum_scatter(
            jnp.einsum(
                "tc,ec->te", grad_matrix, back_triple, preferred_element_type=jnp.float32
            ).astype(jnp.bfloat16),
            "tensor",
            scatter_dimension=0,
            tiled=True,
        ).astype(jnp.float32)
        + grad_first_in
    )
    grad_project, grad_output, grad_up, grad_down = (
        scatter_sum(grad_project_part, "dp", 0),
        scatter_sum(grad_output_part, "dp", 1),
        scatter_sum(grad_up_part, "dp", 0),
        scatter_sum(grad_down_part, "dp", 1),
    )
    head_terms = place_columns(
        jnp.stack(
            (
                jnp.sum(grad_projected[:, 0], axis=0, dtype=jnp.float32),
                jnp.sum(grad_projected[:, 2], axis=0, dtype=jnp.float32),
            )
        ),
        tensor_rank,
        model_width,
    )
    shared_terms = jnp.stack(
        (
            jnp.sum(grad_branch, axis=0, dtype=jnp.float32),
            grad_shift_one,
            jnp.sum(grad_second, axis=0, dtype=jnp.float32),
            grad_shift_two,
        )
    )
    bias_terms = jnp.concatenate((head_terms, shared_terms), axis=0)
    gain_terms = jnp.stack((grad_gain_one, grad_gain_two))
    hidden_terms = place_columns(
        jnp.sum(grad_upper, axis=0, dtype=jnp.float32), tensor_rank, hidden_bias.shape[0]
    )
    grad_gains, grad_bias_rows, grad_hidden_bias = lax.psum(
        (gain_terms, bias_terms, hidden_terms), ("dp", "tensor")
    )
    return (
        layer_out.astype(jnp.bfloat16),
        grad_tokens,
        grad_project,
        grad_output,
        grad_up,
        grad_down,
        grad_gains,
        grad_bias_rows,
        grad_hidden_bias,
    )


def solution(mesh):
    placed = (
        P(("dp", "tensor"), None),
        P("dp", None),
        P(("dp", "tensor"), None),
        P("dp", None, "tensor"),
        P("tensor", "dp"),
        P("dp", "tensor"),
        P("tensor", "dp"),
        P(),
        P(),
        P(),
    )
    fits = mesh.shape["dp"] == 2 * LINES and mesh.shape["tensor"] == 4
    return jax.shard_map(
        per_device_kernels if fits else per_device,
        mesh=mesh,
        in_specs=placed,
        out_specs=(
            P(("dp", "tensor"), None),
            P(("dp", "tensor"), None),
            P("dp", None, "tensor"),
            P("tensor", "dp"),
            P("dp", "tensor"),
            P("tensor", "dp"),
            P(),
            P(),
            P(),
        ),
        check_vma=False,
    )
```

```python
import functools

import jax
import jax.numpy as jnp
from jax import lax
from jax.experimental import pallas as pl
from jax.experimental.pallas import tpu as pltpu
from jax.sharding import PartitionSpec as P

HEAD = 64
EPSILON = 1e-05
NEGATIVE = -1e30
MESH = pl.DeviceIdType.MESH
LINES = 4
CORE, ACROSS, FAR = 1, 2, 3
HALVES = 2
CHUNK = 16
ORDER = (3, 0, 1, 2)
VMEM_BYTES = 60 << 20


def remote(src, dst, send_sem, recv_sem, target):
    return pltpu.make_async_remote_copy(
        src_ref=src,
        dst_ref=dst,
        send_sem=send_sem,
        recv_sem=recv_sem,
        device_id=target,
        device_id_type=MESH,
    )


def position():
    return lax.axis_index("dp"), lax.axis_index("tensor")


def greet(with_line, with_total=False):
    dp, tensor = position()
    barrier = pltpu.get_barrier_semaphore()

    def signal(target):
        pl.semaphore_signal(barrier, inc=1, device_id=target, device_id_type=MESH)

    signal((dp, tensor ^ CORE))
    signal((dp, tensor ^ ACROSS))
    count = 2
    if with_line:
        signal((dp ^ 1, tensor))
        line = dp // 2

        @pl.when(line > 0)
        def _():
            signal((dp - 2, tensor))

        @pl.when(line < LINES - 1)
        def _():
            signal((dp + 2, tensor))

        if with_total:
            signal((dp ^ 4, tensor))
            count += 1
        ends = jnp.where(line > 0, 1, 0) + jnp.where(line < LINES - 1, 1, 0)
        count = count + 1 + ends
    pl.semaphore_wait(barrier, count)


def row_piece(ref, index, size):
    return ref.at[pl.ds(pl.multiple_of(index * size, size), size), :]


def column_piece(ref, index, size):
    return ref.at[:, pl.ds(pl.multiple_of(index * size, size), size)]


class LineGather:
    def __init__(self, own, full, piece, send_sem, recv_sem, local_sem):
        self.own, self.full, self.piece = own, full, piece
        self.send_sem, self.recv_sem, self.local_sem = send_sem, recv_sem, local_sem
        self.dp, self.tensor = position()
        self.line, self.side = self.dp // 2, self.dp % 2
        self.targets = (
            (self.dp + 2, self.tensor),
            (self.dp - 2, self.tensor),
            (self.dp ^ 1, self.tensor),
        )

    def copy(self, index, way, src=None):
        view = self.piece(self.full, index)
        return remote(
            view if src is None else src,
            view,
            self.send_sem.at[way * LINES + index // 2],
            self.recv_sem.at[index],
            self.targets[way],
        )

    def local(self):
        return pltpu.make_async_copy(self.own, self.piece(self.full, self.dp), self.local_sem)

    def start(self):
        self.local().start()

        @pl.when(self.line < LINES - 1)
        def _():
            self.copy(self.dp, 0, self.own).start()

        @pl.when(self.line > 0)
        def _():
            self.copy(self.dp, 1, self.own).start()

        self.copy(self.dp, 2, self.own).start()

    def step(self, distance):
        @pl.when(self.line >= distance)
        def _():
            index = self.dp - 2 * distance
            self.copy(index, 0).wait_recv()

            @pl.when(self.line < LINES - 1)
            def _():
                self.copy(index, 0).start()

            self.copy(index, 2).start()

        @pl.when(self.line + distance < LINES)
        def _():
            index = self.dp + 2 * distance
            self.copy(index, 1).wait_recv()

            @pl.when(self.line > 0)
            def _():
                self.copy(index, 1).start()

            self.copy(index, 2).start()

    def arrive(self):
        self.local().wait()
        for line in range(LINES):
            self.copy(2 * line + 1 - self.side, 2).wait_recv()

    def finish(self):
        for line in range(LINES):
            index = 2 * line + self.side
            self.copy(index, 2).wait_send()

            @pl.when((self.line < LINES - 1) & (line <= self.line))
            def _():
                self.copy(index, 0).wait_send()

            @pl.when((self.line > 0) & (line >= self.line))
            def _():
                self.copy(index, 1).wait_send()


class RowGather:
    def __init__(self, full, rows, send_sem, recv_sem):
        self.full, self.rows = full, rows
        self.send_sem, self.recv_sem = send_sem, recv_sem
        self.dp, self.tensor = position()

    def view(self, rank, half=None):
        if half is None:
            return row_piece(self.full, rank, self.rows)
        return row_piece(self.full, rank * HALVES + half, self.rows // HALVES)

    def near(self, rank):
        view = self.view(rank)
        target = (self.dp, self.tensor ^ CORE)
        return remote(view, view, self.send_sem.at[0], self.recv_sem.at[0], target)

    def across(self, rank, half):
        view, slot = self.view(rank, half), 1 + half
        target = (self.dp, self.tensor ^ ACROSS)
        return remote(view, view, self.send_sem.at[slot], self.recv_sem.at[slot], target)

    def far(self, rank, half):
        view, slot = self.view(rank, half), 1 + HALVES + half
        target = (self.dp, self.tensor ^ CORE)
        return remote(view, view, self.send_sem.at[slot], self.recv_sem.at[slot], target)

    def start(self):
        for half in range(HALVES):
            self.across(self.tensor, half).start()
        self.near(self.tensor).start()

    def wait_near(self):
        self.near(self.tensor ^ CORE).wait_recv()

    def wait_across(self, half):
        self.across(self.tensor ^ ACROSS, half).wait_recv()
        self.far(self.tensor ^ ACROSS, half).start()

    def wait_far(self, half):
        self.far(self.tensor ^ FAR, half).wait_recv()

    def finish(self):
        self.near(self.tensor).wait_send()
        for half in range(HALVES):
            self.across(self.tensor, half).wait_send()
            self.far(self.tensor ^ ACROSS, half).wait_send()


GATHER_SEMS = [pltpu.SemaphoreType.DMA((1 + 2 * HALVES,))] * 2


class RowScatter:
    def __init__(self, near_out, near_in, across_out, across_in, send_sem, recv_sem):
        self.near_out, self.near_in = near_out, near_in
        self.across_out, self.across_in = across_out, across_in
        self.send_sem, self.recv_sem = send_sem, recv_sem
        self.dp, self.tensor = position()

    def near(self, slot):
        return remote(
            self.near_out.at[slot],
            self.near_in.at[slot],
            self.send_sem.at[slot],
            self.recv_sem.at[slot],
            (self.dp, self.tensor ^ CORE),
        )

    def across(self, half):
        rows = self.across_in.shape[0] // HALVES
        return remote(
            row_piece(self.across_out, half, rows),
            row_piece(self.across_in, half, rows),
            self.send_sem.at[2 * HALVES + half],
            self.recv_sem.at[2 * HALVES + half],
            (self.dp, self.tensor ^ ACROSS),
        )

    def give_far(self, half, partial):
        self.near_out[half] = partial.astype(jnp.bfloat16)
        self.near(half).start()

    def give_across(self, half, partial):
        self.near(half).wait_recv()
        rows = partial.shape[0]
        total = partial + self.near_in[half].astype(jnp.float32)
        self.across_out[half * rows : (half + 1) * rows, :] = total.astype(jnp.bfloat16)
        self.across(half).start()

    def give_near(self, half, partial):
        self.near_out[HALVES + half] = partial.astype(jnp.bfloat16)
        self.near(HALVES + half).start()

    def take(self, half, partial):
        self.near(HALVES + half).wait_recv()
        rows = partial.shape[0]
        total = partial + self.near_in[HALVES + half].astype(jnp.float32)
        self.across(half).wait_recv()
        return total + self.across_in[half * rows : (half + 1) * rows, :].astype(jnp.float32)

    def finish(self):
        for slot in range(2 * HALVES):
            self.near(slot).wait_send()
        for half in range(HALVES):
            self.across(half).wait_send()


def scatter_scratch(rows, width):
    half = rows // HALVES
    return [
        pltpu.VMEM((2 * HALVES, half, width), jnp.bfloat16),
        pltpu.VMEM((2 * HALVES, half, width), jnp.bfloat16),
        pltpu.VMEM((rows, width), jnp.bfloat16),
        pltpu.VMEM((rows, width), jnp.bfloat16),
        pltpu.SemaphoreType.DMA((3 * HALVES,)),
        pltpu.SemaphoreType.DMA((3 * HALVES,)),
    ]


def dot(left, right):
    return jnp.dot(left, right, preferred_element_type=jnp.float32)


def dot_nt(left, right):
    return lax.dot_general(left, right, (((1,), (1,)), ((), ())), preferred_element_type=jnp.float32)


def dot_tn(left, right):
    return lax.dot_general(left, right, (((0,), (0,)), ((), ())), preferred_element_type=jnp.float32)


def normalize(rows):
    centred = rows - jnp.mean(rows, axis=-1, keepdims=True)
    inverse = lax.rsqrt(jnp.mean(centred * centred, axis=-1, keepdims=True) + EPSILON)
    return centred * inverse, inverse


def block_rows(ref, rank, rows):
    return ref[pl.ds(pl.multiple_of(rank * rows, rows), rows), :]


def attend_kernel(
    rows,
    tokens,
    triple_own,
    output_own,
    up_own,
    down_own,
    segment_column,
    segment_row,
    bias_rows,
    norm_gains,
    gathered_out,
    triple_out,
    output_out,
    up_full,
    down_full,
    queries,
    key_rows,
    value_rows,
    mixed,
    log_totals,
    normed_out,
    inverse_out,
    first_low,
    gathered,
    triple,
    output,
    value_turned,
    line_send,
    line_recv,
    line_local,
    row_send,
    row_recv,
    near_out,
    near_in,
    across_out,
    across_in,
    sum_send,
    sum_recv,
    save_sem,
):
    dp, tensor = position()
    local = queries.shape[1]
    gather = RowGather(gathered, rows, row_send, row_recv)
    scatter = RowScatter(near_out, near_in, across_out, across_in, sum_send, sum_recv)
    piece = triple_own.shape[0]

    def of_rows(ref, index):
        return row_piece(ref, index, piece)

    def of_columns(ref, index):
        return column_piece(ref, index, piece)

    def line(at, own, full, view):
        return LineGather(own, full, view, line_send.at[at], line_recv.at[at], line_local.at[at])

    triple_line = line(0, triple_own, triple, of_rows)
    output_line = line(1, output_own, output, of_columns)
    up_line = line(2, up_own, up_full, of_rows)
    down_line = line(3, down_own, down_full, of_columns)
    greet(True)
    place = pltpu.make_async_copy(tokens, gather.view(tensor), save_sem.at[0])
    place.start()
    triple_line.start()
    place.wait()
    gather.start()
    triple_line.step(1)
    triple_line.step(2)
    gather.wait_near()
    for half in range(HALVES):
        gather.wait_across(half)
    triple_line.step(3)
    output_line.start()
    up_line.start()
    for half in range(HALVES):
        gather.wait_far(half)
    triple_line.arrive()
    saves = [
        pltpu.make_async_copy(gathered, gathered_out, save_sem.at[0]),
        pltpu.make_async_copy(triple, triple_out, save_sem.at[1]),
    ]
    for save in saves:
        save.start()
    columns = pl.ds(pl.multiple_of(tensor * local, local), local)
    query_bias = bias_rows[0:1, columns]
    value_bias = bias_rows[1:2, columns]

    @pl.loop(0, 4)
    def _(block):
        here = pl.ds(pl.multiple_of(block * rows, rows), rows)
        left = gathered[here, :]
        query = (dot(left, triple[:, :local]) + query_bias).astype(jnp.bfloat16)
        queries[here, :] = query * jnp.bfloat16(HEAD**-0.5)
        key_rows[here, :] = dot(left, triple[:, local : 2 * local]).astype(jnp.bfloat16)
        value = dot(left, triple[:, 2 * local :]) + value_bias
        value_rows[here, :] = value.astype(jnp.bfloat16)
        value_turned[:, here] = value.T.astype(jnp.bfloat16)

    output_line.step(1)
    up_line.step(1)

    def attend(rank):
        here = pl.ds(pl.multiple_of(rank * rows, rows), rows)

        @pl.loop(0, local // (2 * HEAD))
        def _(pair):
            lanes = pl.ds(pl.multiple_of(pair * 2 * HEAD, 2 * HEAD), 2 * HEAD)
            query = queries[here, lanes]
            keys = key_rows[:, lanes]
            same = segment_column[...] == segment_row[:, here]
            lane = lax.broadcasted_iota(jnp.int32, query.shape, 1)
            outs = []
            for side in range(2):
                mine = lane // HEAD == side
                scores = dot_nt(keys, jnp.where(mine, query, jnp.bfloat16(0)))
                scores = jnp.where(same, scores, NEGATIVE)
                top = jnp.max(scores, axis=0, keepdims=True)
                exponent = jnp.exp(scores - top)
                total = jnp.sum(exponent, axis=0, keepdims=True)
                weights = (exponent * (1.0 / total)).astype(jnp.bfloat16)
                head = pair * 2 + side
                outs.append(dot(value_turned[pl.ds(pl.multiple_of(head * HEAD, HEAD), HEAD), :], weights))
                log_totals[pl.ds(head, 1), here] = top + jnp.log(total)
            mixed[here, lanes] = jnp.concatenate(outs, axis=0).T.astype(jnp.bfloat16)

        return mixed[here, :]

    def halves_of(partial):
        half = rows // HALVES
        return [partial[at * half : (at + 1) * half] for at in range(HALVES)]

    far = attend(tensor ^ FAR)
    output_line.step(2)
    output_line.step(3)
    up_line.step(2)
    output_line.arrive()
    save = pltpu.make_async_copy(output, output_out, save_sem.at[2])
    save.start()
    saves.append(save)
    for half, partial in enumerate(halves_of(dot(far, output[...]))):
        scatter.give_far(half, partial)
    other = attend(tensor ^ ACROSS)
    for half, partial in enumerate(halves_of(dot(other, output[...]))):
        scatter.give_across(half, partial)
    up_line.step(3)
    down_line.start()
    near = attend(tensor ^ CORE)
    for half, partial in enumerate(halves_of(dot(near, output[...]))):
        scatter.give_near(half, partial)
    down_line.step(1)
    mine = attend(tensor)
    for half, partial in enumerate(halves_of(dot(mine, output[...]))):
        part = slice(half * rows // HALVES, (half + 1) * rows // HALVES)
        total = scatter.take(half, partial) + bias_rows[2:3, :]
        own_rows = row_piece(gathered, tensor * HALVES + half, rows // HALVES)
        normed, inverse = normalize(own_rows[...].astype(jnp.float32) + total)
        normed_out[part, :] = normed
        inverse_out[part, :] = inverse
        first_low[part, :] = (normed * norm_gains[0:1, :] + bias_rows[3:4, :]).astype(jnp.bfloat16)
    scatter.finish()
    gather.finish()
    down_line.step(2)
    down_line.step(3)
    for each in (up_line, down_line):
        each.arrive()
    for each in (triple_line, output_line, up_line, down_line):
        each.finish()
    for save in saves:
        save.wait()


def attend_forward(tokens, triple_own, output_own, up_own, down_own, segments, bias_rows, norm_gains):
    rows, width = tokens.shape
    length = segments.shape[1]
    local = triple_own.shape[1] // 3
    heads = local // HEAD
    pieces = 2 * LINES
    bf16, f32 = jnp.bfloat16, jnp.float32
    vmem, hbm = pl.BlockSpec(memory_space=pltpu.VMEM), pl.BlockSpec(memory_space=pltpu.HBM)
    hidden = up_own.shape[1]
    return pl.pallas_call(
        functools.partial(attend_kernel, rows),
        out_shape=[
            jax.ShapeDtypeStruct((length, width), bf16),
            jax.ShapeDtypeStruct((width, 3 * local), bf16),
            jax.ShapeDtypeStruct((local, width), bf16),
            jax.ShapeDtypeStruct((width, hidden), bf16),
            jax.ShapeDtypeStruct((hidden, width), bf16),
            jax.ShapeDtypeStruct((length, local), bf16),
            jax.ShapeDtypeStruct((length, local), bf16),
            jax.ShapeDtypeStruct((length, local), bf16),
            jax.ShapeDtypeStruct((length, local), bf16),
            jax.ShapeDtypeStruct((heads, length), f32),
            jax.ShapeDtypeStruct((rows, width), f32),
            jax.ShapeDtypeStruct((rows, 1), f32),
            jax.ShapeDtypeStruct((rows, width), bf16),
        ],
        in_specs=[hbm] * 5 + [vmem] * 4,
        out_specs=[hbm] * 5 + [vmem] * 8,
        scratch_shapes=[
            pltpu.VMEM((length, width), bf16),
            pltpu.VMEM((width, 3 * local), bf16),
            pltpu.VMEM((local, width), bf16),
            pltpu.VMEM((local, length), bf16),
            pltpu.SemaphoreType.DMA((4, 3 * LINES)),
            pltpu.SemaphoreType.DMA((4, pieces)),
            pltpu.SemaphoreType.DMA((4,)),
        ]
        + GATHER_SEMS
        + scatter_scratch(rows, width)
        + [pltpu.SemaphoreType.DMA((3,))],
        compiler_params=pltpu.CompilerParams(
            collective_id=0, has_side_effects=True, vmem_limit_bytes=VMEM_BYTES
        ),
        name="attend_forward",
    )(
        tokens,
        triple_own,
        output_own,
        up_own,
        down_own,
        segments.reshape(length, 1),
        segments.reshape(1, length),
        bias_rows,
        norm_gains,
    )


def feed_kernel(
    rows,
    low_own,
    up_from,
    down_from,
    cotangent,
    normed_one,
    inverse_one,
    norm_gains,
    bias_rows,
    hidden_bias,
    layer_out,
    grad_one,
    branch_low,
    grad_up,
    grad_down,
    sums,
    up,
    down,
    first_all,
    hidden,
    slope,
    second_all,
    upper_low,
    upper,
    kept,
    held,
    grad_two,
    near_out,
    near_in,
    across_out,
    across_in,
    sum_send,
    sum_recv,
    back_near_out,
    back_near_in,
    back_across_out,
    back_across_in,
    back_sum_send,
    back_sum_recv,
    row_send,
    row_recv,
    back_row_send,
    back_row_recv,
    load_sem,
):
    dp, tensor = position()
    half_rows = rows // HALVES
    bf16, f32 = jnp.bfloat16, jnp.float32
    loads = [
        pltpu.make_async_copy(up_from, up, load_sem.at[0]),
        pltpu.make_async_copy(down_from, down, load_sem.at[1]),
        pltpu.make_async_copy(low_own, row_piece(first_all, tensor, rows), load_sem.at[2]),
    ]
    for load in (loads[2], loads[0], loads[1]):
        load.start()
    gather = RowGather(first_all, rows, row_send, row_recv)
    scatter = RowScatter(near_out, near_in, across_out, across_in, sum_send, sum_recv)
    back_gather = RowGather(second_all, rows, back_row_send, back_row_recv)
    back_scatter = RowScatter(
        back_near_out, back_near_in, back_across_out, back_across_in, back_sum_send, back_sum_recv
    )
    greet(False)
    loads[2].wait()
    gather.start()
    loads[0].wait()
    sums[...] = jnp.zeros_like(sums)

    def forward_part(rank, half):
        size = rows if half is None else half_rows
        start = rank * rows + (0 if half is None else half * half_rows)
        here = pl.ds(pl.multiple_of(start, size), size)
        upper[:size, :] = dot(first_all[here, :], up[...]) + hidden_bias[...]

        @pl.loop(0, size // CHUNK)
        def _(chunk):
            part = pl.ds(pl.multiple_of(chunk * CHUNK, CHUNK), CHUNK)
            into = pl.ds(pl.multiple_of(start + chunk * CHUNK, CHUNK), CHUNK)
            value = upper[part, :]
            share = 0.5 + 0.5 * lax.erf(value * (0.5**0.5))
            hidden[into, :] = (value * share).astype(bf16)
            bell = jnp.exp(value * value * -0.5) * (2 * jnp.pi) ** -0.5
            slope[into, :] = share + value * bell

        return dot(hidden[here, :], down[...])

    def backward_part(rank, half):
        size = rows if half is None else half_rows
        start = rank * rows + (0 if half is None else half * half_rows)
        here = pl.ds(pl.multiple_of(start, size), size)
        upper[:size, :] = dot_nt(second_all[here, :], down[...])

        @pl.loop(0, size // CHUNK)
        def _(chunk):
            part = pl.ds(pl.multiple_of(chunk * CHUNK, CHUNK), CHUNK)
            into = pl.ds(pl.multiple_of(start + chunk * CHUNK, CHUNK), CHUNK)
            low = (upper[part, :] * slope[into, :]).astype(bf16)
            upper_low[into, :] = low
            sums[6:7, :] += jnp.sum(low.astype(f32), axis=0, keepdims=True)

        return dot_nt(upper_low[here, :], up[...])

    def sublayer(gathering, scattering, part, before_far):
        mine = part(tensor, None)
        kept[...] = mine
        gathering.wait_near()
        near = part(tensor ^ CORE, None)
        for half in range(HALVES):
            scattering.give_near(half, near[half * half_rows : (half + 1) * half_rows])
        for half in range(HALVES):
            gathering.wait_across(half)
            held[...] = part(tensor ^ ACROSS, half)
            gathering.wait_far(half)
            scattering.give_far(half, part(tensor ^ FAR, half))
            scattering.give_across(half, held[...])
        before_far()

    def over_chunks(half, body):
        @pl.loop(0, half_rows // CHUNK)
        def _(chunk):
            body(pl.ds(pl.multiple_of(half * half_rows + chunk * CHUNK, CHUNK), CHUNK))

    def add_to(row, value):
        sums[row : row + 1, :] += jnp.sum(value, axis=0, keepdims=True)

    loads[1].wait()
    sublayer(gather, scatter, forward_part, lambda: None)
    for half in range(HALVES):
        part = slice(half * half_rows, (half + 1) * half_rows)
        kept[part, :] = scatter.take(half, kept[part, :])

        def second_norm(here):
            first = normed_one[here, :] * norm_gains[0:1, :] + bias_rows[3:4, :]
            normed, inverse = normalize(first + kept[here, :] + bias_rows[4:5, :])
            layer_out[here, :] = (normed * norm_gains[1:2, :] + bias_rows[5:6, :]).astype(bf16)
            grad = cotangent[here, :].astype(f32)
            add_to(5, grad * normed)
            add_to(3, grad)
            total = norm_back(grad * norm_gains[1:2, :], normed, inverse)
            grad_two[here, :] = total
            low = total.astype(bf16)
            add_to(2, low.astype(f32))
            second_all[pl.ds(pl.multiple_of(tensor * rows + here.start, CHUNK), CHUNK), :] = low

        over_chunks(half, second_norm)
    back_gather.start()

    def weight_gradients():
        step = 256

        @pl.loop(0, hidden.shape[1] // step)
        def _(chunk):
            lanes = pl.ds(pl.multiple_of(chunk * step, step), step)
            grad_down[lanes, :] = dot_tn(hidden[:, lanes], second_all[...]).astype(bf16)

        @pl.loop(0, first_all.shape[1] // step)
        def _(chunk):
            lanes = pl.ds(pl.multiple_of(chunk * step, step), step)
            grad_up[lanes, :] = dot_tn(first_all[:, lanes], upper_low[...]).astype(bf16)

    sublayer(back_gather, back_scatter, backward_part, weight_gradients)
    for half in range(HALVES):
        part = slice(half * half_rows, (half + 1) * half_rows)
        kept[part, :] = back_scatter.take(half, kept[part, :])

        def first_norm(here):
            grad = grad_two[here, :] + kept[here, :]
            normed = normed_one[here, :]
            add_to(4, grad * normed)
            add_to(1, grad)
            total = norm_back(grad * norm_gains[0:1, :], normed, inverse_one[here, :])
            grad_one[here, :] = total
            low = total.astype(bf16)
            add_to(0, low.astype(f32))
            branch_low[here, :] = low

        over_chunks(half, first_norm)
    for each in (gather, scatter, back_gather, back_scatter):
        each.finish()


def norm_back(grad, normed, inverse):
    average = jnp.mean(grad, axis=-1, keepdims=True)
    along = jnp.mean(grad * normed, axis=-1, keepdims=True)
    return inverse * (grad - average - normed * along)


def feed_both(
    first_low, up_full, down_full, cotangent, normed, inverse, norm_gains, bias_rows, hidden_bias
):
    rows, width = first_low.shape
    hidden = up_full.shape[1]
    length = 4 * rows
    bf16, f32 = jnp.bfloat16, jnp.float32
    vmem, hbm = pl.BlockSpec(memory_space=pltpu.VMEM), pl.BlockSpec(memory_space=pltpu.HBM)
    return pl.pallas_call(
        functools.partial(feed_kernel, rows),
        out_shape=[
            jax.ShapeDtypeStruct((rows, width), bf16),
            jax.ShapeDtypeStruct((rows, width), f32),
            jax.ShapeDtypeStruct((rows, width), bf16),
            jax.ShapeDtypeStruct((width, hidden), bf16),
            jax.ShapeDtypeStruct((hidden, width), bf16),
            jax.ShapeDtypeStruct((8, width), f32),
        ],
        in_specs=[hbm] * 3 + [vmem] * 6,
        out_specs=[vmem] * 6,
        scratch_shapes=[
            pltpu.VMEM((width, hidden), bf16),
            pltpu.VMEM((hidden, width), bf16),
            pltpu.VMEM((length, width), bf16),
            pltpu.VMEM((length, hidden), bf16),
            pltpu.VMEM((length, hidden), f32),
            pltpu.VMEM((length, width), bf16),
            pltpu.VMEM((length, hidden), bf16),
            pltpu.VMEM((rows, hidden), f32),
            pltpu.VMEM((rows, width), f32),
            pltpu.VMEM((rows // HALVES, width), f32),
            pltpu.VMEM((rows, width), f32),
        ]
        + scatter_scratch(rows, width)
        + scatter_scratch(rows, width)
        + GATHER_SEMS
        + GATHER_SEMS
        + [pltpu.SemaphoreType.DMA((3,))],
        compiler_params=pltpu.CompilerParams(
            collective_id=1, has_side_effects=True, vmem_limit_bytes=VMEM_BYTES
        ),
        name="feed_both",
    )(first_low, up_full, down_full, cotangent, normed, inverse, norm_gains, bias_rows, hidden_bias)


class LineScatter:
    def __init__(self, partial, piece, side_in, line_in, send_sem, recv_sem):
        self.partial, self.piece, self.side_in, self.line_in = partial, piece, side_in, line_in
        self.send_sem, self.recv_sem = send_sem, recv_sem
        self.dp, self.tensor = position()
        self.line, self.side = self.dp // 2, self.dp % 2

    def view(self, line):
        return self.piece(self.partial, 2 * line + self.side)

    def across(self, line):
        return remote(
            self.piece(self.partial, 2 * line + 1 - self.side),
            self.side_in.at[line],
            self.send_sem.at[line],
            self.recv_sem.at[line],
            (self.dp ^ 1, self.tensor),
        )

    def start(self):
        for line in ORDER:
            self.across(line).start()

    def onward(self, line):
        up = line > self.line
        last = jnp.where(up, line, jnp.where(line == self.line - 1, LINES, line))
        return remote(
            self.view(line),
            self.line_in.at[last],
            self.send_sem.at[LINES + line],
            self.recv_sem.at[LINES + last],
            (self.dp + jnp.where(up, 2, -2), self.tensor),
        )

    def wait_slot(self, slot):
        remote(
            self.line_in.at[slot],
            self.line_in.at[slot],
            self.send_sem.at[0],
            self.recv_sem.at[LINES + slot],
            (self.dp ^ 1, self.tensor),
        ).wait_recv()

    def total(self, line):
        return self.view(line)[...].astype(jnp.float32) + self.side_in[line].astype(jnp.float32)

    def relay(self, line):
        @pl.when(self.line != line)
        def _():
            self.across(line).wait_recv()
            first = jnp.where(line > self.line, self.line == 0, self.line == LINES - 1)

            @pl.when(first)
            def _():
                self.view(line)[...] = self.total(line).astype(jnp.bfloat16)

            @pl.when(jnp.logical_not(first))
            def _():
                self.wait_slot(line)
                total = self.total(line) + self.line_in[line].astype(jnp.float32)
                self.view(line)[...] = total.astype(jnp.bfloat16)

            self.onward(line).start()

    def finish(self, result):
        self.across(self.line).wait_recv()
        result[...] = self.total(self.line)

        @pl.when(self.line > 0)
        def _():
            self.wait_slot(self.line)
            result[...] += self.line_in[self.line].astype(jnp.float32)

        @pl.when(self.line < LINES - 1)
        def _():
            self.wait_slot(LINES)
            result[...] += self.line_in[LINES].astype(jnp.float32)

        for line in range(LINES):
            self.across(line).wait_send()

            @pl.when(self.line != line)
            def _():
                self.onward(line).wait_send()


class Total:
    def __init__(self, held, arrived, send_sem, recv_sem):
        self.held, self.arrived, self.send_sem, self.recv_sem = held, arrived, send_sem, recv_sem
        dp, tensor = position()
        self.targets = (
            (dp, tensor ^ CORE),
            (dp ^ 1, tensor),
            (dp ^ 2, tensor),
            (dp ^ 4, tensor),
            (dp, tensor ^ ACROSS),
        )

    def copy(self, step):
        return remote(
            self.held.at[step],
            self.arrived.at[step],
            self.send_sem.at[step],
            self.recv_sem.at[step],
            self.targets[step],
        )

    def start(self):
        self.copy(0).start()

    def step(self, step):
        self.copy(step).wait_recv()
        self.held[step + 1] = self.held[step] + self.arrived[step]
        if step + 1 < len(self.targets):
            self.copy(step + 1).start()

    def finish(self):
        for step in range(len(self.targets)):
            self.copy(step).wait_send()


def attend_back_kernel(
    rows,
    branch_own,
    grad_up_from,
    grad_down_from,
    gathered,
    triple,
    output,
    queries,
    key_rows,
    value_rows,
    mixed,
    log_totals,
    segment_column,
    segment_row,
    grad_one,
    sums,
    grad_tokens,
    project_out,
    output_out,
    up_out,
    down_out,
    totals_out,
    grad_up,
    grad_down,
    grad_output,
    grad_project,
    branch_all,
    mixed_low,
    projected_low,
    key_turned,
    grad_keys,
    grad_values,
    project_side,
    project_line,
    output_side,
    output_line,
    up_side,
    up_line,
    down_side,
    down_line,
    held,
    arrived,
    line_send,
    line_recv,
    total_send,
    total_recv,
    near_out,
    near_in,
    across_out,
    across_in,
    sum_send,
    sum_recv,
    row_send,
    row_recv,
    load_sem,
):
    dp, tensor = position()
    bf16, f32 = jnp.bfloat16, jnp.float32
    half_rows = rows // HALVES
    local = queries.shape[1]
    piece = branch_own.shape[1] // (2 * LINES)
    loads = [
        pltpu.make_async_copy(branch_own, row_piece(branch_all, tensor, rows), load_sem.at[0]),
        pltpu.make_async_copy(grad_down_from, grad_down, load_sem.at[1]),
        pltpu.make_async_copy(grad_up_from, grad_up, load_sem.at[2]),
    ]
    for load in loads:
        load.start()

    def of_rows(ref, index):
        return row_piece(ref, index, piece)

    def of_columns(ref, index):
        return column_piece(ref, index, piece)

    def line(at, partial, view, side_in, line_in):
        return LineScatter(partial, view, side_in, line_in, line_send.at[at], line_recv.at[at])

    project_sum = line(0, grad_project, of_rows, project_side, project_line)
    output_sum = line(1, grad_output, of_columns, output_side, output_line)
    up_sum = line(2, grad_up, of_rows, up_side, up_line)
    down_sum = line(3, grad_down, of_columns, down_side, down_line)
    gather = RowGather(branch_all, rows, row_send, row_recv)
    scatter = RowScatter(near_out, near_in, across_out, across_in, sum_send, sum_recv)
    total = Total(held, arrived, total_send, total_recv)
    greet(True, True)
    loads[0].wait()
    gather.start()
    loads[1].wait()
    down_sum.start()
    loads[2].wait()
    up_sum.start()
    grad_keys[...] = jnp.zeros_like(grad_keys)
    grad_values[...] = jnp.zeros_like(grad_values)
    key_turned[...] = key_rows[...].astype(f32).T.astype(bf16)

    def attend_back(rank):
        here = pl.ds(pl.multiple_of(rank * rows, rows), rows)
        mixed_low[...] = dot_nt(branch_all[here, :], output[...]).astype(bf16)

        @pl.loop(0, local // (2 * HEAD))
        def _(pair):
            lanes = pl.ds(pl.multiple_of(pair * 2 * HEAD, 2 * HEAD), 2 * HEAD)
            query = queries[here, lanes]
            grad = mixed_low[:, lanes]
            keys = key_rows[:, lanes]
            values = value_rows[:, lanes]
            same = segment_column[...] == segment_row[:, here]
            lane = lax.broadcasted_iota(jnp.int32, query.shape, 1)
            outs = []
            for side in range(2):
                mine = lane // HEAD == side
                head = pair * 2 + side
                query_here = jnp.where(mine, query, bf16(0))
                grad_here = jnp.where(mine, grad, bf16(0))
                scores = jnp.where(same, dot_nt(keys, query_here), NEGATIVE)
                weights = jnp.exp(scores - log_totals[pl.ds(head, 1), here])
                grad_weights = dot_nt(values, grad_here)
                along = jnp.sum(weights * grad_weights, axis=0, keepdims=True)
                grad_scores = (weights * (grad_weights - along)).astype(bf16)
                grad_keys[:, lanes] += dot(grad_scores, query_here)
                grad_values[:, lanes] += dot(weights.astype(bf16), grad_here)
                turned = key_turned[pl.ds(pl.multiple_of(head * HEAD, HEAD), HEAD), :]
                outs.append(dot(turned, grad_scores))
            grad_query = jnp.concatenate(outs, axis=0).T * HEAD**-0.5
            projected_low[here, lanes] = grad_query.astype(bf16)

    attend_back(tensor)
    gather.wait_near()
    attend_back(tensor ^ CORE)
    for half in range(HALVES):
        gather.wait_across(half)
    down_sum.relay(3)
    down_sum.relay(0)
    attend_back(tensor ^ ACROSS)
    for half in range(HALVES):
        gather.wait_far(half)
    down_sum.relay(1)
    down_sum.relay(2)
    attend_back(tensor ^ FAR)
    grad_output[...] = dot_tn(mixed[...], branch_all[...]).astype(bf16)
    output_sum.start()
    projected_low[:, local : 2 * local] = grad_keys[...].astype(bf16)
    projected_low[:, 2 * local :] = grad_values[...].astype(bf16)
    step = 256

    @pl.loop(0, gathered.shape[1] // step)
    def _(chunk):
        lanes = pl.ds(pl.multiple_of(chunk * step, step), step)
        grad_project[lanes, :] = dot_tn(gathered[:, lanes], projected_low[...]).astype(bf16)

    project_sum.start()
    held[0] = jnp.zeros(held.shape[1:], f32)
    held[0, 2:8, :] = sums[0:6, :]
    held[0, pl.ds(8 + tensor, 1), :] = sums[6:7, :]
    columns = pl.ds(pl.multiple_of(tensor * local, local), local)
    for row, at in ((0, 0), (1, 2)):
        part = projected_low[:, at * local : (at + 1) * local].astype(f32)
        held[0, row : row + 1, columns] = jnp.sum(part, axis=0, keepdims=True)
    total.start()

    def back_part(rank):
        here = pl.ds(pl.multiple_of(rank * rows, rows), rows)
        partial = dot_nt(projected_low[here, :], triple[...])
        return [partial[half * half_rows : (half + 1) * half_rows] for half in range(HALVES)]

    for half, partial in enumerate(back_part(tensor ^ FAR)):
        scatter.give_far(half, partial)
    for half, partial in enumerate(back_part(tensor ^ ACROSS)):
        scatter.give_across(half, partial)
    for half, partial in enumerate(back_part(tensor ^ CORE)):
        scatter.give_near(half, partial)
    mine = back_part(tensor)
    total.step(0)
    up_sum.relay(3)
    up_sum.relay(0)
    total.step(1)
    for half, partial in enumerate(mine):
        part = slice(half * half_rows, (half + 1) * half_rows)
        grad_tokens[part, :] = scatter.take(half, partial) + grad_one[part, :]
    total.step(2)
    up_sum.relay(1)
    up_sum.relay(2)
    down_sum.finish(down_out)
    total.step(3)
    for at in (3, 0, 1, 2):
        output_sum.relay(at)
    total.step(4)
    totals_out[...] = held[5]
    project_sum.relay(3)
    project_sum.relay(0)
    up_sum.finish(up_out)
    project_sum.relay(1)
    project_sum.relay(2)
    output_sum.finish(output_out)
    project_sum.finish(project_out)
    for each in (gather, scatter, total):
        each.finish()


def attend_backward(
    branch_low,
    grad_up,
    grad_down,
    gathered,
    triple,
    output,
    queries,
    key_rows,
    value_rows,
    mixed,
    log_totals,
    segments,
    grad_one,
    sums,
):
    rows, width = branch_low.shape
    length, local = queries.shape
    hidden = grad_up.shape[1]
    piece = width // (2 * LINES)
    bf16, f32 = jnp.bfloat16, jnp.float32
    vmem, hbm = pl.BlockSpec(memory_space=pltpu.VMEM), pl.BlockSpec(memory_space=pltpu.HBM)
    shapes = ((piece, 3 * local), (local, piece), (piece, hidden), (hidden, piece))
    return pl.pallas_call(
        functools.partial(attend_back_kernel, rows),
        out_shape=[jax.ShapeDtypeStruct((rows, width), f32)]
        + [jax.ShapeDtypeStruct(shape, f32) for shape in shapes]
        + [jax.ShapeDtypeStruct((16, width), f32)],
        in_specs=[hbm] * 3 + [vmem] * 12,
        out_specs=[vmem] * 6,
        scratch_shapes=[
            pltpu.VMEM((width, hidden), bf16),
            pltpu.VMEM((hidden, width), bf16),
            pltpu.VMEM((local, width), bf16),
            pltpu.VMEM((width, 3 * local), bf16),
            pltpu.VMEM((length, width), bf16),
            pltpu.VMEM((rows, local), bf16),
            pltpu.VMEM((length, 3 * local), bf16),
            pltpu.VMEM((local, length), bf16),
            pltpu.VMEM((length, local), f32),
            pltpu.VMEM((length, local), f32),
        ]
        + [
            pltpu.VMEM((count,) + shape, bf16) for shape in shapes for count in (LINES, LINES + 1)
        ]
        + [
            pltpu.VMEM((6, 16, width), f32),
            pltpu.VMEM((5, 16, width), f32),
            pltpu.SemaphoreType.DMA((4, 2 * LINES)),
            pltpu.SemaphoreType.DMA((4, 2 * LINES + 1)),
            pltpu.SemaphoreType.DMA((5,)),
            pltpu.SemaphoreType.DMA((5,)),
        ]
        + scatter_scratch(rows, width)
        + GATHER_SEMS
        + [pltpu.SemaphoreType.DMA((3,))],
        compiler_params=pltpu.CompilerParams(
            collective_id=2, has_side_effects=True, vmem_limit_bytes=VMEM_BYTES
        ),
        name="attend_backward",
    )(
        branch_low,
        grad_up,
        grad_down,
        gathered,
        triple,
        output,
        queries,
        key_rows,
        value_rows,
        mixed,
        log_totals,
        segments.reshape(length, 1),
        segments.reshape(1, length),
        grad_one,
        sums,
    )


def per_device_kernels(
    tokens,
    segments,
    cotangent,
    project_weight,
    output_weight,
    up_weight,
    down_weight,
    norm_gains,
    bias_rows,
    hidden_bias,
):
    (
        gathered,
        triple,
        output,
        up_full,
        down_full,
        queries,
        key_rows,
        value_rows,
        mixed,
        log_totals,
        normed,
        inverse,
        first_low,
    ) = attend_forward(
        tokens,
        project_weight.reshape(project_weight.shape[0], -1),
        output_weight,
        up_weight,
        down_weight,
        segments,
        bias_rows,
        norm_gains,
    )
    local_hidden = up_weight.shape[1]
    local_bias = lax.dynamic_slice_in_dim(
        hidden_bias, lax.axis_index("tensor") * local_hidden, local_hidden, 0
    )
    layer_out, grad_one, branch_low, grad_up, grad_down, sums = feed_both(
        first_low,
        up_full,
        down_full,
        cotangent,
        normed,
        inverse,
        norm_gains,
        bias_rows,
        local_bias.reshape(1, -1),
    )
    grad_tokens, grad_project, grad_output, grad_up, grad_down, totals = attend_backward(
        branch_low,
        grad_up,
        grad_down,
        gathered,
        triple,
        output,
        queries,
        key_rows,
        value_rows,
        mixed,
        log_totals,
        segments,
        grad_one,
        sums,
    )
    return (
        layer_out,
        grad_tokens,
        grad_project.reshape(project_weight.shape),
        grad_output,
        grad_up,
        grad_down,
        totals[6:8],
        totals[0:6],
        totals[8:12].reshape(-1),
    )


def gelu_exact(values):
    return jax.nn.gelu(values, approximate=False)


def layer_norm(token_rows, gain, shift):
    average = jnp.mean(token_rows, axis=-1, keepdims=True)
    centred = token_rows - average
    variance = jnp.mean(centred * centred, axis=-1, keepdims=True)
    inverse = lax.rsqrt(variance + EPSILON)
    normed = centred * inverse
    return (normed * gain + shift, (normed, inverse))


def norm_back_saved(grad_rows, saved, gain):
    normed, inverse = saved
    grad_gain = jnp.sum(grad_rows * normed, axis=0)
    grad_shift = jnp.sum(grad_rows, axis=0)
    grad_normed = grad_rows * gain
    grad_input = inverse * (
        grad_normed
        - jnp.mean(grad_normed, axis=-1, keepdims=True)
        - normed * jnp.mean(grad_normed * normed, axis=-1, keepdims=True)
    )
    return (grad_input, grad_gain, grad_shift)


def split_heads(token_rows):
    return token_rows.reshape(token_rows.shape[0], token_rows.shape[1] // HEAD, HEAD)


def scatter_sum(partial_sum, axis_name, dimension):
    return lax.psum_scatter(
        partial_sum.astype(jnp.bfloat16), axis_name, scatter_dimension=dimension, tiled=True
    ).astype(jnp.float32)


def place_columns(partial_sum, column_block, total_width):
    full_rows = jnp.zeros(partial_sum.shape[:-1] + (total_width,), jnp.float32)
    return lax.dynamic_update_slice_in_dim(
        full_rows, partial_sum, column_block * partial_sum.shape[-1], partial_sum.ndim - 1
    )


def per_device(
    tokens,
    segments,
    cotangent,
    project_weight,
    output_weight,
    up_weight,
    down_weight,
    norm_gains,
    bias_rows,
    hidden_bias,
):
    tensor_rank = lax.axis_index("tensor")
    local_rows, model_width = tokens.shape
    seq_count, seq_length = segments.shape
    group_rows = seq_count * seq_length
    local_width = project_weight.shape[2]
    score_scale = HEAD ** (-0.5)
    block_rows = min(512, seq_length)
    per_sequence = seq_length // block_rows
    count_blocks = group_rows // block_rows
    block_ids = jnp.arange(count_blocks, dtype=jnp.int32)
    triple_full, output_full, upward_full, downward_full = (
        lax.all_gather(project_weight, "dp", axis=0, tiled=True),
        lax.all_gather(output_weight, "dp", axis=1, tiled=True),
        lax.all_gather(up_weight, "dp", axis=0, tiled=True),
        lax.all_gather(down_weight, "dp", axis=1, tiled=True),
    )
    local_hidden = upward_full.shape[1]
    triple_matrix = triple_full.reshape(model_width, 3 * local_width)
    gathered = lax.all_gather(tokens, "tensor", axis=0, tiled=True)
    head_bias = lax.dynamic_slice_in_dim(bias_rows, tensor_rank * local_width, local_width, 1)
    projected = jnp.dot(gathered, triple_matrix, preferred_element_type=jnp.float32).reshape(
        group_rows, 3, local_width
    )
    queries = (projected[:, 0] + head_bias[0]).astype(jnp.bfloat16)
    key_rows = projected[:, 1].astype(jnp.bfloat16)
    value_rows = (projected[:, 2] + head_bias[1]).astype(jnp.bfloat16)

    def block_parts(block_index):
        sequence = block_index // per_sequence
        row_start = block_index * block_rows
        seq_start = sequence * seq_length
        query_block = split_heads(lax.dynamic_slice_in_dim(queries, row_start, block_rows, 0))
        key_block = split_heads(key_rows)
        value_block = split_heads(value_rows)
        seq_ids = lax.dynamic_index_in_dim(segments, sequence, 0, keepdims=False)
        query_ids = lax.dynamic_slice_in_dim(seq_ids, row_start - seq_start, block_rows, 0)
        products = (
            jnp.einsum("qhd,khd->hqk", query_block, key_block, preferred_element_type=jnp.float32)
            * score_scale
        )
        scores = jnp.where((query_ids[:, None] == seq_ids[None, :])[None], products, NEGATIVE)
        return (row_start, query_block, key_block, value_block, scores)

    def forward_block(block_index):
        row_start, query_block, key_block, value_block, scores = block_parts(block_index)
        row_max = jnp.max(scores, axis=-1, keepdims=True)
        exponent = jnp.exp(scores - row_max)
        row_sum = jnp.sum(exponent, axis=-1, keepdims=True)
        weights_low = (exponent / row_sum).astype(jnp.bfloat16)
        mixed_block = jnp.einsum(
            "hqk,khd->qhd", weights_low, value_block, preferred_element_type=jnp.float32
        )
        log_total = row_max[:, :, 0] + jnp.log(row_sum[:, :, 0])
        return (mixed_block.reshape(block_rows, local_width).astype(jnp.bfloat16), log_total)

    mixed_blocks, log_totals = lax.map(forward_block, block_ids)
    mixed_rows = mixed_blocks.reshape(group_rows, local_width)
    branch_out = (
        scatter_sum(
            jnp.dot(mixed_rows, output_full, preferred_element_type=jnp.float32), "tensor", 0
        )
        + bias_rows[2]
    )
    first_out, first_saved = layer_norm(
        tokens.astype(jnp.float32) + branch_out, norm_gains[0], bias_rows[3]
    )
    first_gathered = lax.all_gather(first_out.astype(jnp.bfloat16), "tensor", axis=0, tiled=True)
    local_bias = lax.dynamic_slice_in_dim(hidden_bias, tensor_rank * local_hidden, local_hidden, 0)
    upper_rows = (
        jnp.dot(first_gathered, upward_full, preferred_element_type=jnp.float32) + local_bias
    )
    hidden_full, gelu_back = jax.vjp(gelu_exact, upper_rows)
    hidden_rows = hidden_full.astype(jnp.bfloat16)
    second_out = (
        scatter_sum(
            jnp.dot(hidden_rows, downward_full, preferred_element_type=jnp.float32), "tensor", 0
        )
        + bias_rows[4]
    )
    layer_out, second_saved = layer_norm(first_out + second_out, norm_gains[1], bias_rows[5])
    reloaded = (
        lax.all_gather(project_weight, "dp", axis=0, tiled=True),
        lax.all_gather(output_weight, "dp", axis=1, tiled=True),
        lax.all_gather(up_weight, "dp", axis=0, tiled=True),
        lax.all_gather(down_weight, "dp", axis=1, tiled=True),
    )
    back_triple = reloaded[0].reshape(model_width, 3 * local_width)
    back_output, back_upward, back_downward = (reloaded[1], reloaded[2], reloaded[3])
    grad_layer = cotangent.astype(jnp.float32)
    grad_second_in, grad_gain_two, grad_shift_two = norm_back_saved(
        grad_layer, second_saved, norm_gains[1]
    )
    grad_second = grad_second_in.astype(jnp.bfloat16)
    grad_second_all = lax.all_gather(grad_second, "tensor", axis=0, tiled=True)
    grad_down_part = jnp.einsum(
        "tf,td->fd", hidden_rows, grad_second_all, preferred_element_type=jnp.float32
    )
    grad_hidden = jnp.einsum(
        "td,fd->tf", grad_second_all, back_downward, preferred_element_type=jnp.float32
    )
    grad_upper = gelu_back(grad_hidden)[0].astype(jnp.bfloat16)
    grad_up_part = jnp.einsum(
        "td,tf->df", first_gathered, grad_upper, preferred_element_type=jnp.float32
    )
    grad_first = (
        scatter_sum(
            jnp.einsum("tf,df->td", grad_upper, back_upward, preferred_element_type=jnp.float32),
            "tensor",
            0,
        )
        + grad_second_in
    )
    grad_first_in, grad_gain_one, grad_shift_one = norm_back_saved(grad_first, first_saved, norm_gains[0])
    grad_branch = grad_first_in.astype(jnp.bfloat16)
    grad_branch_all = lax.all_gather(grad_branch, "tensor", axis=0, tiled=True)
    grad_output_part = jnp.einsum(
        "tc,td->cd", mixed_rows, grad_branch_all, preferred_element_type=jnp.float32
    )
    grad_mixed = jnp.einsum(
        "td,cd->tc", grad_branch_all, back_output, preferred_element_type=jnp.float32
    ).astype(jnp.bfloat16)

    def backward_block(block_index):
        row_start, query_block, key_block, value_block, scores = block_parts(block_index)
        weights_full = jnp.exp(scores - log_totals[block_index][:, :, None])
        grad_mixed_block = split_heads(
            lax.dynamic_slice_in_dim(grad_mixed, row_start, block_rows, 0)
        )
        grad_weights = jnp.einsum(
            "qhd,khd->hqk", grad_mixed_block, value_block, preferred_element_type=jnp.float32
        )
        row_dot = jnp.sum(weights_full * grad_weights, axis=-1, keepdims=True)
        grad_scores = (weights_full * (grad_weights - row_dot)).astype(jnp.bfloat16)
        grad_query = (
            jnp.einsum("hqk,khd->qhd", grad_scores, key_block, preferred_element_type=jnp.float32)
            * score_scale
        )
        grad_key = (
            jnp.einsum("hqk,qhd->khd", grad_scores, query_block, preferred_element_type=jnp.float32)
            * score_scale
        )
        grad_value = jnp.einsum(
            "hqk,qhd->khd",
            weights_full.astype(jnp.bfloat16),
            grad_mixed_block,
            preferred_element_type=jnp.float32,
        )
        return (
            grad_query.reshape(block_rows, local_width),
            grad_key.reshape(seq_length, local_width),
            grad_value.reshape(seq_length, local_width),
        )

    query_blocks, key_blocks, value_blocks = lax.map(backward_block, block_ids)
    grad_queries = query_blocks.reshape(group_rows, local_width)
    grad_keys = (
        key_blocks.reshape(seq_count, per_sequence, seq_length, local_width)
        .sum(axis=1)
        .reshape(group_rows, local_width)
    )
    grad_values = (
        value_blocks.reshape(seq_count, per_sequence, seq_length, local_width)
        .sum(axis=1)
        .reshape(group_rows, local_width)
    )
    grad_projected = jnp.stack((grad_queries, grad_keys, grad_values), axis=1).astype(jnp.bfloat16)
    grad_project_part = jnp.einsum(
        "te,tsc->esc", gathered, grad_projected, preferred_element_type=jnp.float32
    )
    grad_matrix = grad_projected.reshape(group_rows, 3 * local_width)
    grad_tokens = (
        lax.psum_scatter(
            jnp.einsum(
                "tc,ec->te", grad_matrix, back_triple, preferred_element_type=jnp.float32
            ).astype(jnp.bfloat16),
            "tensor",
            scatter_dimension=0,
            tiled=True,
        ).astype(jnp.float32)
        + grad_first_in
    )
    grad_project, grad_output, grad_up, grad_down = (
        scatter_sum(grad_project_part, "dp", 0),
        scatter_sum(grad_output_part, "dp", 1),
        scatter_sum(grad_up_part, "dp", 0),
        scatter_sum(grad_down_part, "dp", 1),
    )
    head_terms = place_columns(
        jnp.stack(
            (
                jnp.sum(grad_projected[:, 0], axis=0, dtype=jnp.float32),
                jnp.sum(grad_projected[:, 2], axis=0, dtype=jnp.float32),
            )
        ),
        tensor_rank,
        model_width,
    )
    shared_terms = jnp.stack(
        (
            jnp.sum(grad_branch, axis=0, dtype=jnp.float32),
            grad_shift_one,
            jnp.sum(grad_second, axis=0, dtype=jnp.float32),
            grad_shift_two,
        )
    )
    bias_terms = jnp.concatenate((head_terms, shared_terms), axis=0)
    gain_terms = jnp.stack((grad_gain_one, grad_gain_two))
    hidden_terms = place_columns(
        jnp.sum(grad_upper, axis=0, dtype=jnp.float32), tensor_rank, hidden_bias.shape[0]
    )
    grad_gains, grad_bias_rows, grad_hidden_bias = lax.psum(
        (gain_terms, bias_terms, hidden_terms), ("dp", "tensor")
    )
    return (
        layer_out.astype(jnp.bfloat16),
        grad_tokens,
        grad_project,
        grad_output,
        grad_up,
        grad_down,
        grad_gains,
        grad_bias_rows,
        grad_hidden_bias,
    )


def solution(mesh):
    fits = mesh.shape["dp"] == 2 * LINES and mesh.shape["tensor"] == 4
    placed = (
        P(("dp", "tensor"), None),
        P("dp", None),
        P(("dp", "tensor"), None),
        P("dp", None, "tensor"),
        P("tensor", "dp"),
        P("dp", "tensor"),
        P("tensor", "dp"),
        P(),
        P(),
        P(),
    )
    return jax.shard_map(
        per_device_kernels if fits else per_device,
        mesh=mesh,
        in_specs=placed,
        out_specs=(
            P(("dp", "tensor"), None),
            P(("dp", "tensor"), None),
            P("dp", None, "tensor"),
            P("tensor", "dp"),
            P("dp", "tensor"),
            P("tensor", "dp"),
            P(),
            P(),
            P(),
        ),
        check_vma=False,
    )
```

```python
import functools
import types

import jax
import jax.numpy as jnp
from jax import lax
from jax.experimental import pallas as pl
from jax.experimental.pallas import tpu as pltpu
from jax.sharding import PartitionSpec as P

HEAD = 64
EPSILON = 1e-05
NEGATIVE = -1e30
MESH = pl.DeviceIdType.MESH
LINES = 4
CORE, ACROSS, FAR = 1, 2, 3
HALVES = 2
CHUNK = 16
VMEM_BYTES = 60 << 20


def remote(src, dst, send_sem, recv_sem, target):
    return pltpu.make_async_remote_copy(
        src_ref=src,
        dst_ref=dst,
        send_sem=send_sem,
        recv_sem=recv_sem,
        device_id=target,
        device_id_type=MESH,
    )


def position():
    return lax.axis_index("dp"), lax.axis_index("tensor")


def greet():
    dp, tensor = position()
    barrier = pltpu.get_barrier_semaphore()
    others = [(dp ^ step, tensor) for step in (1, 2, 4, 6)]
    others += [(dp, tensor ^ step) for step in (CORE, ACROSS)]
    for target in others:
        pl.semaphore_signal(barrier, inc=1, device_id=target, device_id_type=MESH)
    pl.semaphore_wait(barrier, len(others))


def row_piece(ref, index, size):
    return ref.at[pl.ds(pl.multiple_of(index * size, size), size), :]


def column_piece(ref, index, size):
    return ref.at[:, pl.ds(pl.multiple_of(index * size, size), size)]


class LineGather:
    def __init__(self, own, full, piece, send_sem, recv_sem, local_sem):
        self.own, self.full, self.piece = own, full, piece
        self.send_sem, self.recv_sem, self.local_sem = send_sem, recv_sem, local_sem
        self.dp, self.tensor = position()
        self.line, self.side = self.dp // 2, self.dp % 2
        self.targets = (
            (self.dp + 2, self.tensor),
            (self.dp - 2, self.tensor),
            (self.dp ^ 1, self.tensor),
        )

    def copy(self, index, way, src=None):
        view = self.piece(self.full, index)
        return remote(
            view if src is None else src,
            view,
            self.send_sem.at[way * LINES + index // 2],
            self.recv_sem.at[index],
            self.targets[way],
        )

    def local(self):
        return pltpu.make_async_copy(self.own, self.piece(self.full, self.dp), self.local_sem)

    def start(self):
        self.local().start()

        @pl.when(self.line < LINES - 1)
        def _():
            self.copy(self.dp, 0, self.own).start()

        @pl.when(self.line > 0)
        def _():
            self.copy(self.dp, 1, self.own).start()

        self.copy(self.dp, 2, self.own).start()

    def step(self, distance):
        @pl.when(self.line >= distance)
        def _():
            index = self.dp - 2 * distance
            self.copy(index, 0).wait_recv()

            @pl.when(self.line < LINES - 1)
            def _():
                self.copy(index, 0).start()

            self.copy(index, 2).start()

        @pl.when(self.line + distance < LINES)
        def _():
            index = self.dp + 2 * distance
            self.copy(index, 1).wait_recv()

            @pl.when(self.line > 0)
            def _():
                self.copy(index, 1).start()

            self.copy(index, 2).start()

    def arrive(self):
        self.local().wait()
        for line in range(LINES):
            self.copy(2 * line + 1 - self.side, 2).wait_recv()

    def finish(self):
        for line in range(LINES):
            index = 2 * line + self.side
            self.copy(index, 2).wait_send()

            @pl.when((self.line < LINES - 1) & (line <= self.line))
            def _():
                self.copy(index, 0).wait_send()

            @pl.when((self.line > 0) & (line >= self.line))
            def _():
                self.copy(index, 1).wait_send()


class RowGather:
    def __init__(self, full, rows, send_sem, recv_sem):
        self.full, self.rows = full, rows
        self.send_sem, self.recv_sem = send_sem, recv_sem
        self.dp, self.tensor = position()

    def view(self, rank, half=None):
        if half is None:
            return row_piece(self.full, rank, self.rows)
        return row_piece(self.full, rank * HALVES + half, self.rows // HALVES)

    def near(self, rank):
        view = self.view(rank)
        target = (self.dp, self.tensor ^ CORE)
        return remote(view, view, self.send_sem.at[0], self.recv_sem.at[0], target)

    def across(self, rank, half):
        view, slot = self.view(rank, half), 1 + half
        target = (self.dp, self.tensor ^ ACROSS)
        return remote(view, view, self.send_sem.at[slot], self.recv_sem.at[slot], target)

    def far(self, rank, half):
        view, slot = self.view(rank, half), 1 + HALVES + half
        target = (self.dp, self.tensor ^ CORE)
        return remote(view, view, self.send_sem.at[slot], self.recv_sem.at[slot], target)

    def start(self):
        for half in range(HALVES):
            self.across(self.tensor, half).start()
        self.near(self.tensor).start()

    def wait_near(self):
        self.near(self.tensor ^ CORE).wait_recv()

    def wait_across(self, half):
        self.across(self.tensor ^ ACROSS, half).wait_recv()
        self.far(self.tensor ^ ACROSS, half).start()

    def wait_far(self, half):
        self.far(self.tensor ^ FAR, half).wait_recv()

    def finish(self):
        self.near(self.tensor).wait_send()
        for half in range(HALVES):
            self.across(self.tensor, half).wait_send()
            self.far(self.tensor ^ ACROSS, half).wait_send()


class RowScatter:
    def __init__(self, near_out, near_in, across_out, across_in, send_sem, recv_sem):
        self.near_out, self.near_in = near_out, near_in
        self.across_out, self.across_in = across_out, across_in
        self.send_sem, self.recv_sem = send_sem, recv_sem
        self.dp, self.tensor = position()

    def near(self, slot):
        return remote(
            self.near_out.at[slot],
            self.near_in.at[slot],
            self.send_sem.at[slot],
            self.recv_sem.at[slot],
            (self.dp, self.tensor ^ CORE),
        )

    def across(self, half):
        rows = self.across_in.shape[0] // HALVES
        return remote(
            row_piece(self.across_out, half, rows),
            row_piece(self.across_in, half, rows),
            self.send_sem.at[2 * HALVES + half],
            self.recv_sem.at[2 * HALVES + half],
            (self.dp, self.tensor ^ ACROSS),
        )

    def give_far(self, half, partial):
        self.near_out[half] = partial.astype(jnp.bfloat16)
        self.near(half).start()

    def give_across(self, half, partial):
        self.near(half).wait_recv()
        rows = partial.shape[0]
        total = partial + self.near_in[half].astype(jnp.float32)
        self.across_out[half * rows : (half + 1) * rows, :] = total.astype(jnp.bfloat16)
        self.across(half).start()

    def give_near(self, half, partial):
        self.near_out[HALVES + half] = partial.astype(jnp.bfloat16)
        self.near(HALVES + half).start()

    def take(self, half, partial):
        self.near(HALVES + half).wait_recv()
        rows = partial.shape[0]
        total = partial + self.near_in[HALVES + half].astype(jnp.float32)
        self.across(half).wait_recv()
        return total + self.across_in[half * rows : (half + 1) * rows, :].astype(jnp.float32)

    def finish(self):
        for slot in range(2 * HALVES):
            self.near(slot).wait_send()
        for half in range(HALVES):
            self.across(half).wait_send()


def dot(left, right):
    return jnp.dot(left, right, preferred_element_type=jnp.float32)


def dot_nt(left, right):
    return lax.dot_general(left, right, (((1,), (1,)), ((), ())), preferred_element_type=jnp.float32)


def dot_tn(left, right):
    return lax.dot_general(left, right, (((0,), (0,)), ((), ())), preferred_element_type=jnp.float32)


def normalize(rows):
    centred = rows - jnp.mean(rows, axis=-1, keepdims=True)
    inverse = lax.rsqrt(jnp.mean(centred * centred, axis=-1, keepdims=True) + EPSILON)
    return centred * inverse, inverse


def norm_back(grad, normed, inverse):
    average = jnp.mean(grad, axis=-1, keepdims=True)
    along = jnp.mean(grad * normed, axis=-1, keepdims=True)
    return inverse * (grad - average - normed * along)


class LineScatter:
    def __init__(self, partial, piece, side_in, line_in, send_sem, recv_sem):
        self.partial, self.piece, self.side_in, self.line_in = partial, piece, side_in, line_in
        self.send_sem, self.recv_sem = send_sem, recv_sem
        self.dp, self.tensor = position()

    def view(self, step):
        return self.piece(self.partial, self.dp ^ (2 * step))

    def across(self, step):
        return remote(
            self.piece(self.partial, self.dp ^ (2 * step) ^ 1),
            self.side_in.at[step],
            self.send_sem.at[step],
            self.recv_sem.at[step],
            (self.dp ^ 1, self.tensor),
        )

    def along(self, step):
        return remote(
            self.view(step),
            self.line_in.at[step - 1],
            self.send_sem.at[LINES + step],
            self.recv_sem.at[LINES + step],
            (self.dp ^ (2 * step), self.tensor),
        )

    def start(self):
        for step in reversed(range(LINES)):
            self.across(step).start()

    def total(self, step):
        self.across(step).wait_recv()
        return self.view(step)[...].astype(jnp.float32) + self.side_in[step].astype(jnp.float32)

    def relay(self, step):
        self.view(step)[...] = self.total(step).astype(jnp.bfloat16)
        self.along(step).start()

    def finish(self, result):
        total = self.total(0)
        for step in range(1, LINES):
            self.along(step).wait_recv()
            total = total + self.line_in[step - 1].astype(jnp.float32)
        result[...] = total
        for step in range(LINES):
            self.across(step).wait_send()
        for step in range(1, LINES):
            self.along(step).wait_send()


class Total:
    def __init__(self, held, arrived, send_sem, recv_sem):
        self.held, self.arrived, self.send_sem, self.recv_sem = held, arrived, send_sem, recv_sem
        dp, tensor = position()
        self.targets = (
            (dp, tensor ^ CORE),
            (dp ^ 1, tensor),
            (dp ^ 2, tensor),
            (dp ^ 4, tensor),
            (dp, tensor ^ ACROSS),
        )

    def copy(self, step):
        return remote(
            self.held.at[step],
            self.arrived.at[step],
            self.send_sem.at[step],
            self.recv_sem.at[step],
            self.targets[step],
        )

    def start(self):
        self.copy(0).start()

    def step(self, step):
        self.copy(step).wait_recv()
        self.held[step + 1] = self.held[step] + self.arrived[step]
        if step + 1 < len(self.targets):
            self.copy(step + 1).start()

    def finish(self):
        for step in range(len(self.targets)):
            self.copy(step).wait_send()


def layer_kernel(names, rows, *refs):
    r = types.SimpleNamespace(**dict(zip(names, refs)))
    dp, tensor = position()
    bf16, f32 = jnp.bfloat16, jnp.float32
    half_rows = rows // HALVES
    local = r.queries.shape[1]
    piece = r.triple_own.shape[0]
    pairs = local // (2 * HEAD)
    near, across, far = tensor ^ CORE, tensor ^ ACROSS, tensor ^ FAR

    def of_rows(ref, index):
        return row_piece(ref, index, piece)

    def of_columns(ref, index):
        return column_piece(ref, index, piece)

    def block(rank, size=rows):
        return pl.ds(pl.multiple_of(rank * size, size), size)

    def split(partial):
        return [partial[half * half_rows : (half + 1) * half_rows] for half in range(HALVES)]

    def part_of(half):
        return slice(half * half_rows, (half + 1) * half_rows)

    lines = [
        LineGather(own, full, view, r.line_send.at[at], r.line_recv.at[at], r.line_local.at[at])
        for at, (own, full, view) in enumerate(
            (
                (r.triple_own, r.triple, of_rows),
                (r.output_own, r.output, of_columns),
                (r.up_own, r.up, of_rows),
                (r.down_own, r.down, of_columns),
            )
        )
    ]
    triple_line, output_line, up_line, down_line = lines
    sums = [
        LineScatter(partial, view, side, along, r.part_send.at[at], r.part_recv.at[at])
        for at, (partial, view, side, along) in enumerate(
            (
                (r.grad_project, of_rows, r.project_side, r.project_line),
                (r.grad_output, of_columns, r.output_side, r.output_line),
                (r.grad_up, of_rows, r.up_side, r.up_line),
                (r.grad_down, of_columns, r.down_side, r.down_line),
            )
        )
    ]
    project_sum, output_sum, up_sum, down_sum = sums
    gathers = [
        RowGather(full, rows, r.row_send.at[at], r.row_recv.at[at])
        for at, full in enumerate((r.gathered, r.first_all, r.second_all, r.branch_all))
    ]
    scatters = [
        RowScatter(*buffers, r.sum_send.at[at], r.sum_recv.at[at])
        for at, buffers in enumerate(
            (
                (r.near_out_a, r.near_in_a, r.across_out_a, r.across_in_a),
                (r.near_out_b, r.near_in_b, r.across_out_b, r.across_in_b),
            )
            * 2
        )
    ]
    total = Total(r.held_totals, r.arrived_totals, r.total_send, r.total_recv)

    def scatter_blocks(scatter, product):
        for half, partial in enumerate(split(product(far))):
            scatter.give_far(half, partial)
        for half, partial in enumerate(split(product(across))):
            scatter.give_across(half, partial)
        for half, partial in enumerate(split(product(near))):
            scatter.give_near(half, partial)

    greet()
    place = pltpu.make_async_copy(r.tokens, gathers[0].view(tensor), r.place_sem)
    place.start()
    triple_line.start()
    place.wait()
    gathers[0].start()
    triple_line.step(1)
    triple_line.step(2)
    gathers[0].wait_near()
    for half in range(HALVES):
        gathers[0].wait_across(half)
    triple_line.step(3)
    output_line.start()
    up_line.start()
    for half in range(HALVES):
        gathers[0].wait_far(half)
    triple_line.arrive()
    columns = pl.ds(pl.multiple_of(tensor * local, local), local)
    query_bias = r.bias_rows[0:1, columns]
    value_bias = r.bias_rows[1:2, columns]

    @pl.loop(0, 4)
    def _(index):
        here = block(index)
        left = r.gathered[here, :]
        query = (dot(left, r.triple[:, :local]) + query_bias).astype(bf16)
        r.queries[here, :] = query * bf16(HEAD**-0.5)
        key = dot(left, r.triple[:, local : 2 * local])
        r.key_rows[here, :] = key.astype(bf16)
        r.key_turned[:, here] = key.T.astype(bf16)
        value = dot(left, r.triple[:, 2 * local :]) + value_bias
        r.value_rows[here, :] = value.astype(bf16)
        r.value_turned[:, here] = value.T.astype(bf16)

    output_line.step(1)
    up_line.step(1)
    down_line.start()

    def head_rows(head):
        return pl.ds(pl.multiple_of(head * HEAD, HEAD), HEAD)

    def attend(rank):
        here = block(rank)

        @pl.loop(0, pairs)
        def _(pair):
            lanes = block(pair, 2 * HEAD)
            query = r.queries[here, lanes]
            keys = r.key_rows[:, lanes]
            same = r.segment_column[...] == r.segment_row[:, here]
            lane = lax.broadcasted_iota(jnp.int32, query.shape, 1)
            outs = []
            for side in range(2):
                scores = dot_nt(keys, jnp.where(lane // HEAD == side, query, bf16(0)))
                scores = jnp.where(same, scores, NEGATIVE)
                top = jnp.max(scores, axis=0, keepdims=True)
                exponent = jnp.exp(scores - top)
                mass = jnp.sum(exponent, axis=0, keepdims=True)
                weights = (exponent * (1.0 / mass)).astype(bf16)
                head = pair * 2 + side
                outs.append(dot(r.value_turned[head_rows(head), :], weights))
                r.log_totals[pl.ds(head, 1), here] = top + jnp.log(mass)
            r.mixed[here, lanes] = jnp.concatenate(outs, axis=0).T.astype(bf16)

        return r.mixed[here, :]

    mixed_far = attend(far)
    output_line.step(2)
    output_line.step(3)
    up_line.step(2)
    output_line.arrive()
    for half, partial in enumerate(split(dot(mixed_far, r.output[...]))):
        scatters[0].give_far(half, partial)
    for half, partial in enumerate(split(dot(attend(across), r.output[...]))):
        scatters[0].give_across(half, partial)
    up_line.step(3)
    down_line.step(1)
    for half, partial in enumerate(split(dot(attend(near), r.output[...]))):
        scatters[0].give_near(half, partial)
    down_line.step(2)
    for half, partial in enumerate(split(dot(attend(tensor), r.output[...]))):
        part = part_of(half)
        own_rows = r.gathered[block(tensor * HALVES + half, half_rows), :].astype(f32)
        normed, inverse = normalize(own_rows + scatters[0].take(half, partial) + r.bias_rows[2:3, :])
        r.normed_one[part, :] = normed
        r.inverse_one[part, :] = inverse
        first = normed * r.norm_gains[0:1, :] + r.bias_rows[3:4, :]
        r.first_all[block(tensor * HALVES + half, half_rows), :] = first.astype(bf16)
    scatters[0].finish()

    gathers[1].start()
    down_line.step(3)
    r.sums[...] = jnp.zeros_like(r.sums)

    def chunks(size, start, body):
        @pl.loop(0, size // CHUNK)
        def _(chunk):
            offset = chunk * CHUNK
            body(
                pl.ds(pl.multiple_of(offset, CHUNK), CHUNK),
                pl.ds(pl.multiple_of(start + offset, CHUNK), CHUNK),
            )

    def extent(rank, half):
        size = rows if half is None else half_rows
        start = rank * rows + (0 if half is None else half * half_rows)
        return start, size, pl.ds(pl.multiple_of(start, size), size)

    def up_part(rank, half=None):
        start, size, here = extent(rank, half)
        r.upper[:size, :] = dot(r.first_all[here, :], r.up[...]) + r.hidden_bias[...]

        def body(part, into):
            value = r.upper[part, :]
            share = 0.5 + 0.5 * lax.erf(value * (0.5**0.5))
            r.hidden[into, :] = (value * share).astype(bf16)
            bell = jnp.exp(value * value * -0.5) * (2 * jnp.pi) ** -0.5
            r.slope[into, :] = share + value * bell

        chunks(size, start, body)

    def down_part(rank, half=None):
        return dot(r.hidden[extent(rank, half)[2], :], r.down[...])

    def back_part(rank, half=None):
        start, size, here = extent(rank, half)
        r.upper[:size, :] = dot_nt(r.second_all[here, :], r.down[...])

        def body(part, into):
            low = (r.upper[part, :] * r.slope[into, :]).astype(bf16)
            r.upper_low[into, :] = low
            r.sums[6:7, :] += jnp.sum(low.astype(f32), axis=0, keepdims=True)

        chunks(size, start, body)
        return dot_nt(r.upper_low[here, :], r.up[...])

    up_line.arrive()
    up_part(tensor)
    gathers[1].wait_near()
    up_part(near)
    for half in range(HALVES):
        gathers[1].wait_across(half)
        up_part(across, half)
        gathers[1].wait_far(half)
        up_part(far, half)
    down_line.arrive()
    scatter_blocks(scatters[1], down_part)
    r.kept[...] = down_part(tensor)

    def add_to(row, value):
        r.sums[row : row + 1, :] += jnp.sum(value, axis=0, keepdims=True)

    def second_norm(_, here):
        first = r.normed_one[here, :] * r.norm_gains[0:1, :] + r.bias_rows[3:4, :]
        normed, inverse = normalize(first + r.kept[here, :] + r.bias_rows[4:5, :])
        shifted = normed * r.norm_gains[1:2, :] + r.bias_rows[5:6, :]
        r.layer_out[here, :] = shifted.astype(bf16)
        grad = r.cotangent[here, :].astype(f32)
        add_to(5, grad * normed)
        add_to(3, grad)
        grad = norm_back(grad * r.norm_gains[1:2, :], normed, inverse)
        r.grad_rows[here, :] = grad
        low = grad.astype(bf16)
        add_to(2, low.astype(f32))
        r.second_all[pl.ds(pl.multiple_of(tensor * rows + here.start, CHUNK), CHUNK), :] = low

    for half in range(HALVES):
        part = part_of(half)
        r.kept[part, :] = scatters[1].take(half, r.kept[part, :])
        chunks(half_rows, half * half_rows, second_norm)
    scatters[1].finish()

    gathers[2].start()
    r.kept[...] = back_part(tensor)
    gathers[2].wait_near()
    for half, partial in enumerate(split(back_part(near))):
        scatters[2].give_near(half, partial)
    for half in range(HALVES):
        gathers[2].wait_across(half)
        r.held[...] = back_part(across, half)
        gathers[2].wait_far(half)
        scatters[2].give_far(half, back_part(far, half))
        scatters[2].give_across(half, r.held[...])

    def weight_grad(left, right, result):
        @pl.loop(0, left.shape[1] // rows)
        def _(index):
            lanes = block(index)
            result[lanes, :] = dot_tn(left[:, lanes], right[...]).astype(bf16)

    weight_grad(r.hidden, r.second_all, r.grad_down)
    down_sum.start()
    weight_grad(r.first_all, r.upper_low, r.grad_up)
    up_sum.start()

    def first_norm(_, here):
        grad = r.grad_rows[here, :] + r.kept[here, :]
        normed = r.normed_one[here, :]
        add_to(4, grad * normed)
        add_to(1, grad)
        grad = norm_back(grad * r.norm_gains[0:1, :], normed, r.inverse_one[here, :])
        r.grad_rows[here, :] = grad
        low = grad.astype(bf16)
        add_to(0, low.astype(f32))
        r.branch_all[pl.ds(pl.multiple_of(tensor * rows + here.start, CHUNK), CHUNK), :] = low

    for half in range(HALVES):
        part = part_of(half)
        r.kept[part, :] = scatters[2].take(half, r.kept[part, :])
        chunks(half_rows, half * half_rows, first_norm)
    scatters[2].finish()

    gathers[3].start()
    grad_keys, grad_values = r.slope.at[:, :local], r.slope.at[:, local : 2 * local]
    r.slope[:, : 2 * local] = jnp.zeros((r.slope.shape[0], 2 * local), f32)

    def attend_back(rank):
        here = block(rank)
        r.mixed_low[...] = dot_nt(r.branch_all[here, :], r.output[...]).astype(bf16)

        @pl.loop(0, pairs)
        def _(pair):
            lanes = block(pair, 2 * HEAD)
            query = r.queries[here, lanes]
            grad = r.mixed_low[:, lanes]
            keys = r.key_rows[:, lanes]
            values = r.value_rows[:, lanes]
            same = r.segment_column[...] == r.segment_row[:, here]
            lane = lax.broadcasted_iota(jnp.int32, query.shape, 1)
            outs = []
            for side in range(2):
                mine = lane // HEAD == side
                head = pair * 2 + side
                query_here = jnp.where(mine, query, bf16(0))
                grad_here = jnp.where(mine, grad, bf16(0))
                scores = jnp.where(same, dot_nt(keys, query_here), NEGATIVE)
                weights = jnp.exp(scores - r.log_totals[pl.ds(head, 1), here])
                grad_weights = dot_nt(values, grad_here)
                along = jnp.sum(weights * grad_weights, axis=0, keepdims=True)
                grad_scores = (weights * (grad_weights - along)).astype(bf16)
                grad_keys[:, lanes] += dot(grad_scores, query_here)
                grad_values[:, lanes] += dot(weights.astype(bf16), grad_here)
                outs.append(dot(r.key_turned[head_rows(head), :], grad_scores))
            grad_query = jnp.concatenate(outs, axis=0).T * HEAD**-0.5
            r.projected_low[here, lanes] = grad_query.astype(bf16)

    attend_back(tensor)
    down_sum.relay(3)
    gathers[3].wait_near()
    attend_back(near)
    down_sum.relay(2)
    for half in range(HALVES):
        gathers[3].wait_across(half)
    attend_back(across)
    down_sum.relay(1)
    for half in range(HALVES):
        gathers[3].wait_far(half)
    r.grad_output[...] = dot_tn(r.mixed[...], r.branch_all[...]).astype(bf16)
    output_sum.start()
    attend_back(far)
    r.projected_low[:, local : 2 * local] = grad_keys[...].astype(bf16)
    r.projected_low[:, 2 * local :] = grad_values[...].astype(bf16)
    weight_grad(r.gathered, r.projected_low, r.grad_project)
    project_sum.start()
    r.held_totals[0] = jnp.zeros(r.held_totals.shape[1:], f32)
    r.held_totals[0, 2:8, :] = r.sums[0:6, :]
    r.held_totals[0, pl.ds(8 + tensor, 1), :] = r.sums[6:7, :]
    for row, at in ((0, 0), (1, 2)):
        low = r.projected_low[:, at * local : (at + 1) * local].astype(f32)
        r.held_totals[0, row : row + 1, columns] = jnp.sum(low, axis=0, keepdims=True)
    total.start()
    up_sum.relay(3)

    def token_part(rank):
        return dot_nt(r.projected_low[block(rank), :], r.triple[...])

    scatter_blocks(scatters[3], token_part)
    total.step(0)
    up_sum.relay(2)
    mine = split(token_part(tensor))
    total.step(1)
    up_sum.relay(1)
    down_sum.finish(r.down_out)
    total.step(2)
    for half, partial in enumerate(mine):
        part = part_of(half)
        r.grad_tokens[part, :] = scatters[3].take(half, partial) + r.grad_rows[part, :]
    for step in (3, 2, 1):
        output_sum.relay(step)
    total.step(3)
    up_sum.finish(r.up_out)
    for step in (3, 2, 1):
        project_sum.relay(step)
    total.step(4)
    r.bias_out[...] = r.held_totals[5, 0:6, :]
    r.gains_out[...] = r.held_totals[5, 6:8, :]
    r.hidden_out[...] = r.held_totals[5, 8:12, :]
    output_sum.finish(r.output_out)
    project_sum.finish(r.project_out)
    scatters[3].finish()
    for each in gathers + lines + [total]:
        each.finish()


def per_device_kernel(
    tokens,
    segments,
    cotangent,
    project_weight,
    output_weight,
    up_weight,
    down_weight,
    norm_gains,
    bias_rows,
    hidden_bias,
):
    rows, width = tokens.shape
    length = segments.shape[1]
    local_hidden = up_weight.shape[1]
    local = output_weight.shape[0]
    piece = project_weight.shape[0]
    bf16, f32 = jnp.bfloat16, jnp.float32
    local_bias = lax.dynamic_slice_in_dim(
        hidden_bias, lax.axis_index("tensor") * local_hidden, local_hidden, 0
    )
    remote_inputs = dict(
        tokens=tokens,
        triple_own=project_weight.reshape(piece, -1),
        output_own=output_weight,
        up_own=up_weight,
        down_own=down_weight,
    )
    inputs = dict(
        segment_column=segments.reshape(length, 1),
        segment_row=segments.reshape(1, length),
        cotangent=cotangent,
        norm_gains=norm_gains,
        bias_rows=bias_rows,
        hidden_bias=local_bias.reshape(1, -1),
    )
    shapes = dict(
        project=(piece, 3 * local),
        output=(local, piece),
        up=(piece, local_hidden),
        down=(local_hidden, piece),
    )
    outputs = dict(layer_out=((rows, width), bf16), grad_tokens=((rows, width), f32))
    outputs |= {name + "_out": (shape, f32) for name, shape in shapes.items()}
    outputs |= dict(
        gains_out=((2, width), f32),
        bias_out=((6, width), f32),
        hidden_out=((4, width), f32),
    )
    scratch = dict(
        gathered=((length, width), bf16),
        triple=((width, 3 * local), bf16),
        output=((local, width), bf16),
        up=((width, local_hidden), bf16),
        down=((local_hidden, width), bf16),
        queries=((length, local), bf16),
        key_rows=((length, local), bf16),
        value_rows=((length, local), bf16),
        key_turned=((local, length), bf16),
        value_turned=((local, length), bf16),
        mixed=((length, local), bf16),
        log_totals=((local // HEAD, length), f32),
        normed_one=((rows, width), f32),
        inverse_one=((rows, 1), f32),
        first_all=((length, width), bf16),
        hidden=((length, local_hidden), bf16),
        slope=((length, local_hidden), f32),
        second_all=((length, width), bf16),
        upper_low=((length, local_hidden), bf16),
        upper=((rows, local_hidden), f32),
        kept=((rows, width), f32),
        held=((rows // HALVES, width), f32),
        grad_rows=((rows, width), f32),
        sums=((8, width), f32),
        branch_all=((length, width), bf16),
        mixed_low=((rows, local), bf16),
        projected_low=((length, 3 * local), bf16),
        grad_project=((width, 3 * local), bf16),
        grad_output=((local, width), bf16),
        grad_up=((width, local_hidden), bf16),
        grad_down=((local_hidden, width), bf16),
        held_totals=((6, 16, width), f32),
        arrived_totals=((5, 16, width), f32),
    )
    for name, shape in shapes.items():
        scratch[name + "_side"] = ((LINES,) + shape, bf16)
        scratch[name + "_line"] = ((LINES - 1,) + shape, bf16)
    for at in "ab":
        for name in ("near_out_", "near_in_"):
            scratch[name + at] = ((2 * HALVES, rows // HALVES, width), bf16)
        for name in ("across_out_", "across_in_"):
            scratch[name + at] = ((rows, width), bf16)
    semaphores = dict(
        line_send=(4, 3 * LINES),
        line_recv=(4, 2 * LINES),
        line_local=(4,),
        part_send=(4, 2 * LINES),
        part_recv=(4, 2 * LINES),
        row_send=(4, 1 + 2 * HALVES),
        row_recv=(4, 1 + 2 * HALVES),
        sum_send=(4, 3 * HALVES),
        sum_recv=(4, 3 * HALVES),
        total_send=(5,),
        total_recv=(5,),
        place_sem=(),
    )
    names = [*remote_inputs, *inputs, *outputs, *scratch, *semaphores]
    vmem, hbm = pl.BlockSpec(memory_space=pltpu.VMEM), pl.BlockSpec(memory_space=pltpu.HBM)
    results = pl.pallas_call(
        functools.partial(layer_kernel, names, rows),
        out_shape=[jax.ShapeDtypeStruct(*leaf) for leaf in outputs.values()],
        in_specs=[hbm] * len(remote_inputs) + [vmem] * len(inputs),
        out_specs=[vmem] * len(outputs),
        scratch_shapes=[pltpu.VMEM(*leaf) for leaf in scratch.values()]
        + [pltpu.SemaphoreType.DMA(shape) for shape in semaphores.values()],
        compiler_params=pltpu.CompilerParams(
            collective_id=0, has_side_effects=True, vmem_limit_bytes=VMEM_BYTES
        ),
        name="layer",
    )(*remote_inputs.values(), *inputs.values())
    result = dict(zip(outputs, results))
    return (
        result["layer_out"],
        result["grad_tokens"],
        result["project_out"].reshape(project_weight.shape),
        result["output_out"],
        result["up_out"],
        result["down_out"],
        result["gains_out"],
        result["bias_out"],
        result["hidden_out"].reshape(-1),
    )


def gelu_exact(values):
    return jax.nn.gelu(values, approximate=False)


def layer_norm(token_rows, gain, shift):
    average = jnp.mean(token_rows, axis=-1, keepdims=True)
    centred = token_rows - average
    variance = jnp.mean(centred * centred, axis=-1, keepdims=True)
    inverse = lax.rsqrt(variance + EPSILON)
    normed = centred * inverse
    return (normed * gain + shift, (normed, inverse))


def norm_back_saved(grad_rows, saved, gain):
    normed, inverse = saved
    grad_gain = jnp.sum(grad_rows * normed, axis=0)
    grad_shift = jnp.sum(grad_rows, axis=0)
    grad_normed = grad_rows * gain
    grad_input = inverse * (
        grad_normed
        - jnp.mean(grad_normed, axis=-1, keepdims=True)
        - normed * jnp.mean(grad_normed * normed, axis=-1, keepdims=True)
    )
    return (grad_input, grad_gain, grad_shift)


def split_heads(token_rows):
    return token_rows.reshape(token_rows.shape[0], token_rows.shape[1] // HEAD, HEAD)


def scatter_sum(partial_sum, axis_name, dimension):
    return lax.psum_scatter(
        partial_sum.astype(jnp.bfloat16), axis_name, scatter_dimension=dimension, tiled=True
    ).astype(jnp.float32)


def place_columns(partial_sum, column_block, total_width):
    full_rows = jnp.zeros(partial_sum.shape[:-1] + (total_width,), jnp.float32)
    return lax.dynamic_update_slice_in_dim(
        full_rows, partial_sum, column_block * partial_sum.shape[-1], partial_sum.ndim - 1
    )


def per_device(
    tokens,
    segments,
    cotangent,
    project_weight,
    output_weight,
    up_weight,
    down_weight,
    norm_gains,
    bias_rows,
    hidden_bias,
):
    tensor_rank = lax.axis_index("tensor")
    local_rows, model_width = tokens.shape
    seq_count, seq_length = segments.shape
    group_rows = seq_count * seq_length
    local_width = project_weight.shape[2]
    score_scale = HEAD ** (-0.5)
    block_rows = min(512, seq_length)
    per_sequence = seq_length // block_rows
    count_blocks = group_rows // block_rows
    block_ids = jnp.arange(count_blocks, dtype=jnp.int32)
    triple_full, output_full, upward_full, downward_full = (
        lax.all_gather(project_weight, "dp", axis=0, tiled=True),
        lax.all_gather(output_weight, "dp", axis=1, tiled=True),
        lax.all_gather(up_weight, "dp", axis=0, tiled=True),
        lax.all_gather(down_weight, "dp", axis=1, tiled=True),
    )
    local_hidden = upward_full.shape[1]
    triple_matrix = triple_full.reshape(model_width, 3 * local_width)
    gathered = lax.all_gather(tokens, "tensor", axis=0, tiled=True)
    head_bias = lax.dynamic_slice_in_dim(bias_rows, tensor_rank * local_width, local_width, 1)
    projected = jnp.dot(gathered, triple_matrix, preferred_element_type=jnp.float32).reshape(
        group_rows, 3, local_width
    )
    queries = (projected[:, 0] + head_bias[0]).astype(jnp.bfloat16)
    key_rows = projected[:, 1].astype(jnp.bfloat16)
    value_rows = (projected[:, 2] + head_bias[1]).astype(jnp.bfloat16)

    def block_parts(block_index):
        sequence = block_index // per_sequence
        row_start = block_index * block_rows
        seq_start = sequence * seq_length
        query_block = split_heads(lax.dynamic_slice_in_dim(queries, row_start, block_rows, 0))
        key_block = split_heads(key_rows)
        value_block = split_heads(value_rows)
        seq_ids = lax.dynamic_index_in_dim(segments, sequence, 0, keepdims=False)
        query_ids = lax.dynamic_slice_in_dim(seq_ids, row_start - seq_start, block_rows, 0)
        products = (
            jnp.einsum("qhd,khd->hqk", query_block, key_block, preferred_element_type=jnp.float32)
            * score_scale
        )
        scores = jnp.where((query_ids[:, None] == seq_ids[None, :])[None], products, NEGATIVE)
        return (row_start, query_block, key_block, value_block, scores)

    def forward_block(block_index):
        row_start, query_block, key_block, value_block, scores = block_parts(block_index)
        row_max = jnp.max(scores, axis=-1, keepdims=True)
        exponent = jnp.exp(scores - row_max)
        row_sum = jnp.sum(exponent, axis=-1, keepdims=True)
        weights_low = (exponent / row_sum).astype(jnp.bfloat16)
        mixed_block = jnp.einsum(
            "hqk,khd->qhd", weights_low, value_block, preferred_element_type=jnp.float32
        )
        log_total = row_max[:, :, 0] + jnp.log(row_sum[:, :, 0])
        return (mixed_block.reshape(block_rows, local_width).astype(jnp.bfloat16), log_total)

    mixed_blocks, log_totals = lax.map(forward_block, block_ids)
    mixed_rows = mixed_blocks.reshape(group_rows, local_width)
    branch_out = (
        scatter_sum(
            jnp.dot(mixed_rows, output_full, preferred_element_type=jnp.float32), "tensor", 0
        )
        + bias_rows[2]
    )
    first_out, first_saved = layer_norm(
        tokens.astype(jnp.float32) + branch_out, norm_gains[0], bias_rows[3]
    )
    first_gathered = lax.all_gather(first_out.astype(jnp.bfloat16), "tensor", axis=0, tiled=True)
    local_bias = lax.dynamic_slice_in_dim(hidden_bias, tensor_rank * local_hidden, local_hidden, 0)
    upper_rows = (
        jnp.dot(first_gathered, upward_full, preferred_element_type=jnp.float32) + local_bias
    )
    hidden_full, gelu_back = jax.vjp(gelu_exact, upper_rows)
    hidden_rows = hidden_full.astype(jnp.bfloat16)
    second_out = (
        scatter_sum(
            jnp.dot(hidden_rows, downward_full, preferred_element_type=jnp.float32), "tensor", 0
        )
        + bias_rows[4]
    )
    layer_out, second_saved = layer_norm(first_out + second_out, norm_gains[1], bias_rows[5])
    reloaded = (
        lax.all_gather(project_weight, "dp", axis=0, tiled=True),
        lax.all_gather(output_weight, "dp", axis=1, tiled=True),
        lax.all_gather(up_weight, "dp", axis=0, tiled=True),
        lax.all_gather(down_weight, "dp", axis=1, tiled=True),
    )
    back_triple = reloaded[0].reshape(model_width, 3 * local_width)
    back_output, back_upward, back_downward = (reloaded[1], reloaded[2], reloaded[3])
    grad_layer = cotangent.astype(jnp.float32)
    grad_second_in, grad_gain_two, grad_shift_two = norm_back_saved(
        grad_layer, second_saved, norm_gains[1]
    )
    grad_second = grad_second_in.astype(jnp.bfloat16)
    grad_second_all = lax.all_gather(grad_second, "tensor", axis=0, tiled=True)
    grad_down_part = jnp.einsum(
        "tf,td->fd", hidden_rows, grad_second_all, preferred_element_type=jnp.float32
    )
    grad_hidden = jnp.einsum(
        "td,fd->tf", grad_second_all, back_downward, preferred_element_type=jnp.float32
    )
    grad_upper = gelu_back(grad_hidden)[0].astype(jnp.bfloat16)
    grad_up_part = jnp.einsum(
        "td,tf->df", first_gathered, grad_upper, preferred_element_type=jnp.float32
    )
    grad_first = (
        scatter_sum(
            jnp.einsum("tf,df->td", grad_upper, back_upward, preferred_element_type=jnp.float32),
            "tensor",
            0,
        )
        + grad_second_in
    )
    grad_first_in, grad_gain_one, grad_shift_one = norm_back_saved(grad_first, first_saved, norm_gains[0])
    grad_branch = grad_first_in.astype(jnp.bfloat16)
    grad_branch_all = lax.all_gather(grad_branch, "tensor", axis=0, tiled=True)
    grad_output_part = jnp.einsum(
        "tc,td->cd", mixed_rows, grad_branch_all, preferred_element_type=jnp.float32
    )
    grad_mixed = jnp.einsum(
        "td,cd->tc", grad_branch_all, back_output, preferred_element_type=jnp.float32
    ).astype(jnp.bfloat16)

    def backward_block(block_index):
        row_start, query_block, key_block, value_block, scores = block_parts(block_index)
        weights_full = jnp.exp(scores - log_totals[block_index][:, :, None])
        grad_mixed_block = split_heads(
            lax.dynamic_slice_in_dim(grad_mixed, row_start, block_rows, 0)
        )
        grad_weights = jnp.einsum(
            "qhd,khd->hqk", grad_mixed_block, value_block, preferred_element_type=jnp.float32
        )
        row_dot = jnp.sum(weights_full * grad_weights, axis=-1, keepdims=True)
        grad_scores = (weights_full * (grad_weights - row_dot)).astype(jnp.bfloat16)
        grad_query = (
            jnp.einsum("hqk,khd->qhd", grad_scores, key_block, preferred_element_type=jnp.float32)
            * score_scale
        )
        grad_key = (
            jnp.einsum("hqk,qhd->khd", grad_scores, query_block, preferred_element_type=jnp.float32)
            * score_scale
        )
        grad_value = jnp.einsum(
            "hqk,qhd->khd",
            weights_full.astype(jnp.bfloat16),
            grad_mixed_block,
            preferred_element_type=jnp.float32,
        )
        return (
            grad_query.reshape(block_rows, local_width),
            grad_key.reshape(seq_length, local_width),
            grad_value.reshape(seq_length, local_width),
        )

    query_blocks, key_blocks, value_blocks = lax.map(backward_block, block_ids)
    grad_queries = query_blocks.reshape(group_rows, local_width)
    grad_keys = (
        key_blocks.reshape(seq_count, per_sequence, seq_length, local_width)
        .sum(axis=1)
        .reshape(group_rows, local_width)
    )
    grad_values = (
        value_blocks.reshape(seq_count, per_sequence, seq_length, local_width)
        .sum(axis=1)
        .reshape(group_rows, local_width)
    )
    grad_projected = jnp.stack((grad_queries, grad_keys, grad_values), axis=1).astype(jnp.bfloat16)
    grad_project_part = jnp.einsum(
        "te,tsc->esc", gathered, grad_projected, preferred_element_type=jnp.float32
    )
    grad_matrix = grad_projected.reshape(group_rows, 3 * local_width)
    grad_tokens = (
        lax.psum_scatter(
            jnp.einsum(
                "tc,ec->te", grad_matrix, back_triple, preferred_element_type=jnp.float32
            ).astype(jnp.bfloat16),
            "tensor",
            scatter_dimension=0,
            tiled=True,
        ).astype(jnp.float32)
        + grad_first_in
    )
    grad_project, grad_output, grad_up, grad_down = (
        scatter_sum(grad_project_part, "dp", 0),
        scatter_sum(grad_output_part, "dp", 1),
        scatter_sum(grad_up_part, "dp", 0),
        scatter_sum(grad_down_part, "dp", 1),
    )
    head_terms = place_columns(
        jnp.stack(
            (
                jnp.sum(grad_projected[:, 0], axis=0, dtype=jnp.float32),
                jnp.sum(grad_projected[:, 2], axis=0, dtype=jnp.float32),
            )
        ),
        tensor_rank,
        model_width,
    )
    shared_terms = jnp.stack(
        (
            jnp.sum(grad_branch, axis=0, dtype=jnp.float32),
            grad_shift_one,
            jnp.sum(grad_second, axis=0, dtype=jnp.float32),
            grad_shift_two,
        )
    )
    bias_terms = jnp.concatenate((head_terms, shared_terms), axis=0)
    gain_terms = jnp.stack((grad_gain_one, grad_gain_two))
    hidden_terms = place_columns(
        jnp.sum(grad_upper, axis=0, dtype=jnp.float32), tensor_rank, hidden_bias.shape[0]
    )
    grad_gains, grad_bias_rows, grad_hidden_bias = lax.psum(
        (gain_terms, bias_terms, hidden_terms), ("dp", "tensor")
    )
    return (
        layer_out.astype(jnp.bfloat16),
        grad_tokens,
        grad_project,
        grad_output,
        grad_up,
        grad_down,
        grad_gains,
        grad_bias_rows,
        grad_hidden_bias,
    )


def solution(mesh):
    fits = mesh.shape["dp"] == 2 * LINES and mesh.shape["tensor"] == 4
    placed = (
        P(("dp", "tensor"), None),
        P("dp", None),
        P(("dp", "tensor"), None),
        P("dp", None, "tensor"),
        P("tensor", "dp"),
        P("dp", "tensor"),
        P("tensor", "dp"),
        P(),
        P(),
        P(),
    )
    return jax.shard_map(
        per_device_kernel if fits else per_device,
        mesh=mesh,
        in_specs=placed,
        out_specs=(
            P(("dp", "tensor"), None),
            P(("dp", "tensor"), None),
            P("dp", None, "tensor"),
            P("tensor", "dp"),
            P("dp", "tensor"),
            P("tensor", "dp"),
            P(),
            P(),
            P(),
        ),
        check_vma=False,
    )
```

```python
import functools
import types

import jax
import jax.numpy as jnp
from jax import lax
from jax.experimental import pallas as pl
from jax.experimental.pallas import tpu as pltpu
from jax.sharding import PartitionSpec as P

HEAD = 64
EPSILON = 1e-05
NEGATIVE = -1e30
MESH = pl.DeviceIdType.MESH
LINES = 4
CORE, ACROSS, FAR = 1, 2, 3
HALVES = 2
CHUNK = 16
VMEM_BYTES = 60 << 20


def remote(src, dst, send_sem, recv_sem, target):
    return pltpu.make_async_remote_copy(
        src_ref=src,
        dst_ref=dst,
        send_sem=send_sem,
        recv_sem=recv_sem,
        device_id=target,
        device_id_type=MESH,
    )


def position():
    return lax.axis_index("dp"), lax.axis_index("tensor")


def greet():
    dp, tensor = position()
    barrier = pltpu.get_barrier_semaphore()
    others = [(dp ^ step, tensor) for step in (1, 2, 4, 6)]
    others += [(dp, tensor ^ step) for step in (CORE, ACROSS)]
    for target in others:
        pl.semaphore_signal(barrier, inc=1, device_id=target, device_id_type=MESH)
    pl.semaphore_wait(barrier, len(others))


def row_piece(ref, index, size):
    return ref.at[pl.ds(pl.multiple_of(index * size, size), size), :]


def column_piece(ref, index, size):
    return ref.at[:, pl.ds(pl.multiple_of(index * size, size), size)]


class LineGather:
    def __init__(self, own, full, piece, send_sem, recv_sem, local_sem):
        self.own, self.full, self.piece = own, full, piece
        self.send_sem, self.recv_sem, self.local_sem = send_sem, recv_sem, local_sem
        self.dp, self.tensor = position()
        self.line, self.side = self.dp // 2, self.dp % 2
        self.targets = (
            (self.dp + 2, self.tensor),
            (self.dp - 2, self.tensor),
            (self.dp ^ 1, self.tensor),
        )

    def copy(self, index, way, src=None):
        view = self.piece(self.full, index)
        return remote(
            view if src is None else src,
            view,
            self.send_sem.at[way * LINES + index // 2],
            self.recv_sem.at[index],
            self.targets[way],
        )

    def local(self):
        return pltpu.make_async_copy(self.own, self.piece(self.full, self.dp), self.local_sem)

    def start_along(self):
        self.local().start()

        @pl.when(self.line < LINES - 1)
        def _():
            self.copy(self.dp, 0, self.own).start()

        @pl.when(self.line > 0)
        def _():
            self.copy(self.dp, 1, self.own).start()

    def start_across(self):
        self.copy(self.dp, 2, self.own).start()

    def step(self, distance):
        @pl.when(self.line >= distance)
        def _():
            index = self.dp - 2 * distance
            self.copy(index, 0).wait_recv()

            @pl.when(self.line < LINES - 1)
            def _():
                self.copy(index, 0).start()

            self.copy(index, 2).start()

        @pl.when(self.line + distance < LINES)
        def _():
            index = self.dp + 2 * distance
            self.copy(index, 1).wait_recv()

            @pl.when(self.line > 0)
            def _():
                self.copy(index, 1).start()

            self.copy(index, 2).start()

    def arrive(self):
        self.local().wait()
        for line in range(LINES):
            self.copy(2 * line + 1 - self.side, 2).wait_recv()

    def finish(self):
        for line in range(LINES):
            index = 2 * line + self.side
            self.copy(index, 2).wait_send()

            @pl.when((self.line < LINES - 1) & (line <= self.line))
            def _():
                self.copy(index, 0).wait_send()

            @pl.when((self.line > 0) & (line >= self.line))
            def _():
                self.copy(index, 1).wait_send()


class RowGather:
    def __init__(self, full, rows, send_sem, recv_sem):
        self.full, self.rows = full, rows
        self.send_sem, self.recv_sem = send_sem, recv_sem
        self.dp, self.tensor = position()

    def view(self, rank, half=None):
        if half is None:
            return row_piece(self.full, rank, self.rows)
        return row_piece(self.full, rank * HALVES + half, self.rows // HALVES)

    def near(self, rank):
        view = self.view(rank)
        target = (self.dp, self.tensor ^ CORE)
        return remote(view, view, self.send_sem.at[0], self.recv_sem.at[0], target)

    def across(self, rank, half):
        view, slot = self.view(rank, half), 1 + half
        target = (self.dp, self.tensor ^ ACROSS)
        return remote(view, view, self.send_sem.at[slot], self.recv_sem.at[slot], target)

    def far(self, rank, half):
        view, slot = self.view(rank, half), 1 + HALVES + half
        target = (self.dp, self.tensor ^ CORE)
        return remote(view, view, self.send_sem.at[slot], self.recv_sem.at[slot], target)

    def start(self):
        for half in range(HALVES):
            self.across(self.tensor, half).start()
        self.near(self.tensor).start()

    def wait_near(self):
        self.near(self.tensor ^ CORE).wait_recv()

    def wait_across(self, half):
        self.across(self.tensor ^ ACROSS, half).wait_recv()
        self.far(self.tensor ^ ACROSS, half).start()

    def wait_far(self, half):
        self.far(self.tensor ^ FAR, half).wait_recv()

    def finish(self):
        self.near(self.tensor).wait_send()
        for half in range(HALVES):
            self.across(self.tensor, half).wait_send()
            self.far(self.tensor ^ ACROSS, half).wait_send()


class RowScatter:
    def __init__(self, near_out, near_in, across_out, across_in, send_sem, recv_sem):
        self.near_out, self.near_in = near_out, near_in
        self.across_out, self.across_in = across_out, across_in
        self.send_sem, self.recv_sem = send_sem, recv_sem
        self.dp, self.tensor = position()

    def near(self, slot):
        return remote(
            self.near_out.at[slot],
            self.near_in.at[slot],
            self.send_sem.at[slot],
            self.recv_sem.at[slot],
            (self.dp, self.tensor ^ CORE),
        )

    def across(self, half):
        rows = self.across_in.shape[0] // HALVES
        return remote(
            row_piece(self.across_out, half, rows),
            row_piece(self.across_in, half, rows),
            self.send_sem.at[2 * HALVES + half],
            self.recv_sem.at[2 * HALVES + half],
            (self.dp, self.tensor ^ ACROSS),
        )

    def give_far(self, half, partial):
        self.near_out[half] = partial.astype(jnp.bfloat16)
        self.near(half).start()

    def give_across(self, half, partial):
        self.near(half).wait_recv()
        rows = partial.shape[0]
        total = partial + self.near_in[half].astype(jnp.float32)
        row_piece(self.across_out, half, rows)[...] = total.astype(jnp.bfloat16)
        self.across(half).start()

    def give_near(self, half, partial):
        self.near_out[HALVES + half] = partial.astype(jnp.bfloat16)
        self.near(HALVES + half).start()

    def take(self, half, partial):
        self.near(HALVES + half).wait_recv()
        rows = partial.shape[0]
        total = partial + self.near_in[HALVES + half].astype(jnp.float32)
        self.across(half).wait_recv()
        return total + row_piece(self.across_in, half, rows)[...].astype(jnp.float32)

    def finish(self):
        for slot in range(2 * HALVES):
            self.near(slot).wait_send()
        for half in range(HALVES):
            self.across(half).wait_send()


def dot(left, right):
    return jnp.dot(left, right, preferred_element_type=jnp.float32)


def dot_nt(left, right):
    return lax.dot_general(left, right, (((1,), (1,)), ((), ())), preferred_element_type=jnp.float32)


def dot_tn(left, right):
    return lax.dot_general(left, right, (((0,), (0,)), ((), ())), preferred_element_type=jnp.float32)


def normalize(rows):
    centred = rows - jnp.mean(rows, axis=-1, keepdims=True)
    inverse = lax.rsqrt(jnp.mean(centred * centred, axis=-1, keepdims=True) + EPSILON)
    return centred * inverse, inverse


def norm_back(grad, normed, inverse):
    average = jnp.mean(grad, axis=-1, keepdims=True)
    along = jnp.mean(grad * normed, axis=-1, keepdims=True)
    return inverse * (grad - average - normed * along)


class DirectGather:
    def __init__(self, own, full, piece, send_sem, recv_sem, local_sem):
        self.own, self.full, self.piece = own, full, piece
        self.send_sem, self.recv_sem, self.local_sem = send_sem, recv_sem, local_sem
        self.dp, self.tensor = position()

    def along(self, step):
        there = self.dp ^ (2 * step)
        return remote(
            self.own,
            self.piece(self.full, self.dp),
            self.send_sem.at[step],
            self.recv_sem.at[step],
            (there, self.tensor),
        )

    def across(self, step, source=None):
        view = self.piece(self.full, self.dp ^ (2 * step))
        return remote(
            view if source is None else source,
            view,
            self.send_sem.at[LINES + step],
            self.recv_sem.at[LINES + step],
            (self.dp ^ 1, self.tensor),
        )

    def local(self):
        return pltpu.make_async_copy(self.own, self.piece(self.full, self.dp), self.local_sem)

    def start_along(self):
        self.local().start()
        for step in range(1, LINES):
            self.along(step).start()

    def start_across(self):
        self.across(0, self.own).start()

    def step(self, step):
        self.along(step).wait_recv()
        self.across(step).start()

    def arrive(self, step):
        self.across(step).wait_recv()

    def finish(self):
        for step in range(LINES):
            self.across(step).wait_send()
        for step in range(1, LINES):
            self.along(step).wait_send()


class ColumnScatter:
    def __init__(self, near_out, near_in, across_out, across_in, send_sem, recv_sem):
        self.near_out, self.near_in = near_out, near_in
        self.across_out, self.across_in = across_out, across_in
        self.send_sem, self.recv_sem = send_sem, recv_sem
        self.dp, self.tensor = position()

    def near(self, slot):
        return remote(
            self.near_out.at[slot],
            self.near_in.at[slot],
            self.send_sem.at[slot],
            self.recv_sem.at[slot],
            (self.dp, self.tensor ^ CORE),
        )

    def across(self, at):
        return remote(
            self.across_out.at[at],
            self.across_in.at[at],
            self.send_sem.at[2 * LINES + at],
            self.recv_sem.at[2 * LINES + at],
            (self.dp, self.tensor ^ ACROSS),
        )

    def give_far(self, at, partial):
        self.near_out[at] = partial.astype(jnp.bfloat16)
        self.near(at).start()

    def give_near(self, at, partial):
        self.near_out[LINES + at] = partial.astype(jnp.bfloat16)
        self.near(LINES + at).start()

    def give_across(self, at, partial):
        self.near(at).wait_recv()
        total = partial + self.near_in[at].astype(jnp.float32)
        self.across_out[at] = total.astype(jnp.bfloat16)
        self.across(at).start()

    def take(self, at, partial):
        self.near(LINES + at).wait_recv()
        total = partial + self.near_in[LINES + at].astype(jnp.float32)
        self.across(at).wait_recv()
        return total + self.across_in[at].astype(jnp.float32)

    def finish(self):
        for slot in range(2 * LINES):
            self.near(slot).wait_send()
        for at in range(LINES):
            self.across(at).wait_send()


class LineScatter:
    def __init__(self, partial, piece, side_in, line_in, send_sem, recv_sem):
        self.partial, self.piece, self.side_in, self.line_in = partial, piece, side_in, line_in
        self.send_sem, self.recv_sem = send_sem, recv_sem
        self.dp, self.tensor = position()

    def view(self, step):
        return self.piece(self.partial, self.dp ^ (2 * step))

    def across(self, step):
        return remote(
            self.piece(self.partial, self.dp ^ (2 * step) ^ 1),
            self.side_in.at[step],
            self.send_sem.at[step],
            self.recv_sem.at[step],
            (self.dp ^ 1, self.tensor),
        )

    def along(self, step):
        return remote(
            self.view(step),
            self.line_in.at[step - 1],
            self.send_sem.at[LINES + step],
            self.recv_sem.at[LINES + step],
            (self.dp ^ (2 * step), self.tensor),
        )

    def start(self):
        for step in reversed(range(LINES)):
            self.across(step).start()

    def total(self, step):
        self.across(step).wait_recv()
        return self.view(step)[...].astype(jnp.float32) + self.side_in[step].astype(jnp.float32)

    def relay(self, step):
        self.view(step)[...] = self.total(step).astype(jnp.bfloat16)
        self.along(step).start()

    def finish(self, result):
        total = self.total(0)
        for step in range(1, LINES):
            self.along(step).wait_recv()
            total = total + self.line_in[step - 1].astype(jnp.float32)
        result[...] = total
        for step in range(LINES):
            self.across(step).wait_send()
        for step in range(1, LINES):
            self.along(step).wait_send()


class Total:
    def __init__(self, held, arrived, send_sem, recv_sem):
        self.held, self.arrived, self.send_sem, self.recv_sem = held, arrived, send_sem, recv_sem
        dp, tensor = position()
        self.targets = (
            (dp ^ 1, tensor),
            (dp, tensor ^ CORE),
            (dp, tensor ^ ACROSS),
            (dp ^ 2, tensor),
            (dp ^ 4, tensor),
        )

    def copy(self, step):
        return remote(
            self.held.at[step],
            self.arrived.at[step],
            self.send_sem.at[step],
            self.recv_sem.at[step],
            self.targets[step],
        )

    def start(self):
        self.copy(0).start()

    def step(self, step):
        self.copy(step).wait_recv()
        self.held[step + 1] = self.held[step] + self.arrived[step]
        if step + 1 < len(self.targets):
            self.copy(step + 1).start()

    def finish(self):
        for step in range(len(self.targets)):
            self.copy(step).wait_send()


def layer_kernel(names, rows, *refs):
    r = types.SimpleNamespace(**dict(zip(names, refs)))
    dp, tensor = position()
    bf16, f32 = jnp.bfloat16, jnp.float32
    half_rows = rows // HALVES
    local = r.queries.shape[1]
    piece = r.triple_own.shape[1]
    pairs = local // (2 * HEAD)
    hidden = r.hidden.shape[1]
    near, across, far = tensor ^ CORE, tensor ^ ACROSS, tensor ^ FAR

    def of_rows(ref, index):
        return row_piece(ref, index, piece)

    def of_columns(ref, index):
        return column_piece(ref, index, piece)

    def of_stack(ref, index):
        return ref.at[:, pl.ds(pl.multiple_of(index * piece, piece), piece), :]

    def block(rank, size=rows):
        return pl.ds(pl.multiple_of(rank * size, size), size)

    def split(partial):
        return [partial[half * half_rows : (half + 1) * half_rows] for half in range(HALVES)]

    def part_of(half):
        return slice(half * half_rows, (half + 1) * half_rows)

    lines = [
        kind(own, full, view, r.line_send.at[at], r.line_recv.at[at], r.line_local.at[at])
        for at, (kind, own, full, view) in enumerate(
            (
                (LineGather, r.triple_own, r.triple, of_stack),
                (DirectGather, r.output_own, r.output, of_columns),
                (LineGather, r.up_own, r.up, of_rows),
                (DirectGather, r.down_own, r.down, of_columns),
            )
        )
    ]
    triple_line, output_line, up_line, down_line = lines
    sums = [
        LineScatter(partial, view, side, along, r.part_send.at[at], r.part_recv.at[at])
        for at, (partial, view, side, along) in enumerate(
            (
                (r.grad_project, of_stack, r.project_side, r.project_line),
                (r.grad_output, of_columns, r.output_side, r.output_line),
                (r.grad_up, of_rows, r.up_side, r.up_line),
                (r.grad_down, of_columns, r.down_side, r.down_line),
            )
        )
    ]
    project_sum, output_sum, up_sum, down_sum = sums
    gathers = [
        RowGather(full, rows, r.row_send.at[at], r.row_recv.at[at])
        for at, full in enumerate((r.gathered, r.first_all, r.second_all, r.branch_all))
    ]
    scatters = [
        kind(*buffers, r.sum_send.at[at], r.sum_recv.at[at])
        for at, (kind, buffers) in enumerate(
            (
                (RowScatter, (r.near_out_a, r.near_in_a, r.across_out_a, r.across_in_a)),
                (ColumnScatter, (r.near_out_b, r.near_in_b, r.across_out_b, r.across_in_b)),
            )
            * 2
        )
    ]
    total = Total(r.held_totals, r.arrived_totals, r.total_send, r.total_recv)

    def column_block(at):
        return block((dp // 2) ^ at, 2 * piece)

    def scatter_columns(scatter, at, product):
        lanes = column_block(at)
        scatter.give_far(at, product(far, lanes))
        middle = product(across, lanes)
        scatter.give_near(at, product(near, lanes))
        r.kept[:, lanes] = product(tensor, lanes)
        scatter.give_across(at, middle)

    def chunks(size, start, body):
        @pl.loop(0, size // CHUNK)
        def _(chunk):
            offset = chunk * CHUNK
            body(
                pl.ds(pl.multiple_of(offset, CHUNK), CHUNK),
                pl.ds(pl.multiple_of(start + offset, CHUNK), CHUNK),
            )

    loads = [
        pltpu.make_async_copy(source, target, r.load_sem.at[at])
        for at, (source, target) in enumerate(
            (
                (r.tokens, gathers[0].view(tensor)),
                (r.segments, r.segment_row),
                (r.bias_from, r.bias_rows),
                (r.gains_from, r.norm_gains),
                (r.hidden_from.at[pl.ds(pl.multiple_of(tensor * hidden, hidden), hidden)], r.hidden_bias),
                (r.cotangent_from, r.cotangent),
            )
        )
    ]
    for load in loads:
        load.start()
    greet()
    triple_line.start_along()
    triple_line.start_across()
    loads[0].wait()
    gathers[0].start()
    triple_line.step(1)
    loads[1].wait()
    numbers = r.segment_row[...].astype(f32)
    r.segment_column[...] = jnp.broadcast_to(numbers, (8, numbers.shape[1])).T[:, :1]
    r.segment_row_f32[...] = numbers
    triple_line.step(2)
    output_line.start_along()
    gathers[0].wait_near()
    for half in range(HALVES):
        gathers[0].wait_across(half)
    triple_line.step(3)
    output_line.start_across()
    up_line.start_along()
    for half in range(HALVES):
        gathers[0].wait_far(half)
    triple_line.arrive()
    for load in loads[2:]:
        load.wait()
    columns = pl.ds(pl.multiple_of(tensor * local, local), local)
    query_bias = r.bias_rows[0:1, columns]
    value_bias = r.bias_rows[1:2, columns]

    @pl.loop(0, 4)
    def _(index):
        here = block(index)
        left = r.gathered[here, :]
        query = (dot(left, r.triple[0]) + query_bias).astype(bf16)
        r.queries[here, :] = query * bf16(HEAD**-0.5)
        key = dot(left, r.triple[1])
        r.key_rows[here, :] = key.astype(bf16)
        r.key_turned[:, here] = key.T.astype(bf16)
        value = dot(left, r.triple[2]) + value_bias
        r.value_rows[here, :] = value.astype(bf16)
        r.value_turned[:, here] = value.T.astype(bf16)

    for step in range(1, LINES):
        output_line.step(step)
    up_line.start_across()
    up_line.step(1)

    def head_rows(head):
        return pl.ds(pl.multiple_of(head * HEAD, HEAD), HEAD)

    def attend(rank):
        here = block(rank)

        @pl.loop(0, pairs)
        def _(pair):
            lanes = block(pair, 2 * HEAD)
            query = r.queries[here, lanes]
            keys = r.key_rows[:, lanes]
            same = r.segment_column[...] == r.segment_row_f32[:, here]
            lane = lax.broadcasted_iota(jnp.int32, query.shape, 1)
            outs = []
            for side in range(2):
                scores = dot_nt(keys, jnp.where(lane // HEAD == side, query, bf16(0)))
                scores = jnp.where(same, scores, NEGATIVE)
                top = jnp.max(scores, axis=0, keepdims=True)
                exponent = jnp.exp(scores - top)
                mass = jnp.sum(exponent, axis=0, keepdims=True)
                weights = (exponent * (1.0 / mass)).astype(bf16)
                head = pair * 2 + side
                outs.append(dot(r.value_turned[head_rows(head), :], weights))
                r.log_totals[pl.ds(head, 1), here] = top + jnp.log(mass)
            r.mixed[here, lanes] = jnp.concatenate(outs, axis=0).T.astype(bf16)

    @pl.loop(0, 4)
    def _(turn):
        rank = tensor ^ (FAR - turn)
        attend(rank)

        @pl.when(turn == 0)
        def _():
            output_line.local().wait()
            for step in range(LINES):
                output_line.arrive(step)

        r.partial[...] = dot(r.mixed[block(rank), :], r.output[...])

        def give(method):
            for half in range(HALVES):
                method(half, r.partial[part_of(half), :])

        @pl.when(turn == 0)
        def _():
            give(scatters[0].give_far)

        @pl.when(turn == 1)
        def _():
            give(scatters[0].give_across)
            up_line.step(2)
            down_line.start_along()

        @pl.when(turn == 2)
        def _():
            give(scatters[0].give_near)

        @pl.when(turn == 3)
        def _():
            up_line.step(3)
            down_line.start_across()

    for half in range(HALVES):
        part = part_of(half)
        r.kept[part, :] = scatters[0].take(half, r.partial[part, :])

        def first_norm(_, here):
            own_rows = r.gathered[pl.ds(pl.multiple_of(tensor * rows + here.start, CHUNK), CHUNK), :]
            normed, inverse = normalize(own_rows.astype(f32) + r.kept[here, :] + r.bias_rows[2:3, :])
            r.normed_one[here, :] = normed
            r.inverse_one[here, :] = inverse
            first = normed * r.norm_gains[0:1, :] + r.bias_rows[3:4, :]
            into = pl.ds(pl.multiple_of(tensor * rows + here.start, CHUNK), CHUNK)
            r.first_all[into, :] = first.astype(bf16)

        chunks(half_rows, half * half_rows, first_norm)
    scatters[0].finish()

    gathers[1].start()
    r.sums[...] = jnp.zeros_like(r.sums)

    def extent(rank, half):
        size = rows if half is None else half_rows
        start = rank * rows + (0 if half is None else half * half_rows)
        return start, size, pl.ds(pl.multiple_of(start, size), size)

    def up_part(rank, half=None):
        start, size, here = extent(rank, half)
        r.upper[:size, :] = dot(r.first_all[here, :], r.up[...]) + r.hidden_bias[...].reshape(1, hidden)

        def body(part, into):
            value = r.upper[part, :]
            share = 0.5 + 0.5 * lax.erf(value * (0.5**0.5))
            r.hidden[into, :] = (value * share).astype(bf16)
            bell = jnp.exp(value * value * -0.5) * (2 * jnp.pi) ** -0.5
            r.slope[into, :] = share + value * bell

        chunks(size, start, body)

    def back_part(rank, half=None):
        start, size, here = extent(rank, half)
        r.upper[:size, :] = dot_nt(r.second_all[here, :], r.down[...])

        def body(part, into):
            low = (r.upper[part, :] * r.slope[into, :]).astype(bf16)
            r.upper_low[into, :] = low
            r.sums[6:7, :] += jnp.sum(low.astype(f32), axis=0, keepdims=True)

        chunks(size, start, body)
        r.partial[:size, :] = dot_nt(r.upper_low[here, :], r.up[...])

    up_line.arrive()

    @pl.loop(0, 2)
    def _(turn):
        @pl.when(turn == 1)
        def _():
            down_line.step(1)
            gathers[1].wait_near()

        up_part(tensor ^ turn)

    def other_chip(gather, body):
        @pl.loop(0, 2 * HALVES)
        def _(turn):
            half, side = turn // 2, turn % 2

            @pl.when(side == 0)
            def _():
                gather.wait_across(half)

            @pl.when(side == 1)
            def _():
                gather.wait_far(half)

            body(half, side)

    def up_other(half, side):
        up_part(tensor ^ (ACROSS + side), half)

        @pl.when(side == 1)
        def _():
            down_line.step(2 + half)

    other_chip(gathers[1], up_other)

    def down_part(rank, lanes):
        return dot(r.hidden[block(rank), :], r.down[:, lanes])

    down_line.local().wait()

    @pl.loop(0, LINES)
    def _(at):
        down_line.arrive(at)
        scatter_columns(scatters[1], at, down_part)

    def add_to(row, value):
        r.sums[row : row + 1, :] += jnp.sum(value, axis=0, keepdims=True)

    def second_norm(_, here):
        first = r.normed_one[here, :] * r.norm_gains[0:1, :] + r.bias_rows[3:4, :]
        normed, inverse = normalize(first + r.kept[here, :] + r.bias_rows[4:5, :])
        shifted = normed * r.norm_gains[1:2, :] + r.bias_rows[5:6, :]
        r.layer_low[here, :] = shifted.astype(bf16)
        grad = r.cotangent[here, :].astype(f32)
        add_to(5, grad * normed)
        add_to(3, grad)
        grad = norm_back(grad * r.norm_gains[1:2, :], normed, inverse)
        r.grad_rows[here, :] = grad
        low = grad.astype(bf16)
        add_to(2, low.astype(f32))
        r.second_all[pl.ds(pl.multiple_of(tensor * rows + here.start, CHUNK), CHUNK), :] = low

    @pl.loop(0, LINES)
    def _(at):
        lanes = column_block(at)
        r.kept[:, lanes] = scatters[1].take(at, r.kept[:, lanes])

    chunks(rows, 0, second_norm)
    saves = []

    def save(source, target):
        saves.append(pltpu.make_async_copy(source, target, r.save_sem.at[len(saves)]))
        saves[-1].start()

    save(r.layer_low, r.layer_out)
    scatters[1].finish()

    gathers[2].start()

    @pl.loop(0, 2)
    def _(turn):
        @pl.when(turn == 1)
        def _():
            gathers[2].wait_near()

        back_part(tensor ^ turn)

        @pl.when(turn == 0)
        def _():
            r.kept[...] = r.partial[...]

        @pl.when(turn == 1)
        def _():
            for half in range(HALVES):
                scatters[2].give_near(half, r.partial[part_of(half), :])

    def back_other(half, side):
        back_part(tensor ^ (ACROSS + side), half)

        @pl.when(side == 0)
        def _():
            r.held[...] = r.partial[:half_rows, :]

        @pl.when(side == 1)
        def _():
            scatters[2].give_far(half, r.partial[:half_rows, :])
            scatters[2].give_across(half, r.held[...])

    other_chip(gathers[2], back_other)

    def weight_grad(left, right, result):
        @pl.loop(0, left.shape[1] // rows)
        def _(index):
            lanes = block(index)
            result[lanes, :] = dot_tn(left[:, lanes], right[...]).astype(bf16)

    weight_grad(r.hidden, r.second_all, r.grad_down)
    down_sum.start()
    weight_grad(r.first_all, r.upper_low, r.grad_up)
    up_sum.start()

    def first_back(_, here):
        grad = r.grad_rows[here, :] + r.kept[here, :]
        normed = r.normed_one[here, :]
        add_to(4, grad * normed)
        add_to(1, grad)
        grad = norm_back(grad * r.norm_gains[0:1, :], normed, r.inverse_one[here, :])
        r.grad_rows[here, :] = grad
        low = grad.astype(bf16)
        add_to(0, low.astype(f32))
        r.branch_all[pl.ds(pl.multiple_of(tensor * rows + here.start, CHUNK), CHUNK), :] = low

    for half in range(HALVES):
        part = part_of(half)
        r.kept[part, :] = scatters[2].take(half, r.kept[part, :])
        chunks(half_rows, half * half_rows, first_back)
    scatters[2].finish()

    gathers[3].start()
    grad_keys, grad_values = r.slope.at[:, :local], r.slope.at[:, local : 2 * local]
    r.slope[:, : 2 * local] = jnp.zeros((r.slope.shape[0], 2 * local), f32)

    def attend_back(rank):
        here = block(rank)
        r.mixed_low[...] = dot_nt(r.branch_all[here, :], r.output[...]).astype(bf16)

        @pl.loop(0, pairs)
        def _(pair):
            lanes = block(pair, 2 * HEAD)
            query = r.queries[here, lanes]
            grad = r.mixed_low[:, lanes]
            keys = r.key_rows[:, lanes]
            values = r.value_rows[:, lanes]
            same = r.segment_column[...] == r.segment_row_f32[:, here]
            lane = lax.broadcasted_iota(jnp.int32, query.shape, 1)
            outs = []
            for side in range(2):
                mine = lane // HEAD == side
                head = pair * 2 + side
                query_here = jnp.where(mine, query, bf16(0))
                grad_here = jnp.where(mine, grad, bf16(0))
                scores = jnp.where(same, dot_nt(keys, query_here), NEGATIVE)
                weights = jnp.exp(scores - r.log_totals[pl.ds(head, 1), here])
                grad_weights = dot_nt(values, grad_here)
                along = jnp.sum(weights * grad_weights, axis=0, keepdims=True)
                grad_scores = (weights * (grad_weights - along)).astype(bf16)
                grad_keys[:, lanes] += dot(grad_scores, query_here)
                grad_values[:, lanes] += dot(weights.astype(bf16), grad_here)
                outs.append(dot(r.key_turned[head_rows(head), :], grad_scores))
            grad_query = jnp.concatenate(outs, axis=0).T * HEAD**-0.5
            r.projected_low[here, lanes] = grad_query.astype(bf16)

    @pl.loop(0, 4)
    def _(turn):
        @pl.when(turn == 1)
        def _():
            gathers[3].wait_near()

        @pl.when(turn == 2)
        def _():
            for half in range(HALVES):
                gathers[3].wait_across(half)

        @pl.when(turn == 3)
        def _():
            for half in range(HALVES):
                gathers[3].wait_far(half)

        attend_back(tensor ^ turn)

        @pl.when(turn < 3)
        def _():
            down_sum.relay(3 - turn)

    up_sum.relay(3)
    r.grad_output[...] = dot_tn(r.mixed[...], r.branch_all[...]).astype(bf16)
    r.projected_low[:, local : 2 * local] = grad_keys[...].astype(bf16)
    r.projected_low[:, 2 * local :] = grad_values[...].astype(bf16)
    r.held_totals[0] = jnp.zeros(r.held_totals.shape[1:], f32)
    r.held_totals[0, 2:8, :] = r.sums[0:6, :]
    r.held_totals[0, pl.ds(8 + tensor, 1), :] = r.sums[6:7, :]
    for row, at in ((0, 0), (1, 2)):
        low = r.projected_low[:, at * local : (at + 1) * local].astype(f32)
        r.held_totals[0, row : row + 1, columns] = jnp.sum(low, axis=0, keepdims=True)
    total.start()
    output_sum.start()
    for at in range(3):
        lanes = slice(at * local, (at + 1) * local)
        weight_grad(r.gathered, r.projected_low.at[:, lanes], r.grad_project.at[at])
    project_sum.start()
    up_sum.relay(2)

    def token_part(rank, lanes):
        product = 0
        for at in range(3):
            left = r.projected_low[block(rank), at * local : (at + 1) * local]
            product += dot_nt(left, r.triple[at, lanes, :])
        return product

    @pl.loop(0, LINES)
    def _(at):
        scatter_columns(scatters[3], at, token_part)

    up_sum.relay(1)
    down_sum.finish(r.down_sum)
    save(r.down_sum, r.down_out)

    @pl.loop(0, LINES)
    def _(at):
        lanes = column_block(at)
        r.grad_rows[:, lanes] += scatters[3].take(at, r.kept[:, lanes])

    save(r.grad_rows, r.grad_tokens)
    total.step(0)
    total.step(1)
    output_sum.relay(3)
    total.step(2)
    output_sum.relay(2)
    output_sum.relay(1)
    up_sum.finish(r.up_sum)
    save(r.up_sum, r.up_out)
    project_sum.relay(3)
    total.step(3)
    project_sum.relay(2)
    output_sum.finish(r.output_sum)
    save(r.output_sum, r.output_out)
    project_sum.relay(1)
    total.step(4)
    r.bias_sum[...] = r.held_totals[5, 0:6, :]
    r.gains_sum[...] = r.held_totals[5, 6:8, :]
    for at in range(4):
        r.hidden_sum[at * hidden : (at + 1) * hidden] = r.held_totals[5, 8 + at, :]
    save(r.bias_sum, r.bias_out)
    save(r.gains_sum, r.gains_out)
    save(r.hidden_sum, r.hidden_out)
    project_sum.finish(r.project_sum)
    save(r.project_sum, r.project_out)
    scatters[3].finish()
    for each in gathers + lines + [total]:
        each.finish()
    for each in saves:
        each.wait()


def copy_kernel(count, *refs):
    sources, targets, held, sem = refs[:count], refs[count : 2 * count], refs[2 * count : -1], refs[-1]
    copies_in = [pltpu.make_async_copy(*pair, sem.at[at]) for at, pair in enumerate(zip(sources, held))]
    copies_out = [
        pltpu.make_async_copy(*pair, sem.at[count + at]) for at, pair in enumerate(zip(held, targets))
    ]
    for copy in copies_in:
        copy.start()
    for arrived, copy in zip(copies_in, copies_out):
        arrived.wait()
        copy.start()
    for copy in copies_out:
        copy.wait()


def per_device_kernel(
    tokens,
    segments,
    cotangent,
    project_weight,
    output_weight,
    up_weight,
    down_weight,
    norm_gains,
    bias_rows,
    hidden_bias,
):
    rows, width = tokens.shape
    length = segments.shape[1]
    local_hidden = up_weight.shape[1]
    local = output_weight.shape[0]
    piece = project_weight.shape[0]
    bf16, f32 = jnp.bfloat16, jnp.float32
    inputs = dict(
        tokens=tokens,
        triple_own=project_weight.transpose(1, 0, 2),
        output_own=output_weight,
        up_own=up_weight,
        down_own=down_weight,
        segments=segments,
        cotangent_from=cotangent,
        gains_from=norm_gains,
        bias_from=bias_rows,
        hidden_from=hidden_bias,
    )
    shapes = dict(
        project=(3, piece, local),
        output=(local, piece),
        up=(piece, local_hidden),
        down=(local_hidden, piece),
    )
    outputs = dict(layer_out=((rows, width), bf16), grad_tokens=((rows, width), f32))
    outputs |= {name + "_out": (shape, f32) for name, shape in shapes.items()}
    outputs |= dict(
        gains_out=((2, width), f32),
        bias_out=((6, width), f32),
        hidden_out=(hidden_bias.shape, f32),
    )
    scratch = dict(
        segment_row=((1, length), jnp.int32),
        segment_row_f32=((1, length), f32),
        segment_column=((length, 1), f32),
        cotangent=((rows, width), bf16),
        norm_gains=(norm_gains.shape, f32),
        bias_rows=(bias_rows.shape, f32),
        hidden_bias=((local_hidden,), f32),
        layer_low=((rows, width), bf16),
        bias_sum=(bias_rows.shape, f32),
        gains_sum=(norm_gains.shape, f32),
        hidden_sum=(hidden_bias.shape, f32),
        partial=((rows, width), f32),
        gathered=((length, width), bf16),
        triple=((3, width, local), bf16),
        output=((local, width), bf16),
        up=((width, local_hidden), bf16),
        down=((local_hidden, width), bf16),
        queries=((length, local), bf16),
        key_rows=((length, local), bf16),
        value_rows=((length, local), bf16),
        key_turned=((local, length), bf16),
        value_turned=((local, length), bf16),
        mixed=((length, local), bf16),
        log_totals=((local // HEAD, length), f32),
        normed_one=((rows, width), f32),
        inverse_one=((rows, 1), f32),
        first_all=((length, width), bf16),
        hidden=((length, local_hidden), bf16),
        slope=((length, local_hidden), f32),
        second_all=((length, width), bf16),
        upper_low=((length, local_hidden), bf16),
        upper=((rows, local_hidden), f32),
        kept=((rows, width), f32),
        held=((rows // HALVES, width), f32),
        grad_rows=((rows, width), f32),
        sums=((8, width), f32),
        branch_all=((length, width), bf16),
        mixed_low=((rows, local), bf16),
        projected_low=((length, 3 * local), bf16),
        grad_project=((3, width, local), bf16),
        grad_output=((local, width), bf16),
        grad_up=((width, local_hidden), bf16),
        grad_down=((local_hidden, width), bf16),
        held_totals=((6, 16, width), f32),
        arrived_totals=((5, 16, width), f32),
    )
    for name, shape in shapes.items():
        scratch[name + "_sum"] = (shape, f32)
        scratch[name + "_side"] = ((LINES,) + shape, bf16)
        scratch[name + "_line"] = ((LINES - 1,) + shape, bf16)
    for name in ("near_out_", "near_in_"):
        scratch[name + "a"] = ((2 * HALVES, rows // HALVES, width), bf16)
        scratch[name + "b"] = ((2 * LINES, rows, 2 * piece), bf16)
    for name in ("across_out_", "across_in_"):
        scratch[name + "a"] = ((rows, width), bf16)
        scratch[name + "b"] = ((LINES, rows, 2 * piece), bf16)
    semaphores = dict(
        line_send=(4, 3 * LINES),
        line_recv=(4, 2 * LINES),
        line_local=(4,),
        part_send=(4, 2 * LINES),
        part_recv=(4, 2 * LINES),
        row_send=(4, 1 + 2 * HALVES),
        row_recv=(4, 1 + 2 * HALVES),
        sum_send=(4, 3 * LINES),
        sum_recv=(4, 3 * LINES),
        total_send=(5,),
        total_recv=(5,),
        load_sem=(6,),
        save_sem=(9,),
    )
    names = [*inputs, *outputs, *scratch, *semaphores]
    hbm = pl.BlockSpec(memory_space=pltpu.HBM)
    results = pl.pallas_call(
        functools.partial(layer_kernel, names, rows),
        out_shape=[jax.ShapeDtypeStruct(*leaf) for leaf in outputs.values()],
        in_specs=[hbm] * len(inputs),
        out_specs=[hbm] * len(outputs),
        scratch_shapes=[pltpu.VMEM(*leaf) for leaf in scratch.values()]
        + [pltpu.SemaphoreType.DMA(shape) for shape in semaphores.values()],
        compiler_params=pltpu.CompilerParams(
            collective_id=0, has_side_effects=True, vmem_limit_bytes=VMEM_BYTES
        ),
        name="layer",
    )(*inputs.values())
    results = pl.pallas_call(
        functools.partial(copy_kernel, len(outputs)),
        out_shape=[jax.ShapeDtypeStruct(*leaf) for leaf in outputs.values()],
        in_specs=[hbm] * len(outputs),
        out_specs=[hbm] * len(outputs),
        scratch_shapes=[pltpu.VMEM(*leaf) for leaf in outputs.values()]
        + [pltpu.SemaphoreType.DMA((2 * len(outputs),))],
        name="copy",
    )(*results)
    result = dict(zip(outputs, results))
    return (
        result["layer_out"],
        result["grad_tokens"],
        result["project_out"].transpose(1, 0, 2),
        result["output_out"],
        result["up_out"],
        result["down_out"],
        result["gains_out"],
        result["bias_out"],
        result["hidden_out"],
    )


def gelu_exact(values):
    return jax.nn.gelu(values, approximate=False)


def layer_norm(token_rows, gain, shift):
    average = jnp.mean(token_rows, axis=-1, keepdims=True)
    centred = token_rows - average
    variance = jnp.mean(centred * centred, axis=-1, keepdims=True)
    inverse = lax.rsqrt(variance + EPSILON)
    normed = centred * inverse
    return (normed * gain + shift, (normed, inverse))


def norm_back_saved(grad_rows, saved, gain):
    normed, inverse = saved
    grad_gain = jnp.sum(grad_rows * normed, axis=0)
    grad_shift = jnp.sum(grad_rows, axis=0)
    grad_normed = grad_rows * gain
    grad_input = inverse * (
        grad_normed
        - jnp.mean(grad_normed, axis=-1, keepdims=True)
        - normed * jnp.mean(grad_normed * normed, axis=-1, keepdims=True)
    )
    return (grad_input, grad_gain, grad_shift)


def split_heads(token_rows):
    return token_rows.reshape(token_rows.shape[0], token_rows.shape[1] // HEAD, HEAD)


def scatter_sum(partial_sum, axis_name, dimension):
    return lax.psum_scatter(
        partial_sum.astype(jnp.bfloat16), axis_name, scatter_dimension=dimension, tiled=True
    ).astype(jnp.float32)


def place_columns(partial_sum, column_block, total_width):
    full_rows = jnp.zeros(partial_sum.shape[:-1] + (total_width,), jnp.float32)
    return lax.dynamic_update_slice_in_dim(
        full_rows, partial_sum, column_block * partial_sum.shape[-1], partial_sum.ndim - 1
    )


def per_device(
    tokens,
    segments,
    cotangent,
    project_weight,
    output_weight,
    up_weight,
    down_weight,
    norm_gains,
    bias_rows,
    hidden_bias,
):
    tensor_rank = lax.axis_index("tensor")
    local_rows, model_width = tokens.shape
    seq_count, seq_length = segments.shape
    group_rows = seq_count * seq_length
    local_width = project_weight.shape[2]
    score_scale = HEAD ** (-0.5)
    block_rows = min(512, seq_length)
    per_sequence = seq_length // block_rows
    count_blocks = group_rows // block_rows
    block_ids = jnp.arange(count_blocks, dtype=jnp.int32)
    triple_full, output_full, upward_full, downward_full = (
        lax.all_gather(project_weight, "dp", axis=0, tiled=True),
        lax.all_gather(output_weight, "dp", axis=1, tiled=True),
        lax.all_gather(up_weight, "dp", axis=0, tiled=True),
        lax.all_gather(down_weight, "dp", axis=1, tiled=True),
    )
    local_hidden = upward_full.shape[1]
    triple_matrix = triple_full.reshape(model_width, 3 * local_width)
    gathered = lax.all_gather(tokens, "tensor", axis=0, tiled=True)
    head_bias = lax.dynamic_slice_in_dim(bias_rows, tensor_rank * local_width, local_width, 1)
    projected = jnp.dot(gathered, triple_matrix, preferred_element_type=jnp.float32).reshape(
        group_rows, 3, local_width
    )
    queries = (projected[:, 0] + head_bias[0]).astype(jnp.bfloat16)
    key_rows = projected[:, 1].astype(jnp.bfloat16)
    value_rows = (projected[:, 2] + head_bias[1]).astype(jnp.bfloat16)

    def block_parts(block_index):
        sequence = block_index // per_sequence
        row_start = block_index * block_rows
        seq_start = sequence * seq_length
        query_block = split_heads(lax.dynamic_slice_in_dim(queries, row_start, block_rows, 0))
        key_block = split_heads(key_rows)
        value_block = split_heads(value_rows)
        seq_ids = lax.dynamic_index_in_dim(segments, sequence, 0, keepdims=False)
        query_ids = lax.dynamic_slice_in_dim(seq_ids, row_start - seq_start, block_rows, 0)
        products = (
            jnp.einsum("qhd,khd->hqk", query_block, key_block, preferred_element_type=jnp.float32)
            * score_scale
        )
        scores = jnp.where((query_ids[:, None] == seq_ids[None, :])[None], products, NEGATIVE)
        return (row_start, query_block, key_block, value_block, scores)

    def forward_block(block_index):
        row_start, query_block, key_block, value_block, scores = block_parts(block_index)
        row_max = jnp.max(scores, axis=-1, keepdims=True)
        exponent = jnp.exp(scores - row_max)
        row_sum = jnp.sum(exponent, axis=-1, keepdims=True)
        weights_low = (exponent / row_sum).astype(jnp.bfloat16)
        mixed_block = jnp.einsum(
            "hqk,khd->qhd", weights_low, value_block, preferred_element_type=jnp.float32
        )
        log_total = row_max[:, :, 0] + jnp.log(row_sum[:, :, 0])
        return (mixed_block.reshape(block_rows, local_width).astype(jnp.bfloat16), log_total)

    mixed_blocks, log_totals = lax.map(forward_block, block_ids)
    mixed_rows = mixed_blocks.reshape(group_rows, local_width)
    branch_out = (
        scatter_sum(
            jnp.dot(mixed_rows, output_full, preferred_element_type=jnp.float32), "tensor", 0
        )
        + bias_rows[2]
    )
    first_out, first_saved = layer_norm(
        tokens.astype(jnp.float32) + branch_out, norm_gains[0], bias_rows[3]
    )
    first_gathered = lax.all_gather(first_out.astype(jnp.bfloat16), "tensor", axis=0, tiled=True)
    local_bias = lax.dynamic_slice_in_dim(hidden_bias, tensor_rank * local_hidden, local_hidden, 0)
    upper_rows = (
        jnp.dot(first_gathered, upward_full, preferred_element_type=jnp.float32) + local_bias
    )
    hidden_full, gelu_back = jax.vjp(gelu_exact, upper_rows)
    hidden_rows = hidden_full.astype(jnp.bfloat16)
    second_out = (
        scatter_sum(
            jnp.dot(hidden_rows, downward_full, preferred_element_type=jnp.float32), "tensor", 0
        )
        + bias_rows[4]
    )
    layer_out, second_saved = layer_norm(first_out + second_out, norm_gains[1], bias_rows[5])
    reloaded = (
        lax.all_gather(project_weight, "dp", axis=0, tiled=True),
        lax.all_gather(output_weight, "dp", axis=1, tiled=True),
        lax.all_gather(up_weight, "dp", axis=0, tiled=True),
        lax.all_gather(down_weight, "dp", axis=1, tiled=True),
    )
    back_triple = reloaded[0].reshape(model_width, 3 * local_width)
    back_output, back_upward, back_downward = (reloaded[1], reloaded[2], reloaded[3])
    grad_layer = cotangent.astype(jnp.float32)
    grad_second_in, grad_gain_two, grad_shift_two = norm_back_saved(
        grad_layer, second_saved, norm_gains[1]
    )
    grad_second = grad_second_in.astype(jnp.bfloat16)
    grad_second_all = lax.all_gather(grad_second, "tensor", axis=0, tiled=True)
    grad_down_part = jnp.einsum(
        "tf,td->fd", hidden_rows, grad_second_all, preferred_element_type=jnp.float32
    )
    grad_hidden = jnp.einsum(
        "td,fd->tf", grad_second_all, back_downward, preferred_element_type=jnp.float32
    )
    grad_upper = gelu_back(grad_hidden)[0].astype(jnp.bfloat16)
    grad_up_part = jnp.einsum(
        "td,tf->df", first_gathered, grad_upper, preferred_element_type=jnp.float32
    )
    grad_first = (
        scatter_sum(
            jnp.einsum("tf,df->td", grad_upper, back_upward, preferred_element_type=jnp.float32),
            "tensor",
            0,
        )
        + grad_second_in
    )
    grad_first_in, grad_gain_one, grad_shift_one = norm_back_saved(grad_first, first_saved, norm_gains[0])
    grad_branch = grad_first_in.astype(jnp.bfloat16)
    grad_branch_all = lax.all_gather(grad_branch, "tensor", axis=0, tiled=True)
    grad_output_part = jnp.einsum(
        "tc,td->cd", mixed_rows, grad_branch_all, preferred_element_type=jnp.float32
    )
    grad_mixed = jnp.einsum(
        "td,cd->tc", grad_branch_all, back_output, preferred_element_type=jnp.float32
    ).astype(jnp.bfloat16)

    def backward_block(block_index):
        row_start, query_block, key_block, value_block, scores = block_parts(block_index)
        weights_full = jnp.exp(scores - log_totals[block_index][:, :, None])
        grad_mixed_block = split_heads(
            lax.dynamic_slice_in_dim(grad_mixed, row_start, block_rows, 0)
        )
        grad_weights = jnp.einsum(
            "qhd,khd->hqk", grad_mixed_block, value_block, preferred_element_type=jnp.float32
        )
        row_dot = jnp.sum(weights_full * grad_weights, axis=-1, keepdims=True)
        grad_scores = (weights_full * (grad_weights - row_dot)).astype(jnp.bfloat16)
        grad_query = (
            jnp.einsum("hqk,khd->qhd", grad_scores, key_block, preferred_element_type=jnp.float32)
            * score_scale
        )
        grad_key = (
            jnp.einsum("hqk,qhd->khd", grad_scores, query_block, preferred_element_type=jnp.float32)
            * score_scale
        )
        grad_value = jnp.einsum(
            "hqk,qhd->khd",
            weights_full.astype(jnp.bfloat16),
            grad_mixed_block,
            preferred_element_type=jnp.float32,
        )
        return (
            grad_query.reshape(block_rows, local_width),
            grad_key.reshape(seq_length, local_width),
            grad_value.reshape(seq_length, local_width),
        )

    query_blocks, key_blocks, value_blocks = lax.map(backward_block, block_ids)
    grad_queries = query_blocks.reshape(group_rows, local_width)
    grad_keys = (
        key_blocks.reshape(seq_count, per_sequence, seq_length, local_width)
        .sum(axis=1)
        .reshape(group_rows, local_width)
    )
    grad_values = (
        value_blocks.reshape(seq_count, per_sequence, seq_length, local_width)
        .sum(axis=1)
        .reshape(group_rows, local_width)
    )
    grad_projected = jnp.stack((grad_queries, grad_keys, grad_values), axis=1).astype(jnp.bfloat16)
    grad_project_part = jnp.einsum(
        "te,tsc->esc", gathered, grad_projected, preferred_element_type=jnp.float32
    )
    grad_matrix = grad_projected.reshape(group_rows, 3 * local_width)
    grad_tokens = (
        lax.psum_scatter(
            jnp.einsum(
                "tc,ec->te", grad_matrix, back_triple, preferred_element_type=jnp.float32
            ).astype(jnp.bfloat16),
            "tensor",
            scatter_dimension=0,
            tiled=True,
        ).astype(jnp.float32)
        + grad_first_in
    )
    grad_project, grad_output, grad_up, grad_down = (
        scatter_sum(grad_project_part, "dp", 0),
        scatter_sum(grad_output_part, "dp", 1),
        scatter_sum(grad_up_part, "dp", 0),
        scatter_sum(grad_down_part, "dp", 1),
    )
    head_terms = place_columns(
        jnp.stack(
            (
                jnp.sum(grad_projected[:, 0], axis=0, dtype=jnp.float32),
                jnp.sum(grad_projected[:, 2], axis=0, dtype=jnp.float32),
            )
        ),
        tensor_rank,
        model_width,
    )
    shared_terms = jnp.stack(
        (
            jnp.sum(grad_branch, axis=0, dtype=jnp.float32),
            grad_shift_one,
            jnp.sum(grad_second, axis=0, dtype=jnp.float32),
            grad_shift_two,
        )
    )
    bias_terms = jnp.concatenate((head_terms, shared_terms), axis=0)
    gain_terms = jnp.stack((grad_gain_one, grad_gain_two))
    hidden_terms = place_columns(
        jnp.sum(grad_upper, axis=0, dtype=jnp.float32), tensor_rank, hidden_bias.shape[0]
    )
    grad_gains, grad_bias_rows, grad_hidden_bias = lax.psum(
        (gain_terms, bias_terms, hidden_terms), ("dp", "tensor")
    )
    return (
        layer_out.astype(jnp.bfloat16),
        grad_tokens,
        grad_project,
        grad_output,
        grad_up,
        grad_down,
        grad_gains,
        grad_bias_rows,
        grad_hidden_bias,
    )


def solution(mesh):
    fits = mesh.shape["dp"] == 2 * LINES and mesh.shape["tensor"] == 4
    placed = (
        P(("dp", "tensor"), None),
        P("dp", None),
        P(("dp", "tensor"), None),
        P("dp", None, "tensor"),
        P("tensor", "dp"),
        P("dp", "tensor"),
        P("tensor", "dp"),
        P(),
        P(),
        P(),
    )
    return jax.shard_map(
        per_device_kernel if fits else per_device,
        mesh=mesh,
        in_specs=placed,
        out_specs=(
            P(("dp", "tensor"), None),
            P(("dp", "tensor"), None),
            P("dp", None, "tensor"),
            P("tensor", "dp"),
            P("dp", "tensor"),
            P("tensor", "dp"),
            P(),
            P(),
            P(),
        ),
        check_vma=False,
    )
```

```python
import functools
import types

import jax
import jax.numpy as jnp
from jax import lax
from jax.experimental import pallas as pl
from jax.experimental.pallas import tpu as pltpu
from jax.sharding import PartitionSpec as P

HEAD = 64
EPSILON = 1e-05
NEGATIVE = -1e30
MESH = pl.DeviceIdType.MESH
LINES = 4
CORE, ACROSS, FAR = 1, 2, 3
HALVES = 2
CHUNK = 16
NORM = 64
ORDER = (3, 2, 1, 0)
VMEM_BYTES = 60 << 20


def remote(src, dst, send_sem, recv_sem, target):
    return pltpu.make_async_remote_copy(
        src_ref=src,
        dst_ref=dst,
        send_sem=send_sem,
        recv_sem=recv_sem,
        device_id=target,
        device_id_type=MESH,
    )


def position():
    return lax.axis_index("dp"), lax.axis_index("tensor")


def greet():
    dp, tensor = position()
    barrier = pltpu.get_barrier_semaphore()
    others = [(dp ^ step, tensor) for step in (1, 2, 4, 6)]
    others += [(dp, tensor ^ step) for step in (CORE, ACROSS)]
    for target in others:
        pl.semaphore_signal(barrier, inc=1, device_id=target, device_id_type=MESH)
    pl.semaphore_wait(barrier, len(others))


def row_piece(ref, index, size):
    return ref.at[pl.ds(pl.multiple_of(index * size, size), size), :]


def column_piece(ref, index, size):
    return ref.at[:, pl.ds(pl.multiple_of(index * size, size), size)]


class LineGather:
    def __init__(self, own, full, piece, send_sem, recv_sem, local_sem):
        self.own, self.full, self.piece = own, full, piece
        self.send_sem, self.recv_sem, self.local_sem = send_sem, recv_sem, local_sem
        self.dp, self.tensor = position()
        self.line, self.side = self.dp // 2, self.dp % 2
        self.targets = (
            (self.dp + 2, self.tensor),
            (self.dp - 2, self.tensor),
            (self.dp ^ 1, self.tensor),
        )

    def copy(self, index, way, src=None):
        view = self.piece(self.full, index)
        return remote(
            view if src is None else src,
            view,
            self.send_sem.at[way * LINES + index // 2],
            self.recv_sem.at[index],
            self.targets[way],
        )

    def local(self):
        return pltpu.make_async_copy(self.own, self.piece(self.full, self.dp), self.local_sem)

    def start_along(self):
        self.local().start()

        @pl.when(self.line < LINES - 1)
        def _():
            self.copy(self.dp, 0, self.own).start()

        @pl.when(self.line > 0)
        def _():
            self.copy(self.dp, 1, self.own).start()

    def start_across(self):
        self.copy(self.dp, 2, self.own).start()

    def step(self, distance):
        @pl.when(self.line >= distance)
        def _():
            index = self.dp - 2 * distance
            self.copy(index, 0).wait_recv()

            @pl.when(self.line < LINES - 1)
            def _():
                self.copy(index, 0).start()

            self.copy(index, 2).start()

        @pl.when(self.line + distance < LINES)
        def _():
            index = self.dp + 2 * distance
            self.copy(index, 1).wait_recv()

            @pl.when(self.line > 0)
            def _():
                self.copy(index, 1).start()

            self.copy(index, 2).start()

    def arrive(self):
        self.local().wait()
        for line in range(LINES):
            self.copy(2 * line + 1 - self.side, 2).wait_recv()

    def finish(self):
        for line in range(LINES):
            index = 2 * line + self.side
            self.copy(index, 2).wait_send()

            @pl.when((self.line < LINES - 1) & (line <= self.line))
            def _():
                self.copy(index, 0).wait_send()

            @pl.when((self.line > 0) & (line >= self.line))
            def _():
                self.copy(index, 1).wait_send()


class RowGather:
    def __init__(self, full, rows, send_sem, recv_sem):
        self.full, self.rows = full, rows
        self.send_sem, self.recv_sem = send_sem, recv_sem
        self.dp, self.tensor = position()

    def view(self, rank, half=None):
        if half is None:
            return row_piece(self.full, rank, self.rows)
        return row_piece(self.full, rank * HALVES + half, self.rows // HALVES)

    def near(self, rank):
        view = self.view(rank)
        target = (self.dp, self.tensor ^ CORE)
        return remote(view, view, self.send_sem.at[0], self.recv_sem.at[0], target)

    def across(self, rank, half):
        view, slot = self.view(rank, half), 1 + half
        target = (self.dp, self.tensor ^ ACROSS)
        return remote(view, view, self.send_sem.at[slot], self.recv_sem.at[slot], target)

    def far(self, rank, half):
        view, slot = self.view(rank, half), 1 + HALVES + half
        target = (self.dp, self.tensor ^ CORE)
        return remote(view, view, self.send_sem.at[slot], self.recv_sem.at[slot], target)

    def start(self):
        for half in range(HALVES):
            self.across(self.tensor, half).start()
        self.near(self.tensor).start()

    def wait_near(self):
        self.near(self.tensor ^ CORE).wait_recv()

    def wait_across(self, half):
        self.across(self.tensor ^ ACROSS, half).wait_recv()
        self.far(self.tensor ^ ACROSS, half).start()

    def wait_far(self, half):
        self.far(self.tensor ^ FAR, half).wait_recv()

    def finish(self):
        self.near(self.tensor).wait_send()
        for half in range(HALVES):
            self.across(self.tensor, half).wait_send()
            self.far(self.tensor ^ ACROSS, half).wait_send()


class RowScatter:
    def __init__(self, near_out, near_in, across_out, across_in, send_sem, recv_sem):
        self.near_out, self.near_in = near_out, near_in
        self.across_out, self.across_in = across_out, across_in
        self.send_sem, self.recv_sem = send_sem, recv_sem
        self.dp, self.tensor = position()

    def near(self, slot):
        return remote(
            self.near_out.at[slot],
            self.near_in.at[slot],
            self.send_sem.at[slot],
            self.recv_sem.at[slot],
            (self.dp, self.tensor ^ CORE),
        )

    def across(self, half):
        rows = self.across_in.shape[0] // HALVES
        return remote(
            row_piece(self.across_out, half, rows),
            row_piece(self.across_in, half, rows),
            self.send_sem.at[2 * HALVES + half],
            self.recv_sem.at[2 * HALVES + half],
            (self.dp, self.tensor ^ ACROSS),
        )

    def give_far(self, half, partial):
        self.near_out[half] = partial.astype(jnp.bfloat16)
        self.near(half).start()

    def give_across(self, half, partial):
        self.near(half).wait_recv()
        rows = partial.shape[0]
        total = partial + self.near_in[half].astype(jnp.float32)
        row_piece(self.across_out, half, rows)[...] = total.astype(jnp.bfloat16)
        self.across(half).start()

    def give_near(self, half, partial):
        self.near_out[HALVES + half] = partial.astype(jnp.bfloat16)
        self.near(HALVES + half).start()

    def take(self, half, partial):
        self.near(HALVES + half).wait_recv()
        rows = partial.shape[0]
        total = partial + self.near_in[HALVES + half].astype(jnp.float32)
        self.across(half).wait_recv()
        return total + row_piece(self.across_in, half, rows)[...].astype(jnp.float32)

    def finish(self):
        for slot in range(2 * HALVES):
            self.near(slot).wait_send()
        for half in range(HALVES):
            self.across(half).wait_send()


def dot(left, right):
    return jnp.dot(left, right, preferred_element_type=jnp.float32)


def dot_nt(left, right):
    return lax.dot_general(left, right, (((1,), (1,)), ((), ())), preferred_element_type=jnp.float32)


def dot_tn(left, right):
    return lax.dot_general(left, right, (((0,), (0,)), ((), ())), preferred_element_type=jnp.float32)


def normalize(rows):
    centred = rows - jnp.mean(rows, axis=-1, keepdims=True)
    inverse = lax.rsqrt(jnp.mean(centred * centred, axis=-1, keepdims=True) + EPSILON)
    return centred * inverse, inverse


def norm_back(grad, normed, inverse):
    average = jnp.mean(grad, axis=-1, keepdims=True)
    along = jnp.mean(grad * normed, axis=-1, keepdims=True)
    return inverse * (grad - average - normed * along)


class LineFirstScatter:
    def __init__(self, partial, piece, line_in, across_out, across_in, send_sem, recv_sem):
        self.partial, self.piece, self.line_in = partial, piece, line_in
        self.across_out, self.across_in = across_out, across_in
        self.send_sem, self.recv_sem = send_sem, recv_sem
        self.dp, self.tensor = position()

    def view(self, step):
        return self.piece(self.partial, (self.dp // 2) ^ step)

    def along(self, step):
        return remote(
            self.view(step),
            self.line_in.at[step // 2 if step != 2 else 2],
            self.send_sem.at[step],
            self.recv_sem.at[step],
            (self.dp ^ (2 if step != 2 else 4), self.tensor),
        )

    def across(self):
        return remote(
            self.across_out,
            self.across_in,
            self.send_sem.at[0],
            self.recv_sem.at[0],
            (self.dp ^ 1, self.tensor),
        )

    def start(self):
        self.along(3).start()
        self.along(1).start()

    def relay(self):
        self.along(3).wait_recv()
        total = self.view(2)[...].astype(jnp.float32) + self.line_in[1].astype(jnp.float32)
        self.view(2)[...] = total.astype(jnp.bfloat16)
        self.along(2).start()

    def turn(self, result):
        total = self.view(0)[...].astype(jnp.float32)
        for step, slot in ((1, 0), (2, 2)):
            self.along(step).wait_recv()
            total = total + self.line_in[slot].astype(jnp.float32)
        width = result.shape[1]
        first, second = total[:, :width], total[:, width:]
        even = self.dp % 2 == 0
        result[...] = jnp.where(even, first, second)
        self.across_out[...] = jnp.where(even, second, first).astype(jnp.bfloat16)
        self.across().start()

    def finish(self, result):
        self.across().wait_recv()
        result[...] += self.across_in[...].astype(jnp.float32)
        self.across().wait_send()
        for step in range(1, LINES):
            self.along(step).wait_send()


class DirectGather:
    def __init__(self, own, full, piece, send_sem, recv_sem, local_sem):
        self.own, self.full, self.piece = own, full, piece
        self.send_sem, self.recv_sem, self.local_sem = send_sem, recv_sem, local_sem
        self.dp, self.tensor = position()

    def along(self, step):
        there = self.dp ^ (2 * step)
        return remote(
            self.own,
            self.piece(self.full, self.dp),
            self.send_sem.at[step],
            self.recv_sem.at[step],
            (there, self.tensor),
        )

    def across(self, step, source=None):
        view = self.piece(self.full, self.dp ^ (2 * step))
        return remote(
            view if source is None else source,
            view,
            self.send_sem.at[LINES + step],
            self.recv_sem.at[LINES + step],
            (self.dp ^ 1, self.tensor),
        )

    def local(self):
        return pltpu.make_async_copy(self.own, self.piece(self.full, self.dp), self.local_sem)

    def start_along(self):
        self.local().start()
        for step in range(1, LINES):
            self.along(step).start()

    def start_across(self):
        self.across(0, self.own).start()

    def step(self, step):
        self.along(step).wait_recv()
        self.across(step).start()

    def arrive(self, step):
        self.across(step).wait_recv()

    def finish(self):
        for step in range(LINES):
            self.across(step).wait_send()
        for step in range(1, LINES):
            self.along(step).wait_send()


class ColumnScatter:
    def __init__(self, near_out, near_in, across_out, across_in, send_sem, recv_sem):
        self.near_out, self.near_in = near_out, near_in
        self.across_out, self.across_in = across_out, across_in
        self.send_sem, self.recv_sem = send_sem, recv_sem
        self.dp, self.tensor = position()

    def near(self, slot):
        return remote(
            self.near_out.at[slot],
            self.near_in.at[slot],
            self.send_sem.at[slot],
            self.recv_sem.at[slot],
            (self.dp, self.tensor ^ CORE),
        )

    def across(self, at):
        return remote(
            self.across_out.at[at],
            self.across_in.at[at],
            self.send_sem.at[2 * LINES + at],
            self.recv_sem.at[2 * LINES + at],
            (self.dp, self.tensor ^ ACROSS),
        )

    def give_far(self, at, partial):
        self.near_out[at] = partial.astype(jnp.bfloat16)
        self.near(at).start()

    def give_near(self, at, partial):
        self.near_out[LINES + at] = partial.astype(jnp.bfloat16)
        self.near(LINES + at).start()

    def give_across(self, at, partial):
        self.near(at).wait_recv()
        total = partial + self.near_in[at].astype(jnp.float32)
        self.across_out[at] = total.astype(jnp.bfloat16)
        self.across(at).start()

    def take(self, at, partial):
        self.near(LINES + at).wait_recv()
        total = partial + self.near_in[LINES + at].astype(jnp.float32)
        self.across(at).wait_recv()
        return total + self.across_in[at].astype(jnp.float32)

    def finish(self):
        for slot in range(2 * LINES):
            self.near(slot).wait_send()
        for at in range(LINES):
            self.across(at).wait_send()


class LineScatter:
    def __init__(self, partial, piece, side_in, line_in, send_sem, recv_sem):
        self.partial, self.piece, self.side_in, self.line_in = partial, piece, side_in, line_in
        self.send_sem, self.recv_sem = send_sem, recv_sem
        self.dp, self.tensor = position()

    def view(self, step):
        return self.piece(self.partial, self.dp ^ (2 * step))

    def across(self, step):
        return remote(
            self.piece(self.partial, self.dp ^ (2 * step) ^ 1),
            self.side_in.at[step],
            self.send_sem.at[step],
            self.recv_sem.at[step],
            (self.dp ^ 1, self.tensor),
        )

    def along(self, step):
        return remote(
            self.view(step),
            self.line_in.at[step // 2 if step != 2 else 2],
            self.send_sem.at[LINES + step],
            self.recv_sem.at[LINES + step],
            (self.dp ^ (2 if step != 2 else 4), self.tensor),
        )

    def start(self):
        for step in ORDER:
            self.across(step).start()

    def total(self, step):
        self.across(step).wait_recv()
        return self.view(step)[...].astype(jnp.float32) + self.side_in[step].astype(jnp.float32)

    def relay(self, step):
        total = self.total(step)
        if step == 2:
            self.along(3).wait_recv()
            total = total + self.line_in[1].astype(jnp.float32)
        self.view(step)[...] = total.astype(jnp.bfloat16)
        self.along(step).start()

    def finish(self, result):
        total = self.total(0)
        self.along(1).wait_recv()
        total = total + self.line_in[0].astype(jnp.float32)
        self.along(2).wait_recv()
        result[...] = total + self.line_in[2].astype(jnp.float32)
        for step in range(LINES):
            self.across(step).wait_send()
        for step in range(1, LINES):
            self.along(step).wait_send()


class Total:
    def __init__(self, held, arrived, send_sem, recv_sem):
        self.held, self.arrived, self.send_sem, self.recv_sem = held, arrived, send_sem, recv_sem
        dp, tensor = position()
        self.targets = (
            (dp ^ 1, tensor),
            (dp ^ 2, tensor),
            (dp ^ 4, tensor),
            (dp, tensor ^ ACROSS),
            (dp, tensor ^ CORE),
        )

    def copy(self, step):
        return remote(
            self.held.at[step],
            self.arrived.at[step],
            self.send_sem.at[step],
            self.recv_sem.at[step],
            self.targets[step],
        )

    def start(self):
        self.copy(0).start()

    def step(self, step):
        self.copy(step).wait_recv()
        self.held[step + 1] = self.held[step] + self.arrived[step]
        if step + 1 < len(self.targets):
            self.copy(step + 1).start()

    def finish(self):
        for step in range(len(self.targets)):
            self.copy(step).wait_send()


def layer_kernel(names, rows, *refs):
    r = types.SimpleNamespace(**dict(zip(names, refs)))
    dp, tensor = position()
    bf16, f32 = jnp.bfloat16, jnp.float32
    half_rows = rows // HALVES
    local = r.queries.shape[1]
    piece = r.triple_own.shape[1]
    pairs = local // (2 * HEAD)
    hidden = r.hidden.shape[1]
    near, across, far = tensor ^ CORE, tensor ^ ACROSS, tensor ^ FAR

    def of_rows(ref, index):
        return row_piece(ref, index, piece)

    def of_columns(ref, index):
        return column_piece(ref, index, piece)

    def of_stack(ref, index):
        return ref.at[:, pl.ds(pl.multiple_of(index * piece, piece), piece), :]

    def of_half_stack(half):
        size = piece // HALVES

        def view(ref, index):
            return ref.at[:, pl.ds(pl.multiple_of(index * piece + half * size, size), size), :]

        return view, r.triple_own.at[:, half * size : (half + 1) * size, :]

    def block(rank, size=rows):
        return pl.ds(pl.multiple_of(rank * size, size), size)

    def split(partial):
        return [partial[half * half_rows : (half + 1) * half_rows] for half in range(HALVES)]

    def part_of(half):
        return slice(half * half_rows, (half + 1) * half_rows)

    (view_a, own_a), (view_b, own_b) = of_half_stack(0), of_half_stack(1)
    lines = [
        kind(own, full, view, r.line_send.at[at], r.line_recv.at[at], r.line_local.at[at])
        for at, (kind, own, full, view) in enumerate(
            (
                (LineGather, own_a, r.triple, view_a),
                (LineGather, own_b, r.triple, view_b),
                (DirectGather, r.output_own, r.output, of_columns),
                (LineGather, r.up_own, r.up, of_rows),
                (DirectGather, r.down_own, r.down, of_columns),
            )
        )
    ]
    *triple_lines, output_line, up_line, down_line = lines
    sums = [
        LineScatter(partial, view, side, along, r.part_send.at[at], r.part_recv.at[at])
        for at, (partial, view, side, along) in enumerate(
            (
                (r.grad_project, of_stack, r.project_side, r.project_line),
                (r.grad_output, of_columns, r.output_side, r.output_line),
                (r.grad_up, of_rows, r.up_side, r.up_line),
                (r.grad_down.at[: hidden // 2, :], of_columns, r.down_side, r.down_line),
            )
        )
    ]
    project_sum, output_sum, up_sum, down_sum = sums

    def of_both(ref, index):
        return column_piece(ref, index, 2 * piece)

    rest_sum = LineFirstScatter(
        r.grad_down.at[hidden // 2 :, :],
        of_both,
        r.rest_line,
        r.rest_out,
        r.rest_in,
        r.part_send.at[4],
        r.part_recv.at[4],
    )
    down_top, down_rest = r.down_sum.at[: hidden // 2, :], r.down_sum.at[hidden // 2 :, :]
    gathers = [
        RowGather(full, rows, r.row_send.at[at], r.row_recv.at[at])
        for at, full in enumerate((r.gathered, r.first_all, r.second_all, r.branch_all))
    ]
    scatters = [
        kind(*buffers, r.sum_send.at[at], r.sum_recv.at[at])
        for at, (kind, buffers) in enumerate(
            (
                (RowScatter, (r.near_out_a, r.near_in_a, r.across_out_a, r.across_in_a)),
                (ColumnScatter, (r.near_out_b, r.near_in_b, r.across_out_b, r.across_in_b)),
            )
            * 2
        )
    ]
    total = Total(r.held_totals, r.arrived_totals, r.total_send, r.total_recv)

    def column_block(at):
        return block((dp // 2) ^ at, 2 * piece)

    def scatter_columns(scatter, at):
        scatter.give_far(at, r.columns[block(far), :])
        scatter.give_near(at, r.columns[block(near), :])
        scatter.give_across(at, r.columns[block(across), :])
        r.kept[:, column_block(at)] = r.columns[block(tensor), :]

    def chunks(size, start, body, step=CHUNK):
        @pl.loop(0, size // step)
        def _(chunk):
            offset = chunk * step
            body(
                pl.ds(pl.multiple_of(offset, step), step),
                pl.ds(pl.multiple_of(start + offset, step), step),
            )

    loads = [
        pltpu.make_async_copy(source, target, r.load_sem.at[at])
        for at, (source, target) in enumerate(
            (
                (r.tokens, gathers[0].view(tensor)),
                (r.segments, r.segment_row),
                (r.bias_from, r.bias_rows),
                (r.gains_from, r.norm_gains),
                (r.hidden_from.at[pl.ds(pl.multiple_of(tensor * hidden, hidden), hidden)], r.hidden_bias),
                (r.cotangent_from, r.cotangent),
            )
        )
    ]
    for load in loads:
        load.start()
    greet()
    for line in triple_lines:
        line.start_along()
        line.start_across()
    loads[0].wait()
    gathers[0].start()
    for line in triple_lines:
        line.step(1)
    loads[1].wait()
    numbers = r.segment_row[...].astype(f32)
    r.segment_column[...] = jnp.broadcast_to(numbers, (8, numbers.shape[1])).T[:, :1]
    r.segment_row_f32[...] = numbers
    for line in triple_lines:
        line.step(2)
    gathers[0].wait_near()
    for half in range(HALVES):
        gathers[0].wait_across(half)
    for line in triple_lines:
        line.step(3)
    output_line.start_along()
    output_line.start_across()
    up_line.start_along()
    up_line.start_across()
    for half in range(HALVES):
        gathers[0].wait_far(half)
    for line in triple_lines:
        line.arrive()
    for load in loads[2:]:
        load.wait()
    columns = pl.ds(pl.multiple_of(tensor * local, local), local)
    query_bias = r.bias_rows[0:1, columns]
    value_bias = r.bias_rows[1:2, columns]

    @pl.loop(0, 4)
    def _(index):
        here = block(index)
        left = r.gathered[here, :]
        query = (dot(left, r.triple[0]) + query_bias).astype(bf16)
        r.queries[here, :] = query * bf16(HEAD**-0.5)
        key = dot(left, r.triple[1])
        r.key_rows[here, :] = key.astype(bf16)
        r.key_turned[:, here] = key.T.astype(bf16)
        value = dot(left, r.triple[2]) + value_bias
        r.value_rows[here, :] = value.astype(bf16)
        r.value_turned[:, here] = value.T.astype(bf16)

    for step in range(1, LINES):
        output_line.step(step)

    def head_rows(head):
        return pl.ds(pl.multiple_of(head * HEAD, HEAD), HEAD)

    def attend(here, pair):
        lanes = block(pair, 2 * HEAD)
        query = r.queries[here, lanes]
        keys = r.key_rows[:, lanes]
        same = r.segment_column[...] == r.segment_row_f32[:, here]
        lane = lax.broadcasted_iota(jnp.int32, query.shape, 1)
        outs = []
        for side in range(2):
            scores = dot_nt(keys, jnp.where(lane // HEAD == side, query, bf16(0)))
            scores = jnp.where(same, scores, NEGATIVE)
            top = jnp.max(scores, axis=0, keepdims=True)
            exponent = jnp.exp(scores - top)
            mass = jnp.sum(exponent, axis=0, keepdims=True)
            weights = (exponent * (1.0 / mass)).astype(bf16)
            head = pair * 2 + side
            outs.append(dot(r.value_turned[head_rows(head), :], weights))
            r.log_totals[pl.ds(head, 1), here] = top + jnp.log(mass)
        r.mixed[here, lanes] = jnp.concatenate(outs, axis=0).T.astype(bf16)

    @pl.loop(0, 4 * pairs)
    def _(turn):
        rank, pair = tensor ^ (FAR - turn // pairs), turn % pairs
        here = block(rank)
        attend(here, pair)

        def give(rank, method):
            r.partial[...] = dot(r.mixed[block(rank), :], r.output[...])
            for half in range(HALVES):
                method(half, r.partial[part_of(half), :])

        def after(index):
            return pl.when(turn == index)

        @after(0)
        def _():
            up_line.step(1)

        @after(3)
        def _():
            output_line.local().wait()
            for step in range(LINES):
                output_line.arrive(step)
            give(far, scatters[0].give_far)
            give(across, scatters[0].give_across)

        @after(4)
        def _():
            up_line.step(2)
            down_line.start_along()

        @after(5)
        def _():
            give(near, scatters[0].give_near)

        @after(7)
        def _():
            up_line.step(3)
            down_line.start_across()

    r.partial[...] = dot(r.mixed[block(tensor), :], r.output[...])
    for half in range(HALVES):
        part = part_of(half)
        r.kept[part, :] = scatters[0].take(half, r.partial[part, :])

        def first_norm(_, here):
            own_rows = r.gathered[pl.ds(pl.multiple_of(tensor * rows + here.start, NORM), NORM), :]
            normed, inverse = normalize(own_rows.astype(f32) + r.kept[here, :] + r.bias_rows[2:3, :])
            r.normed_one[here, :] = normed
            r.inverse_one[here, :] = inverse
            first = normed * r.norm_gains[0:1, :] + r.bias_rows[3:4, :]
            into = pl.ds(pl.multiple_of(tensor * rows + here.start, NORM), NORM)
            r.first_all[into, :] = first.astype(bf16)

        chunks(half_rows, half * half_rows, first_norm, NORM)
    scatters[0].finish()

    gathers[1].start()
    r.sums[...] = jnp.zeros_like(r.sums)

    def extent(rank, half):
        size = rows if half is None else half_rows
        start = rank * rows + (0 if half is None else half * half_rows)
        return start, size, pl.ds(pl.multiple_of(start, size), size)

    def up_part(rank, half=None):
        start, size, here = extent(rank, half)
        r.upper[:size, :] = dot(r.first_all[here, :], r.up[...]) + r.hidden_bias[...].reshape(1, hidden)

        def body(part, into):
            value = r.upper[part, :]
            share = 0.5 + 0.5 * lax.erf(value * (0.5**0.5))
            r.hidden[into, :] = (value * share).astype(bf16)
            bell = jnp.exp(value * value * -0.5) * (2 * jnp.pi) ** -0.5
            r.slope[into, :] = share + value * bell

        chunks(size, start, body)

    def back_part(rank, half=None):
        start, size, here = extent(rank, half)
        r.upper[:size, :] = dot_nt(r.second_all[here, :], r.down[...])

        def body(part, into):
            low = (r.upper[part, :] * r.slope[into, :]).astype(bf16)
            r.upper_low[into, :] = low
            r.sums[6:7, :] += jnp.sum(low.astype(f32), axis=0, keepdims=True)

        chunks(size, start, body)
        r.partial[:size, :] = dot_nt(r.upper_low[here, :], r.up[...])

    up_line.arrive()

    @pl.loop(0, 2)
    def _(turn):
        @pl.when(turn == 1)
        def _():
            down_line.step(1)
            gathers[1].wait_near()

        up_part(tensor ^ turn)

    def other_chip(gather, body):
        @pl.loop(0, 2 * HALVES)
        def _(turn):
            half, side = turn // 2, turn % 2

            @pl.when(side == 0)
            def _():
                gather.wait_across(half)

            body(half, side)

    def up_other(half, side):
        @pl.when(side == 1)
        def _():
            gathers[1].wait_far(half)

        up_part(tensor ^ (ACROSS + side), half)

        @pl.when(side == 1)
        def _():
            down_line.step(2 + half)

    other_chip(gathers[1], up_other)

    down_line.local().wait()

    @pl.loop(0, LINES)
    def _(at):
        down_line.arrive(at)
        r.columns[...] = dot(r.hidden[...], r.down[:, column_block(at)])
        scatter_columns(scatters[1], at)

    def add_to(row, value):
        r.sums[row : row + 1, :] += jnp.sum(value, axis=0, keepdims=True)

    def second_norm(_, here):
        first = r.normed_one[here, :] * r.norm_gains[0:1, :] + r.bias_rows[3:4, :]
        normed, inverse = normalize(first + r.kept[here, :] + r.bias_rows[4:5, :])
        shifted = normed * r.norm_gains[1:2, :] + r.bias_rows[5:6, :]
        r.layer_low[here, :] = shifted.astype(bf16)
        grad = r.cotangent[here, :].astype(f32)
        add_to(5, grad * normed)
        add_to(3, grad)
        grad = norm_back(grad * r.norm_gains[1:2, :], normed, inverse)
        r.grad_rows[here, :] = grad
        low = grad.astype(bf16)
        add_to(2, low.astype(f32))
        r.second_all[pl.ds(pl.multiple_of(tensor * rows + here.start, NORM), NORM), :] = low

    @pl.loop(0, LINES)
    def _(at):
        lanes = column_block(at)
        r.kept[:, lanes] = scatters[1].take(at, r.kept[:, lanes])

    chunks(rows, 0, second_norm, NORM)
    saves = []

    def save(source, target):
        saves.append(pltpu.make_async_copy(source, target, r.save_sem.at[len(saves)]))
        saves[-1].start()

    save(r.layer_low, r.layer_out)
    scatters[1].finish()

    gathers[2].start()

    @pl.loop(0, 2)
    def _(turn):
        @pl.when(turn == 1)
        def _():
            gathers[2].wait_near()

        back_part(tensor ^ turn)

        @pl.when(turn == 0)
        def _():
            r.kept[...] = r.partial[...]

        @pl.when(turn == 1)
        def _():
            for half in range(HALVES):
                scatters[2].give_near(half, r.partial[part_of(half), :])

    def weight_grad(left, right, result, chip=None, add=False):
        depth = slice(None) if chip is None else block(chip, 2 * rows)

        @pl.loop(0, left.shape[1] // rows)
        def _(index):
            lanes = block(index)
            product = dot_tn(left[depth, lanes], right[depth, :])
            if add:
                product += result[lanes, :].astype(f32)
            result[lanes, :] = product.astype(bf16)

    weight_grad(r.hidden, r.second_all, r.grad_down, tensor // 2)

    def back_other(half, side):
        @pl.when((side == 1) & (half < HALVES - 1))
        def _():
            gathers[2].wait_far(half)

        @pl.when((side == 0) & (half == HALVES - 1))
        def _():
            gathers[2].wait_far(half)
            weight_grad(r.hidden, r.second_all, r.grad_down, 1 - tensor // 2, True)
            rest_sum.start()
            down_sum.start()

        back_part(tensor ^ (ACROSS + side), half)

        @pl.when(side == 0)
        def _():
            r.held[...] = r.partial[:half_rows, :]

        @pl.when(side == 1)
        def _():
            scatters[2].give_far(half, r.partial[:half_rows, :])
            scatters[2].give_across(half, r.held[...])

    other_chip(gathers[2], back_other)

    weight_grad(r.first_all, r.upper_low, r.grad_up)
    up_sum.start()

    def first_back(_, here):
        grad = r.grad_rows[here, :] + r.kept[here, :]
        normed = r.normed_one[here, :]
        add_to(4, grad * normed)
        add_to(1, grad)
        grad = norm_back(grad * r.norm_gains[0:1, :], normed, r.inverse_one[here, :])
        r.grad_rows[here, :] = grad
        low = grad.astype(bf16)
        add_to(0, low.astype(f32))
        r.branch_all[pl.ds(pl.multiple_of(tensor * rows + here.start, NORM), NORM), :] = low

    for half in range(HALVES):
        part = part_of(half)
        r.kept[part, :] = scatters[2].take(half, r.kept[part, :])
        chunks(half_rows, half * half_rows, first_back, NORM)
        if half == 0:
            rest_sum.relay()
            down_sum.relay(3)
    scatters[2].finish()

    gathers[3].start()
    grad_keys, grad_values = r.slope.at[:, :local], r.slope.at[:, local : 2 * local]
    r.slope[:, : 2 * local] = jnp.zeros((r.slope.shape[0], 2 * local), f32)

    def attend_back(rank):
        here = block(rank)
        r.mixed_low[...] = dot_nt(r.branch_all[here, :], r.output[...]).astype(bf16)

        @pl.loop(0, pairs)
        def _(pair):
            lanes = block(pair, 2 * HEAD)
            query = r.queries[here, lanes]
            grad = r.mixed_low[:, lanes]
            keys = r.key_rows[:, lanes]
            values = r.value_rows[:, lanes]
            same = r.segment_column[...] == r.segment_row_f32[:, here]
            lane = lax.broadcasted_iota(jnp.int32, query.shape, 1)
            outs = []
            for side in range(2):
                mine = lane // HEAD == side
                head = pair * 2 + side
                query_here = jnp.where(mine, query, bf16(0))
                grad_here = jnp.where(mine, grad, bf16(0))
                scores = jnp.where(same, dot_nt(keys, query_here), NEGATIVE)
                weights = jnp.exp(scores - r.log_totals[pl.ds(head, 1), here])
                grad_weights = dot_nt(values, grad_here)
                along = jnp.sum(weights * grad_weights, axis=0, keepdims=True)
                grad_scores = (weights * (grad_weights - along)).astype(bf16)
                grad_keys[:, lanes] += dot(grad_scores, query_here)
                grad_values[:, lanes] += dot(weights.astype(bf16), grad_here)
                outs.append(dot(r.key_turned[head_rows(head), :], grad_scores))
            grad_query = jnp.concatenate(outs, axis=0).T * HEAD**-0.5
            r.projected_low[here, lanes] = grad_query.astype(bf16)

    @pl.loop(0, 4)
    def _(turn):
        @pl.when(turn == 1)
        def _():
            gathers[3].wait_near()

        @pl.when(turn == 2)
        def _():
            for half in range(HALVES):
                gathers[3].wait_across(half)

        @pl.when(turn == 3)
        def _():
            for half in range(HALVES):
                gathers[3].wait_far(half)

        attend_back(tensor ^ turn)

        @pl.when(turn == 1)
        def _():
            down_sum.relay(1)
            up_sum.relay(3)
            down_sum.relay(2)

        @pl.when(turn == 2)
        def _():
            rest_sum.turn(down_rest)

    up_sum.relay(1)
    r.grad_output[...] = dot_tn(r.mixed[...], r.branch_all[...]).astype(bf16)
    r.projected_low[:, local : 2 * local] = grad_keys[...].astype(bf16)
    r.projected_low[:, 2 * local :] = grad_values[...].astype(bf16)
    r.held_totals[0] = jnp.zeros(r.held_totals.shape[1:], f32)
    r.held_totals[0, 2:8, :] = r.sums[0:6, :]
    r.held_totals[0, pl.ds(8 + tensor, 1), :] = r.sums[6:7, :]
    for row, at in ((0, 0), (1, 2)):
        low = r.projected_low[:, at * local : (at + 1) * local].astype(f32)
        r.held_totals[0, row : row + 1, columns] = jnp.sum(low, axis=0, keepdims=True)
    total.start()
    for at in range(3):
        lanes = slice(at * local, (at + 1) * local)
        weight_grad(r.gathered, r.projected_low.at[:, lanes], r.grad_project.at[at])
    project_sum.start()
    output_sum.start()
    up_sum.relay(2)

    @pl.loop(0, LINES)
    def _(at):
        lanes = column_block(at)
        product = 0
        for part in range(3):
            left = r.projected_low[:, part * local : (part + 1) * local]
            product += dot_nt(left, r.triple[part, lanes, :])
        r.columns[...] = product
        scatter_columns(scatters[3], at)

    total.step(0)
    project_sum.relay(3)
    down_sum.finish(down_top)
    rest_sum.finish(down_rest)
    save(r.down_sum, r.down_out)

    def take_tokens(at):
        lanes = column_block(at)
        r.grad_rows[:, lanes] += scatters[3].take(at, r.kept[:, lanes])

    take_tokens(0)
    take_tokens(1)
    take_tokens(2)
    project_sum.relay(2)
    take_tokens(3)
    save(r.grad_rows, r.grad_tokens)
    project_sum.relay(1)
    total.step(1)
    up_sum.finish(r.up_sum)
    save(r.up_sum, r.up_out)
    output_sum.relay(3)
    total.step(2)
    output_sum.relay(2)
    output_sum.relay(1)
    total.step(3)
    project_sum.finish(r.project_sum)
    save(r.project_sum, r.project_out)
    total.step(4)
    r.bias_sum[...] = r.held_totals[5, 0:6, :]
    r.gains_sum[...] = r.held_totals[5, 6:8, :]
    for at in range(4):
        r.hidden_sum[at * hidden : (at + 1) * hidden] = r.held_totals[5, 8 + at, :]
    save(r.bias_sum, r.bias_out)
    save(r.gains_sum, r.gains_out)
    save(r.hidden_sum, r.hidden_out)
    scatters[3].finish()
    output_sum.finish(r.output_sum)
    save(r.output_sum, r.output_out)
    for each in gathers + lines + [total]:
        each.finish()
    for each in saves:
        each.wait()


def copy_kernel(count, *refs):
    sources, targets, held, sem = refs[:count], refs[count : 2 * count], refs[2 * count : -1], refs[-1]
    copies_in = [pltpu.make_async_copy(*pair, sem.at[at]) for at, pair in enumerate(zip(sources, held))]
    copies_out = [
        pltpu.make_async_copy(*pair, sem.at[count + at]) for at, pair in enumerate(zip(held, targets))
    ]
    for copy in copies_in:
        copy.start()
    for arrived, copy in zip(copies_in, copies_out):
        arrived.wait()
        copy.start()
    for copy in copies_out:
        copy.wait()


def per_device_kernel(
    tokens,
    segments,
    cotangent,
    project_weight,
    output_weight,
    up_weight,
    down_weight,
    norm_gains,
    bias_rows,
    hidden_bias,
):
    rows, width = tokens.shape
    length = segments.shape[1]
    local_hidden = up_weight.shape[1]
    local = output_weight.shape[0]
    piece = project_weight.shape[0]
    bf16, f32 = jnp.bfloat16, jnp.float32
    inputs = dict(
        tokens=tokens,
        triple_own=project_weight.transpose(1, 0, 2),
        output_own=output_weight,
        up_own=up_weight,
        down_own=down_weight,
        segments=segments,
        cotangent_from=cotangent,
        gains_from=norm_gains,
        bias_from=bias_rows,
        hidden_from=hidden_bias,
    )
    shapes = dict(
        project=(3, piece, local),
        output=(local, piece),
        up=(piece, local_hidden),
        down=(local_hidden, piece),
    )
    outputs = dict(layer_out=((rows, width), bf16), grad_tokens=((rows, width), f32))
    outputs |= {name + "_out": (shape, f32) for name, shape in shapes.items()}
    outputs |= dict(
        gains_out=((2, width), f32),
        bias_out=((6, width), f32),
        hidden_out=(hidden_bias.shape, f32),
    )
    scratch = dict(
        segment_row=((1, length), jnp.int32),
        segment_row_f32=((1, length), f32),
        segment_column=((length, 1), f32),
        cotangent=((rows, width), bf16),
        norm_gains=(norm_gains.shape, f32),
        bias_rows=(bias_rows.shape, f32),
        hidden_bias=((local_hidden,), f32),
        layer_low=((rows, width), bf16),
        bias_sum=(bias_rows.shape, f32),
        gains_sum=(norm_gains.shape, f32),
        hidden_sum=(hidden_bias.shape, f32),
        partial=((rows, width), f32),
        gathered=((length, width), bf16),
        triple=((3, width, local), bf16),
        output=((local, width), bf16),
        up=((width, local_hidden), bf16),
        down=((local_hidden, width), bf16),
        queries=((length, local), bf16),
        key_rows=((length, local), bf16),
        value_rows=((length, local), bf16),
        key_turned=((local, length), bf16),
        value_turned=((local, length), bf16),
        mixed=((length, local), bf16),
        log_totals=((local // HEAD, length), f32),
        normed_one=((rows, width), f32),
        inverse_one=((rows, 1), f32),
        first_all=((length, width), bf16),
        hidden=((length, local_hidden), bf16),
        slope=((length, local_hidden), f32),
        second_all=((length, width), bf16),
        upper_low=((length, local_hidden), bf16),
        upper=((rows, local_hidden), f32),
        columns=((length, 2 * piece), f32),
        kept=((rows, width), f32),
        held=((rows // HALVES, width), f32),
        grad_rows=((rows, width), f32),
        sums=((8, width), f32),
        branch_all=((length, width), bf16),
        mixed_low=((rows, local), bf16),
        projected_low=((length, 3 * local), bf16),
        grad_project=((3, width, local), bf16),
        grad_output=((local, width), bf16),
        grad_up=((width, local_hidden), bf16),
        grad_down=((local_hidden, width), bf16),
        held_totals=((6, 16, width), f32),
        arrived_totals=((5, 16, width), f32),
    )
    for name, shape in shapes.items():
        scratch[name + "_sum"] = (shape, f32)
        moved = (local_hidden // 2, piece) if name == "down" else shape
        scratch[name + "_side"] = ((LINES,) + moved, bf16)
        scratch[name + "_line"] = ((LINES - 1,) + moved, bf16)
    scratch |= dict(
        rest_line=((LINES - 1, local_hidden // 2, 2 * piece), bf16),
        rest_out=((local_hidden // 2, piece), bf16),
        rest_in=((local_hidden // 2, piece), bf16),
    )
    for name in ("near_out_", "near_in_"):
        scratch[name + "a"] = ((2 * HALVES, rows // HALVES, width), bf16)
        scratch[name + "b"] = ((2 * LINES, rows, 2 * piece), bf16)
    for name in ("across_out_", "across_in_"):
        scratch[name + "a"] = ((rows, width), bf16)
        scratch[name + "b"] = ((LINES, rows, 2 * piece), bf16)
    semaphores = dict(
        line_send=(5, 3 * LINES),
        line_recv=(5, 2 * LINES),
        line_local=(5,),
        part_send=(5, 2 * LINES),
        part_recv=(5, 2 * LINES),
        row_send=(4, 1 + 2 * HALVES),
        row_recv=(4, 1 + 2 * HALVES),
        sum_send=(4, 3 * LINES),
        sum_recv=(4, 3 * LINES),
        total_send=(5,),
        total_recv=(5,),
        load_sem=(6,),
        save_sem=(9,),
    )
    names = [*inputs, *outputs, *scratch, *semaphores]
    hbm = pl.BlockSpec(memory_space=pltpu.HBM)
    results = pl.pallas_call(
        functools.partial(layer_kernel, names, rows),
        out_shape=[jax.ShapeDtypeStruct(*leaf) for leaf in outputs.values()],
        in_specs=[hbm] * len(inputs),
        out_specs=[hbm] * len(outputs),
        scratch_shapes=[pltpu.VMEM(*leaf) for leaf in scratch.values()]
        + [pltpu.SemaphoreType.DMA(shape) for shape in semaphores.values()],
        compiler_params=pltpu.CompilerParams(
            collective_id=0, has_side_effects=True, vmem_limit_bytes=VMEM_BYTES
        ),
        name="layer",
    )(*inputs.values())
    results = pl.pallas_call(
        functools.partial(copy_kernel, len(outputs)),
        out_shape=[jax.ShapeDtypeStruct(*leaf) for leaf in outputs.values()],
        in_specs=[hbm] * len(outputs),
        out_specs=[hbm] * len(outputs),
        scratch_shapes=[pltpu.VMEM(*leaf) for leaf in outputs.values()]
        + [pltpu.SemaphoreType.DMA((2 * len(outputs),))],
        name="copy",
    )(*results)
    result = dict(zip(outputs, results))
    return (
        result["layer_out"],
        result["grad_tokens"],
        result["project_out"].transpose(1, 0, 2),
        result["output_out"],
        result["up_out"],
        result["down_out"],
        result["gains_out"],
        result["bias_out"],
        result["hidden_out"],
    )


def gelu_exact(values):
    return jax.nn.gelu(values, approximate=False)


def layer_norm(token_rows, gain, shift):
    average = jnp.mean(token_rows, axis=-1, keepdims=True)
    centred = token_rows - average
    variance = jnp.mean(centred * centred, axis=-1, keepdims=True)
    inverse = lax.rsqrt(variance + EPSILON)
    normed = centred * inverse
    return (normed * gain + shift, (normed, inverse))


def norm_back_saved(grad_rows, saved, gain):
    normed, inverse = saved
    grad_gain = jnp.sum(grad_rows * normed, axis=0)
    grad_shift = jnp.sum(grad_rows, axis=0)
    grad_normed = grad_rows * gain
    grad_input = inverse * (
        grad_normed
        - jnp.mean(grad_normed, axis=-1, keepdims=True)
        - normed * jnp.mean(grad_normed * normed, axis=-1, keepdims=True)
    )
    return (grad_input, grad_gain, grad_shift)


def split_heads(token_rows):
    return token_rows.reshape(token_rows.shape[0], token_rows.shape[1] // HEAD, HEAD)


def scatter_sum(partial_sum, axis_name, dimension):
    return lax.psum_scatter(
        partial_sum.astype(jnp.bfloat16), axis_name, scatter_dimension=dimension, tiled=True
    ).astype(jnp.float32)


def place_columns(partial_sum, column_block, total_width):
    full_rows = jnp.zeros(partial_sum.shape[:-1] + (total_width,), jnp.float32)
    return lax.dynamic_update_slice_in_dim(
        full_rows, partial_sum, column_block * partial_sum.shape[-1], partial_sum.ndim - 1
    )


def per_device(
    tokens,
    segments,
    cotangent,
    project_weight,
    output_weight,
    up_weight,
    down_weight,
    norm_gains,
    bias_rows,
    hidden_bias,
):
    tensor_rank = lax.axis_index("tensor")
    local_rows, model_width = tokens.shape
    seq_count, seq_length = segments.shape
    group_rows = seq_count * seq_length
    local_width = project_weight.shape[2]
    score_scale = HEAD ** (-0.5)
    block_rows = min(512, seq_length)
    per_sequence = seq_length // block_rows
    count_blocks = group_rows // block_rows
    block_ids = jnp.arange(count_blocks, dtype=jnp.int32)
    triple_full, output_full, upward_full, downward_full = (
        lax.all_gather(project_weight, "dp", axis=0, tiled=True),
        lax.all_gather(output_weight, "dp", axis=1, tiled=True),
        lax.all_gather(up_weight, "dp", axis=0, tiled=True),
        lax.all_gather(down_weight, "dp", axis=1, tiled=True),
    )
    local_hidden = upward_full.shape[1]
    triple_matrix = triple_full.reshape(model_width, 3 * local_width)
    gathered = lax.all_gather(tokens, "tensor", axis=0, tiled=True)
    head_bias = lax.dynamic_slice_in_dim(bias_rows, tensor_rank * local_width, local_width, 1)
    projected = jnp.dot(gathered, triple_matrix, preferred_element_type=jnp.float32).reshape(
        group_rows, 3, local_width
    )
    queries = (projected[:, 0] + head_bias[0]).astype(jnp.bfloat16)
    key_rows = projected[:, 1].astype(jnp.bfloat16)
    value_rows = (projected[:, 2] + head_bias[1]).astype(jnp.bfloat16)

    def block_parts(block_index):
        sequence = block_index // per_sequence
        row_start = block_index * block_rows
        seq_start = sequence * seq_length
        query_block = split_heads(lax.dynamic_slice_in_dim(queries, row_start, block_rows, 0))
        key_block = split_heads(key_rows)
        value_block = split_heads(value_rows)
        seq_ids = lax.dynamic_index_in_dim(segments, sequence, 0, keepdims=False)
        query_ids = lax.dynamic_slice_in_dim(seq_ids, row_start - seq_start, block_rows, 0)
        products = (
            jnp.einsum("qhd,khd->hqk", query_block, key_block, preferred_element_type=jnp.float32)
            * score_scale
        )
        scores = jnp.where((query_ids[:, None] == seq_ids[None, :])[None], products, NEGATIVE)
        return (row_start, query_block, key_block, value_block, scores)

    def forward_block(block_index):
        row_start, query_block, key_block, value_block, scores = block_parts(block_index)
        row_max = jnp.max(scores, axis=-1, keepdims=True)
        exponent = jnp.exp(scores - row_max)
        row_sum = jnp.sum(exponent, axis=-1, keepdims=True)
        weights_low = (exponent / row_sum).astype(jnp.bfloat16)
        mixed_block = jnp.einsum(
            "hqk,khd->qhd", weights_low, value_block, preferred_element_type=jnp.float32
        )
        log_total = row_max[:, :, 0] + jnp.log(row_sum[:, :, 0])
        return (mixed_block.reshape(block_rows, local_width).astype(jnp.bfloat16), log_total)

    mixed_blocks, log_totals = lax.map(forward_block, block_ids)
    mixed_rows = mixed_blocks.reshape(group_rows, local_width)
    branch_out = (
        scatter_sum(
            jnp.dot(mixed_rows, output_full, preferred_element_type=jnp.float32), "tensor", 0
        )
        + bias_rows[2]
    )
    first_out, first_saved = layer_norm(
        tokens.astype(jnp.float32) + branch_out, norm_gains[0], bias_rows[3]
    )
    first_gathered = lax.all_gather(first_out.astype(jnp.bfloat16), "tensor", axis=0, tiled=True)
    local_bias = lax.dynamic_slice_in_dim(hidden_bias, tensor_rank * local_hidden, local_hidden, 0)
    upper_rows = (
        jnp.dot(first_gathered, upward_full, preferred_element_type=jnp.float32) + local_bias
    )
    hidden_full, gelu_back = jax.vjp(gelu_exact, upper_rows)
    hidden_rows = hidden_full.astype(jnp.bfloat16)
    second_out = (
        scatter_sum(
            jnp.dot(hidden_rows, downward_full, preferred_element_type=jnp.float32), "tensor", 0
        )
        + bias_rows[4]
    )
    layer_out, second_saved = layer_norm(first_out + second_out, norm_gains[1], bias_rows[5])
    reloaded = (
        lax.all_gather(project_weight, "dp", axis=0, tiled=True),
        lax.all_gather(output_weight, "dp", axis=1, tiled=True),
        lax.all_gather(up_weight, "dp", axis=0, tiled=True),
        lax.all_gather(down_weight, "dp", axis=1, tiled=True),
    )
    back_triple = reloaded[0].reshape(model_width, 3 * local_width)
    back_output, back_upward, back_downward = (reloaded[1], reloaded[2], reloaded[3])
    grad_layer = cotangent.astype(jnp.float32)
    grad_second_in, grad_gain_two, grad_shift_two = norm_back_saved(
        grad_layer, second_saved, norm_gains[1]
    )
    grad_second = grad_second_in.astype(jnp.bfloat16)
    grad_second_all = lax.all_gather(grad_second, "tensor", axis=0, tiled=True)
    grad_down_part = jnp.einsum(
        "tf,td->fd", hidden_rows, grad_second_all, preferred_element_type=jnp.float32
    )
    grad_hidden = jnp.einsum(
        "td,fd->tf", grad_second_all, back_downward, preferred_element_type=jnp.float32
    )
    grad_upper = gelu_back(grad_hidden)[0].astype(jnp.bfloat16)
    grad_up_part = jnp.einsum(
        "td,tf->df", first_gathered, grad_upper, preferred_element_type=jnp.float32
    )
    grad_first = (
        scatter_sum(
            jnp.einsum("tf,df->td", grad_upper, back_upward, preferred_element_type=jnp.float32),
            "tensor",
            0,
        )
        + grad_second_in
    )
    grad_first_in, grad_gain_one, grad_shift_one = norm_back_saved(grad_first, first_saved, norm_gains[0])
    grad_branch = grad_first_in.astype(jnp.bfloat16)
    grad_branch_all = lax.all_gather(grad_branch, "tensor", axis=0, tiled=True)
    grad_output_part = jnp.einsum(
        "tc,td->cd", mixed_rows, grad_branch_all, preferred_element_type=jnp.float32
    )
    grad_mixed = jnp.einsum(
        "td,cd->tc", grad_branch_all, back_output, preferred_element_type=jnp.float32
    ).astype(jnp.bfloat16)

    def backward_block(block_index):
        row_start, query_block, key_block, value_block, scores = block_parts(block_index)
        weights_full = jnp.exp(scores - log_totals[block_index][:, :, None])
        grad_mixed_block = split_heads(
            lax.dynamic_slice_in_dim(grad_mixed, row_start, block_rows, 0)
        )
        grad_weights = jnp.einsum(
            "qhd,khd->hqk", grad_mixed_block, value_block, preferred_element_type=jnp.float32
        )
        row_dot = jnp.sum(weights_full * grad_weights, axis=-1, keepdims=True)
        grad_scores = (weights_full * (grad_weights - row_dot)).astype(jnp.bfloat16)
        grad_query = (
            jnp.einsum("hqk,khd->qhd", grad_scores, key_block, preferred_element_type=jnp.float32)
            * score_scale
        )
        grad_key = (
            jnp.einsum("hqk,qhd->khd", grad_scores, query_block, preferred_element_type=jnp.float32)
            * score_scale
        )
        grad_value = jnp.einsum(
            "hqk,qhd->khd",
            weights_full.astype(jnp.bfloat16),
            grad_mixed_block,
            preferred_element_type=jnp.float32,
        )
        return (
            grad_query.reshape(block_rows, local_width),
            grad_key.reshape(seq_length, local_width),
            grad_value.reshape(seq_length, local_width),
        )

    query_blocks, key_blocks, value_blocks = lax.map(backward_block, block_ids)
    grad_queries = query_blocks.reshape(group_rows, local_width)
    grad_keys = (
        key_blocks.reshape(seq_count, per_sequence, seq_length, local_width)
        .sum(axis=1)
        .reshape(group_rows, local_width)
    )
    grad_values = (
        value_blocks.reshape(seq_count, per_sequence, seq_length, local_width)
        .sum(axis=1)
        .reshape(group_rows, local_width)
    )
    grad_projected = jnp.stack((grad_queries, grad_keys, grad_values), axis=1).astype(jnp.bfloat16)
    grad_project_part = jnp.einsum(
        "te,tsc->esc", gathered, grad_projected, preferred_element_type=jnp.float32
    )
    grad_matrix = grad_projected.reshape(group_rows, 3 * local_width)
    grad_tokens = (
        lax.psum_scatter(
            jnp.einsum(
                "tc,ec->te", grad_matrix, back_triple, preferred_element_type=jnp.float32
            ).astype(jnp.bfloat16),
            "tensor",
            scatter_dimension=0,
            tiled=True,
        ).astype(jnp.float32)
        + grad_first_in
    )
    grad_project, grad_output, grad_up, grad_down = (
        scatter_sum(grad_project_part, "dp", 0),
        scatter_sum(grad_output_part, "dp", 1),
        scatter_sum(grad_up_part, "dp", 0),
        scatter_sum(grad_down_part, "dp", 1),
    )
    head_terms = place_columns(
        jnp.stack(
            (
                jnp.sum(grad_projected[:, 0], axis=0, dtype=jnp.float32),
                jnp.sum(grad_projected[:, 2], axis=0, dtype=jnp.float32),
            )
        ),
        tensor_rank,
        model_width,
    )
    shared_terms = jnp.stack(
        (
            jnp.sum(grad_branch, axis=0, dtype=jnp.float32),
            grad_shift_one,
            jnp.sum(grad_second, axis=0, dtype=jnp.float32),
            grad_shift_two,
        )
    )
    bias_terms = jnp.concatenate((head_terms, shared_terms), axis=0)
    gain_terms = jnp.stack((grad_gain_one, grad_gain_two))
    hidden_terms = place_columns(
        jnp.sum(grad_upper, axis=0, dtype=jnp.float32), tensor_rank, hidden_bias.shape[0]
    )
    grad_gains, grad_bias_rows, grad_hidden_bias = lax.psum(
        (gain_terms, bias_terms, hidden_terms), ("dp", "tensor")
    )
    return (
        layer_out.astype(jnp.bfloat16),
        grad_tokens,
        grad_project,
        grad_output,
        grad_up,
        grad_down,
        grad_gains,
        grad_bias_rows,
        grad_hidden_bias,
    )


def solution(mesh):
    fits = mesh.shape["dp"] == 2 * LINES and mesh.shape["tensor"] == 4
    placed = (
        P(("dp", "tensor"), None),
        P("dp", None),
        P(("dp", "tensor"), None),
        P("dp", None, "tensor"),
        P("tensor", "dp"),
        P("dp", "tensor"),
        P("tensor", "dp"),
        P(),
        P(),
        P(),
    )
    return jax.shard_map(
        per_device_kernel if fits else per_device,
        mesh=mesh,
        in_specs=placed,
        out_specs=(
            P(("dp", "tensor"), None),
            P(("dp", "tensor"), None),
            P("dp", None, "tensor"),
            P("tensor", "dp"),
            P("dp", "tensor"),
            P("tensor", "dp"),
            P(),
            P(),
            P(),
        ),
        check_vma=False,
    )
```

```python
import functools
import types

import jax
import jax.numpy as jnp
from jax import lax
from jax.experimental import pallas as pl
from jax.experimental.pallas import tpu as pltpu
from jax.sharding import PartitionSpec as P

HEAD = 64
EPSILON = 1e-05
NEGATIVE = -1e30
MESH = pl.DeviceIdType.MESH
LINES = 4
CORE, ACROSS, FAR = 1, 2, 3
HALVES = 2
CHUNK = 16
NORM = 64
ORDER = (3, 2, 1, 0)
VMEM_BYTES = 60 << 20


def remote(src, dst, send_sem, recv_sem, target):
    return pltpu.make_async_remote_copy(
        src_ref=src,
        dst_ref=dst,
        send_sem=send_sem,
        recv_sem=recv_sem,
        device_id=target,
        device_id_type=MESH,
    )


def position():
    return lax.axis_index("dp"), lax.axis_index("tensor")


def greet():
    dp, tensor = position()
    barrier = pltpu.get_barrier_semaphore()
    others = [(dp ^ step, tensor) for step in (1, 2, 4, 6)]
    others += [(dp, tensor ^ step) for step in (CORE, ACROSS)]
    for target in others:
        pl.semaphore_signal(barrier, inc=1, device_id=target, device_id_type=MESH)
    pl.semaphore_wait(barrier, len(others))


def row_piece(ref, index, size):
    return ref.at[pl.ds(pl.multiple_of(index * size, size), size), :]


def column_piece(ref, index, size):
    return ref.at[:, pl.ds(pl.multiple_of(index * size, size), size)]


class LineGather:
    def __init__(self, own, full, piece, send_sem, recv_sem, local_sem):
        self.own, self.full, self.piece = own, full, piece
        self.send_sem, self.recv_sem, self.local_sem = send_sem, recv_sem, local_sem
        self.dp, self.tensor = position()
        self.line, self.side = self.dp // 2, self.dp % 2
        self.targets = (
            (self.dp + 2, self.tensor),
            (self.dp - 2, self.tensor),
            (self.dp ^ 1, self.tensor),
        )

    def copy(self, index, way, src=None):
        view = self.piece(self.full, index)
        return remote(
            view if src is None else src,
            view,
            self.send_sem.at[way * LINES + index // 2],
            self.recv_sem.at[index],
            self.targets[way],
        )

    def local(self):
        return pltpu.make_async_copy(self.own, self.piece(self.full, self.dp), self.local_sem)

    def start_along(self):
        self.local().start()

        @pl.when(self.line < LINES - 1)
        def _():
            self.copy(self.dp, 0, self.own).start()

        @pl.when(self.line > 0)
        def _():
            self.copy(self.dp, 1, self.own).start()

    def start_across(self):
        self.copy(self.dp, 2, self.own).start()

    def step_along(self, distance):
        @pl.when(self.line >= distance)
        def _():
            self.copy(self.dp - 2 * distance, 0).wait_recv()

            @pl.when(self.line < LINES - 1)
            def _():
                self.copy(self.dp - 2 * distance, 0).start()

        @pl.when(self.line + distance < LINES)
        def _():
            self.copy(self.dp + 2 * distance, 1).wait_recv()

            @pl.when(self.line > 0)
            def _():
                self.copy(self.dp + 2 * distance, 1).start()

    def step_across(self, distance):
        @pl.when(self.line >= distance)
        def _():
            self.copy(self.dp - 2 * distance, 2).start()

        @pl.when(self.line + distance < LINES)
        def _():
            self.copy(self.dp + 2 * distance, 2).start()

    def step(self, distance):
        self.step_along(distance)
        self.step_across(distance)

    def arrive_block(self, at):
        self.copy(self.dp ^ (2 * at) ^ 1, 2).wait_recv()

    def arrive(self):
        self.local().wait()
        for line in range(LINES):
            self.copy(2 * line + 1 - self.side, 2).wait_recv()

    def finish(self):
        for line in range(LINES):
            index = 2 * line + self.side
            self.copy(index, 2).wait_send()

            @pl.when((self.line < LINES - 1) & (line <= self.line))
            def _():
                self.copy(index, 0).wait_send()

            @pl.when((self.line > 0) & (line >= self.line))
            def _():
                self.copy(index, 1).wait_send()


class RowGather:
    def __init__(self, full, rows, send_sem, recv_sem):
        self.full, self.rows = full, rows
        self.send_sem, self.recv_sem = send_sem, recv_sem
        self.dp, self.tensor = position()

    def view(self, rank, half=None):
        if half is None:
            return row_piece(self.full, rank, self.rows)
        return row_piece(self.full, rank * HALVES + half, self.rows // HALVES)

    def near(self, rank):
        view = self.view(rank)
        target = (self.dp, self.tensor ^ CORE)
        return remote(view, view, self.send_sem.at[0], self.recv_sem.at[0], target)

    def across(self, rank, half):
        view, slot = self.view(rank, half), 1 + half
        target = (self.dp, self.tensor ^ ACROSS)
        return remote(view, view, self.send_sem.at[slot], self.recv_sem.at[slot], target)

    def far(self, rank, half):
        view, slot = self.view(rank, half), 1 + HALVES + half
        target = (self.dp, self.tensor ^ CORE)
        return remote(view, view, self.send_sem.at[slot], self.recv_sem.at[slot], target)

    def start_half(self, half):
        self.across(self.tensor, half).start()

    def start_near(self):
        self.near(self.tensor).start()

    def start(self):
        for half in range(HALVES):
            self.start_half(half)
        self.start_near()

    def wait_near(self):
        self.near(self.tensor ^ CORE).wait_recv()

    def wait_across(self, half):
        self.across(self.tensor ^ ACROSS, half).wait_recv()
        self.far(self.tensor ^ ACROSS, half).start()

    def wait_far(self, half):
        self.far(self.tensor ^ FAR, half).wait_recv()

    def finish(self):
        self.near(self.tensor).wait_send()
        for half in range(HALVES):
            self.across(self.tensor, half).wait_send()
            self.far(self.tensor ^ ACROSS, half).wait_send()


class RowScatter:
    def __init__(self, near_out, near_in, across_out, across_in, send_sem, recv_sem):
        self.near_out, self.near_in = near_out, near_in
        self.across_out, self.across_in = across_out, across_in
        self.send_sem, self.recv_sem = send_sem, recv_sem
        self.dp, self.tensor = position()

    def near(self, slot):
        return remote(
            self.near_out.at[slot],
            self.near_in.at[slot],
            self.send_sem.at[slot],
            self.recv_sem.at[slot],
            (self.dp, self.tensor ^ CORE),
        )

    def across(self, half):
        rows = self.across_in.shape[0] // HALVES
        return remote(
            row_piece(self.across_out, half, rows),
            row_piece(self.across_in, half, rows),
            self.send_sem.at[2 * HALVES + half],
            self.recv_sem.at[2 * HALVES + half],
            (self.dp, self.tensor ^ ACROSS),
        )

    def give_far(self, half, partial):
        self.near_out[half] = partial.astype(jnp.bfloat16)
        self.near(half).start()

    def give_across(self, half, partial):
        self.near(half).wait_recv()
        rows = partial.shape[0]
        total = partial + self.near_in[half].astype(jnp.float32)
        row_piece(self.across_out, half, rows)[...] = total.astype(jnp.bfloat16)
        self.across(half).start()

    def give_near(self, half, partial):
        self.near_out[HALVES + half] = partial.astype(jnp.bfloat16)
        self.near(HALVES + half).start()

    def take(self, half, partial):
        self.near(HALVES + half).wait_recv()
        rows = partial.shape[0]
        total = partial + self.near_in[HALVES + half].astype(jnp.float32)
        self.across(half).wait_recv()
        return total + row_piece(self.across_in, half, rows)[...].astype(jnp.float32)

    def finish(self):
        for slot in range(2 * HALVES):
            self.near(slot).wait_send()
        for half in range(HALVES):
            self.across(half).wait_send()


def dot(left, right):
    return jnp.dot(left, right, preferred_element_type=jnp.float32)


def dot_nt(left, right):
    return lax.dot_general(left, right, (((1,), (1,)), ((), ())), preferred_element_type=jnp.float32)


def dot_tn(left, right):
    return lax.dot_general(left, right, (((0,), (0,)), ((), ())), preferred_element_type=jnp.float32)


def normalize(rows):
    centred = rows - jnp.mean(rows, axis=-1, keepdims=True)
    inverse = lax.rsqrt(jnp.mean(centred * centred, axis=-1, keepdims=True) + EPSILON)
    return centred * inverse, inverse


def norm_back(grad, normed, inverse):
    average = jnp.mean(grad, axis=-1, keepdims=True)
    along = jnp.mean(grad * normed, axis=-1, keepdims=True)
    return inverse * (grad - average - normed * along)


class LineFirstScatter:
    def __init__(self, partial, piece, line_in, across_out, across_in, send_sem, recv_sem):
        self.partial, self.piece, self.line_in = partial, piece, line_in
        self.across_out, self.across_in = across_out, across_in
        self.send_sem, self.recv_sem = send_sem, recv_sem
        self.dp, self.tensor = position()

    def view(self, step):
        return self.piece(self.partial, (self.dp // 2) ^ step)

    def along(self, step):
        return remote(
            self.view(step),
            self.line_in.at[step // 2 if step != 2 else 2],
            self.send_sem.at[step],
            self.recv_sem.at[step],
            (self.dp ^ (2 if step != 2 else 4), self.tensor),
        )

    def across(self):
        return remote(
            self.across_out,
            self.across_in,
            self.send_sem.at[0],
            self.recv_sem.at[0],
            (self.dp ^ 1, self.tensor),
        )

    def start(self):
        self.along(3).start()

    def relay(self):
        self.along(3).wait_recv()
        total = self.view(2)[...].astype(jnp.float32) + self.line_in[1].astype(jnp.float32)
        self.view(2)[...] = total.astype(jnp.bfloat16)
        self.along(2).start()
        self.along(1).start()

    def turn(self, result):
        total = self.view(0)[...].astype(jnp.float32)
        for step, slot in ((1, 0), (2, 2)):
            self.along(step).wait_recv()
            total = total + self.line_in[slot].astype(jnp.float32)
        width = result.shape[1]
        first, second = total[:, :width], total[:, width:]
        even = self.dp % 2 == 0
        result[...] = jnp.where(even, first, second)
        self.across_out[...] = jnp.where(even, second, first).astype(jnp.bfloat16)
        self.across().start()

    def finish(self, result):
        self.across().wait_recv()
        result[...] += self.across_in[...].astype(jnp.float32)
        self.across().wait_send()
        for step in range(1, LINES):
            self.along(step).wait_send()


class DirectGather:
    def __init__(self, own, full, piece, send_sem, recv_sem, local_sem):
        self.own, self.full, self.piece = own, full, piece
        self.send_sem, self.recv_sem, self.local_sem = send_sem, recv_sem, local_sem
        self.dp, self.tensor = position()

    def along(self, step):
        there = self.dp ^ (2 * step)
        return remote(
            self.own,
            self.piece(self.full, self.dp),
            self.send_sem.at[step],
            self.recv_sem.at[step],
            (there, self.tensor),
        )

    def across(self, step, source=None):
        view = self.piece(self.full, self.dp ^ (2 * step))
        return remote(
            view if source is None else source,
            view,
            self.send_sem.at[LINES + step],
            self.recv_sem.at[LINES + step],
            (self.dp ^ 1, self.tensor),
        )

    def local(self):
        return pltpu.make_async_copy(self.own, self.piece(self.full, self.dp), self.local_sem)

    def start_along(self):
        self.local().start()
        for step in range(1, LINES):
            self.along(step).start()

    def start_across(self):
        self.across(0, self.own).start()

    def step(self, step):
        self.along(step).wait_recv()
        self.across(step).start()

    def arrive(self, step):
        self.across(step).wait_recv()

    def finish(self):
        for step in range(LINES):
            self.across(step).wait_send()
        for step in range(1, LINES):
            self.along(step).wait_send()


class ColumnScatter:
    def __init__(self, near_out, near_in, across_out, across_in, send_sem, recv_sem):
        self.near_out, self.near_in = near_out, near_in
        self.across_out, self.across_in = across_out, across_in
        self.send_sem, self.recv_sem = send_sem, recv_sem
        self.dp, self.tensor = position()

    def near(self, slot):
        return remote(
            self.near_out.at[slot],
            self.near_in.at[slot],
            self.send_sem.at[slot],
            self.recv_sem.at[slot],
            (self.dp, self.tensor ^ CORE),
        )

    def across(self, at):
        return remote(
            self.across_out.at[at],
            self.across_in.at[at],
            self.send_sem.at[2 * LINES + at],
            self.recv_sem.at[2 * LINES + at],
            (self.dp, self.tensor ^ ACROSS),
        )

    def give_far(self, at, partial):
        self.near_out[at] = partial.astype(jnp.bfloat16)
        self.near(at).start()

    def give_near(self, at, partial):
        self.near_out[LINES + at] = partial.astype(jnp.bfloat16)
        self.near(LINES + at).start()

    def give_across(self, at, partial):
        self.near(at).wait_recv()
        total = partial + self.near_in[at].astype(jnp.float32)
        self.across_out[at] = total.astype(jnp.bfloat16)
        self.across(at).start()

    def take(self, at, partial):
        self.near(LINES + at).wait_recv()
        total = partial + self.near_in[LINES + at].astype(jnp.float32)
        self.across(at).wait_recv()
        return total + self.across_in[at].astype(jnp.float32)

    def finish(self):
        for slot in range(2 * LINES):
            self.near(slot).wait_send()
        for at in range(LINES):
            self.across(at).wait_send()


class LineScatter:
    def __init__(self, partial, piece, side_in, line_in, send_sem, recv_sem):
        self.partial, self.piece, self.side_in, self.line_in = partial, piece, side_in, line_in
        self.send_sem, self.recv_sem = send_sem, recv_sem
        self.dp, self.tensor = position()

    def view(self, step):
        return self.piece(self.partial, self.dp ^ (2 * step))

    def across(self, step):
        return remote(
            self.piece(self.partial, self.dp ^ (2 * step) ^ 1),
            self.side_in.at[step],
            self.send_sem.at[step],
            self.recv_sem.at[step],
            (self.dp ^ 1, self.tensor),
        )

    def along(self, step):
        return remote(
            self.view(step),
            self.line_in.at[step // 2 if step != 2 else 2],
            self.send_sem.at[LINES + step],
            self.recv_sem.at[LINES + step],
            (self.dp ^ (2 if step != 2 else 4), self.tensor),
        )

    def start(self, order=ORDER):
        for step in order:
            self.across(step).start()

    def total(self, step):
        self.across(step).wait_recv()
        return self.view(step)[...].astype(jnp.float32) + self.side_in[step].astype(jnp.float32)

    def relay(self, step):
        total = self.total(step)
        if step == 2:
            self.along(3).wait_recv()
            total = total + self.line_in[1].astype(jnp.float32)
        self.view(step)[...] = total.astype(jnp.bfloat16)
        self.along(step).start()

    def finish(self, result):
        total = self.total(0)
        self.along(1).wait_recv()
        total = total + self.line_in[0].astype(jnp.float32)
        self.along(2).wait_recv()
        result[...] = total + self.line_in[2].astype(jnp.float32)
        for step in range(LINES):
            self.across(step).wait_send()
        for step in range(1, LINES):
            self.along(step).wait_send()


class Total:
    def __init__(self, held, arrived, send_sem, recv_sem):
        self.held, self.arrived, self.send_sem, self.recv_sem = held, arrived, send_sem, recv_sem
        dp, tensor = position()
        self.targets = (
            (dp ^ 1, tensor),
            (dp ^ 2, tensor),
            (dp ^ 4, tensor),
            (dp, tensor ^ ACROSS),
            (dp, tensor ^ CORE),
        )

    def copy(self, step):
        return remote(
            self.held.at[step],
            self.arrived.at[step],
            self.send_sem.at[step],
            self.recv_sem.at[step],
            self.targets[step],
        )

    def start(self):
        self.copy(0).start()

    def step(self, step):
        self.copy(step).wait_recv()
        self.held[step + 1] = self.held[step] + self.arrived[step]
        if step + 1 < len(self.targets):
            self.copy(step + 1).start()

    def finish(self):
        for step in range(len(self.targets)):
            self.copy(step).wait_send()


def layer_kernel(names, rows, *refs):
    r = types.SimpleNamespace(**dict(zip(names, refs)))
    dp, tensor = position()
    bf16, f32 = jnp.bfloat16, jnp.float32
    half_rows = rows // HALVES
    local = r.queries.shape[1]
    piece = r.triple_own.shape[1]
    pairs = local // (2 * HEAD)
    hidden = r.hidden.shape[1]
    near, across, far = tensor ^ CORE, tensor ^ ACROSS, tensor ^ FAR

    def of_rows(ref, index):
        return row_piece(ref, index, piece)

    def of_columns(ref, index):
        return column_piece(ref, index, piece)

    def of_stack(ref, index):
        return ref.at[:, pl.ds(pl.multiple_of(index * piece, piece), piece), :]

    def of_half_stack(half):
        size = piece // HALVES

        def view(ref, index):
            return ref.at[:, pl.ds(pl.multiple_of(index * piece + half * size, size), size), :]

        return view, r.triple_own.at[:, half * size : (half + 1) * size, :]

    def block(rank, size=rows):
        return pl.ds(pl.multiple_of(rank * size, size), size)

    def split(partial):
        return [partial[half * half_rows : (half + 1) * half_rows] for half in range(HALVES)]

    def part_of(half):
        return slice(half * half_rows, (half + 1) * half_rows)

    (view_a, own_a), (view_b, own_b) = of_half_stack(0), of_half_stack(1)
    lines = [
        kind(own, full, view, r.line_send.at[at], r.line_recv.at[at], r.line_local.at[at])
        for at, (kind, own, full, view) in enumerate(
            (
                (LineGather, own_a, r.triple, view_a),
                (LineGather, own_b, r.triple, view_b),
                (DirectGather, r.output_own, r.output, of_columns),
                (LineGather, r.up_own, r.up, of_rows),
                (LineGather, r.down_own, r.down, of_columns),
            )
        )
    ]
    *triple_lines, output_line, up_line, down_line = lines
    sums = [
        LineScatter(partial, view, side, along, r.part_send.at[at], r.part_recv.at[at])
        for at, (partial, view, side, along) in enumerate(
            (
                (r.grad_project, of_stack, r.project_side, r.project_line),
                (r.grad_output, of_columns, r.output_side, r.output_line),
                (r.grad_up, of_rows, r.up_side, r.up_line),
                (r.grad_down.at[: hidden // 2, :], of_columns, r.down_side, r.down_line),
            )
        )
    ]
    project_sum, output_sum, up_sum, down_sum = sums

    def of_both(ref, index):
        return column_piece(ref, index, 2 * piece)

    rest_sum = LineFirstScatter(
        r.grad_down.at[hidden // 2 :, :],
        of_both,
        r.rest_line,
        r.rest_out,
        r.rest_in,
        r.part_send.at[4],
        r.part_recv.at[4],
    )
    down_top, down_rest = r.down_sum.at[: hidden // 2, :], r.down_sum.at[hidden // 2 :, :]
    gathers = [
        RowGather(full, rows, r.row_send.at[at], r.row_recv.at[at])
        for at, full in enumerate((r.gathered, r.first_all, r.second_all, r.branch_all))
    ]
    scatters = [
        kind(*buffers, r.sum_send.at[at], r.sum_recv.at[at])
        for at, (kind, buffers) in enumerate(
            (
                (RowScatter, (r.near_out_a, r.near_in_a, r.across_out_a, r.across_in_a)),
                (ColumnScatter, (r.near_out_b, r.near_in_b, r.across_out_b, r.across_in_b)),
            )
            * 2
        )
    ]
    total = Total(r.held_totals, r.arrived_totals, r.total_send, r.total_recv)

    def column_block(at):
        return block((dp // 2) ^ at, 2 * piece)

    def scatter_columns(scatter, at):
        scatter.give_far(at, r.columns[block(far), :])
        scatter.give_near(at, r.columns[block(near), :])
        scatter.give_across(at, r.columns[block(across), :])
        r.kept[:, column_block(at)] = r.columns[block(tensor), :]

    def chunks(size, start, body, step=CHUNK):
        @pl.loop(0, size // step)
        def _(chunk):
            offset = chunk * step
            body(
                pl.ds(pl.multiple_of(offset, step), step),
                pl.ds(pl.multiple_of(start + offset, step), step),
            )

    loads = [
        pltpu.make_async_copy(source, target, r.load_sem.at[at])
        for at, (source, target) in enumerate(
            (
                (r.tokens, gathers[0].view(tensor)),
                (r.segments, r.segment_row),
                (r.bias_from, r.bias_rows),
                (r.gains_from, r.norm_gains),
                (r.hidden_from.at[pl.ds(pl.multiple_of(tensor * hidden, hidden), hidden)], r.hidden_bias),
                (r.cotangent_from, r.cotangent),
            )
        )
    ]
    for load in loads:
        load.start()
    greet()
    for line in triple_lines:
        line.start_along()
        line.start_across()
    loads[0].wait()
    gathers[0].start()
    for line in triple_lines:
        line.step(1)
    loads[1].wait()
    numbers = r.segment_row[...].astype(f32)
    r.segment_column[...] = jnp.broadcast_to(numbers, (8, numbers.shape[1])).T[:, :1]
    r.segment_row_f32[...] = numbers
    for line in triple_lines:
        line.step(2)
    gathers[0].wait_near()
    for half in range(HALVES):
        gathers[0].wait_across(half)
    for line in triple_lines:
        line.step(3)
    output_line.start_along()
    output_line.start_across()
    up_line.start_along()
    up_line.start_across()
    down_line.start_along()
    for half in range(HALVES):
        gathers[0].wait_far(half)
    for line in triple_lines:
        line.arrive()
    for load in loads[2:]:
        load.wait()
    columns = pl.ds(pl.multiple_of(tensor * local, local), local)
    query_bias = r.bias_rows[0:1, columns]
    value_bias = r.bias_rows[1:2, columns]

    @pl.loop(0, 4)
    def _(index):
        here = block(index)
        left = r.gathered[here, :]
        query = (dot(left, r.triple[0]) + query_bias).astype(bf16)
        r.queries[here, :] = query * bf16(HEAD**-0.5)
        key = dot(left, r.triple[1])
        r.key_rows[here, :] = key.astype(bf16)
        r.key_turned[:, here] = key.T.astype(bf16)
        value = dot(left, r.triple[2]) + value_bias
        r.value_rows[here, :] = value.astype(bf16)
        r.value_turned[:, here] = value.T.astype(bf16)

    for step in range(1, LINES):
        output_line.step(step)

    def head_rows(head):
        return pl.ds(pl.multiple_of(head * HEAD, HEAD), HEAD)

    def attend(here, pair):
        lanes = block(pair, 2 * HEAD)
        query = r.queries[here, lanes]
        keys = r.key_rows[:, lanes]
        same = r.segment_column[...] == r.segment_row_f32[:, here]
        lane = lax.broadcasted_iota(jnp.int32, query.shape, 1)
        outs = []
        for side in range(2):
            scores = dot_nt(keys, jnp.where(lane // HEAD == side, query, bf16(0)))
            scores = jnp.where(same, scores, NEGATIVE)
            top = jnp.max(scores, axis=0, keepdims=True)
            exponent = jnp.exp(scores - top)
            mass = jnp.sum(exponent, axis=0, keepdims=True)
            weights = (exponent * (1.0 / mass)).astype(bf16)
            head = pair * 2 + side
            outs.append(dot(r.value_turned[head_rows(head), :], weights))
            r.log_totals[pl.ds(head, 1), here] = top + jnp.log(mass)
        r.mixed[here, lanes] = jnp.concatenate(outs, axis=0).T.astype(bf16)

    @pl.loop(0, 4 * pairs)
    def _(turn):
        rank, pair = tensor ^ (FAR - turn // pairs), turn % pairs
        here = block(rank)
        attend(here, pair)

        def give(rank, method):
            r.partial[...] = dot(r.mixed[block(rank), :], r.output[...])
            for half in range(HALVES):
                method(half, r.partial[part_of(half), :])

        def after(index):
            return pl.when(turn == index)

        @after(0)
        def _():
            up_line.step(1)

        @after(3)
        def _():
            output_line.local().wait()
            for step in range(LINES):
                output_line.arrive(step)
            give(far, scatters[0].give_far)
            give(across, scatters[0].give_across)

        @after(4)
        def _():
            up_line.step(2)
            down_line.step_along(1)

        @after(5)
        def _():
            give(near, scatters[0].give_near)

        @after(7)
        def _():
            up_line.step(3)
            down_line.start_across()
            down_line.step_across(1)

    r.partial[...] = dot(r.mixed[block(tensor), :], r.output[...])
    for half in range(HALVES):
        part = part_of(half)
        r.kept[part, :] = scatters[0].take(half, r.partial[part, :])

        def first_norm(_, here):
            own_rows = r.gathered[pl.ds(pl.multiple_of(tensor * rows + here.start, NORM), NORM), :]
            normed, inverse = normalize(own_rows.astype(f32) + r.kept[here, :] + r.bias_rows[2:3, :])
            r.normed_one[here, :] = normed
            r.inverse_one[here, :] = inverse
            first = normed * r.norm_gains[0:1, :] + r.bias_rows[3:4, :]
            into = pl.ds(pl.multiple_of(tensor * rows + here.start, NORM), NORM)
            r.first_all[into, :] = first.astype(bf16)

        chunks(half_rows, half * half_rows, first_norm, NORM)
        gathers[1].start_half(half)
    scatters[0].finish()

    gathers[1].start_near()
    r.sums[...] = jnp.zeros_like(r.sums)

    def extent(rank, half):
        size = rows if half is None else half_rows
        start = rank * rows + (0 if half is None else half * half_rows)
        return start, size, pl.ds(pl.multiple_of(start, size), size)

    def up_part(rank, half=None):
        start, size, here = extent(rank, half)
        r.upper[:size, :] = dot(r.first_all[here, :], r.up[...]) + r.hidden_bias[...].reshape(1, hidden)

        def body(part, into):
            value = r.upper[part, :]
            share = 0.5 + 0.5 * lax.erf(value * (0.5**0.5))
            r.hidden[into, :] = (value * share).astype(bf16)
            bell = jnp.exp(value * value * -0.5) * (2 * jnp.pi) ** -0.5
            r.slope[into, :] = share + value * bell

        chunks(size, start, body)

    def back_part(rank, half=None):
        start, size, here = extent(rank, half)
        r.upper[:size, :] = dot_nt(r.second_all[here, :], r.down[...])

        def body(part, into):
            low = (r.upper[part, :] * r.slope[into, :]).astype(bf16)
            r.upper_low[into, :] = low
            r.sums[6:7, :] += jnp.sum(low.astype(f32), axis=0, keepdims=True)

        chunks(size, start, body)
        r.partial[:size, :] = dot_nt(r.upper_low[here, :], r.up[...])

    down_line.step(2)
    up_line.arrive()

    @pl.loop(0, 2)
    def _(turn):
        @pl.when(turn == 1)
        def _():
            gathers[1].wait_near()
            down_line.step(3)

        up_part(tensor ^ turn)

    def other_chip(gather, body):
        @pl.loop(0, 2 * HALVES)
        def _(turn):
            half, side = turn // 2, turn % 2

            @pl.when(side == 0)
            def _():
                gather.wait_across(half)

            body(half, side)

    def up_other(half, side):
        @pl.when(side == 1)
        def _():
            gathers[1].wait_far(half)

        up_part(tensor ^ (ACROSS + side), half)

    other_chip(gathers[1], up_other)

    down_line.local().wait()

    @pl.loop(0, LINES)
    def _(at):
        down_line.arrive_block(at)
        r.columns[...] = dot(r.hidden[...], r.down[:, column_block(at)])
        scatter_columns(scatters[1], at)

    def add_to(row, value):
        r.sums[row : row + 1, :] += jnp.sum(value, axis=0, keepdims=True)

    def second_norm(_, here):
        first = r.normed_one[here, :] * r.norm_gains[0:1, :] + r.bias_rows[3:4, :]
        normed, inverse = normalize(first + r.kept[here, :] + r.bias_rows[4:5, :])
        shifted = normed * r.norm_gains[1:2, :] + r.bias_rows[5:6, :]
        r.layer_low[here, :] = shifted.astype(bf16)
        grad = r.cotangent[here, :].astype(f32)
        add_to(5, grad * normed)
        add_to(3, grad)
        grad = norm_back(grad * r.norm_gains[1:2, :], normed, inverse)
        r.grad_rows[here, :] = grad
        low = grad.astype(bf16)
        add_to(2, low.astype(f32))
        r.second_all[pl.ds(pl.multiple_of(tensor * rows + here.start, NORM), NORM), :] = low

    @pl.loop(0, LINES)
    def _(at):
        lanes = column_block(at)
        r.kept[:, lanes] = scatters[1].take(at, r.kept[:, lanes])

    for half in range(HALVES):
        chunks(half_rows, half * half_rows, second_norm, NORM)
        gathers[2].start_half(half)
    saves = []

    def save(source, target):
        saves.append(pltpu.make_async_copy(source, target, r.save_sem.at[len(saves)]))
        saves[-1].start()

    save(r.layer_low, r.layer_out)
    scatters[1].finish()

    gathers[2].start_near()

    @pl.loop(0, 2)
    def _(turn):
        @pl.when(turn == 1)
        def _():
            gathers[2].wait_near()

        back_part(tensor ^ turn)

        @pl.when(turn == 0)
        def _():
            r.kept[...] = r.partial[...]

        @pl.when(turn == 1)
        def _():
            for half in range(HALVES):
                scatters[2].give_near(half, r.partial[part_of(half), :])

    def weight_grad(left, right, result, chip=None, add=False):
        depth = slice(None) if chip is None else block(chip, 2 * rows)

        @pl.loop(0, left.shape[1] // rows)
        def _(index):
            lanes = block(index)
            product = dot_tn(left[depth, lanes], right[depth, :])
            if add:
                product += result[lanes, :].astype(f32)
            result[lanes, :] = product.astype(bf16)

    weight_grad(r.hidden, r.second_all, r.grad_down, tensor // 2)

    def back_other(half, side):
        @pl.when((side == 1) & (half < HALVES - 1))
        def _():
            gathers[2].wait_far(half)

        @pl.when((side == 0) & (half == HALVES - 1))
        def _():
            gathers[2].wait_far(half)
            weight_grad(r.hidden, r.second_all, r.grad_down, 1 - tensor // 2, True)
            rest_sum.start()
            down_sum.start()

        back_part(tensor ^ (ACROSS + side), half)

        @pl.when(side == 0)
        def _():
            r.held[...] = r.partial[:half_rows, :]

        @pl.when(side == 1)
        def _():
            scatters[2].give_far(half, r.partial[:half_rows, :])
            scatters[2].give_across(half, r.held[...])

    other_chip(gathers[2], back_other)

    weight_grad(r.first_all, r.upper_low, r.grad_up)
    up_sum.start()

    def first_back(_, here):
        grad = r.grad_rows[here, :] + r.kept[here, :]
        normed = r.normed_one[here, :]
        add_to(4, grad * normed)
        add_to(1, grad)
        grad = norm_back(grad * r.norm_gains[0:1, :], normed, r.inverse_one[here, :])
        r.grad_rows[here, :] = grad
        low = grad.astype(bf16)
        add_to(0, low.astype(f32))
        r.branch_all[pl.ds(pl.multiple_of(tensor * rows + here.start, NORM), NORM), :] = low

    for half in range(HALVES):
        part = part_of(half)
        r.kept[part, :] = scatters[2].take(half, r.kept[part, :])
        chunks(half_rows, half * half_rows, first_back, NORM)
        gathers[3].start_half(half)
        if half == 0:
            rest_sum.relay()
            down_sum.relay(3)
    scatters[2].finish()

    gathers[3].start_near()
    grad_keys, grad_values = r.slope.at[:, :local], r.slope.at[:, local : 2 * local]
    r.slope[:, : 2 * local] = jnp.zeros((r.slope.shape[0], 2 * local), f32)

    def attend_back(rank):
        here = block(rank)
        r.mixed_low[...] = dot_nt(r.branch_all[here, :], r.output[...]).astype(bf16)

        @pl.loop(0, pairs)
        def _(pair):
            lanes = block(pair, 2 * HEAD)
            query = r.queries[here, lanes]
            grad = r.mixed_low[:, lanes]
            keys = r.key_rows[:, lanes]
            values = r.value_rows[:, lanes]
            same = r.segment_column[...] == r.segment_row_f32[:, here]
            lane = lax.broadcasted_iota(jnp.int32, query.shape, 1)
            outs = []
            for side in range(2):
                mine = lane // HEAD == side
                head = pair * 2 + side
                query_here = jnp.where(mine, query, bf16(0))
                grad_here = jnp.where(mine, grad, bf16(0))
                scores = jnp.where(same, dot_nt(keys, query_here), NEGATIVE)
                weights = jnp.exp(scores - r.log_totals[pl.ds(head, 1), here])
                grad_weights = dot_nt(values, grad_here)
                along = jnp.sum(weights * grad_weights, axis=0, keepdims=True)
                grad_scores = (weights * (grad_weights - along)).astype(bf16)
                grad_keys[:, lanes] += dot(grad_scores, query_here)
                grad_values[:, lanes] += dot(weights.astype(bf16), grad_here)
                outs.append(dot(r.key_turned[head_rows(head), :], grad_scores))
            grad_query = jnp.concatenate(outs, axis=0).T * HEAD**-0.5
            r.projected_low[here, lanes] = grad_query.astype(bf16)

    @pl.loop(0, 4)
    def _(turn):
        @pl.when(turn == 1)
        def _():
            gathers[3].wait_near()

        @pl.when(turn == 2)
        def _():
            for half in range(HALVES):
                gathers[3].wait_across(half)

        @pl.when(turn == 3)
        def _():
            for half in range(HALVES):
                gathers[3].wait_far(half)
            r.grad_output[...] = dot_tn(r.mixed[...], r.branch_all[...]).astype(bf16)
            output_sum.start()

        attend_back(tensor ^ turn)

        @pl.when(turn == 0)
        def _():
            down_sum.relay(1)

        @pl.when(turn == 1)
        def _():
            up_sum.relay(3)

        @pl.when(turn == 2)
        def _():
            down_sum.relay(2)
            rest_sum.turn(down_rest)

    up_sum.relay(2)
    up_sum.relay(1)
    r.projected_low[:, local : 2 * local] = grad_keys[...].astype(bf16)
    r.projected_low[:, 2 * local :] = grad_values[...].astype(bf16)
    r.held_totals[0] = jnp.zeros(r.held_totals.shape[1:], f32)
    r.held_totals[0, 2:8, :] = r.sums[0:6, :]
    r.held_totals[0, pl.ds(8 + tensor, 1), :] = r.sums[6:7, :]
    for row, at in ((0, 0), (1, 2)):
        low = r.projected_low[:, at * local : (at + 1) * local].astype(f32)
        r.held_totals[0, row : row + 1, columns] = jnp.sum(low, axis=0, keepdims=True)
    total.start()
    for at in range(3):
        lanes = slice(at * local, (at + 1) * local)
        weight_grad(r.gathered, r.projected_low.at[:, lanes], r.grad_project.at[at])
    project_sum.start((3, 1, 2, 0))

    @pl.loop(0, LINES)
    def _(at):
        lanes = column_block(at)
        product = 0
        for part in range(3):
            left = r.projected_low[:, part * local : (part + 1) * local]
            product += dot_nt(left, r.triple[part, lanes, :])
        r.columns[...] = product
        scatter_columns(scatters[3], at)

    total.step(0)
    output_sum.relay(3)
    project_sum.relay(3)
    down_sum.finish(down_top)
    rest_sum.finish(down_rest)
    save(r.down_sum, r.down_out)

    def take_tokens(at):
        lanes = column_block(at)
        r.grad_rows[:, lanes] += scatters[3].take(at, r.kept[:, lanes])

    take_tokens(0)
    take_tokens(1)
    output_sum.relay(2)
    take_tokens(2)
    project_sum.relay(1)
    total.step(1)
    take_tokens(3)
    save(r.grad_rows, r.grad_tokens)
    project_sum.relay(2)
    up_sum.finish(r.up_sum)
    save(r.up_sum, r.up_out)
    total.step(2)
    output_sum.relay(1)
    total.step(3)
    project_sum.finish(r.project_sum)
    save(r.project_sum, r.project_out)
    total.step(4)
    r.bias_sum[...] = r.held_totals[5, 0:6, :]
    r.gains_sum[...] = r.held_totals[5, 6:8, :]
    for at in range(4):
        r.hidden_sum[at * hidden : (at + 1) * hidden] = r.held_totals[5, 8 + at, :]
    save(r.bias_sum, r.bias_out)
    save(r.gains_sum, r.gains_out)
    save(r.hidden_sum, r.hidden_out)
    scatters[3].finish()
    output_sum.finish(r.output_sum)
    save(r.output_sum, r.output_out)
    for each in gathers + lines + [total]:
        each.finish()
    for each in saves:
        each.wait()


def copy_kernel(count, *refs):
    sources, targets, held, sem = refs[:count], refs[count : 2 * count], refs[2 * count : -1], refs[-1]
    copies_in = [pltpu.make_async_copy(*pair, sem.at[at]) for at, pair in enumerate(zip(sources, held))]
    copies_out = [
        pltpu.make_async_copy(*pair, sem.at[count + at]) for at, pair in enumerate(zip(held, targets))
    ]
    for copy in copies_in:
        copy.start()
    for arrived, copy in zip(copies_in, copies_out):
        arrived.wait()
        copy.start()
    for copy in copies_out:
        copy.wait()


def per_device_kernel(
    tokens,
    segments,
    cotangent,
    project_weight,
    output_weight,
    up_weight,
    down_weight,
    norm_gains,
    bias_rows,
    hidden_bias,
):
    rows, width = tokens.shape
    length = segments.shape[1]
    local_hidden = up_weight.shape[1]
    local = output_weight.shape[0]
    piece = project_weight.shape[0]
    bf16, f32 = jnp.bfloat16, jnp.float32
    inputs = dict(
        tokens=tokens,
        triple_own=project_weight.transpose(1, 0, 2),
        output_own=output_weight,
        up_own=up_weight,
        down_own=down_weight,
        segments=segments,
        cotangent_from=cotangent,
        gains_from=norm_gains,
        bias_from=bias_rows,
        hidden_from=hidden_bias,
    )
    shapes = dict(
        project=(3, piece, local),
        output=(local, piece),
        up=(piece, local_hidden),
        down=(local_hidden, piece),
    )
    outputs = dict(layer_out=((rows, width), bf16), grad_tokens=((rows, width), f32))
    outputs |= {name + "_out": (shape, f32) for name, shape in shapes.items()}
    outputs |= dict(
        gains_out=((2, width), f32),
        bias_out=((6, width), f32),
        hidden_out=(hidden_bias.shape, f32),
    )
    scratch = dict(
        segment_row=((1, length), jnp.int32),
        segment_row_f32=((1, length), f32),
        segment_column=((length, 1), f32),
        cotangent=((rows, width), bf16),
        norm_gains=(norm_gains.shape, f32),
        bias_rows=(bias_rows.shape, f32),
        hidden_bias=((local_hidden,), f32),
        layer_low=((rows, width), bf16),
        bias_sum=(bias_rows.shape, f32),
        gains_sum=(norm_gains.shape, f32),
        hidden_sum=(hidden_bias.shape, f32),
        partial=((rows, width), f32),
        gathered=((length, width), bf16),
        triple=((3, width, local), bf16),
        output=((local, width), bf16),
        up=((width, local_hidden), bf16),
        down=((local_hidden, width), bf16),
        queries=((length, local), bf16),
        key_rows=((length, local), bf16),
        value_rows=((length, local), bf16),
        key_turned=((local, length), bf16),
        value_turned=((local, length), bf16),
        mixed=((length, local), bf16),
        log_totals=((local // HEAD, length), f32),
        normed_one=((rows, width), f32),
        inverse_one=((rows, 1), f32),
        first_all=((length, width), bf16),
        hidden=((length, local_hidden), bf16),
        slope=((length, local_hidden), f32),
        second_all=((length, width), bf16),
        upper_low=((length, local_hidden), bf16),
        upper=((rows, local_hidden), f32),
        columns=((length, 2 * piece), f32),
        kept=((rows, width), f32),
        held=((rows // HALVES, width), f32),
        grad_rows=((rows, width), f32),
        sums=((8, width), f32),
        branch_all=((length, width), bf16),
        mixed_low=((rows, local), bf16),
        projected_low=((length, 3 * local), bf16),
        grad_project=((3, width, local), bf16),
        grad_output=((local, width), bf16),
        grad_up=((width, local_hidden), bf16),
        grad_down=((local_hidden, width), bf16),
        held_totals=((6, 16, width), f32),
        arrived_totals=((5, 16, width), f32),
    )
    for name, shape in shapes.items():
        scratch[name + "_sum"] = (shape, f32)
        moved = (local_hidden // 2, piece) if name == "down" else shape
        scratch[name + "_side"] = ((LINES,) + moved, bf16)
        scratch[name + "_line"] = ((LINES - 1,) + moved, bf16)
    scratch |= dict(
        rest_line=((LINES - 1, local_hidden // 2, 2 * piece), bf16),
        rest_out=((local_hidden // 2, piece), bf16),
        rest_in=((local_hidden // 2, piece), bf16),
    )
    for name in ("near_out_", "near_in_"):
        scratch[name + "a"] = ((2 * HALVES, rows // HALVES, width), bf16)
        scratch[name + "b"] = ((2 * LINES, rows, 2 * piece), bf16)
    for name in ("across_out_", "across_in_"):
        scratch[name + "a"] = ((rows, width), bf16)
        scratch[name + "b"] = ((LINES, rows, 2 * piece), bf16)
    semaphores = dict(
        line_send=(5, 3 * LINES),
        line_recv=(5, 2 * LINES),
        line_local=(5,),
        part_send=(5, 2 * LINES),
        part_recv=(5, 2 * LINES),
        row_send=(4, 1 + 2 * HALVES),
        row_recv=(4, 1 + 2 * HALVES),
        sum_send=(4, 3 * LINES),
        sum_recv=(4, 3 * LINES),
        total_send=(5,),
        total_recv=(5,),
        load_sem=(6,),
        save_sem=(9,),
    )
    names = [*inputs, *outputs, *scratch, *semaphores]
    hbm = pl.BlockSpec(memory_space=pltpu.HBM)
    results = pl.pallas_call(
        functools.partial(layer_kernel, names, rows),
        out_shape=[jax.ShapeDtypeStruct(*leaf) for leaf in outputs.values()],
        in_specs=[hbm] * len(inputs),
        out_specs=[hbm] * len(outputs),
        scratch_shapes=[pltpu.VMEM(*leaf) for leaf in scratch.values()]
        + [pltpu.SemaphoreType.DMA(shape) for shape in semaphores.values()],
        compiler_params=pltpu.CompilerParams(
            collective_id=0, has_side_effects=True, vmem_limit_bytes=VMEM_BYTES
        ),
        name="layer",
    )(*inputs.values())
    results = pl.pallas_call(
        functools.partial(copy_kernel, len(outputs)),
        out_shape=[jax.ShapeDtypeStruct(*leaf) for leaf in outputs.values()],
        in_specs=[hbm] * len(outputs),
        out_specs=[hbm] * len(outputs),
        scratch_shapes=[pltpu.VMEM(*leaf) for leaf in outputs.values()]
        + [pltpu.SemaphoreType.DMA((2 * len(outputs),))],
        name="copy",
    )(*results)
    result = dict(zip(outputs, results))
    return (
        result["layer_out"],
        result["grad_tokens"],
        result["project_out"].transpose(1, 0, 2),
        result["output_out"],
        result["up_out"],
        result["down_out"],
        result["gains_out"],
        result["bias_out"],
        result["hidden_out"],
    )


def gelu_exact(values):
    return jax.nn.gelu(values, approximate=False)


def layer_norm(token_rows, gain, shift):
    average = jnp.mean(token_rows, axis=-1, keepdims=True)
    centred = token_rows - average
    variance = jnp.mean(centred * centred, axis=-1, keepdims=True)
    inverse = lax.rsqrt(variance + EPSILON)
    normed = centred * inverse
    return (normed * gain + shift, (normed, inverse))


def norm_back_saved(grad_rows, saved, gain):
    normed, inverse = saved
    grad_gain = jnp.sum(grad_rows * normed, axis=0)
    grad_shift = jnp.sum(grad_rows, axis=0)
    grad_normed = grad_rows * gain
    grad_input = inverse * (
        grad_normed
        - jnp.mean(grad_normed, axis=-1, keepdims=True)
        - normed * jnp.mean(grad_normed * normed, axis=-1, keepdims=True)
    )
    return (grad_input, grad_gain, grad_shift)


def split_heads(token_rows):
    return token_rows.reshape(token_rows.shape[0], token_rows.shape[1] // HEAD, HEAD)


def scatter_sum(partial_sum, axis_name, dimension):
    return lax.psum_scatter(
        partial_sum.astype(jnp.bfloat16), axis_name, scatter_dimension=dimension, tiled=True
    ).astype(jnp.float32)


def place_columns(partial_sum, column_block, total_width):
    full_rows = jnp.zeros(partial_sum.shape[:-1] + (total_width,), jnp.float32)
    return lax.dynamic_update_slice_in_dim(
        full_rows, partial_sum, column_block * partial_sum.shape[-1], partial_sum.ndim - 1
    )


def per_device(
    tokens,
    segments,
    cotangent,
    project_weight,
    output_weight,
    up_weight,
    down_weight,
    norm_gains,
    bias_rows,
    hidden_bias,
):
    tensor_rank = lax.axis_index("tensor")
    local_rows, model_width = tokens.shape
    seq_count, seq_length = segments.shape
    group_rows = seq_count * seq_length
    local_width = project_weight.shape[2]
    score_scale = HEAD ** (-0.5)
    block_rows = min(512, seq_length)
    per_sequence = seq_length // block_rows
    count_blocks = group_rows // block_rows
    block_ids = jnp.arange(count_blocks, dtype=jnp.int32)
    triple_full, output_full, upward_full, downward_full = (
        lax.all_gather(project_weight, "dp", axis=0, tiled=True),
        lax.all_gather(output_weight, "dp", axis=1, tiled=True),
        lax.all_gather(up_weight, "dp", axis=0, tiled=True),
        lax.all_gather(down_weight, "dp", axis=1, tiled=True),
    )
    local_hidden = upward_full.shape[1]
    triple_matrix = triple_full.reshape(model_width, 3 * local_width)
    gathered = lax.all_gather(tokens, "tensor", axis=0, tiled=True)
    head_bias = lax.dynamic_slice_in_dim(bias_rows, tensor_rank * local_width, local_width, 1)
    projected = jnp.dot(gathered, triple_matrix, preferred_element_type=jnp.float32).reshape(
        group_rows, 3, local_width
    )
    queries = (projected[:, 0] + head_bias[0]).astype(jnp.bfloat16)
    key_rows = projected[:, 1].astype(jnp.bfloat16)
    value_rows = (projected[:, 2] + head_bias[1]).astype(jnp.bfloat16)

    def block_parts(block_index):
        sequence = block_index // per_sequence
        row_start = block_index * block_rows
        seq_start = sequence * seq_length
        query_block = split_heads(lax.dynamic_slice_in_dim(queries, row_start, block_rows, 0))
        key_block = split_heads(key_rows)
        value_block = split_heads(value_rows)
        seq_ids = lax.dynamic_index_in_dim(segments, sequence, 0, keepdims=False)
        query_ids = lax.dynamic_slice_in_dim(seq_ids, row_start - seq_start, block_rows, 0)
        products = (
            jnp.einsum("qhd,khd->hqk", query_block, key_block, preferred_element_type=jnp.float32)
            * score_scale
        )
        scores = jnp.where((query_ids[:, None] == seq_ids[None, :])[None], products, NEGATIVE)
        return (row_start, query_block, key_block, value_block, scores)

    def forward_block(block_index):
        row_start, query_block, key_block, value_block, scores = block_parts(block_index)
        row_max = jnp.max(scores, axis=-1, keepdims=True)
        exponent = jnp.exp(scores - row_max)
        row_sum = jnp.sum(exponent, axis=-1, keepdims=True)
        weights_low = (exponent / row_sum).astype(jnp.bfloat16)
        mixed_block = jnp.einsum(
            "hqk,khd->qhd", weights_low, value_block, preferred_element_type=jnp.float32
        )
        log_total = row_max[:, :, 0] + jnp.log(row_sum[:, :, 0])
        return (mixed_block.reshape(block_rows, local_width).astype(jnp.bfloat16), log_total)

    mixed_blocks, log_totals = lax.map(forward_block, block_ids)
    mixed_rows = mixed_blocks.reshape(group_rows, local_width)
    branch_out = (
        scatter_sum(
            jnp.dot(mixed_rows, output_full, preferred_element_type=jnp.float32), "tensor", 0
        )
        + bias_rows[2]
    )
    first_out, first_saved = layer_norm(
        tokens.astype(jnp.float32) + branch_out, norm_gains[0], bias_rows[3]
    )
    first_gathered = lax.all_gather(first_out.astype(jnp.bfloat16), "tensor", axis=0, tiled=True)
    local_bias = lax.dynamic_slice_in_dim(hidden_bias, tensor_rank * local_hidden, local_hidden, 0)
    upper_rows = (
        jnp.dot(first_gathered, upward_full, preferred_element_type=jnp.float32) + local_bias
    )
    hidden_full, gelu_back = jax.vjp(gelu_exact, upper_rows)
    hidden_rows = hidden_full.astype(jnp.bfloat16)
    second_out = (
        scatter_sum(
            jnp.dot(hidden_rows, downward_full, preferred_element_type=jnp.float32), "tensor", 0
        )
        + bias_rows[4]
    )
    layer_out, second_saved = layer_norm(first_out + second_out, norm_gains[1], bias_rows[5])
    reloaded = (
        lax.all_gather(project_weight, "dp", axis=0, tiled=True),
        lax.all_gather(output_weight, "dp", axis=1, tiled=True),
        lax.all_gather(up_weight, "dp", axis=0, tiled=True),
        lax.all_gather(down_weight, "dp", axis=1, tiled=True),
    )
    back_triple = reloaded[0].reshape(model_width, 3 * local_width)
    back_output, back_upward, back_downward = (reloaded[1], reloaded[2], reloaded[3])
    grad_layer = cotangent.astype(jnp.float32)
    grad_second_in, grad_gain_two, grad_shift_two = norm_back_saved(
        grad_layer, second_saved, norm_gains[1]
    )
    grad_second = grad_second_in.astype(jnp.bfloat16)
    grad_second_all = lax.all_gather(grad_second, "tensor", axis=0, tiled=True)
    grad_down_part = jnp.einsum(
        "tf,td->fd", hidden_rows, grad_second_all, preferred_element_type=jnp.float32
    )
    grad_hidden = jnp.einsum(
        "td,fd->tf", grad_second_all, back_downward, preferred_element_type=jnp.float32
    )
    grad_upper = gelu_back(grad_hidden)[0].astype(jnp.bfloat16)
    grad_up_part = jnp.einsum(
        "td,tf->df", first_gathered, grad_upper, preferred_element_type=jnp.float32
    )
    grad_first = (
        scatter_sum(
            jnp.einsum("tf,df->td", grad_upper, back_upward, preferred_element_type=jnp.float32),
            "tensor",
            0,
        )
        + grad_second_in
    )
    grad_first_in, grad_gain_one, grad_shift_one = norm_back_saved(grad_first, first_saved, norm_gains[0])
    grad_branch = grad_first_in.astype(jnp.bfloat16)
    grad_branch_all = lax.all_gather(grad_branch, "tensor", axis=0, tiled=True)
    grad_output_part = jnp.einsum(
        "tc,td->cd", mixed_rows, grad_branch_all, preferred_element_type=jnp.float32
    )
    grad_mixed = jnp.einsum(
        "td,cd->tc", grad_branch_all, back_output, preferred_element_type=jnp.float32
    ).astype(jnp.bfloat16)

    def backward_block(block_index):
        row_start, query_block, key_block, value_block, scores = block_parts(block_index)
        weights_full = jnp.exp(scores - log_totals[block_index][:, :, None])
        grad_mixed_block = split_heads(
            lax.dynamic_slice_in_dim(grad_mixed, row_start, block_rows, 0)
        )
        grad_weights = jnp.einsum(
            "qhd,khd->hqk", grad_mixed_block, value_block, preferred_element_type=jnp.float32
        )
        row_dot = jnp.sum(weights_full * grad_weights, axis=-1, keepdims=True)
        grad_scores = (weights_full * (grad_weights - row_dot)).astype(jnp.bfloat16)
        grad_query = (
            jnp.einsum("hqk,khd->qhd", grad_scores, key_block, preferred_element_type=jnp.float32)
            * score_scale
        )
        grad_key = (
            jnp.einsum("hqk,qhd->khd", grad_scores, query_block, preferred_element_type=jnp.float32)
            * score_scale
        )
        grad_value = jnp.einsum(
            "hqk,qhd->khd",
            weights_full.astype(jnp.bfloat16),
            grad_mixed_block,
            preferred_element_type=jnp.float32,
        )
        return (
            grad_query.reshape(block_rows, local_width),
            grad_key.reshape(seq_length, local_width),
            grad_value.reshape(seq_length, local_width),
        )

    query_blocks, key_blocks, value_blocks = lax.map(backward_block, block_ids)
    grad_queries = query_blocks.reshape(group_rows, local_width)
    grad_keys = (
        key_blocks.reshape(seq_count, per_sequence, seq_length, local_width)
        .sum(axis=1)
        .reshape(group_rows, local_width)
    )
    grad_values = (
        value_blocks.reshape(seq_count, per_sequence, seq_length, local_width)
        .sum(axis=1)
        .reshape(group_rows, local_width)
    )
    grad_projected = jnp.stack((grad_queries, grad_keys, grad_values), axis=1).astype(jnp.bfloat16)
    grad_project_part = jnp.einsum(
        "te,tsc->esc", gathered, grad_projected, preferred_element_type=jnp.float32
    )
    grad_matrix = grad_projected.reshape(group_rows, 3 * local_width)
    grad_tokens = (
        lax.psum_scatter(
            jnp.einsum(
                "tc,ec->te", grad_matrix, back_triple, preferred_element_type=jnp.float32
            ).astype(jnp.bfloat16),
            "tensor",
            scatter_dimension=0,
            tiled=True,
        ).astype(jnp.float32)
        + grad_first_in
    )
    grad_project, grad_output, grad_up, grad_down = (
        scatter_sum(grad_project_part, "dp", 0),
        scatter_sum(grad_output_part, "dp", 1),
        scatter_sum(grad_up_part, "dp", 0),
        scatter_sum(grad_down_part, "dp", 1),
    )
    head_terms = place_columns(
        jnp.stack(
            (
                jnp.sum(grad_projected[:, 0], axis=0, dtype=jnp.float32),
                jnp.sum(grad_projected[:, 2], axis=0, dtype=jnp.float32),
            )
        ),
        tensor_rank,
        model_width,
    )
    shared_terms = jnp.stack(
        (
            jnp.sum(grad_branch, axis=0, dtype=jnp.float32),
            grad_shift_one,
            jnp.sum(grad_second, axis=0, dtype=jnp.float32),
            grad_shift_two,
        )
    )
    bias_terms = jnp.concatenate((head_terms, shared_terms), axis=0)
    gain_terms = jnp.stack((grad_gain_one, grad_gain_two))
    hidden_terms = place_columns(
        jnp.sum(grad_upper, axis=0, dtype=jnp.float32), tensor_rank, hidden_bias.shape[0]
    )
    grad_gains, grad_bias_rows, grad_hidden_bias = lax.psum(
        (gain_terms, bias_terms, hidden_terms), ("dp", "tensor")
    )
    return (
        layer_out.astype(jnp.bfloat16),
        grad_tokens,
        grad_project,
        grad_output,
        grad_up,
        grad_down,
        grad_gains,
        grad_bias_rows,
        grad_hidden_bias,
    )


def solution(mesh):
    fits = mesh.shape["dp"] == 2 * LINES and mesh.shape["tensor"] == 4
    placed = (
        P(("dp", "tensor"), None),
        P("dp", None),
        P(("dp", "tensor"), None),
        P("dp", None, "tensor"),
        P("tensor", "dp"),
        P("dp", "tensor"),
        P("tensor", "dp"),
        P(),
        P(),
        P(),
    )
    return jax.shard_map(
        per_device_kernel if fits else per_device,
        mesh=mesh,
        in_specs=placed,
        out_specs=(
            P(("dp", "tensor"), None),
            P(("dp", "tensor"), None),
            P("dp", None, "tensor"),
            P("tensor", "dp"),
            P("dp", "tensor"),
            P("tensor", "dp"),
            P(),
            P(),
            P(),
        ),
        check_vma=False,
    )
```

```python
import functools
import types

import jax
import jax.numpy as jnp
from jax import lax
from jax.experimental import pallas as pl
from jax.experimental.pallas import tpu as pltpu
from jax.sharding import PartitionSpec as P

HEAD = 64
EPSILON = 1e-05
NEGATIVE = -1e30
MESH = pl.DeviceIdType.MESH
LINES = 4
CORE, ACROSS, FAR = 1, 2, 3
HALVES = 2
CHUNK = 16
NORM = 64
ORDER = (3, 2, 1, 0)
VMEM_BYTES = 60 << 20


def remote(src, dst, send_sem, recv_sem, target):
    return pltpu.make_async_remote_copy(
        src_ref=src,
        dst_ref=dst,
        send_sem=send_sem,
        recv_sem=recv_sem,
        device_id=target,
        device_id_type=MESH,
    )


def position():
    return lax.axis_index("dp"), lax.axis_index("tensor")


def greet():
    dp, tensor = position()
    barrier = pltpu.get_barrier_semaphore()
    others = [(dp ^ step, tensor) for step in (1, 2, 4, 6)]
    others += [(dp, tensor ^ step) for step in (CORE, ACROSS)]
    for target in others:
        pl.semaphore_signal(barrier, inc=1, device_id=target, device_id_type=MESH)
    pl.semaphore_wait(barrier, len(others))


def row_piece(ref, index, size):
    return ref.at[pl.ds(pl.multiple_of(index * size, size), size), :]


def column_piece(ref, index, size):
    return ref.at[:, pl.ds(pl.multiple_of(index * size, size), size)]


class LineGather:
    def __init__(self, own, full, piece, send_sem, recv_sem, local_sem):
        self.own, self.full, self.piece = own, full, piece
        self.send_sem, self.recv_sem, self.local_sem = send_sem, recv_sem, local_sem
        self.dp, self.tensor = position()
        self.line, self.side = self.dp // 2, self.dp % 2
        self.targets = (
            (self.dp + 2, self.tensor),
            (self.dp - 2, self.tensor),
            (self.dp ^ 1, self.tensor),
        )

    def copy(self, index, way, src=None):
        view = self.piece(self.full, index)
        return remote(
            view if src is None else src,
            view,
            self.send_sem.at[(LINES - 1) * way - way % 2 + index // 2],
            self.recv_sem.at[index],
            self.targets[way],
        )

    def local(self):
        return pltpu.make_async_copy(self.own, self.piece(self.full, self.dp), self.local_sem)

    def start_along(self):
        self.local().start()

        @pl.when(self.line < LINES - 1)
        def _():
            self.copy(self.dp, 0, self.own).start()

        @pl.when(self.line > 0)
        def _():
            self.copy(self.dp, 1, self.own).start()

    def start_across(self):
        self.copy(self.dp, 2, self.own).start()

    def step_along(self, distance):
        @pl.when(self.line >= distance)
        def _():
            self.copy(self.dp - 2 * distance, 0).wait_recv()

            @pl.when(self.line < LINES - 1)
            def _():
                self.copy(self.dp - 2 * distance, 0).start()

        @pl.when(self.line + distance < LINES)
        def _():
            self.copy(self.dp + 2 * distance, 1).wait_recv()

            @pl.when(self.line > 0)
            def _():
                self.copy(self.dp + 2 * distance, 1).start()

    def step_across(self, distance):
        @pl.when(self.line >= distance)
        def _():
            self.copy(self.dp - 2 * distance, 2).start()

        @pl.when(self.line + distance < LINES)
        def _():
            self.copy(self.dp + 2 * distance, 2).start()

    def step(self, distance):
        self.step_along(distance)
        self.step_across(distance)

    def arrive_block(self, at):
        self.copy(self.dp ^ (2 * at) ^ 1, 2).wait_recv()

    def arrive(self):
        self.local().wait()
        for line in range(LINES):
            self.copy(2 * line + 1 - self.side, 2).wait_recv()

    def finish(self):
        for line in range(LINES):
            index = 2 * line + self.side
            self.copy(index, 2).wait_send()

            @pl.when((self.line < LINES - 1) & (line <= self.line))
            def _():
                self.copy(index, 0).wait_send()

            @pl.when((self.line > 0) & (line >= self.line))
            def _():
                self.copy(index, 1).wait_send()


class RowGather:
    def __init__(self, full, rows, send_sem, recv_sem):
        self.full, self.rows = full, rows
        self.send_sem, self.recv_sem = send_sem, recv_sem
        self.dp, self.tensor = position()

    def view(self, rank, half=None):
        if half is None:
            return row_piece(self.full, rank, self.rows)
        return row_piece(self.full, rank * HALVES + half, self.rows // HALVES)

    def near(self, rank):
        view = self.view(rank)
        target = (self.dp, self.tensor ^ CORE)
        return remote(view, view, self.send_sem.at[0], self.recv_sem.at[0], target)

    def across(self, rank, half):
        view, slot = self.view(rank, half), 1 + half
        target = (self.dp, self.tensor ^ ACROSS)
        return remote(view, view, self.send_sem.at[slot], self.recv_sem.at[slot], target)

    def far(self, rank, half):
        view, slot = self.view(rank, half), 1 + HALVES + half
        target = (self.dp, self.tensor ^ CORE)
        return remote(view, view, self.send_sem.at[slot], self.recv_sem.at[slot], target)

    def start_half(self, half):
        self.across(self.tensor, half).start()

    def start_near(self):
        self.near(self.tensor).start()

    def start(self):
        for half in range(HALVES):
            self.start_half(half)
        self.start_near()

    def wait_near(self):
        self.near(self.tensor ^ CORE).wait_recv()

    def wait_across(self, half):
        self.across(self.tensor ^ ACROSS, half).wait_recv()
        self.far(self.tensor ^ ACROSS, half).start()

    def wait_far(self, half):
        self.far(self.tensor ^ FAR, half).wait_recv()

    def finish(self):
        self.near(self.tensor).wait_send()
        for half in range(HALVES):
            self.across(self.tensor, half).wait_send()
            self.far(self.tensor ^ ACROSS, half).wait_send()


class RowScatter:
    def __init__(self, near_out, near_in, across_out, across_in, send_sem, recv_sem):
        self.near_out, self.near_in = near_out, near_in
        self.across_out, self.across_in = across_out, across_in
        self.send_sem, self.recv_sem = send_sem, recv_sem
        self.dp, self.tensor = position()

    def near(self, slot):
        return remote(
            self.near_out.at[slot],
            self.near_in.at[slot],
            self.send_sem.at[slot],
            self.recv_sem.at[slot],
            (self.dp, self.tensor ^ CORE),
        )

    def across(self, half):
        rows = self.across_in.shape[0] // HALVES
        return remote(
            row_piece(self.across_out, half, rows),
            row_piece(self.across_in, half, rows),
            self.send_sem.at[2 * HALVES + half],
            self.recv_sem.at[2 * HALVES + half],
            (self.dp, self.tensor ^ ACROSS),
        )

    def give_far(self, half, partial):
        self.near_out[half] = partial.astype(jnp.bfloat16)
        self.near(half).start()

    def give_across(self, half, partial):
        self.near(half).wait_recv()
        rows = partial.shape[0]
        total = partial + self.near_in[half].astype(jnp.float32)
        row_piece(self.across_out, half, rows)[...] = total.astype(jnp.bfloat16)
        self.across(half).start()

    def give_near(self, half, partial):
        self.near_out[HALVES + half] = partial.astype(jnp.bfloat16)
        self.near(HALVES + half).start()

    def take(self, half, partial):
        self.near(HALVES + half).wait_recv()
        rows = partial.shape[0]
        total = partial + self.near_in[HALVES + half].astype(jnp.float32)
        self.across(half).wait_recv()
        return total + row_piece(self.across_in, half, rows)[...].astype(jnp.float32)

    def finish(self):
        for slot in range(2 * HALVES):
            self.near(slot).wait_send()
        for half in range(HALVES):
            self.across(half).wait_send()


def dot(left, right):
    return jnp.dot(left, right, preferred_element_type=jnp.float32)


def dot_nt(left, right):
    return lax.dot_general(left, right, (((1,), (1,)), ((), ())), preferred_element_type=jnp.float32)


def dot_tn(left, right):
    return lax.dot_general(left, right, (((0,), (0,)), ((), ())), preferred_element_type=jnp.float32)


def normalize(rows):
    centred = rows - jnp.mean(rows, axis=-1, keepdims=True)
    inverse = lax.rsqrt(jnp.mean(centred * centred, axis=-1, keepdims=True) + EPSILON)
    return centred * inverse, inverse


def norm_back(grad, normed, inverse):
    average = jnp.mean(grad, axis=-1, keepdims=True)
    along = jnp.mean(grad * normed, axis=-1, keepdims=True)
    return inverse * (grad - average - normed * along)


class PairGather:
    def __init__(self, own, full, piece, pair, send_sem, recv_sem, local_sem):
        self.own, self.full, self.piece, self.pair = own, full, piece, pair
        self.send_sem, self.recv_sem, self.local_sem = send_sem, recv_sem, local_sem
        self.dp, self.tensor = position()
        self.line = self.dp // 2

    def local(self):
        return pltpu.make_async_copy(self.own, self.piece(self.full, self.dp), self.local_sem)

    def across(self):
        return remote(
            self.own,
            self.piece(self.full, self.dp),
            self.send_sem.at[0],
            self.recv_sem.at[LINES],
            (self.dp ^ 1, self.tensor),
        )

    def along(self, line, way):
        view = self.pair(self.full, line)
        return remote(
            view,
            view,
            self.send_sem.at[1 + way * 2 + line],
            self.recv_sem.at[line],
            (self.dp + 2 - 4 * way, self.tensor),
        )

    def start(self):
        self.local().start()
        self.across().start()

    def begin(self):
        self.local().wait()
        self.across().wait_recv()

        @pl.when(self.line < LINES - 1)
        def _():
            self.along(self.line, 0).start()

        @pl.when(self.line > 0)
        def _():
            self.along(self.line, 1).start()

    def step(self, distance):
        @pl.when(self.line >= distance)
        def _():
            self.along(self.line - distance, 0).wait_recv()

            @pl.when(self.line < LINES - 1)
            def _():
                self.along(self.line - distance, 0).start()

        @pl.when(self.line + distance < LINES)
        def _():
            self.along(self.line + distance, 1).wait_recv()

            @pl.when(self.line > 0)
            def _():
                self.along(self.line + distance, 1).start()

    def finish(self):
        self.across().wait_send()
        for line in range(LINES):

            @pl.when((self.line < LINES - 1) & (line <= self.line))
            def _():
                self.along(line, 0).wait_send()

            @pl.when((self.line > 0) & (line >= self.line))
            def _():
                self.along(line, 1).wait_send()


class LineFirstScatter:
    def __init__(self, partial, piece, line_in, across_out, across_in, send_sem, recv_sem):
        self.partial, self.piece, self.line_in = partial, piece, line_in
        self.across_out, self.across_in = across_out, across_in
        self.send_sem, self.recv_sem = send_sem, recv_sem
        self.dp, self.tensor = position()

    def view(self, step):
        return self.piece(self.partial, (self.dp // 2) ^ step)

    def along(self, step):
        return remote(
            self.view(step),
            self.line_in.at[step // 2 if step != 2 else 2],
            self.send_sem.at[step],
            self.recv_sem.at[step],
            (self.dp ^ (2 if step != 2 else 4), self.tensor),
        )

    def across(self):
        return remote(
            self.across_out,
            self.across_in,
            self.send_sem.at[0],
            self.recv_sem.at[0],
            (self.dp ^ 1, self.tensor),
        )

    def start(self):
        self.along(3).start()

    def relay(self):
        self.along(3).wait_recv()
        total = self.view(2)[...].astype(jnp.float32) + self.line_in[1].astype(jnp.float32)
        self.view(2)[...] = total.astype(jnp.bfloat16)
        self.along(2).start()
        self.along(1).start()

    def turn(self, result):
        total = self.view(0)[...].astype(jnp.float32)
        for step, slot in ((1, 0), (2, 2)):
            self.along(step).wait_recv()
            total = total + self.line_in[slot].astype(jnp.float32)
        first, second = jnp.split(total, 2, 0 if result.shape[1] == total.shape[1] else 1)
        even = self.dp % 2 == 0
        result[...] = jnp.where(even, first, second)
        self.across_out[...] = jnp.where(even, second, first).astype(jnp.bfloat16)
        self.across().start()

    def finish(self, result):
        self.across().wait_recv()
        result[...] += self.across_in[...].astype(jnp.float32)
        self.across().wait_send()
        for step in range(1, LINES):
            self.along(step).wait_send()


class DirectGather:
    def __init__(self, own, full, piece, send_sem, recv_sem, local_sem):
        self.own, self.full, self.piece = own, full, piece
        self.send_sem, self.recv_sem, self.local_sem = send_sem, recv_sem, local_sem
        self.dp, self.tensor = position()

    def along(self, step):
        there = self.dp ^ (2 * step)
        return remote(
            self.own,
            self.piece(self.full, self.dp),
            self.send_sem.at[step],
            self.recv_sem.at[step],
            (there, self.tensor),
        )

    def across(self, step, source=None):
        view = self.piece(self.full, self.dp ^ (2 * step))
        return remote(
            view if source is None else source,
            view,
            self.send_sem.at[LINES + step],
            self.recv_sem.at[LINES + step],
            (self.dp ^ 1, self.tensor),
        )

    def local(self):
        return pltpu.make_async_copy(self.own, self.piece(self.full, self.dp), self.local_sem)

    def start_along(self):
        self.local().start()
        for step in range(1, LINES):
            self.along(step).start()

    def start_across(self):
        self.across(0, self.own).start()

    def step(self, step):
        self.along(step).wait_recv()
        self.across(step).start()

    def arrive(self, step):
        self.across(step).wait_recv()

    def finish(self):
        for step in range(LINES):
            self.across(step).wait_send()
        for step in range(1, LINES):
            self.along(step).wait_send()


class ColumnScatter:
    def __init__(self, near_out, near_in, across_out, across_in, send_sem, recv_sem):
        self.near_out, self.near_in = near_out, near_in
        self.across_out, self.across_in = across_out, across_in
        self.send_sem, self.recv_sem = send_sem, recv_sem
        self.dp, self.tensor = position()

    def near(self, slot):
        return remote(
            self.near_out.at[slot],
            self.near_in.at[slot],
            self.send_sem.at[slot],
            self.recv_sem.at[slot],
            (self.dp, self.tensor ^ CORE),
        )

    def across(self, at):
        return remote(
            self.across_out.at[at],
            self.across_in.at[at],
            self.send_sem.at[2 * LINES + at],
            self.recv_sem.at[2 * LINES + at],
            (self.dp, self.tensor ^ ACROSS),
        )

    def give_far(self, at, partial):
        self.near_out[at] = partial.astype(jnp.bfloat16)
        self.near(at).start()

    def give_near(self, at, partial):
        self.near_out[LINES + at] = partial.astype(jnp.bfloat16)
        self.near(LINES + at).start()

    def give_across(self, at, partial):
        self.near(at).wait_recv()
        total = partial + self.near_in[at].astype(jnp.float32)
        self.across_out[at] = total.astype(jnp.bfloat16)
        self.across(at).start()

    def take(self, at, partial):
        self.near(LINES + at).wait_recv()
        total = partial + self.near_in[LINES + at].astype(jnp.float32)
        self.across(at).wait_recv()
        return total + self.across_in[at].astype(jnp.float32)

    def finish(self):
        for slot in range(2 * LINES):
            self.near(slot).wait_send()
        for at in range(LINES):
            self.across(at).wait_send()


class LineScatter:
    def __init__(self, partial, piece, side_in, line_in, send_sem, recv_sem):
        self.partial, self.piece, self.side_in, self.line_in = partial, piece, side_in, line_in
        self.send_sem, self.recv_sem = send_sem, recv_sem
        self.dp, self.tensor = position()

    def view(self, step):
        return self.piece(self.partial, self.dp ^ (2 * step))

    def across(self, step):
        return remote(
            self.piece(self.partial, self.dp ^ (2 * step) ^ 1),
            self.side_in.at[step],
            self.send_sem.at[step],
            self.recv_sem.at[step],
            (self.dp ^ 1, self.tensor),
        )

    def along(self, step):
        return remote(
            self.view(step),
            self.line_in.at[step // 2 if step != 2 else 2],
            self.send_sem.at[LINES + step],
            self.recv_sem.at[LINES + step],
            (self.dp ^ (2 if step != 2 else 4), self.tensor),
        )

    def start(self, order=ORDER):
        for step in order:
            self.across(step).start()

    def total(self, step):
        self.across(step).wait_recv()
        return self.view(step)[...].astype(jnp.float32) + self.side_in[step].astype(jnp.float32)

    def relay(self, step):
        total = self.total(step)
        if step == 2:
            self.along(3).wait_recv()
            total = total + self.line_in[1].astype(jnp.float32)
        self.view(step)[...] = total.astype(jnp.bfloat16)
        self.along(step).start()

    def finish(self, result):
        total = self.total(0)
        self.along(1).wait_recv()
        total = total + self.line_in[0].astype(jnp.float32)
        self.along(2).wait_recv()
        result[...] = total + self.line_in[2].astype(jnp.float32)
        for step in range(LINES):
            self.across(step).wait_send()
        for step in range(1, LINES):
            self.along(step).wait_send()


class Total:
    def __init__(self, held, arrived, send_sem, recv_sem):
        self.held, self.arrived, self.send_sem, self.recv_sem = held, arrived, send_sem, recv_sem
        dp, tensor = position()
        self.targets = (
            (dp ^ 1, tensor),
            (dp ^ 2, tensor),
            (dp ^ 4, tensor),
            (dp, tensor ^ ACROSS),
            (dp, tensor ^ CORE),
        )

    def copy(self, step):
        return remote(
            self.held.at[step],
            self.arrived.at[step],
            self.send_sem.at[step],
            self.recv_sem.at[step],
            self.targets[step],
        )

    def start(self):
        self.copy(0).start()

    def step(self, step):
        self.copy(step).wait_recv()
        self.held[step + 1] = self.held[step] + self.arrived[step]
        if step + 1 < len(self.targets):
            self.copy(step + 1).start()

    def finish(self):
        for step in range(len(self.targets)):
            self.copy(step).wait_send()


def layer_kernel(names, rows, *refs):
    r = types.SimpleNamespace(**dict(zip(names, refs)))
    dp, tensor = position()
    bf16, f32 = jnp.bfloat16, jnp.float32
    half_rows = rows // HALVES
    local = r.queries.shape[1]
    piece = r.triple_own.shape[1]
    pairs = local // (2 * HEAD)
    length, hidden = r.hidden.shape
    near, across, far = tensor ^ CORE, tensor ^ ACROSS, tensor ^ FAR

    def of_rows(ref, index):
        return row_piece(ref, index, piece)

    def of_columns(ref, index):
        return column_piece(ref, index, piece)

    def of_stack(ref, index):
        return ref.at[:, pl.ds(pl.multiple_of(index * piece, piece), piece), :]

    def of_half_stack(half):
        size = piece // HALVES

        def view(ref, index):
            return ref.at[:, pl.ds(pl.multiple_of(index * piece + half * size, size), size), :]

        return view, r.triple_own.at[:, half * size : (half + 1) * size, :]

    def block(rank, size=rows):
        return pl.ds(pl.multiple_of(rank * size, size), size)

    def split(partial):
        return [partial[half * half_rows : (half + 1) * half_rows] for half in range(HALVES)]

    def part_of(half):
        return slice(half * half_rows, (half + 1) * half_rows)

    (view_a, own_a), (view_b, own_b) = of_half_stack(0), of_half_stack(1)
    lines = [
        kind(own, full, view, r.line_send.at[at], r.line_recv.at[at], r.line_local.at[at])
        for at, (kind, own, full, view) in enumerate(
            (
                (LineGather, own_a, r.triple, view_a),
                (LineGather, own_b, r.triple, view_b),
                (DirectGather, r.output_own, r.output, of_columns),
                (LineGather, r.up_own, r.up, of_rows),
                (LineGather, r.down_own.at[: hidden // 2, :], r.down.at[: hidden // 2, :], of_columns),
            )
        )
    ]
    *triple_lines, output_line, up_line, down_line = lines

    def of_both(ref, index):
        return column_piece(ref, index, 2 * piece)

    rest_line = PairGather(
        r.down_own.at[hidden // 2 :, :],
        r.down.at[hidden // 2 :, :],
        of_columns,
        of_both,
        r.pair_send,
        r.pair_recv,
        r.pair_local,
    )
    sums = [
        LineScatter(partial, view, side, along, r.part_send.at[at], r.part_recv.at[at])
        for at, (partial, view, side, along) in enumerate(
            (
                (r.grad_project, of_stack, r.project_side, r.project_line),
                (r.grad_output, of_columns, r.output_side, r.output_line),
                (r.grad_up, of_rows, r.up_side, r.up_line),
                (r.grad_down.at[: hidden // 2, :], of_columns, r.down_side, r.down_line),
            )
        )
    ]
    project_sum, output_sum, up_sum, down_sum = sums

    rest_sum = LineFirstScatter(
        r.grad_down.at[hidden // 2 :, :],
        of_both,
        r.rest_line,
        r.rest_out,
        r.rest_in,
        r.rest_send.at[0],
        r.rest_recv.at[0],
    )
    down_top, down_rest = r.down_sum.at[: hidden // 2, :], r.down_sum.at[hidden // 2 :, :]
    gathers = [
        RowGather(full, rows, r.row_send, r.row_recv)
        for full in (r.gathered, r.first_all, r.second_all, r.branch_all)
    ]
    row_buffers = r.near_out_a, r.near_in_a, r.across_out_a, r.across_in_a
    column_buffers = r.near_out_b, r.near_in_b, r.across_out_b, r.across_in_b
    scatters = [
        RowScatter(*row_buffers, r.row_sum_send, r.row_sum_recv),
        ColumnScatter(*column_buffers, r.column_sum_send, r.column_sum_recv),
    ] * 2
    total = Total(r.held_totals, r.arrived_totals, r.total_send, r.total_recv)

    def column_block(at):
        return block((dp // 2) ^ at, 2 * piece)

    def scatter_columns(scatter, at):
        scatter.give_far(at, r.columns[block(far), :])
        scatter.give_near(at, r.columns[block(near), :])
        scatter.give_across(at, r.columns[block(across), :])
        r.kept[:, column_block(at)] = r.columns[block(tensor), :]

    def chunks(size, start, body, step=CHUNK):
        @pl.loop(0, size // step)
        def _(chunk):
            offset = chunk * step
            body(
                pl.ds(pl.multiple_of(offset, step), step),
                pl.ds(pl.multiple_of(start + offset, step), step),
            )

    loads = [
        pltpu.make_async_copy(source, target, r.load_sem.at[at])
        for at, (source, target) in enumerate(
            (
                (r.tokens, gathers[0].view(tensor)),
                (r.segments, r.segment_row),
                (r.bias_from, r.bias_rows),
                (r.gains_from, r.norm_gains),
                (r.hidden_from.at[pl.ds(pl.multiple_of(tensor * hidden, hidden), hidden)], r.hidden_bias),
                (r.cotangent_from, r.cotangent),
            )
        )
    ]
    for load in loads:
        load.start()
    greet()
    for line in triple_lines:
        line.start_along()
        line.start_across()
    loads[0].wait()
    gathers[0].start()
    for line in triple_lines:
        line.step(1)
    loads[1].wait()
    numbers = r.segment_row[...].astype(f32)
    r.segment_column[...] = jnp.broadcast_to(numbers, (8, numbers.shape[1])).T[:, :1]
    r.segment_row_f32[...] = numbers
    for line in triple_lines:
        line.step(2)
    gathers[0].wait_near()
    for half in range(HALVES):
        gathers[0].wait_across(half)
    for line in triple_lines:
        line.step(3)
    output_line.start_along()
    output_line.start_across()
    rest_line.start()
    up_line.start_along()
    down_line.start_along()
    for half in range(HALVES):
        gathers[0].wait_far(half)
    for line in triple_lines:
        line.arrive()
    for load in loads[2:]:
        load.wait()
    columns = pl.ds(pl.multiple_of(tensor * local, local), local)
    query_bias = r.bias_rows[0:1, columns]
    value_bias = r.bias_rows[1:2, columns]

    @pl.loop(0, 4)
    def _(index):
        here = block(index)
        left = r.gathered[here, :]
        query = (dot(left, r.triple[0]) + query_bias).astype(bf16)
        r.queries[here, :] = query * bf16(HEAD**-0.5)
        key = dot(left, r.triple[1])
        r.key_rows[here, :] = key.astype(bf16)
        r.key_turned[:, here] = key.T.astype(bf16)
        value = dot(left, r.triple[2]) + value_bias
        r.value_rows[here, :] = value.astype(bf16)
        r.value_turned[:, here] = value.T.astype(bf16)

    for step in range(1, LINES):
        output_line.step(step)
    up_line.start_across()

    def head_rows(head):
        return pl.ds(pl.multiple_of(head * HEAD, HEAD), HEAD)

    def attend(here, pair):
        lanes = block(pair, 2 * HEAD)
        query = r.queries[here, lanes]
        keys = r.key_rows[:, lanes]
        same = r.segment_column[...] == r.segment_row_f32[:, here]
        lane = lax.broadcasted_iota(jnp.int32, query.shape, 1)
        outs = []
        for side in range(2):
            scores = dot_nt(keys, jnp.where(lane // HEAD == side, query, bf16(0)))
            scores = jnp.where(same, scores, NEGATIVE)
            top = jnp.max(scores, axis=0, keepdims=True)
            exponent = jnp.exp(scores - top)
            mass = jnp.sum(exponent, axis=0, keepdims=True)
            weights = (exponent * (1.0 / mass)).astype(bf16)
            head = pair * 2 + side
            outs.append(dot(r.value_turned[head_rows(head), :], weights))
            r.log_totals[pl.ds(head, 1), here] = top + jnp.log(mass)
        r.mixed[here, lanes] = jnp.concatenate(outs, axis=0).T.astype(bf16)

    @pl.loop(0, 4 * pairs)
    def _(turn):
        rank, pair = tensor ^ (FAR - turn // pairs), turn % pairs
        here = block(rank)
        attend(here, pair)

        def give(rank, method):
            r.partial[...] = dot(r.mixed[block(rank), :], r.output[...])
            for half in range(HALVES):
                method(half, r.partial[part_of(half), :])

        def after(index):
            return pl.when(turn == index)

        @after(0)
        def _():
            up_line.step(1)

        @after(1)
        def _():
            rest_line.begin()

        @after(3)
        def _():
            output_line.local().wait()
            for step in range(LINES):
                output_line.arrive(step)
            give(far, scatters[0].give_far)
            give(across, scatters[0].give_across)

        @after(4)
        def _():
            up_line.step(2)
            down_line.step_along(1)

        @after(5)
        def _():
            give(near, scatters[0].give_near)

        @after(7)
        def _():
            rest_line.step(1)
            up_line.step(3)
            down_line.start_across()
            down_line.step_across(1)

    r.partial[...] = dot(r.mixed[block(tensor), :], r.output[...])
    gathers[0].finish()
    for half in range(HALVES):
        part = part_of(half)
        r.kept[part, :] = scatters[0].take(half, r.partial[part, :])

        def first_norm(_, here):
            own_rows = r.gathered[pl.ds(pl.multiple_of(tensor * rows + here.start, NORM), NORM), :]
            normed, inverse = normalize(own_rows.astype(f32) + r.kept[here, :] + r.bias_rows[2:3, :])
            r.normed_one[here, :] = normed
            r.inverse_one[here, :] = inverse
            first = normed * r.norm_gains[0:1, :] + r.bias_rows[3:4, :]
            into = pl.ds(pl.multiple_of(tensor * rows + here.start, NORM), NORM)
            r.first_all[into, :] = first.astype(bf16)

        chunks(half_rows, half * half_rows, first_norm, NORM)
        gathers[1].start_half(half)
    scatters[0].finish()

    gathers[1].start_near()
    r.sums[...] = jnp.zeros_like(r.sums)

    def extent(rank, half):
        size = rows if half is None else half_rows
        start = rank * rows + (0 if half is None else half * half_rows)
        return start, size, pl.ds(pl.multiple_of(start, size), size)

    def up_part(rank, half=None):
        start, size, here = extent(rank, half)
        r.upper[:size, :] = dot(r.first_all[here, :], r.up[...]) + r.hidden_bias[...].reshape(1, hidden)

        def body(part, into):
            value = r.upper[part, :]
            share = 0.5 + 0.5 * lax.erf(value * (0.5**0.5))
            r.hidden[into, :] = (value * share).astype(bf16)
            bell = jnp.exp(value * value * -0.5) * (2 * jnp.pi) ** -0.5
            r.slope[into, :] = share + value * bell

        chunks(size, start, body)

    def back_part(rank, half=None):
        start, size, here = extent(rank, half)
        r.upper[:size, :] = dot_nt(r.second_all[here, :], r.down[...])

        def body(part, into):
            low = (r.upper[part, :] * r.slope[into, :]).astype(bf16)
            r.upper_low[into, :] = low
            r.sums[6:7, :] += jnp.sum(low.astype(f32), axis=0, keepdims=True)

        chunks(size, start, body)
        r.partial[:size, :] = dot_nt(r.upper_low[here, :], r.up[...])

    down_line.step(2)
    up_line.arrive()

    @pl.loop(0, 2)
    def _(turn):
        @pl.when(turn == 1)
        def _():
            gathers[1].wait_near()
            down_line.step(3)
            rest_line.step(2)

        up_part(tensor ^ turn)

    def other_chip(gather, body):
        @pl.loop(0, 2 * HALVES)
        def _(turn):
            half, side = turn // 2, turn % 2

            @pl.when(side == 0)
            def _():
                gather.wait_across(half)

            body(half, side)

    def up_other(half, side):
        @pl.when(side == 1)
        def _():
            gathers[1].wait_far(half)

        up_part(tensor ^ (ACROSS + side), half)

    other_chip(gathers[1], up_other)

    rest_line.step(3)
    down_line.local().wait()

    @pl.loop(0, LINES)
    def _(at):
        down_line.arrive_block(at)
        r.columns[...] = dot(r.hidden[...], r.down[:, column_block(at)])
        scatter_columns(scatters[1], at)

    def add_to(row, value):
        r.sums[row : row + 1, :] += jnp.sum(value, axis=0, keepdims=True)

    def second_norm(_, here):
        first = r.normed_one[here, :] * r.norm_gains[0:1, :] + r.bias_rows[3:4, :]
        normed, inverse = normalize(first + r.kept[here, :] + r.bias_rows[4:5, :])
        shifted = normed * r.norm_gains[1:2, :] + r.bias_rows[5:6, :]
        r.layer_low[here, :] = shifted.astype(bf16)
        grad = r.cotangent[here, :].astype(f32)
        add_to(5, grad * normed)
        add_to(3, grad)
        grad = norm_back(grad * r.norm_gains[1:2, :], normed, inverse)
        r.grad_rows[here, :] = grad
        low = grad.astype(bf16)
        add_to(2, low.astype(f32))
        r.second_all[pl.ds(pl.multiple_of(tensor * rows + here.start, NORM), NORM), :] = low

    @pl.loop(0, LINES)
    def _(at):
        lanes = column_block(at)
        r.kept[:, lanes] = scatters[1].take(at, r.kept[:, lanes])

    gathers[1].finish()
    for half in range(HALVES):
        chunks(half_rows, half * half_rows, second_norm, NORM)
        gathers[2].start_half(half)
    saves = []

    def save(source, target):
        saves.append(pltpu.make_async_copy(source, target, r.save_sem.at[len(saves)]))
        saves[-1].start()

    save(r.layer_low, r.layer_out)
    scatters[1].finish()

    gathers[2].start_near()

    @pl.loop(0, 2)
    def _(turn):
        @pl.when(turn == 1)
        def _():
            gathers[2].wait_near()

        back_part(tensor ^ turn)

        @pl.when(turn == 0)
        def _():
            r.kept[...] = r.partial[...]

        @pl.when(turn == 1)
        def _():
            for half in range(HALVES):
                scatters[2].give_near(half, r.partial[part_of(half), :])

    def weight_grad(left, right, result, chip=None, add=False):
        depth = slice(None) if chip is None else block(chip, 2 * rows)

        @pl.loop(0, left.shape[1] // rows)
        def _(index):
            lanes = block(index)
            product = dot_tn(left[depth, lanes], right[depth, :])
            if add:
                product += result[lanes, :].astype(f32)
            result[lanes, :] = product.astype(bf16)

    weight_grad(r.hidden, r.second_all, r.grad_down, tensor // 2)

    def back_other(half, side):
        @pl.when((side == 1) & (half < HALVES - 1))
        def _():
            gathers[2].wait_far(half)

        @pl.when((side == 0) & (half == HALVES - 1))
        def _():
            gathers[2].wait_far(half)
            weight_grad(r.hidden, r.second_all, r.grad_down, 1 - tensor // 2, True)
            rest_sum.start()
            down_sum.start()

        back_part(tensor ^ (ACROSS + side), half)

        @pl.when(side == 0)
        def _():
            r.held[...] = r.partial[:half_rows, :]

        @pl.when(side == 1)
        def _():
            scatters[2].give_far(half, r.partial[:half_rows, :])
            scatters[2].give_across(half, r.held[...])

    other_chip(gathers[2], back_other)

    weight_grad(r.first_all, r.upper_low, r.grad_up)
    up_sum.start()

    def first_back(_, here):
        grad = r.grad_rows[here, :] + r.kept[here, :]
        normed = r.normed_one[here, :]
        add_to(4, grad * normed)
        add_to(1, grad)
        grad = norm_back(grad * r.norm_gains[0:1, :], normed, r.inverse_one[here, :])
        r.grad_rows[here, :] = grad
        low = grad.astype(bf16)
        add_to(0, low.astype(f32))
        r.branch_all[pl.ds(pl.multiple_of(tensor * rows + here.start, NORM), NORM), :] = low

    gathers[2].finish()
    for half in range(HALVES):
        part = part_of(half)
        r.kept[part, :] = scatters[2].take(half, r.kept[part, :])
        chunks(half_rows, half * half_rows, first_back, NORM)
        gathers[3].start_half(half)
        if half == 0:
            rest_sum.relay()
            down_sum.relay(3)
    scatters[2].finish()

    gathers[3].start_near()
    grad_keys, grad_values = r.slope.at[:, :local], r.slope.at[:, local : 2 * local]
    r.slope[:, : 2 * local] = jnp.zeros((r.slope.shape[0], 2 * local), f32)

    def attend_back(rank):
        here = block(rank)
        r.mixed_low[...] = dot_nt(r.branch_all[here, :], r.output[...]).astype(bf16)

        @pl.loop(0, pairs)
        def _(pair):
            lanes = block(pair, 2 * HEAD)
            query = r.queries[here, lanes]
            grad = r.mixed_low[:, lanes]
            keys = r.key_rows[:, lanes]
            values = r.value_rows[:, lanes]
            same = r.segment_column[...] == r.segment_row_f32[:, here]
            lane = lax.broadcasted_iota(jnp.int32, query.shape, 1)
            outs = []
            for side in range(2):
                mine = lane // HEAD == side
                head = pair * 2 + side
                query_here = jnp.where(mine, query, bf16(0))
                grad_here = jnp.where(mine, grad, bf16(0))
                scores = jnp.where(same, dot_nt(keys, query_here), NEGATIVE)
                weights = jnp.exp(scores - r.log_totals[pl.ds(head, 1), here])
                grad_weights = dot_nt(values, grad_here)
                along = jnp.sum(weights * grad_weights, axis=0, keepdims=True)
                grad_scores = (weights * (grad_weights - along)).astype(bf16)
                grad_keys[:, lanes] += dot(grad_scores, query_here)
                grad_values[:, lanes] += dot(weights.astype(bf16), grad_here)
                outs.append(dot(r.key_turned[head_rows(head), :], grad_scores))
            grad_query = jnp.concatenate(outs, axis=0).T * HEAD**-0.5
            r.projected_low[here, lanes] = grad_query.astype(bf16)

    @pl.loop(0, 4)
    def _(turn):
        @pl.when(turn == 1)
        def _():
            gathers[3].wait_near()

        @pl.when(turn == 2)
        def _():
            for half in range(HALVES):
                gathers[3].wait_across(half)

        @pl.when(turn == 3)
        def _():
            for half in range(HALVES):
                gathers[3].wait_far(half)
            r.grad_output[...] = dot_tn(r.mixed[...], r.branch_all[...]).astype(bf16)
            output_sum.start()

        attend_back(tensor ^ turn)

        @pl.when(turn == 0)
        def _():
            down_sum.relay(1)

        @pl.when(turn == 1)
        def _():
            up_sum.relay(3)

        @pl.when(turn == 2)
        def _():
            down_sum.relay(2)
            rest_sum.turn(down_rest)

    up_sum.relay(2)
    up_sum.relay(1)
    r.projected_low[:, local : 2 * local] = grad_keys[...].astype(bf16)
    r.projected_low[:, 2 * local :] = grad_values[...].astype(bf16)
    r.held_totals[0] = jnp.zeros(r.held_totals.shape[1:], f32)
    r.held_totals[0, 2:8, :] = r.sums[0:6, :]
    r.held_totals[0, pl.ds(8 + tensor, 1), :] = r.sums[6:7, :]
    shifts = dot(jnp.ones((CHUNK, length), bf16), r.projected_low[...])
    for row, at in ((0, 0), (1, 2)):
        r.held_totals[0, row : row + 1, columns] = shifts[:1, at * local : (at + 1) * local]
    total.start()

    @pl.loop(0, r.gathered.shape[1] // rows)
    def _(index):
        lanes = block(index)
        product = dot_tn(r.gathered[:, lanes], r.projected_low[...]).astype(bf16)
        for at in range(3):
            r.grad_project[at, lanes, :] = product[:, at * local : (at + 1) * local]

    project_sum.start()

    @pl.loop(0, LINES)
    def _(at):
        lanes = column_block(at)
        product = 0
        for part in range(3):
            left = r.projected_low[:, part * local : (part + 1) * local]
            product += dot_nt(left, r.triple[part, lanes, :])
        r.columns[...] = product
        scatter_columns(scatters[3], at)

    total.step(0)
    output_sum.relay(3)
    project_sum.relay(3)
    down_sum.finish(down_top)
    rest_sum.finish(down_rest)
    save(r.down_sum, r.down_out)

    def take_tokens(at):
        lanes = column_block(at)
        r.grad_rows[:, lanes] += scatters[3].take(at, r.kept[:, lanes])

    take_tokens(0)
    take_tokens(1)
    output_sum.relay(2)
    take_tokens(2)
    total.step(1)
    take_tokens(3)
    save(r.grad_rows, r.grad_tokens)
    gathers[3].finish()
    for each in lines + [rest_line]:
        each.finish()
    project_sum.relay(2)
    project_sum.relay(1)
    scatters[3].finish()
    up_sum.finish(r.up_sum)
    save(r.up_sum, r.up_out)
    total.step(2)
    output_sum.relay(1)
    total.step(3)
    project_sum.finish(r.project_sum)
    save(r.project_sum, r.project_out)
    total.step(4)
    r.bias_sum[...] = r.held_totals[5, 0:6, :]
    r.gains_sum[...] = r.held_totals[5, 6:8, :]
    for at in range(4):
        r.hidden_sum[at * hidden : (at + 1) * hidden] = r.held_totals[5, 8 + at, :]
    save(r.bias_sum, r.bias_out)
    save(r.gains_sum, r.gains_out)
    save(r.hidden_sum, r.hidden_out)
    output_sum.finish(r.output_sum)
    save(r.output_sum, r.output_out)
    total.finish()
    for each in saves:
        each.wait()


def copy_kernel(count, *refs):
    sources, targets, held, sem = refs[:count], refs[count : 2 * count], refs[2 * count : -1], refs[-1]
    copies_in = [pltpu.make_async_copy(*pair, sem.at[at]) for at, pair in enumerate(zip(sources, held))]
    copies_out = [
        pltpu.make_async_copy(*pair, sem.at[count + at]) for at, pair in enumerate(zip(held, targets))
    ]
    for copy in copies_in:
        copy.start()
    for arrived, copy in zip(copies_in, copies_out):
        arrived.wait()
        copy.start()
    for copy in copies_out:
        copy.wait()


def per_device_kernel(
    tokens,
    segments,
    cotangent,
    project_weight,
    output_weight,
    up_weight,
    down_weight,
    norm_gains,
    bias_rows,
    hidden_bias,
):
    rows, width = tokens.shape
    length = segments.shape[1]
    local_hidden = up_weight.shape[1]
    local = output_weight.shape[0]
    piece = project_weight.shape[0]
    bf16, f32 = jnp.bfloat16, jnp.float32
    inputs = dict(
        tokens=tokens,
        triple_own=project_weight.transpose(1, 0, 2),
        output_own=output_weight,
        up_own=up_weight,
        down_own=down_weight,
        segments=segments,
        cotangent_from=cotangent,
        gains_from=norm_gains,
        bias_from=bias_rows,
        hidden_from=hidden_bias,
    )
    shapes = dict(
        project=(3, piece, local),
        output=(local, piece),
        up=(piece, local_hidden),
        down=(local_hidden, piece),
    )
    outputs = dict(layer_out=((rows, width), bf16), grad_tokens=((rows, width), f32))
    outputs |= {name + "_out": (shape, f32) for name, shape in shapes.items()}
    outputs |= dict(
        gains_out=((2, width), f32),
        bias_out=((6, width), f32),
        hidden_out=(hidden_bias.shape, f32),
    )
    scratch = dict(
        segment_row=((1, length), jnp.int32),
        segment_row_f32=((1, length), f32),
        segment_column=((length, 1), f32),
        cotangent=((rows, width), bf16),
        norm_gains=(norm_gains.shape, f32),
        bias_rows=(bias_rows.shape, f32),
        hidden_bias=((local_hidden,), f32),
        layer_low=((rows, width), bf16),
        bias_sum=(bias_rows.shape, f32),
        gains_sum=(norm_gains.shape, f32),
        hidden_sum=(hidden_bias.shape, f32),
        partial=((rows, width), f32),
        gathered=((length, width), bf16),
        triple=((3, width, local), bf16),
        output=((local, width), bf16),
        up=((width, local_hidden), bf16),
        down=((local_hidden, width), bf16),
        queries=((length, local), bf16),
        key_rows=((length, local), bf16),
        value_rows=((length, local), bf16),
        key_turned=((local, length), bf16),
        value_turned=((local, length), bf16),
        mixed=((length, local), bf16),
        log_totals=((local // HEAD, length), f32),
        normed_one=((rows, width), f32),
        inverse_one=((rows, 1), f32),
        first_all=((length, width), bf16),
        hidden=((length, local_hidden), bf16),
        slope=((length, local_hidden), f32),
        second_all=((length, width), bf16),
        upper_low=((length, local_hidden), bf16),
        upper=((rows, local_hidden), f32),
        columns=((length, 2 * piece), f32),
        kept=((rows, width), f32),
        held=((rows // HALVES, width), f32),
        grad_rows=((rows, width), f32),
        sums=((8, width), f32),
        branch_all=((length, width), bf16),
        mixed_low=((rows, local), bf16),
        projected_low=((length, 3 * local), bf16),
        grad_project=((3, width, local), bf16),
        grad_output=((local, width), bf16),
        grad_up=((width, local_hidden), bf16),
        grad_down=((local_hidden, width), bf16),
        held_totals=((6, 16, width), f32),
        arrived_totals=((5, 16, width), f32),
    )
    for name, shape in shapes.items():
        scratch[name + "_sum"] = (shape, f32)
        moved = (local_hidden // 2, piece) if name == "down" else shape
        scratch[name + "_side"] = ((LINES,) + moved, bf16)
        scratch[name + "_line"] = ((LINES - 1,) + moved, bf16)
    scratch |= dict(
        rest_line=((LINES - 1, local_hidden // 2, 2 * piece), bf16),
        rest_out=((local_hidden // 2, piece), bf16),
        rest_in=((local_hidden // 2, piece), bf16),
    )
    for name in ("near_out_", "near_in_"):
        scratch[name + "a"] = ((2 * HALVES, rows // HALVES, width), bf16)
        scratch[name + "b"] = ((2 * LINES, rows, 2 * piece), bf16)
    for name in ("across_out_", "across_in_"):
        scratch[name + "a"] = ((rows, width), bf16)
        scratch[name + "b"] = ((LINES, rows, 2 * piece), bf16)
    semaphores = dict(
        line_send=(5, 3 * LINES - 2),
        line_recv=(5, 2 * LINES),
        line_local=(5,),
        part_send=(4, 2 * LINES),
        part_recv=(4, 2 * LINES),
        pair_send=(2 * LINES - 1,),
        pair_recv=(LINES + 1,),
        pair_local=(),
        rest_send=(1, LINES),
        rest_recv=(1, LINES),
        row_send=(1 + 2 * HALVES,),
        row_recv=(1 + 2 * HALVES,),
        row_sum_send=(3 * HALVES,),
        row_sum_recv=(3 * HALVES,),
        column_sum_send=(3 * LINES,),
        column_sum_recv=(3 * LINES,),
        total_send=(5,),
        total_recv=(5,),
        load_sem=(6,),
        save_sem=(9,),
    )
    names = [*inputs, *outputs, *scratch, *semaphores]
    hbm = pl.BlockSpec(memory_space=pltpu.HBM)
    results = pl.pallas_call(
        functools.partial(layer_kernel, names, rows),
        out_shape=[jax.ShapeDtypeStruct(*leaf) for leaf in outputs.values()],
        in_specs=[hbm] * len(inputs),
        out_specs=[hbm] * len(outputs),
        scratch_shapes=[pltpu.VMEM(*leaf) for leaf in scratch.values()]
        + [pltpu.SemaphoreType.DMA(shape) for shape in semaphores.values()],
        compiler_params=pltpu.CompilerParams(
            collective_id=0, has_side_effects=True, vmem_limit_bytes=VMEM_BYTES
        ),
        name="layer",
    )(*inputs.values())
    results = pl.pallas_call(
        functools.partial(copy_kernel, len(outputs)),
        out_shape=[jax.ShapeDtypeStruct(*leaf) for leaf in outputs.values()],
        in_specs=[hbm] * len(outputs),
        out_specs=[hbm] * len(outputs),
        scratch_shapes=[pltpu.VMEM(*leaf) for leaf in outputs.values()]
        + [pltpu.SemaphoreType.DMA((2 * len(outputs),))],
        name="copy",
    )(*results)
    result = dict(zip(outputs, results))
    return (
        result["layer_out"],
        result["grad_tokens"],
        result["project_out"].transpose(1, 0, 2),
        result["output_out"],
        result["up_out"],
        result["down_out"],
        result["gains_out"],
        result["bias_out"],
        result["hidden_out"],
    )


def gelu_exact(values):
    return jax.nn.gelu(values, approximate=False)


def layer_norm(token_rows, gain, shift):
    average = jnp.mean(token_rows, axis=-1, keepdims=True)
    centred = token_rows - average
    variance = jnp.mean(centred * centred, axis=-1, keepdims=True)
    inverse = lax.rsqrt(variance + EPSILON)
    normed = centred * inverse
    return (normed * gain + shift, (normed, inverse))


def norm_back_saved(grad_rows, saved, gain):
    normed, inverse = saved
    grad_gain = jnp.sum(grad_rows * normed, axis=0)
    grad_shift = jnp.sum(grad_rows, axis=0)
    grad_normed = grad_rows * gain
    grad_input = inverse * (
        grad_normed
        - jnp.mean(grad_normed, axis=-1, keepdims=True)
        - normed * jnp.mean(grad_normed * normed, axis=-1, keepdims=True)
    )
    return (grad_input, grad_gain, grad_shift)


def split_heads(token_rows):
    return token_rows.reshape(token_rows.shape[0], token_rows.shape[1] // HEAD, HEAD)


def scatter_sum(partial_sum, axis_name, dimension):
    return lax.psum_scatter(
        partial_sum.astype(jnp.bfloat16), axis_name, scatter_dimension=dimension, tiled=True
    ).astype(jnp.float32)


def place_columns(partial_sum, column_block, total_width):
    full_rows = jnp.zeros(partial_sum.shape[:-1] + (total_width,), jnp.float32)
    return lax.dynamic_update_slice_in_dim(
        full_rows, partial_sum, column_block * partial_sum.shape[-1], partial_sum.ndim - 1
    )


def per_device(
    tokens,
    segments,
    cotangent,
    project_weight,
    output_weight,
    up_weight,
    down_weight,
    norm_gains,
    bias_rows,
    hidden_bias,
):
    tensor_rank = lax.axis_index("tensor")
    local_rows, model_width = tokens.shape
    seq_count, seq_length = segments.shape
    group_rows = seq_count * seq_length
    local_width = project_weight.shape[2]
    score_scale = HEAD ** (-0.5)
    block_rows = min(512, seq_length)
    per_sequence = seq_length // block_rows
    count_blocks = group_rows // block_rows
    block_ids = jnp.arange(count_blocks, dtype=jnp.int32)
    triple_full, output_full, upward_full, downward_full = (
        lax.all_gather(project_weight, "dp", axis=0, tiled=True),
        lax.all_gather(output_weight, "dp", axis=1, tiled=True),
        lax.all_gather(up_weight, "dp", axis=0, tiled=True),
        lax.all_gather(down_weight, "dp", axis=1, tiled=True),
    )
    local_hidden = upward_full.shape[1]
    triple_matrix = triple_full.reshape(model_width, 3 * local_width)
    gathered = lax.all_gather(tokens, "tensor", axis=0, tiled=True)
    head_bias = lax.dynamic_slice_in_dim(bias_rows, tensor_rank * local_width, local_width, 1)
    projected = jnp.dot(gathered, triple_matrix, preferred_element_type=jnp.float32).reshape(
        group_rows, 3, local_width
    )
    queries = (projected[:, 0] + head_bias[0]).astype(jnp.bfloat16)
    key_rows = projected[:, 1].astype(jnp.bfloat16)
    value_rows = (projected[:, 2] + head_bias[1]).astype(jnp.bfloat16)

    def block_parts(block_index):
        sequence = block_index // per_sequence
        row_start = block_index * block_rows
        seq_start = sequence * seq_length
        query_block = split_heads(lax.dynamic_slice_in_dim(queries, row_start, block_rows, 0))
        key_block = split_heads(key_rows)
        value_block = split_heads(value_rows)
        seq_ids = lax.dynamic_index_in_dim(segments, sequence, 0, keepdims=False)
        query_ids = lax.dynamic_slice_in_dim(seq_ids, row_start - seq_start, block_rows, 0)
        products = (
            jnp.einsum("qhd,khd->hqk", query_block, key_block, preferred_element_type=jnp.float32)
            * score_scale
        )
        scores = jnp.where((query_ids[:, None] == seq_ids[None, :])[None], products, NEGATIVE)
        return (row_start, query_block, key_block, value_block, scores)

    def forward_block(block_index):
        row_start, query_block, key_block, value_block, scores = block_parts(block_index)
        row_max = jnp.max(scores, axis=-1, keepdims=True)
        exponent = jnp.exp(scores - row_max)
        row_sum = jnp.sum(exponent, axis=-1, keepdims=True)
        weights_low = (exponent / row_sum).astype(jnp.bfloat16)
        mixed_block = jnp.einsum(
            "hqk,khd->qhd", weights_low, value_block, preferred_element_type=jnp.float32
        )
        log_total = row_max[:, :, 0] + jnp.log(row_sum[:, :, 0])
        return (mixed_block.reshape(block_rows, local_width).astype(jnp.bfloat16), log_total)

    mixed_blocks, log_totals = lax.map(forward_block, block_ids)
    mixed_rows = mixed_blocks.reshape(group_rows, local_width)
    branch_out = (
        scatter_sum(
            jnp.dot(mixed_rows, output_full, preferred_element_type=jnp.float32), "tensor", 0
        )
        + bias_rows[2]
    )
    first_out, first_saved = layer_norm(
        tokens.astype(jnp.float32) + branch_out, norm_gains[0], bias_rows[3]
    )
    first_gathered = lax.all_gather(first_out.astype(jnp.bfloat16), "tensor", axis=0, tiled=True)
    local_bias = lax.dynamic_slice_in_dim(hidden_bias, tensor_rank * local_hidden, local_hidden, 0)
    upper_rows = (
        jnp.dot(first_gathered, upward_full, preferred_element_type=jnp.float32) + local_bias
    )
    hidden_full, gelu_back = jax.vjp(gelu_exact, upper_rows)
    hidden_rows = hidden_full.astype(jnp.bfloat16)
    second_out = (
        scatter_sum(
            jnp.dot(hidden_rows, downward_full, preferred_element_type=jnp.float32), "tensor", 0
        )
        + bias_rows[4]
    )
    layer_out, second_saved = layer_norm(first_out + second_out, norm_gains[1], bias_rows[5])
    reloaded = (
        lax.all_gather(project_weight, "dp", axis=0, tiled=True),
        lax.all_gather(output_weight, "dp", axis=1, tiled=True),
        lax.all_gather(up_weight, "dp", axis=0, tiled=True),
        lax.all_gather(down_weight, "dp", axis=1, tiled=True),
    )
    back_triple = reloaded[0].reshape(model_width, 3 * local_width)
    back_output, back_upward, back_downward = (reloaded[1], reloaded[2], reloaded[3])
    grad_layer = cotangent.astype(jnp.float32)
    grad_second_in, grad_gain_two, grad_shift_two = norm_back_saved(
        grad_layer, second_saved, norm_gains[1]
    )
    grad_second = grad_second_in.astype(jnp.bfloat16)
    grad_second_all = lax.all_gather(grad_second, "tensor", axis=0, tiled=True)
    grad_down_part = jnp.einsum(
        "tf,td->fd", hidden_rows, grad_second_all, preferred_element_type=jnp.float32
    )
    grad_hidden = jnp.einsum(
        "td,fd->tf", grad_second_all, back_downward, preferred_element_type=jnp.float32
    )
    grad_upper = gelu_back(grad_hidden)[0].astype(jnp.bfloat16)
    grad_up_part = jnp.einsum(
        "td,tf->df", first_gathered, grad_upper, preferred_element_type=jnp.float32
    )
    grad_first = (
        scatter_sum(
            jnp.einsum("tf,df->td", grad_upper, back_upward, preferred_element_type=jnp.float32),
            "tensor",
            0,
        )
        + grad_second_in
    )
    grad_first_in, grad_gain_one, grad_shift_one = norm_back_saved(grad_first, first_saved, norm_gains[0])
    grad_branch = grad_first_in.astype(jnp.bfloat16)
    grad_branch_all = lax.all_gather(grad_branch, "tensor", axis=0, tiled=True)
    grad_output_part = jnp.einsum(
        "tc,td->cd", mixed_rows, grad_branch_all, preferred_element_type=jnp.float32
    )
    grad_mixed = jnp.einsum(
        "td,cd->tc", grad_branch_all, back_output, preferred_element_type=jnp.float32
    ).astype(jnp.bfloat16)

    def backward_block(block_index):
        row_start, query_block, key_block, value_block, scores = block_parts(block_index)
        weights_full = jnp.exp(scores - log_totals[block_index][:, :, None])
        grad_mixed_block = split_heads(
            lax.dynamic_slice_in_dim(grad_mixed, row_start, block_rows, 0)
        )
        grad_weights = jnp.einsum(
            "qhd,khd->hqk", grad_mixed_block, value_block, preferred_element_type=jnp.float32
        )
        row_dot = jnp.sum(weights_full * grad_weights, axis=-1, keepdims=True)
        grad_scores = (weights_full * (grad_weights - row_dot)).astype(jnp.bfloat16)
        grad_query = (
            jnp.einsum("hqk,khd->qhd", grad_scores, key_block, preferred_element_type=jnp.float32)
            * score_scale
        )
        grad_key = (
            jnp.einsum("hqk,qhd->khd", grad_scores, query_block, preferred_element_type=jnp.float32)
            * score_scale
        )
        grad_value = jnp.einsum(
            "hqk,qhd->khd",
            weights_full.astype(jnp.bfloat16),
            grad_mixed_block,
            preferred_element_type=jnp.float32,
        )
        return (
            grad_query.reshape(block_rows, local_width),
            grad_key.reshape(seq_length, local_width),
            grad_value.reshape(seq_length, local_width),
        )

    query_blocks, key_blocks, value_blocks = lax.map(backward_block, block_ids)
    grad_queries = query_blocks.reshape(group_rows, local_width)
    grad_keys = (
        key_blocks.reshape(seq_count, per_sequence, seq_length, local_width)
        .sum(axis=1)
        .reshape(group_rows, local_width)
    )
    grad_values = (
        value_blocks.reshape(seq_count, per_sequence, seq_length, local_width)
        .sum(axis=1)
        .reshape(group_rows, local_width)
    )
    grad_projected = jnp.stack((grad_queries, grad_keys, grad_values), axis=1).astype(jnp.bfloat16)
    grad_project_part = jnp.einsum(
        "te,tsc->esc", gathered, grad_projected, preferred_element_type=jnp.float32
    )
    grad_matrix = grad_projected.reshape(group_rows, 3 * local_width)
    grad_tokens = (
        lax.psum_scatter(
            jnp.einsum(
                "tc,ec->te", grad_matrix, back_triple, preferred_element_type=jnp.float32
            ).astype(jnp.bfloat16),
            "tensor",
            scatter_dimension=0,
            tiled=True,
        ).astype(jnp.float32)
        + grad_first_in
    )
    grad_project, grad_output, grad_up, grad_down = (
        scatter_sum(grad_project_part, "dp", 0),
        scatter_sum(grad_output_part, "dp", 1),
        scatter_sum(grad_up_part, "dp", 0),
        scatter_sum(grad_down_part, "dp", 1),
    )
    head_terms = place_columns(
        jnp.stack(
            (
                jnp.sum(grad_projected[:, 0], axis=0, dtype=jnp.float32),
                jnp.sum(grad_projected[:, 2], axis=0, dtype=jnp.float32),
            )
        ),
        tensor_rank,
        model_width,
    )
    shared_terms = jnp.stack(
        (
            jnp.sum(grad_branch, axis=0, dtype=jnp.float32),
            grad_shift_one,
            jnp.sum(grad_second, axis=0, dtype=jnp.float32),
            grad_shift_two,
        )
    )
    bias_terms = jnp.concatenate((head_terms, shared_terms), axis=0)
    gain_terms = jnp.stack((grad_gain_one, grad_gain_two))
    hidden_terms = place_columns(
        jnp.sum(grad_upper, axis=0, dtype=jnp.float32), tensor_rank, hidden_bias.shape[0]
    )
    grad_gains, grad_bias_rows, grad_hidden_bias = lax.psum(
        (gain_terms, bias_terms, hidden_terms), ("dp", "tensor")
    )
    return (
        layer_out.astype(jnp.bfloat16),
        grad_tokens,
        grad_project,
        grad_output,
        grad_up,
        grad_down,
        grad_gains,
        grad_bias_rows,
        grad_hidden_bias,
    )


def solution(mesh):
    fits = mesh.shape["dp"] == 2 * LINES and mesh.shape["tensor"] == 4
    placed = (
        P(("dp", "tensor"), None),
        P("dp", None),
        P(("dp", "tensor"), None),
        P("dp", None, "tensor"),
        P("tensor", "dp"),
        P("dp", "tensor"),
        P("tensor", "dp"),
        P(),
        P(),
        P(),
    )
    return jax.shard_map(
        per_device_kernel if fits else per_device,
        mesh=mesh,
        in_specs=placed,
        out_specs=(
            P(("dp", "tensor"), None),
            P(("dp", "tensor"), None),
            P("dp", None, "tensor"),
            P("tensor", "dp"),
            P("dp", "tensor"),
            P("tensor", "dp"),
            P(),
            P(),
            P(),
        ),
        check_vma=False,
    )
```

```python
import functools
import types

import jax
import jax.numpy as jnp
from jax import lax
from jax.experimental import pallas as pl
from jax.experimental.pallas import tpu as pltpu
from jax.sharding import PartitionSpec as P

HEAD = 64
EPSILON = 1e-05
NEGATIVE = -1e30
MESH = pl.DeviceIdType.MESH
LINES = 4
CORE, ACROSS, FAR = 1, 2, 3
HALVES = 2
CHUNK = 16
NORM = 64
ORDER = (3, 2, 1, 0)
VMEM_BYTES = 60 << 20


def remote(src, dst, send_sem, recv_sem, target):
    return pltpu.make_async_remote_copy(
        src_ref=src,
        dst_ref=dst,
        send_sem=send_sem,
        recv_sem=recv_sem,
        device_id=target,
        device_id_type=MESH,
    )


def position():
    return lax.axis_index("dp"), lax.axis_index("tensor")


def greet():
    dp, tensor = position()
    barrier = pltpu.get_barrier_semaphore()
    others = [(dp ^ step, tensor) for step in (1, 2, 4, 6)]
    others += [(dp, tensor ^ step) for step in (CORE, ACROSS)]
    for target in others:
        pl.semaphore_signal(barrier, inc=1, device_id=target, device_id_type=MESH)
    pl.semaphore_wait(barrier, len(others))


def row_piece(ref, index, size):
    return ref.at[pl.ds(pl.multiple_of(index * size, size), size), :]


def column_piece(ref, index, size):
    return ref.at[:, pl.ds(pl.multiple_of(index * size, size), size)]


class LineGather:
    def __init__(self, own, full, piece, send_sem, recv_sem, local_sem):
        self.own, self.full, self.piece = own, full, piece
        self.send_sem, self.recv_sem, self.local_sem = send_sem, recv_sem, local_sem
        self.dp, self.tensor = position()
        self.line, self.side = self.dp // 2, self.dp % 2
        self.targets = (
            (self.dp + 2, self.tensor),
            (self.dp - 2, self.tensor),
            (self.dp ^ 1, self.tensor),
        )

    def copy(self, index, way, src=None):
        view = self.piece(self.full, index)
        return remote(
            view if src is None else src,
            view,
            self.send_sem.at[(LINES - 1) * way - way % 2 + index // 2],
            self.recv_sem.at[index],
            self.targets[way],
        )

    def local(self):
        return pltpu.make_async_copy(self.own, self.piece(self.full, self.dp), self.local_sem)

    def start_along(self):
        self.local().start()

        @pl.when(self.line < LINES - 1)
        def _():
            self.copy(self.dp, 0, self.own).start()

        @pl.when(self.line > 0)
        def _():
            self.copy(self.dp, 1, self.own).start()

    def start_across(self):
        self.copy(self.dp, 2, self.own).start()

    def step_along(self, distance):
        @pl.when(self.line >= distance)
        def _():
            self.copy(self.dp - 2 * distance, 0).wait_recv()

            @pl.when(self.line < LINES - 1)
            def _():
                self.copy(self.dp - 2 * distance, 0).start()

        @pl.when(self.line + distance < LINES)
        def _():
            self.copy(self.dp + 2 * distance, 1).wait_recv()

            @pl.when(self.line > 0)
            def _():
                self.copy(self.dp + 2 * distance, 1).start()

    def step_across(self, distance):
        @pl.when(self.line >= distance)
        def _():
            self.copy(self.dp - 2 * distance, 2).start()

        @pl.when(self.line + distance < LINES)
        def _():
            self.copy(self.dp + 2 * distance, 2).start()

    def step(self, distance):
        self.step_along(distance)
        self.step_across(distance)

    def arrive_block(self, at):
        self.copy(self.dp ^ (2 * at) ^ 1, 2).wait_recv()

    def arrive(self):
        self.local().wait()
        for line in range(LINES):
            self.copy(2 * line + 1 - self.side, 2).wait_recv()

    def finish(self):
        for line in range(LINES):
            index = 2 * line + self.side
            self.copy(index, 2).wait_send()

            @pl.when((self.line < LINES - 1) & (line <= self.line))
            def _():
                self.copy(index, 0).wait_send()

            @pl.when((self.line > 0) & (line >= self.line))
            def _():
                self.copy(index, 1).wait_send()


class RowGather:
    def __init__(self, full, rows, send_sem, recv_sem):
        self.full, self.rows = full, rows
        self.send_sem, self.recv_sem = send_sem, recv_sem
        self.dp, self.tensor = position()

    def view(self, rank, half=None):
        if half is None:
            return row_piece(self.full, rank, self.rows)
        return row_piece(self.full, rank * HALVES + half, self.rows // HALVES)

    def near(self, rank):
        view = self.view(rank)
        target = (self.dp, self.tensor ^ CORE)
        return remote(view, view, self.send_sem.at[0], self.recv_sem.at[0], target)

    def across(self, rank, half):
        view, slot = self.view(rank, half), 1 + half
        target = (self.dp, self.tensor ^ ACROSS)
        return remote(view, view, self.send_sem.at[slot], self.recv_sem.at[slot], target)

    def far(self, rank, half):
        view, slot = self.view(rank, half), 1 + HALVES + half
        target = (self.dp, self.tensor ^ CORE)
        return remote(view, view, self.send_sem.at[slot], self.recv_sem.at[slot], target)

    def start_half(self, half):
        self.across(self.tensor, half).start()

    def start_near(self):
        self.near(self.tensor).start()

    def start(self):
        for half in range(HALVES):
            self.start_half(half)
        self.start_near()

    def wait_near(self):
        self.near(self.tensor ^ CORE).wait_recv()

    def wait_across(self, half):
        self.across(self.tensor ^ ACROSS, half).wait_recv()
        self.far(self.tensor ^ ACROSS, half).start()

    def wait_far(self, half):
        self.far(self.tensor ^ FAR, half).wait_recv()

    def finish(self):
        self.near(self.tensor).wait_send()
        for half in range(HALVES):
            self.across(self.tensor, half).wait_send()
            self.far(self.tensor ^ ACROSS, half).wait_send()


class RowScatter:
    def __init__(self, near_out, near_in, across_out, across_in, send_sem, recv_sem):
        self.near_out, self.near_in = near_out, near_in
        self.across_out, self.across_in = across_out, across_in
        self.send_sem, self.recv_sem = send_sem, recv_sem
        self.dp, self.tensor = position()

    def near(self, slot):
        return remote(
            self.near_out.at[slot],
            self.near_in.at[slot],
            self.send_sem.at[slot],
            self.recv_sem.at[slot],
            (self.dp, self.tensor ^ CORE),
        )

    def across(self, half):
        rows = self.across_in.shape[0] // HALVES
        return remote(
            row_piece(self.across_out, half, rows),
            row_piece(self.across_in, half, rows),
            self.send_sem.at[2 * HALVES + half],
            self.recv_sem.at[2 * HALVES + half],
            (self.dp, self.tensor ^ ACROSS),
        )

    def give_far(self, half, partial):
        self.near_out[half] = partial.astype(jnp.bfloat16)
        self.near(half).start()

    def give_across(self, half, partial):
        self.near(half).wait_recv()
        rows = partial.shape[0]
        total = partial + self.near_in[half].astype(jnp.float32)
        row_piece(self.across_out, half, rows)[...] = total.astype(jnp.bfloat16)
        self.across(half).start()

    def give_near(self, half, partial):
        self.near_out[HALVES + half] = partial.astype(jnp.bfloat16)
        self.near(HALVES + half).start()

    def take(self, half, partial):
        self.near(HALVES + half).wait_recv()
        rows = partial.shape[0]
        total = partial + self.near_in[HALVES + half].astype(jnp.float32)
        self.across(half).wait_recv()
        return total + row_piece(self.across_in, half, rows)[...].astype(jnp.float32)

    def finish(self):
        for slot in range(2 * HALVES):
            self.near(slot).wait_send()
        for half in range(HALVES):
            self.across(half).wait_send()


def dot(left, right):
    return jnp.dot(left, right, preferred_element_type=jnp.float32)


def dot_nt(left, right):
    return lax.dot_general(left, right, (((1,), (1,)), ((), ())), preferred_element_type=jnp.float32)


def dot_tn(left, right):
    return lax.dot_general(left, right, (((0,), (0,)), ((), ())), preferred_element_type=jnp.float32)


def normalize(rows):
    centred = rows - jnp.mean(rows, axis=-1, keepdims=True)
    inverse = lax.rsqrt(jnp.mean(centred * centred, axis=-1, keepdims=True) + EPSILON)
    return centred * inverse, inverse


def norm_back(grad, normed, inverse):
    average = jnp.mean(grad, axis=-1, keepdims=True)
    along = jnp.mean(grad * normed, axis=-1, keepdims=True)
    return inverse * (grad - average - normed * along)


class PairGather:
    def __init__(self, own, full, piece, pair, send_sem, recv_sem, local_sem):
        self.own, self.full, self.piece, self.pair = own, full, piece, pair
        self.send_sem, self.recv_sem, self.local_sem = send_sem, recv_sem, local_sem
        self.dp, self.tensor = position()
        self.line = self.dp // 2

    def local(self):
        return pltpu.make_async_copy(self.own, self.piece(self.full, self.dp), self.local_sem)

    def across(self):
        return remote(
            self.own,
            self.piece(self.full, self.dp),
            self.send_sem.at[0],
            self.recv_sem.at[LINES],
            (self.dp ^ 1, self.tensor),
        )

    def along(self, line, way):
        view = self.pair(self.full, line)
        return remote(
            view,
            view,
            self.send_sem.at[1 + way * 2 + line],
            self.recv_sem.at[line],
            (self.dp + 2 - 4 * way, self.tensor),
        )

    def start(self):
        self.local().start()
        self.across().start()

    def begin(self):
        self.local().wait()
        self.across().wait_recv()

        @pl.when(self.line < LINES - 1)
        def _():
            self.along(self.line, 0).start()

        @pl.when(self.line > 0)
        def _():
            self.along(self.line, 1).start()

    def step(self, distance):
        @pl.when(self.line >= distance)
        def _():
            self.along(self.line - distance, 0).wait_recv()

            @pl.when(self.line < LINES - 1)
            def _():
                self.along(self.line - distance, 0).start()

        @pl.when(self.line + distance < LINES)
        def _():
            self.along(self.line + distance, 1).wait_recv()

            @pl.when(self.line > 0)
            def _():
                self.along(self.line + distance, 1).start()

    def finish(self):
        self.across().wait_send()
        for line in range(LINES):

            @pl.when((self.line < LINES - 1) & (line <= self.line))
            def _():
                self.along(line, 0).wait_send()

            @pl.when((self.line > 0) & (line >= self.line))
            def _():
                self.along(line, 1).wait_send()


class LineFirstScatter:
    def __init__(self, partial, piece, line_in, across_out, across_in, send_sem, recv_sem):
        self.partial, self.piece, self.line_in = partial, piece, line_in
        self.across_out, self.across_in = across_out, across_in
        self.send_sem, self.recv_sem = send_sem, recv_sem
        self.dp, self.tensor = position()

    def view(self, step):
        return self.piece(self.partial, (self.dp // 2) ^ step)

    def along(self, step):
        return remote(
            self.view(step),
            self.line_in.at[step // 2 if step != 2 else 2],
            self.send_sem.at[step],
            self.recv_sem.at[step],
            (self.dp ^ (2 if step != 2 else 4), self.tensor),
        )

    def across(self):
        return remote(
            self.across_out,
            self.across_in,
            self.send_sem.at[0],
            self.recv_sem.at[0],
            (self.dp ^ 1, self.tensor),
        )

    def start(self):
        self.along(3).start()

    def relay(self):
        self.along(3).wait_recv()
        total = self.view(2)[...].astype(jnp.float32) + self.line_in[1].astype(jnp.float32)
        self.view(2)[...] = total.astype(jnp.bfloat16)
        self.along(2).start()
        self.along(1).start()

    def turn(self, result):
        total = self.view(0)[...].astype(jnp.float32)
        for step, slot in ((1, 0), (2, 2)):
            self.along(step).wait_recv()
            total = total + self.line_in[slot].astype(jnp.float32)
        first, second = jnp.split(total, 2, 0 if result.shape[1] == total.shape[1] else 1)
        even = self.dp % 2 == 0
        result[...] = jnp.where(even, first, second)
        self.across_out[...] = jnp.where(even, second, first).astype(jnp.bfloat16)
        self.across().start()

    def finish(self, result):
        self.across().wait_recv()
        result[...] += self.across_in[...].astype(jnp.float32)
        self.across().wait_send()
        for step in range(1, LINES):
            self.along(step).wait_send()


class DirectGather:
    def __init__(self, own, full, piece, send_sem, recv_sem, local_sem):
        self.own, self.full, self.piece = own, full, piece
        self.send_sem, self.recv_sem, self.local_sem = send_sem, recv_sem, local_sem
        self.dp, self.tensor = position()

    def along(self, step):
        there = self.dp ^ (2 * step)
        return remote(
            self.own,
            self.piece(self.full, self.dp),
            self.send_sem.at[step],
            self.recv_sem.at[step],
            (there, self.tensor),
        )

    def across(self, step, source=None):
        view = self.piece(self.full, self.dp ^ (2 * step))
        return remote(
            view if source is None else source,
            view,
            self.send_sem.at[LINES + step],
            self.recv_sem.at[LINES + step],
            (self.dp ^ 1, self.tensor),
        )

    def local(self):
        return pltpu.make_async_copy(self.own, self.piece(self.full, self.dp), self.local_sem)

    def start_along(self):
        self.local().start()
        for step in range(1, LINES):
            self.along(step).start()

    def start_across(self):
        self.across(0, self.own).start()

    def step(self, step):
        self.along(step).wait_recv()
        self.across(step).start()

    def arrive(self, step):
        self.across(step).wait_recv()

    def finish(self):
        for step in range(LINES):
            self.across(step).wait_send()
        for step in range(1, LINES):
            self.along(step).wait_send()


class ColumnScatter:
    def __init__(self, near_out, near_in, across_out, across_in, send_sem, recv_sem):
        self.near_out, self.near_in = near_out, near_in
        self.across_out, self.across_in = across_out, across_in
        self.send_sem, self.recv_sem = send_sem, recv_sem
        self.dp, self.tensor = position()

    def near(self, slot):
        return remote(
            self.near_out.at[slot],
            self.near_in.at[slot],
            self.send_sem.at[slot],
            self.recv_sem.at[slot],
            (self.dp, self.tensor ^ CORE),
        )

    def across(self, at):
        return remote(
            self.across_out.at[at],
            self.across_in.at[at],
            self.send_sem.at[2 * LINES + at],
            self.recv_sem.at[2 * LINES + at],
            (self.dp, self.tensor ^ ACROSS),
        )

    def give_far(self, at, partial):
        self.near_out[at] = partial.astype(jnp.bfloat16)
        self.near(at).start()

    def give_near(self, at, partial):
        self.near_out[LINES + at] = partial.astype(jnp.bfloat16)
        self.near(LINES + at).start()

    def give_across(self, at, partial):
        self.near(at).wait_recv()
        total = partial + self.near_in[at].astype(jnp.float32)
        self.across_out[at] = total.astype(jnp.bfloat16)
        self.across(at).start()

    def take(self, at, partial):
        self.near(LINES + at).wait_recv()
        total = partial + self.near_in[LINES + at].astype(jnp.float32)
        self.across(at).wait_recv()
        return total + self.across_in[at].astype(jnp.float32)

    def finish(self):
        for slot in range(2 * LINES):
            self.near(slot).wait_send()
        for at in range(LINES):
            self.across(at).wait_send()


class LineScatter:
    def __init__(self, partial, piece, side_in, line_in, send_sem, recv_sem):
        self.partial, self.piece, self.side_in, self.line_in = partial, piece, side_in, line_in
        self.send_sem, self.recv_sem = send_sem, recv_sem
        self.dp, self.tensor = position()

    def view(self, step):
        return self.piece(self.partial, self.dp ^ (2 * step))

    def across(self, step):
        return remote(
            self.piece(self.partial, self.dp ^ (2 * step) ^ 1),
            self.side_in.at[step],
            self.send_sem.at[step],
            self.recv_sem.at[step],
            (self.dp ^ 1, self.tensor),
        )

    def along(self, step):
        return remote(
            self.view(step),
            self.line_in.at[step // 2 if step != 2 else 2],
            self.send_sem.at[LINES + step],
            self.recv_sem.at[LINES + step],
            (self.dp ^ (2 if step != 2 else 4), self.tensor),
        )

    def start(self, order=ORDER):
        for step in order:
            self.across(step).start()

    def total(self, step):
        self.across(step).wait_recv()
        return self.view(step)[...].astype(jnp.float32) + self.side_in[step].astype(jnp.float32)

    def relay(self, step):
        total = self.total(step)
        if step == 2:
            self.along(3).wait_recv()
            total = total + self.line_in[1].astype(jnp.float32)
        self.view(step)[...] = total.astype(jnp.bfloat16)
        self.along(step).start()

    def finish(self, result):
        total = self.total(0)
        self.along(1).wait_recv()
        total = total + self.line_in[0].astype(jnp.float32)
        self.along(2).wait_recv()
        result[...] = total + self.line_in[2].astype(jnp.float32)
        for step in range(LINES):
            self.across(step).wait_send()
        for step in range(1, LINES):
            self.along(step).wait_send()


class Total:
    def __init__(self, held, arrived, send_sem, recv_sem):
        self.held, self.arrived, self.send_sem, self.recv_sem = held, arrived, send_sem, recv_sem
        dp, tensor = position()
        self.targets = (
            (dp ^ 1, tensor),
            (dp ^ 2, tensor),
            (dp ^ 4, tensor),
            (dp, tensor ^ ACROSS),
            (dp, tensor ^ CORE),
        )

    def copy(self, step):
        return remote(
            self.held.at[step],
            self.arrived.at[step],
            self.send_sem.at[step],
            self.recv_sem.at[step],
            self.targets[step],
        )

    def start(self):
        self.copy(0).start()

    def step(self, step):
        self.copy(step).wait_recv()
        self.held[step + 1] = self.held[step] + self.arrived[step]
        if step + 1 < len(self.targets):
            self.copy(step + 1).start()

    def finish(self):
        for step in range(len(self.targets)):
            self.copy(step).wait_send()


def layer_kernel(names, rows, *refs):
    r = types.SimpleNamespace(**dict(zip(names, refs)))
    dp, tensor = position()
    bf16, f32 = jnp.bfloat16, jnp.float32
    half_rows = rows // HALVES
    local = r.queries.shape[1]
    piece = r.triple_own.shape[1]
    pairs = local // (2 * HEAD)
    length, hidden = r.hidden.shape
    near, across, far = tensor ^ CORE, tensor ^ ACROSS, tensor ^ FAR

    def of_rows(ref, index):
        return row_piece(ref, index, piece)

    def of_columns(ref, index):
        return column_piece(ref, index, piece)

    def of_stack(ref, index):
        return ref.at[:, pl.ds(pl.multiple_of(index * piece, piece), piece), :]

    def of_half_stack(half):
        size = piece // HALVES

        def view(ref, index):
            return ref.at[:, pl.ds(pl.multiple_of(index * piece + half * size, size), size), :]

        return view, r.triple_own.at[:, half * size : (half + 1) * size, :]

    def block(rank, size=rows):
        return pl.ds(pl.multiple_of(rank * size, size), size)

    def split(partial):
        return [partial[half * half_rows : (half + 1) * half_rows] for half in range(HALVES)]

    def part_of(half):
        return slice(half * half_rows, (half + 1) * half_rows)

    (view_a, own_a), (view_b, own_b) = of_half_stack(0), of_half_stack(1)
    lines = [
        kind(own, full, view, r.line_send.at[at], r.line_recv.at[at], r.line_local.at[at])
        for at, (kind, own, full, view) in enumerate(
            (
                (LineGather, own_a, r.triple, view_a),
                (LineGather, own_b, r.triple, view_b),
                (DirectGather, r.output_own, r.output, of_columns),
                (LineGather, r.up_own, r.up, of_rows),
                (LineGather, r.down_own.at[: hidden // 2, :], r.down.at[: hidden // 2, :], of_columns),
            )
        )
    ]
    *triple_lines, output_line, up_line, down_line = lines

    def of_both(ref, index):
        return column_piece(ref, index, 2 * piece)

    rest_line = PairGather(
        r.down_own.at[hidden // 2 :, :],
        r.down.at[hidden // 2 :, :],
        of_columns,
        of_both,
        r.pair_send,
        r.pair_recv,
        r.pair_local,
    )
    sums = [
        LineScatter(partial, view, side, along, r.part_send.at[at], r.part_recv.at[at])
        for at, (partial, view, side, along) in enumerate(
            (
                (r.grad_project, of_stack, r.project_side, r.project_line),
                (r.grad_output, of_columns, r.output_side, r.output_line),
                (r.grad_up, of_rows, r.up_side, r.up_line),
                (r.grad_down.at[: hidden // 2, :], of_columns, r.down_side, r.down_line),
            )
        )
    ]
    project_sum, output_sum, up_sum, down_sum = sums

    rest_sum = LineFirstScatter(
        r.grad_down.at[hidden // 2 :, :],
        of_both,
        r.rest_line,
        r.rest_out,
        r.rest_in,
        r.rest_send.at[0],
        r.rest_recv.at[0],
    )
    down_top, down_rest = r.down_sum.at[: hidden // 2, :], r.down_sum.at[hidden // 2 :, :]
    gathers = [
        RowGather(full, rows, r.row_send, r.row_recv)
        for full in (r.gathered, r.first_all, r.second_all, r.branch_all)
    ]
    row_buffers = r.near_out_a, r.near_in_a, r.across_out_a, r.across_in_a
    column_buffers = r.near_out_b, r.near_in_b, r.across_out_b, r.across_in_b
    scatters = [
        RowScatter(*row_buffers, r.row_sum_send, r.row_sum_recv),
        ColumnScatter(*column_buffers, r.column_sum_send, r.column_sum_recv),
    ] * 2
    total = Total(r.held_totals, r.arrived_totals, r.total_send, r.total_recv)

    def column_pair(at):
        return block((dp // 4) ^ at, 4 * piece)

    def give_halves(method, at, partial):
        for half in range(HALVES):
            method(at * HALVES + half, partial[part_of(half)])

    def keep_near(scatter, at, product):
        give_halves(scatter.give_near, at, product(near, column_pair(at)))
        r.kept[:, column_pair(at)] = product(tensor, column_pair(at))

    def take_columns(scatter, result, at):
        part, lanes = block(at % HALVES, half_rows), column_pair(at // HALVES)
        result[part, lanes] = scatter.take(at, r.kept[part, lanes])

    def chunks(size, start, body, step=CHUNK):
        @pl.loop(0, size // step)
        def _(chunk):
            offset = chunk * step
            body(
                pl.ds(pl.multiple_of(offset, step), step),
                pl.ds(pl.multiple_of(start + offset, step), step),
            )

    loads = [
        pltpu.make_async_copy(source, target, r.load_sem.at[at])
        for at, (source, target) in enumerate(
            (
                (r.tokens, gathers[0].view(tensor)),
                (r.segments, r.segment_row),
                (r.bias_from, r.bias_rows),
                (r.gains_from, r.norm_gains),
                (r.hidden_from.at[pl.ds(pl.multiple_of(tensor * hidden, hidden), hidden)], r.hidden_bias),
                (r.cotangent_from, r.cotangent),
            )
        )
    ]
    for load in loads:
        load.start()
    greet()
    for line in triple_lines:
        line.start_along()
        line.start_across()
    loads[0].wait()
    gathers[0].start()
    for line in triple_lines:
        line.step(1)
    loads[1].wait()
    numbers = r.segment_row[...].astype(f32)
    r.segment_column[...] = jnp.broadcast_to(numbers, (8, numbers.shape[1])).T[:, :1]
    r.segment_row_f32[...] = numbers
    for line in triple_lines:
        line.step(2)
    gathers[0].wait_near()
    for half in range(HALVES):
        gathers[0].wait_across(half)
    for line in triple_lines:
        line.step(3)
    output_line.start_along()
    output_line.start_across()
    rest_line.start()
    up_line.start_along()
    down_line.start_along()
    for half in range(HALVES):
        gathers[0].wait_far(half)
    for line in triple_lines:
        line.arrive()
    for load in loads[2:]:
        load.wait()
    columns = pl.ds(pl.multiple_of(tensor * local, local), local)
    query_bias = r.bias_rows[0:1, columns]
    value_bias = r.bias_rows[1:2, columns]

    @pl.loop(0, 4)
    def _(index):
        here = block(index)
        left = r.gathered[here, :]
        query = (dot(left, r.triple[0]) + query_bias).astype(bf16)
        r.queries[here, :] = query * bf16(HEAD**-0.5)
        key = dot(left, r.triple[1])
        r.key_rows[here, :] = key.astype(bf16)
        r.key_turned[:, here] = key.T.astype(bf16)
        value = dot(left, r.triple[2]) + value_bias
        r.value_rows[here, :] = value.astype(bf16)
        r.value_turned[:, here] = value.T.astype(bf16)

    for step in range(1, LINES):
        output_line.step(step)
    up_line.start_across()

    def head_rows(head):
        return pl.ds(pl.multiple_of(head * HEAD, HEAD), HEAD)

    def attend(here, pair):
        lanes = block(pair, 2 * HEAD)
        query = r.queries[here, lanes]
        keys = r.key_rows[:, lanes]
        same = r.segment_column[...] == r.segment_row_f32[:, here]
        lane = lax.broadcasted_iota(jnp.int32, query.shape, 1)
        outs = []
        for side in range(2):
            scores = dot_nt(keys, jnp.where(lane // HEAD == side, query, bf16(0)))
            scores = jnp.where(same, scores, NEGATIVE)
            top = jnp.max(scores, axis=0, keepdims=True)
            exponent = jnp.exp(scores - top)
            mass = jnp.sum(exponent, axis=0, keepdims=True)
            weights = (exponent * (1.0 / mass)).astype(bf16)
            head = pair * 2 + side
            outs.append(dot(r.value_turned[head_rows(head), :], weights))
            r.log_totals[pl.ds(head, 1), here] = top + jnp.log(mass)
        r.mixed[here, lanes] = jnp.concatenate(outs, axis=0).T.astype(bf16)

    @pl.loop(0, 4 * pairs)
    def _(turn):
        rank, pair = tensor ^ (FAR - turn // pairs), turn % pairs
        here = block(rank)
        attend(here, pair)

        def give(rank, method):
            r.partial[...] = dot(r.mixed[block(rank), :], r.output[...])
            for half in range(HALVES):
                method(half, r.partial[part_of(half), :])

        def after(index):
            return pl.when(turn == index)

        @after(0)
        def _():
            up_line.step(1)

        @after(1)
        def _():
            rest_line.begin()

        @after(3)
        def _():
            output_line.local().wait()
            for step in range(LINES):
                output_line.arrive(step)
            give(far, scatters[0].give_far)
            give(across, scatters[0].give_across)

        @after(4)
        def _():
            up_line.step(2)
            down_line.step_along(1)

        @after(5)
        def _():
            give(near, scatters[0].give_near)

        @after(7)
        def _():
            rest_line.step(1)
            up_line.step(3)
            down_line.start_across()
            down_line.step_across(1)

    r.partial[...] = dot(r.mixed[block(tensor), :], r.output[...])
    gathers[0].finish()
    for half in range(HALVES):
        part = part_of(half)
        r.kept[part, :] = scatters[0].take(half, r.partial[part, :])

        def first_norm(_, here):
            own_rows = r.gathered[pl.ds(pl.multiple_of(tensor * rows + here.start, NORM), NORM), :]
            normed, inverse = normalize(own_rows.astype(f32) + r.kept[here, :] + r.bias_rows[2:3, :])
            r.normed_one[here, :] = normed
            r.inverse_one[here, :] = inverse
            first = normed * r.norm_gains[0:1, :] + r.bias_rows[3:4, :]
            into = pl.ds(pl.multiple_of(tensor * rows + here.start, NORM), NORM)
            r.first_all[into, :] = first.astype(bf16)

        chunks(half_rows, half * half_rows, first_norm, NORM)
        gathers[1].start_half(half)
    scatters[0].finish()

    gathers[1].start_near()
    r.sums[...] = jnp.zeros_like(r.sums)

    def extent(rank, half):
        size = rows if half is None else half_rows
        start = rank * rows + (0 if half is None else half * half_rows)
        return start, size, pl.ds(pl.multiple_of(start, size), size)

    def up_part(rank, half=None):
        start, size, here = extent(rank, half)
        r.upper[:size, :] = dot(r.first_all[here, :], r.up[...]) + r.hidden_bias[...].reshape(1, hidden)

        def body(part, into):
            value = r.upper[part, :]
            share = 0.5 + 0.5 * lax.erf(value * (0.5**0.5))
            r.hidden[into, :] = (value * share).astype(bf16)
            bell = jnp.exp(value * value * -0.5) * (2 * jnp.pi) ** -0.5
            r.slope[into, :] = share + value * bell

        chunks(size, start, body)

    def back_part(rank, half=None):
        start, size, here = extent(rank, half)
        r.upper[:size, :] = dot_nt(r.second_all[here, :], r.down[...])

        def body(part, into):
            low = (r.upper[part, :] * r.slope[into, :]).astype(bf16)
            r.upper_low[into, :] = low
            r.sums[6:7, :] += jnp.sum(low.astype(f32), axis=0, keepdims=True)

        chunks(size, start, body)
        r.partial[:size, :] = dot_nt(r.upper_low[here, :], r.up[...])

    down_line.step(2)
    up_line.arrive()

    @pl.loop(0, 2)
    def _(turn):
        @pl.when(turn == 1)
        def _():
            gathers[1].wait_near()
            down_line.step(3)
            rest_line.step(2)

        up_part(tensor ^ turn)

    def other_chip(gather, body):
        @pl.loop(0, 2 * HALVES)
        def _(turn):
            half, side = turn // 2, turn % 2

            @pl.when(side == 0)
            def _():
                gather.wait_across(half)

            body(half, side)

    def up_other(half, side):
        @pl.when(side == 1)
        def _():
            gathers[1].wait_far(half)

        up_part(tensor ^ (ACROSS + side), half)

    def down_part(rank, lanes):
        return dot(r.hidden[block(rank), :], r.down[:, lanes])

    def send_unit(at, half):
        def product(rank):
            return dot(r.hidden[extent(rank, half)[2], :], r.down[:, column_pair(at)])

        scatters[1].give_far(at * HALVES + half, product(far))
        scatters[1].give_across(at * HALVES + half, product(across))

    def up_and_send(half, side):
        up_other(half, side)

        @pl.when((side == 1) & (half == 0))
        def _():
            down_line.local().wait()
            down_line.arrive_block(0)
            down_line.arrive_block(1)
            send_unit(0, 0)

    other_chip(gathers[1], up_and_send)

    send_unit(0, 1)
    keep_near(scatters[1], 0, down_part)
    rest_line.step(3)
    down_line.arrive_block(2)
    down_line.arrive_block(3)
    send_unit(1, 0)
    send_unit(1, 1)
    keep_near(scatters[1], 1, down_part)

    def add_to(row, value):
        r.sums[row : row + 1, :] += jnp.sum(value, axis=0, keepdims=True)

    def second_norm(_, here):
        first = r.normed_one[here, :] * r.norm_gains[0:1, :] + r.bias_rows[3:4, :]
        normed, inverse = normalize(first + r.kept[here, :] + r.bias_rows[4:5, :])
        shifted = normed * r.norm_gains[1:2, :] + r.bias_rows[5:6, :]
        r.layer_low[here, :] = shifted.astype(bf16)
        grad = r.cotangent[here, :].astype(f32)
        add_to(5, grad * normed)
        add_to(3, grad)
        grad = norm_back(grad * r.norm_gains[1:2, :], normed, inverse)
        r.grad_rows[here, :] = grad
        low = grad.astype(bf16)
        add_to(2, low.astype(f32))
        r.second_all[pl.ds(pl.multiple_of(tensor * rows + here.start, NORM), NORM), :] = low

    gathers[1].finish()
    for half in range(HALVES):
        for at in range(2):
            take_columns(scatters[1], r.kept, at * HALVES + half)
        chunks(half_rows, half * half_rows, second_norm, NORM)
        gathers[2].start_half(half)
    saves = []

    def save(source, target):
        saves.append(pltpu.make_async_copy(source, target, r.save_sem.at[len(saves)]))
        saves[-1].start()

    save(r.layer_low, r.layer_out)
    scatters[1].finish()

    gathers[2].start_near()

    @pl.loop(0, 2)
    def _(turn):
        @pl.when(turn == 1)
        def _():
            gathers[2].wait_near()

        back_part(tensor ^ turn)

        @pl.when(turn == 0)
        def _():
            r.kept[...] = r.partial[...]

        @pl.when(turn == 1)
        def _():
            for half in range(HALVES):
                scatters[2].give_near(half, r.partial[part_of(half), :])

    def weight_grad(left, right, result, chip=None, add=False):
        depth = slice(None) if chip is None else block(chip, 2 * rows)

        @pl.loop(0, left.shape[1] // rows)
        def _(index):
            lanes = block(index)
            product = dot_tn(left[depth, lanes], right[depth, :])
            if add:
                product += result[lanes, :].astype(f32)
            result[lanes, :] = product.astype(bf16)

    weight_grad(r.hidden, r.second_all, r.grad_down, tensor // 2)

    def back_other(half, side):
        @pl.when((side == 1) & (half < HALVES - 1))
        def _():
            gathers[2].wait_far(half)

        @pl.when((side == 0) & (half == HALVES - 1))
        def _():
            gathers[2].wait_far(half)
            weight_grad(r.hidden, r.second_all, r.grad_down, 1 - tensor // 2, True)
            rest_sum.start()
            down_sum.start()

        back_part(tensor ^ (ACROSS + side), half)

        @pl.when(side == 0)
        def _():
            r.held[...] = r.partial[:half_rows, :]

        @pl.when(side == 1)
        def _():
            scatters[2].give_far(half, r.partial[:half_rows, :])
            scatters[2].give_across(half, r.held[...])

    other_chip(gathers[2], back_other)

    weight_grad(r.first_all, r.upper_low, r.grad_up)
    up_sum.start()

    def first_back(_, here):
        grad = r.grad_rows[here, :] + r.kept[here, :]
        normed = r.normed_one[here, :]
        add_to(4, grad * normed)
        add_to(1, grad)
        grad = norm_back(grad * r.norm_gains[0:1, :], normed, r.inverse_one[here, :])
        r.grad_rows[here, :] = grad
        low = grad.astype(bf16)
        add_to(0, low.astype(f32))
        r.branch_all[pl.ds(pl.multiple_of(tensor * rows + here.start, NORM), NORM), :] = low

    gathers[2].finish()
    for half in range(HALVES):
        part = part_of(half)
        r.kept[part, :] = scatters[2].take(half, r.kept[part, :])
        chunks(half_rows, half * half_rows, first_back, NORM)
        gathers[3].start_half(half)
        if half == 0:
            rest_sum.relay()
            down_sum.relay(3)
    scatters[2].finish()

    gathers[3].start_near()
    grad_keys, grad_values = r.slope.at[:, :local], r.slope.at[:, local : 2 * local]
    r.slope[:, : 2 * local] = jnp.zeros((r.slope.shape[0], 2 * local), f32)

    def attend_back(rank):
        here = block(rank)
        r.mixed_low[...] = dot_nt(r.branch_all[here, :], r.output[...]).astype(bf16)

        @pl.loop(0, pairs)
        def _(pair):
            lanes = block(pair, 2 * HEAD)
            query = r.queries[here, lanes]
            grad = r.mixed_low[:, lanes]
            keys = r.key_rows[:, lanes]
            values = r.value_rows[:, lanes]
            same = r.segment_column[...] == r.segment_row_f32[:, here]
            lane = lax.broadcasted_iota(jnp.int32, query.shape, 1)
            outs = []
            for side in range(2):
                mine = lane // HEAD == side
                head = pair * 2 + side
                query_here = jnp.where(mine, query, bf16(0))
                grad_here = jnp.where(mine, grad, bf16(0))
                scores = jnp.where(same, dot_nt(keys, query_here), NEGATIVE)
                weights = jnp.exp(scores - r.log_totals[pl.ds(head, 1), here])
                grad_weights = dot_nt(values, grad_here)
                along = jnp.sum(weights * grad_weights, axis=0, keepdims=True)
                grad_scores = (weights * (grad_weights - along)).astype(bf16)
                grad_keys[:, lanes] += dot(grad_scores, query_here)
                grad_values[:, lanes] += dot(weights.astype(bf16), grad_here)
                outs.append(dot(r.key_turned[head_rows(head), :], grad_scores))
            grad_query = jnp.concatenate(outs, axis=0).T * HEAD**-0.5
            r.projected_low[here, lanes] = grad_query.astype(bf16)

    @pl.loop(0, 4)
    def _(turn):
        @pl.when(turn == 1)
        def _():
            gathers[3].wait_near()

        @pl.when(turn == 2)
        def _():
            for half in range(HALVES):
                gathers[3].wait_across(half)

        @pl.when(turn == 3)
        def _():
            for half in range(HALVES):
                gathers[3].wait_far(half)
            r.grad_output[...] = dot_tn(r.mixed[...], r.branch_all[...]).astype(bf16)
            output_sum.start()

        attend_back(tensor ^ turn)

        @pl.when(turn == 0)
        def _():
            down_sum.relay(1)

        @pl.when(turn == 1)
        def _():
            up_sum.relay(3)

        @pl.when(turn == 2)
        def _():
            down_sum.relay(2)
            rest_sum.turn(down_rest)

    up_sum.relay(2)
    up_sum.relay(1)
    r.projected_low[:, local : 2 * local] = grad_keys[...].astype(bf16)
    r.projected_low[:, 2 * local :] = grad_values[...].astype(bf16)
    r.held_totals[0] = jnp.zeros(r.held_totals.shape[1:], f32)
    r.held_totals[0, 2:8, :] = r.sums[0:6, :]
    r.held_totals[0, pl.ds(8 + tensor, 1), :] = r.sums[6:7, :]
    shifts = dot(jnp.ones((CHUNK, length), bf16), r.projected_low[...])
    for row, at in ((0, 0), (1, 2)):
        r.held_totals[0, row : row + 1, columns] = shifts[:1, at * local : (at + 1) * local]
    total.start()

    @pl.loop(0, r.gathered.shape[1] // rows)
    def _(index):
        lanes = block(index)
        product = dot_tn(r.gathered[:, lanes], r.projected_low[...]).astype(bf16)
        for at in range(3):
            r.grad_project[at, lanes, :] = product[:, at * local : (at + 1) * local]

    project_sum.start()

    def token_part(rank, lanes):
        product = 0
        for part in range(3):
            left = r.projected_low[block(rank), part * local : (part + 1) * local]
            product += dot_nt(left, r.triple[part, lanes, :])
        return product

    @pl.loop(0, 2)
    def _(at):
        give_halves(scatters[3].give_far, at, token_part(far, column_pair(at)))
        give_halves(scatters[3].give_across, at, token_part(across, column_pair(at)))
        keep_near(scatters[3], at, token_part)

    total.step(0)
    output_sum.relay(3)
    project_sum.relay(3)
    down_sum.finish(down_top)
    rest_sum.finish(down_rest)
    save(r.down_sum, r.down_out)

    def take_tokens(at):
        part, lanes = part_of(at % HALVES), column_pair(at // HALVES)
        r.grad_rows[part, lanes] += scatters[3].take(at, r.kept[part, lanes])

    take_tokens(0)
    take_tokens(1)
    output_sum.relay(2)
    take_tokens(2)
    total.step(1)
    take_tokens(3)
    save(r.grad_rows, r.grad_tokens)
    gathers[3].finish()
    for each in lines + [rest_line]:
        each.finish()
    project_sum.relay(2)
    project_sum.relay(1)
    scatters[3].finish()
    up_sum.finish(r.up_sum)
    save(r.up_sum, r.up_out)
    total.step(2)
    output_sum.relay(1)
    total.step(3)
    project_sum.finish(r.project_sum)
    save(r.project_sum, r.project_out)
    total.step(4)
    r.bias_sum[...] = r.held_totals[5, 0:6, :]
    r.gains_sum[...] = r.held_totals[5, 6:8, :]
    for at in range(4):
        r.hidden_sum[at * hidden : (at + 1) * hidden] = r.held_totals[5, 8 + at, :]
    save(r.bias_sum, r.bias_out)
    save(r.gains_sum, r.gains_out)
    save(r.hidden_sum, r.hidden_out)
    output_sum.finish(r.output_sum)
    save(r.output_sum, r.output_out)
    total.finish()
    for each in saves:
        each.wait()


def copy_kernel(count, *refs):
    sources, targets, held, sem = refs[:count], refs[count : 2 * count], refs[2 * count : -1], refs[-1]
    copies_in = [pltpu.make_async_copy(*pair, sem.at[at]) for at, pair in enumerate(zip(sources, held))]
    copies_out = [
        pltpu.make_async_copy(*pair, sem.at[count + at]) for at, pair in enumerate(zip(held, targets))
    ]
    for copy in copies_in:
        copy.start()
    for arrived, copy in zip(copies_in, copies_out):
        arrived.wait()
        copy.start()
    for copy in copies_out:
        copy.wait()


def per_device_kernel(
    tokens,
    segments,
    cotangent,
    project_weight,
    output_weight,
    up_weight,
    down_weight,
    norm_gains,
    bias_rows,
    hidden_bias,
):
    rows, width = tokens.shape
    length = segments.shape[1]
    local_hidden = up_weight.shape[1]
    local = output_weight.shape[0]
    piece = project_weight.shape[0]
    bf16, f32 = jnp.bfloat16, jnp.float32
    inputs = dict(
        tokens=tokens,
        triple_own=project_weight.transpose(1, 0, 2),
        output_own=output_weight,
        up_own=up_weight,
        down_own=down_weight,
        segments=segments,
        cotangent_from=cotangent,
        gains_from=norm_gains,
        bias_from=bias_rows,
        hidden_from=hidden_bias,
    )
    shapes = dict(
        project=(3, piece, local),
        output=(local, piece),
        up=(piece, local_hidden),
        down=(local_hidden, piece),
    )
    outputs = dict(layer_out=((rows, width), bf16), grad_tokens=((rows, width), f32))
    outputs |= {name + "_out": (shape, f32) for name, shape in shapes.items()}
    outputs |= dict(
        gains_out=((2, width), f32),
        bias_out=((6, width), f32),
        hidden_out=(hidden_bias.shape, f32),
    )
    scratch = dict(
        segment_row=((1, length), jnp.int32),
        segment_row_f32=((1, length), f32),
        segment_column=((length, 1), f32),
        cotangent=((rows, width), bf16),
        norm_gains=(norm_gains.shape, f32),
        bias_rows=(bias_rows.shape, f32),
        hidden_bias=((local_hidden,), f32),
        layer_low=((rows, width), bf16),
        bias_sum=(bias_rows.shape, f32),
        gains_sum=(norm_gains.shape, f32),
        hidden_sum=(hidden_bias.shape, f32),
        partial=((rows, width), f32),
        gathered=((length, width), bf16),
        triple=((3, width, local), bf16),
        output=((local, width), bf16),
        up=((width, local_hidden), bf16),
        down=((local_hidden, width), bf16),
        queries=((length, local), bf16),
        key_rows=((length, local), bf16),
        value_rows=((length, local), bf16),
        key_turned=((local, length), bf16),
        value_turned=((local, length), bf16),
        mixed=((length, local), bf16),
        log_totals=((local // HEAD, length), f32),
        normed_one=((rows, width), f32),
        inverse_one=((rows, 1), f32),
        first_all=((length, width), bf16),
        hidden=((length, local_hidden), bf16),
        slope=((length, local_hidden), f32),
        second_all=((length, width), bf16),
        upper_low=((length, local_hidden), bf16),
        upper=((rows, local_hidden), f32),
        kept=((rows, width), f32),
        held=((rows // HALVES, width), f32),
        grad_rows=((rows, width), f32),
        sums=((8, width), f32),
        branch_all=((length, width), bf16),
        mixed_low=((rows, local), bf16),
        projected_low=((length, 3 * local), bf16),
        grad_project=((3, width, local), bf16),
        grad_output=((local, width), bf16),
        grad_up=((width, local_hidden), bf16),
        grad_down=((local_hidden, width), bf16),
        held_totals=((6, 16, width), f32),
        arrived_totals=((5, 16, width), f32),
    )
    for name, shape in shapes.items():
        scratch[name + "_sum"] = (shape, f32)
        moved = (local_hidden // 2, piece) if name == "down" else shape
        scratch[name + "_side"] = ((LINES,) + moved, bf16)
        scratch[name + "_line"] = ((LINES - 1,) + moved, bf16)
    scratch |= dict(
        rest_line=((LINES - 1, local_hidden // 2, 2 * piece), bf16),
        rest_out=((local_hidden // 2, piece), bf16),
        rest_in=((local_hidden // 2, piece), bf16),
    )
    for name in ("near_out_", "near_in_"):
        scratch[name + "a"] = ((2 * HALVES, rows // HALVES, width), bf16)
        scratch[name + "b"] = ((2 * LINES, rows // HALVES, 4 * piece), bf16)
    for name in ("across_out_", "across_in_"):
        scratch[name + "a"] = ((rows, width), bf16)
        scratch[name + "b"] = ((LINES, rows // HALVES, 4 * piece), bf16)
    semaphores = dict(
        line_send=(5, 3 * LINES - 2),
        line_recv=(5, 2 * LINES),
        line_local=(5,),
        part_send=(4, 2 * LINES),
        part_recv=(4, 2 * LINES),
        pair_send=(2 * LINES - 1,),
        pair_recv=(LINES + 1,),
        pair_local=(),
        rest_send=(1, LINES),
        rest_recv=(1, LINES),
        row_send=(1 + 2 * HALVES,),
        row_recv=(1 + 2 * HALVES,),
        row_sum_send=(3 * HALVES,),
        row_sum_recv=(3 * HALVES,),
        column_sum_send=(3 * LINES,),
        column_sum_recv=(3 * LINES,),
        total_send=(5,),
        total_recv=(5,),
        load_sem=(6,),
        save_sem=(9,),
    )
    names = [*inputs, *outputs, *scratch, *semaphores]
    hbm = pl.BlockSpec(memory_space=pltpu.HBM)
    results = pl.pallas_call(
        functools.partial(layer_kernel, names, rows),
        out_shape=[jax.ShapeDtypeStruct(*leaf) for leaf in outputs.values()],
        in_specs=[hbm] * len(inputs),
        out_specs=[hbm] * len(outputs),
        scratch_shapes=[pltpu.VMEM(*leaf) for leaf in scratch.values()]
        + [pltpu.SemaphoreType.DMA(shape) for shape in semaphores.values()],
        compiler_params=pltpu.CompilerParams(
            collective_id=0, has_side_effects=True, vmem_limit_bytes=VMEM_BYTES
        ),
        name="layer",
    )(*inputs.values())
    results = pl.pallas_call(
        functools.partial(copy_kernel, len(outputs)),
        out_shape=[jax.ShapeDtypeStruct(*leaf) for leaf in outputs.values()],
        in_specs=[hbm] * len(outputs),
        out_specs=[hbm] * len(outputs),
        scratch_shapes=[pltpu.VMEM(*leaf) for leaf in outputs.values()]
        + [pltpu.SemaphoreType.DMA((2 * len(outputs),))],
        name="copy",
    )(*results)
    result = dict(zip(outputs, results))
    return (
        result["layer_out"],
        result["grad_tokens"],
        result["project_out"].transpose(1, 0, 2),
        result["output_out"],
        result["up_out"],
        result["down_out"],
        result["gains_out"],
        result["bias_out"],
        result["hidden_out"],
    )


def gelu_exact(values):
    return jax.nn.gelu(values, approximate=False)


def layer_norm(token_rows, gain, shift):
    average = jnp.mean(token_rows, axis=-1, keepdims=True)
    centred = token_rows - average
    variance = jnp.mean(centred * centred, axis=-1, keepdims=True)
    inverse = lax.rsqrt(variance + EPSILON)
    normed = centred * inverse
    return (normed * gain + shift, (normed, inverse))


def norm_back_saved(grad_rows, saved, gain):
    normed, inverse = saved
    grad_gain = jnp.sum(grad_rows * normed, axis=0)
    grad_shift = jnp.sum(grad_rows, axis=0)
    grad_normed = grad_rows * gain
    grad_input = inverse * (
        grad_normed
        - jnp.mean(grad_normed, axis=-1, keepdims=True)
        - normed * jnp.mean(grad_normed * normed, axis=-1, keepdims=True)
    )
    return (grad_input, grad_gain, grad_shift)


def split_heads(token_rows):
    return token_rows.reshape(token_rows.shape[0], token_rows.shape[1] // HEAD, HEAD)


def scatter_sum(partial_sum, axis_name, dimension):
    return lax.psum_scatter(
        partial_sum.astype(jnp.bfloat16), axis_name, scatter_dimension=dimension, tiled=True
    ).astype(jnp.float32)


def place_columns(partial_sum, column_block, total_width):
    full_rows = jnp.zeros(partial_sum.shape[:-1] + (total_width,), jnp.float32)
    return lax.dynamic_update_slice_in_dim(
        full_rows, partial_sum, column_block * partial_sum.shape[-1], partial_sum.ndim - 1
    )


def per_device(
    tokens,
    segments,
    cotangent,
    project_weight,
    output_weight,
    up_weight,
    down_weight,
    norm_gains,
    bias_rows,
    hidden_bias,
):
    tensor_rank = lax.axis_index("tensor")
    local_rows, model_width = tokens.shape
    seq_count, seq_length = segments.shape
    group_rows = seq_count * seq_length
    local_width = project_weight.shape[2]
    score_scale = HEAD ** (-0.5)
    block_rows = min(512, seq_length)
    per_sequence = seq_length // block_rows
    count_blocks = group_rows // block_rows
    block_ids = jnp.arange(count_blocks, dtype=jnp.int32)
    triple_full, output_full, upward_full, downward_full = (
        lax.all_gather(project_weight, "dp", axis=0, tiled=True),
        lax.all_gather(output_weight, "dp", axis=1, tiled=True),
        lax.all_gather(up_weight, "dp", axis=0, tiled=True),
        lax.all_gather(down_weight, "dp", axis=1, tiled=True),
    )
    local_hidden = upward_full.shape[1]
    triple_matrix = triple_full.reshape(model_width, 3 * local_width)
    gathered = lax.all_gather(tokens, "tensor", axis=0, tiled=True)
    head_bias = lax.dynamic_slice_in_dim(bias_rows, tensor_rank * local_width, local_width, 1)
    projected = jnp.dot(gathered, triple_matrix, preferred_element_type=jnp.float32).reshape(
        group_rows, 3, local_width
    )
    queries = (projected[:, 0] + head_bias[0]).astype(jnp.bfloat16)
    key_rows = projected[:, 1].astype(jnp.bfloat16)
    value_rows = (projected[:, 2] + head_bias[1]).astype(jnp.bfloat16)

    def block_parts(block_index):
        sequence = block_index // per_sequence
        row_start = block_index * block_rows
        seq_start = sequence * seq_length
        query_block = split_heads(lax.dynamic_slice_in_dim(queries, row_start, block_rows, 0))
        key_block = split_heads(key_rows)
        value_block = split_heads(value_rows)
        seq_ids = lax.dynamic_index_in_dim(segments, sequence, 0, keepdims=False)
        query_ids = lax.dynamic_slice_in_dim(seq_ids, row_start - seq_start, block_rows, 0)
        products = (
            jnp.einsum("qhd,khd->hqk", query_block, key_block, preferred_element_type=jnp.float32)
            * score_scale
        )
        scores = jnp.where((query_ids[:, None] == seq_ids[None, :])[None], products, NEGATIVE)
        return (row_start, query_block, key_block, value_block, scores)

    def forward_block(block_index):
        row_start, query_block, key_block, value_block, scores = block_parts(block_index)
        row_max = jnp.max(scores, axis=-1, keepdims=True)
        exponent = jnp.exp(scores - row_max)
        row_sum = jnp.sum(exponent, axis=-1, keepdims=True)
        weights_low = (exponent / row_sum).astype(jnp.bfloat16)
        mixed_block = jnp.einsum(
            "hqk,khd->qhd", weights_low, value_block, preferred_element_type=jnp.float32
        )
        log_total = row_max[:, :, 0] + jnp.log(row_sum[:, :, 0])
        return (mixed_block.reshape(block_rows, local_width).astype(jnp.bfloat16), log_total)

    mixed_blocks, log_totals = lax.map(forward_block, block_ids)
    mixed_rows = mixed_blocks.reshape(group_rows, local_width)
    branch_out = (
        scatter_sum(
            jnp.dot(mixed_rows, output_full, preferred_element_type=jnp.float32), "tensor", 0
        )
        + bias_rows[2]
    )
    first_out, first_saved = layer_norm(
        tokens.astype(jnp.float32) + branch_out, norm_gains[0], bias_rows[3]
    )
    first_gathered = lax.all_gather(first_out.astype(jnp.bfloat16), "tensor", axis=0, tiled=True)
    local_bias = lax.dynamic_slice_in_dim(hidden_bias, tensor_rank * local_hidden, local_hidden, 0)
    upper_rows = (
        jnp.dot(first_gathered, upward_full, preferred_element_type=jnp.float32) + local_bias
    )
    hidden_full, gelu_back = jax.vjp(gelu_exact, upper_rows)
    hidden_rows = hidden_full.astype(jnp.bfloat16)
    second_out = (
        scatter_sum(
            jnp.dot(hidden_rows, downward_full, preferred_element_type=jnp.float32), "tensor", 0
        )
        + bias_rows[4]
    )
    layer_out, second_saved = layer_norm(first_out + second_out, norm_gains[1], bias_rows[5])
    reloaded = (
        lax.all_gather(project_weight, "dp", axis=0, tiled=True),
        lax.all_gather(output_weight, "dp", axis=1, tiled=True),
        lax.all_gather(up_weight, "dp", axis=0, tiled=True),
        lax.all_gather(down_weight, "dp", axis=1, tiled=True),
    )
    back_triple = reloaded[0].reshape(model_width, 3 * local_width)
    back_output, back_upward, back_downward = (reloaded[1], reloaded[2], reloaded[3])
    grad_layer = cotangent.astype(jnp.float32)
    grad_second_in, grad_gain_two, grad_shift_two = norm_back_saved(
        grad_layer, second_saved, norm_gains[1]
    )
    grad_second = grad_second_in.astype(jnp.bfloat16)
    grad_second_all = lax.all_gather(grad_second, "tensor", axis=0, tiled=True)
    grad_down_part = jnp.einsum(
        "tf,td->fd", hidden_rows, grad_second_all, preferred_element_type=jnp.float32
    )
    grad_hidden = jnp.einsum(
        "td,fd->tf", grad_second_all, back_downward, preferred_element_type=jnp.float32
    )
    grad_upper = gelu_back(grad_hidden)[0].astype(jnp.bfloat16)
    grad_up_part = jnp.einsum(
        "td,tf->df", first_gathered, grad_upper, preferred_element_type=jnp.float32
    )
    grad_first = (
        scatter_sum(
            jnp.einsum("tf,df->td", grad_upper, back_upward, preferred_element_type=jnp.float32),
            "tensor",
            0,
        )
        + grad_second_in
    )
    grad_first_in, grad_gain_one, grad_shift_one = norm_back_saved(grad_first, first_saved, norm_gains[0])
    grad_branch = grad_first_in.astype(jnp.bfloat16)
    grad_branch_all = lax.all_gather(grad_branch, "tensor", axis=0, tiled=True)
    grad_output_part = jnp.einsum(
        "tc,td->cd", mixed_rows, grad_branch_all, preferred_element_type=jnp.float32
    )
    grad_mixed = jnp.einsum(
        "td,cd->tc", grad_branch_all, back_output, preferred_element_type=jnp.float32
    ).astype(jnp.bfloat16)

    def backward_block(block_index):
        row_start, query_block, key_block, value_block, scores = block_parts(block_index)
        weights_full = jnp.exp(scores - log_totals[block_index][:, :, None])
        grad_mixed_block = split_heads(
            lax.dynamic_slice_in_dim(grad_mixed, row_start, block_rows, 0)
        )
        grad_weights = jnp.einsum(
            "qhd,khd->hqk", grad_mixed_block, value_block, preferred_element_type=jnp.float32
        )
        row_dot = jnp.sum(weights_full * grad_weights, axis=-1, keepdims=True)
        grad_scores = (weights_full * (grad_weights - row_dot)).astype(jnp.bfloat16)
        grad_query = (
            jnp.einsum("hqk,khd->qhd", grad_scores, key_block, preferred_element_type=jnp.float32)
            * score_scale
        )
        grad_key = (
            jnp.einsum("hqk,qhd->khd", grad_scores, query_block, preferred_element_type=jnp.float32)
            * score_scale
        )
        grad_value = jnp.einsum(
            "hqk,qhd->khd",
            weights_full.astype(jnp.bfloat16),
            grad_mixed_block,
            preferred_element_type=jnp.float32,
        )
        return (
            grad_query.reshape(block_rows, local_width),
            grad_key.reshape(seq_length, local_width),
            grad_value.reshape(seq_length, local_width),
        )

    query_blocks, key_blocks, value_blocks = lax.map(backward_block, block_ids)
    grad_queries = query_blocks.reshape(group_rows, local_width)
    grad_keys = (
        key_blocks.reshape(seq_count, per_sequence, seq_length, local_width)
        .sum(axis=1)
        .reshape(group_rows, local_width)
    )
    grad_values = (
        value_blocks.reshape(seq_count, per_sequence, seq_length, local_width)
        .sum(axis=1)
        .reshape(group_rows, local_width)
    )
    grad_projected = jnp.stack((grad_queries, grad_keys, grad_values), axis=1).astype(jnp.bfloat16)
    grad_project_part = jnp.einsum(
        "te,tsc->esc", gathered, grad_projected, preferred_element_type=jnp.float32
    )
    grad_matrix = grad_projected.reshape(group_rows, 3 * local_width)
    grad_tokens = (
        lax.psum_scatter(
            jnp.einsum(
                "tc,ec->te", grad_matrix, back_triple, preferred_element_type=jnp.float32
            ).astype(jnp.bfloat16),
            "tensor",
            scatter_dimension=0,
            tiled=True,
        ).astype(jnp.float32)
        + grad_first_in
    )
    grad_project, grad_output, grad_up, grad_down = (
        scatter_sum(grad_project_part, "dp", 0),
        scatter_sum(grad_output_part, "dp", 1),
        scatter_sum(grad_up_part, "dp", 0),
        scatter_sum(grad_down_part, "dp", 1),
    )
    head_terms = place_columns(
        jnp.stack(
            (
                jnp.sum(grad_projected[:, 0], axis=0, dtype=jnp.float32),
                jnp.sum(grad_projected[:, 2], axis=0, dtype=jnp.float32),
            )
        ),
        tensor_rank,
        model_width,
    )
    shared_terms = jnp.stack(
        (
            jnp.sum(grad_branch, axis=0, dtype=jnp.float32),
            grad_shift_one,
            jnp.sum(grad_second, axis=0, dtype=jnp.float32),
            grad_shift_two,
        )
    )
    bias_terms = jnp.concatenate((head_terms, shared_terms), axis=0)
    gain_terms = jnp.stack((grad_gain_one, grad_gain_two))
    hidden_terms = place_columns(
        jnp.sum(grad_upper, axis=0, dtype=jnp.float32), tensor_rank, hidden_bias.shape[0]
    )
    grad_gains, grad_bias_rows, grad_hidden_bias = lax.psum(
        (gain_terms, bias_terms, hidden_terms), ("dp", "tensor")
    )
    return (
        layer_out.astype(jnp.bfloat16),
        grad_tokens,
        grad_project,
        grad_output,
        grad_up,
        grad_down,
        grad_gains,
        grad_bias_rows,
        grad_hidden_bias,
    )


def solution(mesh):
    fits = mesh.shape["dp"] == 2 * LINES and mesh.shape["tensor"] == 4
    placed = (
        P(("dp", "tensor"), None),
        P("dp", None),
        P(("dp", "tensor"), None),
        P("dp", None, "tensor"),
        P("tensor", "dp"),
        P("dp", "tensor"),
        P("tensor", "dp"),
        P(),
        P(),
        P(),
    )
    return jax.shard_map(
        per_device_kernel if fits else per_device,
        mesh=mesh,
        in_specs=placed,
        out_specs=(
            P(("dp", "tensor"), None),
            P(("dp", "tensor"), None),
            P("dp", None, "tensor"),
            P("tensor", "dp"),
            P("dp", "tensor"),
            P("tensor", "dp"),
            P(),
            P(),
            P(),
        ),
        check_vma=False,
    )
```

```python
import functools
import types

import jax
import jax.numpy as jnp
from jax import lax
from jax.experimental import pallas as pl
from jax.experimental.pallas import tpu as pltpu
from jax.sharding import PartitionSpec as P

HEAD = 64
EPSILON = 1e-05
NEGATIVE = -1e30
MESH = pl.DeviceIdType.MESH
LINES = 4
CORE, ACROSS, FAR = 1, 2, 3
HALVES = 2
CHUNK = 16
NORM = 64
ORDER = (3, 2, 1, 0)
VMEM_BYTES = 60 << 20


def remote(src, dst, send_sem, recv_sem, target):
    return pltpu.make_async_remote_copy(
        src_ref=src,
        dst_ref=dst,
        send_sem=send_sem,
        recv_sem=recv_sem,
        device_id=target,
        device_id_type=MESH,
    )


def position():
    return lax.axis_index("dp"), lax.axis_index("tensor")


def greet():
    dp, tensor = position()
    barrier = pltpu.get_barrier_semaphore()
    others = [(dp ^ step, tensor) for step in (1, 2, 4, 6)]
    others += [(dp, tensor ^ step) for step in (CORE, ACROSS)]
    for target in others:
        pl.semaphore_signal(barrier, inc=1, device_id=target, device_id_type=MESH)
    pl.semaphore_wait(barrier, len(others))


def row_piece(ref, index, size):
    return ref.at[pl.ds(pl.multiple_of(index * size, size), size), :]


def column_piece(ref, index, size):
    return ref.at[:, pl.ds(pl.multiple_of(index * size, size), size)]


class LineGather:
    def __init__(self, own, full, piece, send_sem, recv_sem, local_sem):
        self.own, self.full, self.piece = own, full, piece
        self.send_sem, self.recv_sem, self.local_sem = send_sem, recv_sem, local_sem
        self.dp, self.tensor = position()
        self.line, self.side = self.dp // 2, self.dp % 2
        up = self.dp + jnp.where(self.line < LINES - 1, 2, -2)
        down = self.dp + jnp.where(self.line > 0, -2, 2)
        self.targets = (
            (up, self.tensor),
            (down, self.tensor),
            (self.dp ^ 1, self.tensor),
        )

    def copy(self, index, way, src=None):
        view = self.piece(self.full, index)
        return remote(
            view if src is None else src,
            view,
            self.send_sem.at[(LINES - 1) * way - way % 2 + index // 2],
            self.recv_sem.at[index],
            self.targets[way],
        )

    def local(self):
        return pltpu.make_async_copy(self.own, self.piece(self.full, self.dp), self.local_sem)

    def start_along(self):
        self.local().start()

        @pl.when(self.line < LINES - 1)
        def _():
            self.copy(self.dp, 0, self.own).start()

        @pl.when(self.line > 0)
        def _():
            self.copy(self.dp, 1, self.own).start()

    def start_across(self):
        self.copy(self.dp, 2, self.own).start()

    def step_along(self, distance):
        @pl.when(self.line >= distance)
        def _():
            self.copy(self.dp - 2 * distance, 0).wait_recv()

            @pl.when(self.line < LINES - 1)
            def _():
                self.copy(self.dp - 2 * distance, 0).start()

        @pl.when(self.line + distance < LINES)
        def _():
            self.copy(self.dp + 2 * distance, 1).wait_recv()

            @pl.when(self.line > 0)
            def _():
                self.copy(self.dp + 2 * distance, 1).start()

    def step_across(self, distance):
        @pl.when(self.line >= distance)
        def _():
            self.copy(self.dp - 2 * distance, 2).start()

        @pl.when(self.line + distance < LINES)
        def _():
            self.copy(self.dp + 2 * distance, 2).start()

    def step(self, distance):
        self.step_along(distance)
        self.step_across(distance)

    def arrive_block(self, at):
        self.copy(self.dp ^ (2 * at) ^ 1, 2).wait_recv()

    def arrive(self):
        self.local().wait()
        for line in range(LINES):
            self.copy(2 * line + 1 - self.side, 2).wait_recv()

    def finish(self):
        for line in range(LINES):
            index = 2 * line + self.side
            self.copy(index, 2).wait_send()

            @pl.when((self.line < LINES - 1) & (line <= self.line))
            def _():
                self.copy(index, 0).wait_send()

            @pl.when((self.line > 0) & (line >= self.line))
            def _():
                self.copy(index, 1).wait_send()


class RowGather:
    def __init__(self, full, rows, send_sem, recv_sem):
        self.full, self.rows = full, rows
        self.send_sem, self.recv_sem = send_sem, recv_sem
        self.dp, self.tensor = position()

    def view(self, rank, half=None):
        if half is None:
            return row_piece(self.full, rank, self.rows)
        return row_piece(self.full, rank * HALVES + half, self.rows // HALVES)

    def near(self, rank):
        view = self.view(rank)
        target = (self.dp, self.tensor ^ CORE)
        return remote(view, view, self.send_sem.at[0], self.recv_sem.at[0], target)

    def across(self, rank, half):
        view, slot = self.view(rank, half), 1 + half
        target = (self.dp, self.tensor ^ ACROSS)
        return remote(view, view, self.send_sem.at[slot], self.recv_sem.at[slot], target)

    def far(self, rank, half):
        view, slot = self.view(rank, half), 1 + HALVES + half
        target = (self.dp, self.tensor ^ CORE)
        return remote(view, view, self.send_sem.at[slot], self.recv_sem.at[slot], target)

    def start_half(self, half):
        self.across(self.tensor, half).start()

    def start_near(self):
        self.near(self.tensor).start()

    def start(self):
        for half in range(HALVES):
            self.start_half(half)
        self.start_near()

    def wait_near(self):
        self.near(self.tensor ^ CORE).wait_recv()

    def wait_across(self, half):
        self.across(self.tensor ^ ACROSS, half).wait_recv()
        self.far(self.tensor ^ ACROSS, half).start()

    def wait_far(self, half):
        self.far(self.tensor ^ FAR, half).wait_recv()

    def finish(self):
        self.near(self.tensor).wait_send()
        for half in range(HALVES):
            self.across(self.tensor, half).wait_send()
            self.far(self.tensor ^ ACROSS, half).wait_send()


class RowScatter:
    def __init__(self, near_out, near_in, across_out, across_in, send_sem, recv_sem):
        self.near_out, self.near_in = near_out, near_in
        self.across_out, self.across_in = across_out, across_in
        self.send_sem, self.recv_sem = send_sem, recv_sem
        self.dp, self.tensor = position()

    def near(self, slot):
        return remote(
            self.near_out.at[slot],
            self.near_in.at[slot],
            self.send_sem.at[slot],
            self.recv_sem.at[slot],
            (self.dp, self.tensor ^ CORE),
        )

    def across(self, half):
        rows = self.across_in.shape[0] // HALVES
        return remote(
            row_piece(self.across_out, half, rows),
            row_piece(self.across_in, half, rows),
            self.send_sem.at[2 * HALVES + half],
            self.recv_sem.at[2 * HALVES + half],
            (self.dp, self.tensor ^ ACROSS),
        )

    def give_far(self, half, partial):
        self.near_out[half] = partial.astype(jnp.bfloat16)
        self.near(half).start()

    def give_across(self, half, partial):
        self.near(half).wait_recv()
        rows = partial.shape[0]
        total = partial + self.near_in[half].astype(jnp.float32)
        row_piece(self.across_out, half, rows)[...] = total.astype(jnp.bfloat16)
        self.across(half).start()

    def give_near(self, half, partial):
        self.near_out[HALVES + half] = partial.astype(jnp.bfloat16)
        self.near(HALVES + half).start()

    def take(self, half, partial):
        self.near(HALVES + half).wait_recv()
        rows = partial.shape[0]
        total = partial + self.near_in[HALVES + half].astype(jnp.float32)
        self.across(half).wait_recv()
        return total + row_piece(self.across_in, half, rows)[...].astype(jnp.float32)

    def finish(self):
        for slot in range(2 * HALVES):
            self.near(slot).wait_send()
        for half in range(HALVES):
            self.across(half).wait_send()


def dot(left, right):
    return jnp.dot(left, right, preferred_element_type=jnp.float32)


def dot_nt(left, right):
    return lax.dot_general(left, right, (((1,), (1,)), ((), ())), preferred_element_type=jnp.float32)


def dot_tn(left, right):
    return lax.dot_general(left, right, (((0,), (0,)), ((), ())), preferred_element_type=jnp.float32)


def normalize(rows):
    centred = rows - jnp.mean(rows, axis=-1, keepdims=True)
    inverse = lax.rsqrt(jnp.mean(centred * centred, axis=-1, keepdims=True) + EPSILON)
    return centred * inverse, inverse


def norm_back(grad, normed, inverse):
    average = jnp.mean(grad, axis=-1, keepdims=True)
    along = jnp.mean(grad * normed, axis=-1, keepdims=True)
    return inverse * (grad - average - normed * along)


class PairGather:
    def __init__(self, own, full, piece, pair, send_sem, recv_sem, local_sem):
        self.own, self.full, self.piece, self.pair = own, full, piece, pair
        self.send_sem, self.recv_sem, self.local_sem = send_sem, recv_sem, local_sem
        self.dp, self.tensor = position()
        self.line = self.dp // 2
        self.up = jnp.where(self.line < LINES - 1, 2, -2)
        self.down = jnp.where(self.line > 0, -2, 2)

    def local(self):
        return pltpu.make_async_copy(self.own, self.piece(self.full, self.dp), self.local_sem)

    def across(self):
        return remote(
            self.own,
            self.piece(self.full, self.dp),
            self.send_sem.at[0],
            self.recv_sem.at[LINES],
            (self.dp ^ 1, self.tensor),
        )

    def along(self, line, way):
        view = self.pair(self.full, line)
        return remote(
            view,
            view,
            self.send_sem.at[1 + way * 2 + line],
            self.recv_sem.at[line],
            (self.dp + (self.up if way == 0 else self.down), self.tensor),
        )

    def start(self):
        self.local().start()
        self.across().start()

    def begin(self):
        self.local().wait()
        self.across().wait_recv()

        @pl.when(self.line < LINES - 1)
        def _():
            self.along(self.line, 0).start()

        @pl.when(self.line > 0)
        def _():
            self.along(self.line, 1).start()

    def step(self, distance):
        @pl.when(self.line >= distance)
        def _():
            self.along(self.line - distance, 0).wait_recv()

            @pl.when(self.line < LINES - 1)
            def _():
                self.along(self.line - distance, 0).start()

        @pl.when(self.line + distance < LINES)
        def _():
            self.along(self.line + distance, 1).wait_recv()

            @pl.when(self.line > 0)
            def _():
                self.along(self.line + distance, 1).start()

    def finish(self):
        self.across().wait_send()
        for line in range(LINES):

            @pl.when((self.line < LINES - 1) & (line <= self.line))
            def _():
                self.along(line, 0).wait_send()

            @pl.when((self.line > 0) & (line >= self.line))
            def _():
                self.along(line, 1).wait_send()


class LineFirstScatter:
    def __init__(self, partial, piece, line_in, across_out, across_in, send_sem, recv_sem):
        self.partial, self.piece, self.line_in = partial, piece, line_in
        self.across_out, self.across_in = across_out, across_in
        self.send_sem, self.recv_sem = send_sem, recv_sem
        self.dp, self.tensor = position()

    def view(self, step):
        return self.piece(self.partial, (self.dp // 2) ^ step)

    def along(self, step):
        return remote(
            self.view(step),
            self.line_in.at[step // 2 if step != 2 else 2],
            self.send_sem.at[step],
            self.recv_sem.at[step],
            (self.dp ^ (2 if step != 2 else 4), self.tensor),
        )

    def across(self):
        return remote(
            self.across_out,
            self.across_in,
            self.send_sem.at[0],
            self.recv_sem.at[0],
            (self.dp ^ 1, self.tensor),
        )

    def start(self):
        self.along(3).start()

    def relay(self):
        self.along(3).wait_recv()
        total = self.view(2)[...].astype(jnp.float32) + self.line_in[1].astype(jnp.float32)
        self.view(2)[...] = total.astype(jnp.bfloat16)
        self.along(2).start()
        self.along(1).start()

    def turn(self, result):
        total = self.view(0)[...].astype(jnp.float32)
        for step, slot in ((1, 0), (2, 2)):
            self.along(step).wait_recv()
            total = total + self.line_in[slot].astype(jnp.float32)
        first, second = jnp.split(total, 2, 0 if result.shape[1] == total.shape[1] else 1)
        even = self.dp % 2 == 0
        result[...] = jnp.where(even, first, second)
        self.across_out[...] = jnp.where(even, second, first).astype(jnp.bfloat16)
        self.across().start()

    def finish(self, result):
        self.across().wait_recv()
        result[...] += self.across_in[...].astype(jnp.float32)
        self.across().wait_send()
        for step in range(1, LINES):
            self.along(step).wait_send()


class DirectGather:
    def __init__(self, own, full, piece, send_sem, recv_sem, local_sem):
        self.own, self.full, self.piece = own, full, piece
        self.send_sem, self.recv_sem, self.local_sem = send_sem, recv_sem, local_sem
        self.dp, self.tensor = position()

    def along(self, step):
        there = self.dp ^ (2 * step)
        return remote(
            self.own,
            self.piece(self.full, self.dp),
            self.send_sem.at[step],
            self.recv_sem.at[step],
            (there, self.tensor),
        )

    def across(self, step, source=None):
        view = self.piece(self.full, self.dp ^ (2 * step))
        return remote(
            view if source is None else source,
            view,
            self.send_sem.at[LINES + step],
            self.recv_sem.at[LINES + step],
            (self.dp ^ 1, self.tensor),
        )

    def local(self):
        return pltpu.make_async_copy(self.own, self.piece(self.full, self.dp), self.local_sem)

    def start_along(self):
        self.local().start()
        for step in range(1, LINES):
            self.along(step).start()

    def start_across(self):
        self.across(0, self.own).start()

    def step(self, step):
        self.along(step).wait_recv()
        self.across(step).start()

    def arrive(self, step):
        self.across(step).wait_recv()

    def finish(self):
        for step in range(LINES):
            self.across(step).wait_send()
        for step in range(1, LINES):
            self.along(step).wait_send()


class ColumnScatter:
    def __init__(self, near_out, near_in, across_out, across_in, send_sem, recv_sem):
        self.near_out, self.near_in = near_out, near_in
        self.across_out, self.across_in = across_out, across_in
        self.send_sem, self.recv_sem = send_sem, recv_sem
        self.dp, self.tensor = position()

    def near(self, slot):
        return remote(
            self.near_out.at[slot],
            self.near_in.at[slot],
            self.send_sem.at[slot],
            self.recv_sem.at[slot],
            (self.dp, self.tensor ^ CORE),
        )

    def across(self, at):
        return remote(
            self.across_out.at[at],
            self.across_in.at[at],
            self.send_sem.at[2 * LINES + at],
            self.recv_sem.at[2 * LINES + at],
            (self.dp, self.tensor ^ ACROSS),
        )

    def give_far(self, at, partial):
        self.near_out[at] = partial.astype(jnp.bfloat16)
        self.near(at).start()

    def give_near(self, at, partial):
        self.near_out[LINES + at] = partial.astype(jnp.bfloat16)
        self.near(LINES + at).start()

    def give_across(self, at, partial):
        self.near(at).wait_recv()
        total = partial + self.near_in[at].astype(jnp.float32)
        self.across_out[at] = total.astype(jnp.bfloat16)
        self.across(at).start()

    def take(self, at, partial):
        self.near(LINES + at).wait_recv()
        total = partial + self.near_in[LINES + at].astype(jnp.float32)
        self.across(at).wait_recv()
        return total + self.across_in[at].astype(jnp.float32)

    def finish(self):
        for slot in range(2 * LINES):
            self.near(slot).wait_send()
        for at in range(LINES):
            self.across(at).wait_send()


class LineScatter:
    def __init__(self, partial, piece, side_in, line_in, send_sem, recv_sem):
        self.partial, self.piece, self.side_in, self.line_in = partial, piece, side_in, line_in
        self.send_sem, self.recv_sem = send_sem, recv_sem
        self.dp, self.tensor = position()

    def view(self, step):
        return self.piece(self.partial, self.dp ^ (2 * step))

    def across(self, step):
        return remote(
            self.piece(self.partial, self.dp ^ (2 * step) ^ 1),
            self.side_in.at[step],
            self.send_sem.at[step],
            self.recv_sem.at[step],
            (self.dp ^ 1, self.tensor),
        )

    def along(self, step):
        return remote(
            self.view(step),
            self.line_in.at[step // 2 if step != 2 else 2],
            self.send_sem.at[LINES + step],
            self.recv_sem.at[LINES + step],
            (self.dp ^ (2 if step != 2 else 4), self.tensor),
        )

    def start(self, order=ORDER):
        for step in order:
            self.across(step).start()

    def total(self, step):
        self.across(step).wait_recv()
        return self.view(step)[...].astype(jnp.float32) + self.side_in[step].astype(jnp.float32)

    def relay(self, step):
        total = self.total(step)
        if step == 2:
            self.along(3).wait_recv()
            total = total + self.line_in[1].astype(jnp.float32)
        self.view(step)[...] = total.astype(jnp.bfloat16)
        self.along(step).start()

    def finish(self, result):
        total = self.total(0)
        self.along(1).wait_recv()
        total = total + self.line_in[0].astype(jnp.float32)
        self.along(2).wait_recv()
        result[...] = total + self.line_in[2].astype(jnp.float32)
        for step in range(LINES):
            self.across(step).wait_send()
        for step in range(1, LINES):
            self.along(step).wait_send()


class Total:
    def __init__(self, held, arrived, send_sem, recv_sem):
        self.held, self.arrived, self.send_sem, self.recv_sem = held, arrived, send_sem, recv_sem
        dp, tensor = position()
        self.targets = (
            (dp ^ 1, tensor),
            (dp ^ 2, tensor),
            (dp ^ 4, tensor),
            (dp, tensor ^ ACROSS),
            (dp, tensor ^ CORE),
        )

    def copy(self, step):
        return remote(
            self.held.at[step],
            self.arrived.at[step],
            self.send_sem.at[step],
            self.recv_sem.at[step],
            self.targets[step],
        )

    def start(self):
        self.copy(0).start()

    def step(self, step):
        self.copy(step).wait_recv()
        self.held[step + 1] = self.held[step] + self.arrived[step]
        if step + 1 < len(self.targets):
            self.copy(step + 1).start()

    def finish(self):
        for step in range(len(self.targets)):
            self.copy(step).wait_send()


def layer_kernel(names, rows, *refs):
    r = types.SimpleNamespace(**dict(zip(names, refs)))
    dp, tensor = position()
    bf16, f32 = jnp.bfloat16, jnp.float32
    half_rows = rows // HALVES
    local = r.queries.shape[1]
    piece = r.triple_own.shape[1]
    pairs = local // (2 * HEAD)
    length, hidden = r.hidden.shape
    near, across, far = tensor ^ CORE, tensor ^ ACROSS, tensor ^ FAR

    def of_rows(ref, index):
        return row_piece(ref, index, piece)

    def of_columns(ref, index):
        return column_piece(ref, index, piece)

    def of_stack(ref, index):
        return ref.at[:, pl.ds(pl.multiple_of(index * piece, piece), piece), :]

    def of_half_stack(half):
        size = piece // HALVES

        def view(ref, index):
            return ref.at[:, pl.ds(pl.multiple_of(index * piece + half * size, size), size), :]

        return view, r.triple_own.at[:, half * size : (half + 1) * size, :]

    def block(rank, size=rows):
        return pl.ds(pl.multiple_of(rank * size, size), size)

    def split(partial):
        return [partial[half * half_rows : (half + 1) * half_rows] for half in range(HALVES)]

    def part_of(half):
        return slice(half * half_rows, (half + 1) * half_rows)

    (view_a, own_a), (view_b, own_b) = of_half_stack(0), of_half_stack(1)
    lines = [
        kind(own, full, view, r.line_send.at[at], r.line_recv.at[at], r.line_local.at[at])
        for at, (kind, own, full, view) in enumerate(
            (
                (LineGather, own_a, r.triple, view_a),
                (LineGather, own_b, r.triple, view_b),
                (DirectGather, r.output_own, r.output, of_columns),
                (LineGather, r.up_own, r.up, of_rows),
                (LineGather, r.down_own.at[: hidden // 2, :], r.down.at[: hidden // 2, :], of_columns),
            )
        )
    ]
    *triple_lines, output_line, up_line, down_line = lines

    def of_both(ref, index):
        return column_piece(ref, index, 2 * piece)

    rest_line = PairGather(
        r.down_own.at[hidden // 2 :, :],
        r.down.at[hidden // 2 :, :],
        of_columns,
        of_both,
        r.pair_send,
        r.pair_recv,
        r.pair_local,
    )
    sums = [
        LineScatter(partial, view, side, along, r.part_send.at[at], r.part_recv.at[at])
        for at, (partial, view, side, along) in enumerate(
            (
                (r.grad_project, of_stack, r.project_side, r.project_line),
                (r.grad_output, of_columns, r.output_side, r.output_line),
                (r.grad_up, of_rows, r.up_side, r.up_line),
                (r.grad_down.at[: hidden // 2, :], of_columns, r.down_side, r.down_line),
            )
        )
    ]
    project_sum, output_sum, up_sum, down_sum = sums

    rest_sum = LineFirstScatter(
        r.grad_down.at[hidden // 2 :, :],
        of_both,
        r.rest_line,
        r.rest_out,
        r.rest_in,
        r.rest_send.at[0],
        r.rest_recv.at[0],
    )
    down_top, down_rest = r.down_sum.at[: hidden // 2, :], r.down_sum.at[hidden // 2 :, :]
    gathers = [
        RowGather(full, rows, r.row_send, r.row_recv)
        for full in (r.gathered, r.first_all, r.second_all, r.branch_all)
    ]
    row_buffers = r.near_out_a, r.near_in_a, r.across_out_a, r.across_in_a
    column_buffers = r.near_out_b, r.near_in_b, r.across_out_b, r.across_in_b
    scatters = [
        RowScatter(*row_buffers, r.row_sum_send, r.row_sum_recv),
        ColumnScatter(*column_buffers, r.column_sum_send, r.column_sum_recv),
    ] * 2
    total = Total(r.held_totals, r.arrived_totals, r.total_send, r.total_recv)

    def column_pair(at):
        return block((dp // 4) ^ at, 4 * piece)

    def give_halves(method, at, partial):
        for half in range(HALVES):
            method(at * HALVES + half, partial[part_of(half)])

    def keep_near(scatter, at, product):
        give_halves(scatter.give_near, at, product(near, column_pair(at)))
        r.kept[:, column_pair(at)] = product(tensor, column_pair(at))

    def take_columns(scatter, result, at):
        part, lanes = block(at % HALVES, half_rows), column_pair(at // HALVES)
        result[part, lanes] = scatter.take(at, r.kept[part, lanes])

    def chunks(size, start, body, step=CHUNK):
        @pl.loop(0, size // step)
        def _(chunk):
            offset = chunk * step
            body(
                pl.ds(pl.multiple_of(offset, step), step),
                pl.ds(pl.multiple_of(start + offset, step), step),
            )

    loads = [
        pltpu.make_async_copy(source, target, r.load_sem.at[at])
        for at, (source, target) in enumerate(
            (
                (r.tokens, gathers[0].view(tensor)),
                (r.segments, r.segment_row),
                (r.bias_from, r.bias_rows),
                (r.gains_from, r.norm_gains),
                (r.hidden_from.at[pl.ds(pl.multiple_of(tensor * hidden, hidden), hidden)], r.hidden_bias),
                (r.cotangent_from, r.cotangent),
            )
        )
    ]
    for load in loads:
        load.start()
    greet()
    for line in triple_lines:
        line.start_along()
        line.start_across()
    loads[0].wait()
    gathers[0].start()
    for line in triple_lines:
        line.step(1)
    loads[1].wait()
    numbers = r.segment_row[...].astype(f32)
    r.segment_column[...] = jnp.broadcast_to(numbers, (8, numbers.shape[1])).T[:, :1]
    r.segment_row_f32[...] = numbers
    for line in triple_lines:
        line.step(2)
    gathers[0].wait_near()
    for half in range(HALVES):
        gathers[0].wait_across(half)
    for line in triple_lines:
        line.step(3)
    output_line.start_along()
    output_line.start_across()
    rest_line.start()
    up_line.start_along()
    down_line.start_along()
    for half in range(HALVES):
        gathers[0].wait_far(half)
    for line in triple_lines:
        line.arrive()
    for load in loads[2:]:
        load.wait()
    columns = pl.ds(pl.multiple_of(tensor * local, local), local)
    query_bias = r.bias_rows[0:1, columns]
    value_bias = r.bias_rows[1:2, columns]

    @pl.loop(0, 4)
    def _(index):
        here = block(index)
        left = r.gathered[here, :]
        query = (dot(left, r.triple[0]) + query_bias).astype(bf16)
        r.queries[here, :] = query * bf16(HEAD**-0.5)
        key = dot(left, r.triple[1])
        r.key_rows[here, :] = key.astype(bf16)
        r.key_turned[:, here] = key.T.astype(bf16)
        value = dot(left, r.triple[2]) + value_bias
        r.value_rows[here, :] = value.astype(bf16)
        r.value_turned[:, here] = value.T.astype(bf16)

    for step in range(1, LINES):
        output_line.step(step)
    up_line.start_across()

    def head_rows(head):
        return pl.ds(pl.multiple_of(head * HEAD, HEAD), HEAD)

    def attend(here, pair):
        lanes = block(pair, 2 * HEAD)
        query = r.queries[here, lanes]
        keys = r.key_rows[:, lanes]
        same = r.segment_column[...] == r.segment_row_f32[:, here]
        lane = lax.broadcasted_iota(jnp.int32, query.shape, 1)
        outs = []
        for side in range(2):
            scores = dot_nt(keys, jnp.where(lane // HEAD == side, query, bf16(0)))
            scores = jnp.where(same, scores, NEGATIVE)
            top = jnp.max(scores, axis=0, keepdims=True)
            exponent = jnp.exp(scores - top)
            mass = jnp.sum(exponent, axis=0, keepdims=True)
            weights = (exponent * (1.0 / mass)).astype(bf16)
            head = pair * 2 + side
            outs.append(dot(r.value_turned[head_rows(head), :], weights))
            r.log_totals[pl.ds(head, 1), here] = top + jnp.log(mass)
        r.mixed[here, lanes] = jnp.concatenate(outs, axis=0).T.astype(bf16)

    @pl.loop(0, 4 * pairs)
    def _(turn):
        rank, pair = tensor ^ (FAR - turn // pairs), turn % pairs
        here = block(rank)
        attend(here, pair)

        def give(rank, method):
            r.partial[...] = dot(r.mixed[block(rank), :], r.output[...])
            for half in range(HALVES):
                method(half, r.partial[part_of(half), :])

        def after(index):
            return pl.when(turn == index)

        @after(0)
        def _():
            up_line.step(1)

        @after(1)
        def _():
            rest_line.begin()

        @after(3)
        def _():
            output_line.local().wait()
            for step in range(LINES):
                output_line.arrive(step)
            give(far, scatters[0].give_far)
            give(across, scatters[0].give_across)

        @after(4)
        def _():
            up_line.step(2)
            down_line.step_along(1)

        @after(5)
        def _():
            give(near, scatters[0].give_near)

        @after(7)
        def _():
            rest_line.step(1)
            up_line.step(3)
            down_line.start_across()
            down_line.step_across(1)

    r.partial[...] = dot(r.mixed[block(tensor), :], r.output[...])
    gathers[0].finish()
    for half in range(HALVES):
        part = part_of(half)
        r.kept[part, :] = scatters[0].take(half, r.partial[part, :])

        def first_norm(_, here):
            own_rows = r.gathered[pl.ds(pl.multiple_of(tensor * rows + here.start, NORM), NORM), :]
            normed, inverse = normalize(own_rows.astype(f32) + r.kept[here, :] + r.bias_rows[2:3, :])
            r.normed_one[here, :] = normed
            r.inverse_one[here, :] = inverse
            first = normed * r.norm_gains[0:1, :] + r.bias_rows[3:4, :]
            into = pl.ds(pl.multiple_of(tensor * rows + here.start, NORM), NORM)
            r.first_all[into, :] = first.astype(bf16)

        chunks(half_rows, half * half_rows, first_norm, NORM)
        gathers[1].start_half(half)
    scatters[0].finish()

    gathers[1].start_near()
    r.sums[...] = jnp.zeros_like(r.sums)

    def extent(rank, half):
        size = rows if half is None else half_rows
        start = rank * rows + (0 if half is None else half * half_rows)
        return start, size, pl.ds(pl.multiple_of(start, size), size)

    def up_part(rank, half=None):
        start, size, here = extent(rank, half)
        r.upper[:size, :] = dot(r.first_all[here, :], r.up[...]) + r.hidden_bias[...].reshape(1, hidden)

        def body(part, into):
            value = r.upper[part, :]
            share = 0.5 + 0.5 * lax.erf(value * (0.5**0.5))
            r.hidden[into, :] = (value * share).astype(bf16)
            bell = jnp.exp(value * value * -0.5) * (2 * jnp.pi) ** -0.5
            r.slope[into, :] = share + value * bell

        chunks(size, start, body)

    def back_part(rank, half=None):
        start, size, here = extent(rank, half)
        r.upper[:size, :] = dot_nt(r.second_all[here, :], r.down[...])

        def body(part, into):
            low = (r.upper[part, :] * r.slope[into, :]).astype(bf16)
            r.upper_low[into, :] = low
            r.sums[6:7, :] += jnp.sum(low.astype(f32), axis=0, keepdims=True)

        chunks(size, start, body)
        r.partial[:size, :] = dot_nt(r.upper_low[here, :], r.up[...])

    down_line.step(2)
    up_line.arrive()

    @pl.loop(0, 2)
    def _(turn):
        @pl.when(turn == 1)
        def _():
            gathers[1].wait_near()
            down_line.step(3)
            rest_line.step(2)

        up_part(tensor ^ turn)

    def other_chip(gather, body):
        @pl.loop(0, 2 * HALVES)
        def _(turn):
            half, side = turn // 2, turn % 2

            @pl.when(turn == 0)
            def _():
                gather.wait_across(0)

            body(half, side)

    def up_other(half, side):
        @pl.when(side == 1)
        def _():
            gathers[1].wait_far(half)

        up_part(tensor ^ (ACROSS + side), half)

    def down_part(rank, lanes):
        return dot(r.hidden[block(rank), :], r.down[:, lanes])

    def send_unit(at, half):
        def product(rank):
            return dot(r.hidden[extent(rank, half)[2], :], r.down[:, column_pair(at)])

        scatters[1].give_far(at * HALVES + half, product(far))
        scatters[1].give_across(at * HALVES + half, product(across))

    def up_and_send(half, side):
        up_other(half, side)

        @pl.when((side == 1) & (half == 0))
        def _():
            gathers[1].wait_across(1)
            down_line.local().wait()
            down_line.arrive_block(0)
            down_line.arrive_block(1)
            send_unit(0, 0)

    other_chip(gathers[1], up_and_send)

    send_unit(0, 1)
    keep_near(scatters[1], 0, down_part)
    rest_line.step(3)
    down_line.arrive_block(2)
    down_line.arrive_block(3)
    send_unit(1, 0)
    send_unit(1, 1)
    keep_near(scatters[1], 1, down_part)

    def add_to(row, value):
        r.sums[row : row + 1, :] += jnp.sum(value, axis=0, keepdims=True)

    def second_norm(_, here):
        first = r.normed_one[here, :] * r.norm_gains[0:1, :] + r.bias_rows[3:4, :]
        normed, inverse = normalize(first + r.kept[here, :] + r.bias_rows[4:5, :])
        shifted = normed * r.norm_gains[1:2, :] + r.bias_rows[5:6, :]
        r.layer_low[here, :] = shifted.astype(bf16)
        grad = r.cotangent[here, :].astype(f32)
        add_to(5, grad * normed)
        add_to(3, grad)
        grad = norm_back(grad * r.norm_gains[1:2, :], normed, inverse)
        r.grad_rows[here, :] = grad
        low = grad.astype(bf16)
        add_to(2, low.astype(f32))
        r.second_all[pl.ds(pl.multiple_of(tensor * rows + here.start, NORM), NORM), :] = low

    gathers[1].finish()
    for half in range(HALVES):
        for at in range(2):
            take_columns(scatters[1], r.kept, at * HALVES + half)
        chunks(half_rows, half * half_rows, second_norm, NORM)
        gathers[2].start_half(half)
    saves = []

    def save(source, target):
        saves.append(pltpu.make_async_copy(source, target, r.save_sem.at[len(saves)]))
        saves[-1].start()

    save(r.layer_low, r.layer_out)
    scatters[1].finish()

    gathers[2].start_near()

    @pl.loop(0, 2)
    def _(turn):
        @pl.when(turn == 1)
        def _():
            gathers[2].wait_near()

        back_part(tensor ^ turn)

        @pl.when(turn == 0)
        def _():
            r.kept[...] = r.partial[...]

        @pl.when(turn == 1)
        def _():
            for half in range(HALVES):
                scatters[2].give_near(half, r.partial[part_of(half), :])

    def weight_grad(left, right, result, chip=None, add=False):
        depth = slice(None) if chip is None else block(chip, 2 * rows)

        @pl.loop(0, left.shape[1] // rows)
        def _(index):
            lanes = block(index)
            product = dot_tn(left[depth, lanes], right[depth, :])
            if add:
                product += result[lanes, :].astype(f32)
            result[lanes, :] = product.astype(bf16)

    weight_grad(r.hidden, r.second_all, r.grad_down, tensor // 2)

    def back_other(half, side):
        @pl.when((side == 1) & (half < HALVES - 1))
        def _():
            gathers[2].wait_far(half)

        @pl.when((side == 0) & (half == HALVES - 1))
        def _():
            gathers[2].wait_far(half)
            weight_grad(r.hidden, r.second_all, r.grad_down, 1 - tensor // 2, True)
            rest_sum.start()
            down_sum.start()

        back_part(tensor ^ (ACROSS + side), half)

        @pl.when(side == 0)
        def _():
            r.held[...] = r.partial[:half_rows, :]

        @pl.when(side == 1)
        def _():
            scatters[2].give_far(half, r.partial[:half_rows, :])

            @pl.when(half == 0)
            def _():
                gathers[2].wait_across(1)

            scatters[2].give_across(half, r.held[...])

    other_chip(gathers[2], back_other)

    weight_grad(r.first_all, r.upper_low, r.grad_up)
    up_sum.start()

    def first_back(_, here):
        grad = r.grad_rows[here, :] + r.kept[here, :]
        normed = r.normed_one[here, :]
        add_to(4, grad * normed)
        add_to(1, grad)
        grad = norm_back(grad * r.norm_gains[0:1, :], normed, r.inverse_one[here, :])
        r.grad_rows[here, :] = grad
        low = grad.astype(bf16)
        add_to(0, low.astype(f32))
        r.branch_all[pl.ds(pl.multiple_of(tensor * rows + here.start, NORM), NORM), :] = low

    gathers[2].finish()
    for half in range(HALVES):
        part = part_of(half)
        r.kept[part, :] = scatters[2].take(half, r.kept[part, :])
        chunks(half_rows, half * half_rows, first_back, NORM)
        gathers[3].start_half(half)
        if half == 0:
            rest_sum.relay()
            down_sum.relay(3)
    scatters[2].finish()

    gathers[3].start_near()
    grad_keys, grad_values = r.slope.at[:, :local], r.slope.at[:, local : 2 * local]
    r.slope[:, : 2 * local] = jnp.zeros((r.slope.shape[0], 2 * local), f32)

    def attend_back(rank):
        here = block(rank)
        r.mixed_low[...] = dot_nt(r.branch_all[here, :], r.output[...]).astype(bf16)

        @pl.loop(0, pairs)
        def _(pair):
            lanes = block(pair, 2 * HEAD)
            query = r.queries[here, lanes]
            grad = r.mixed_low[:, lanes]
            keys = r.key_rows[:, lanes]
            values = r.value_rows[:, lanes]
            same = r.segment_column[...] == r.segment_row_f32[:, here]
            lane = lax.broadcasted_iota(jnp.int32, query.shape, 1)
            outs = []
            for side in range(2):
                mine = lane // HEAD == side
                head = pair * 2 + side
                query_here = jnp.where(mine, query, bf16(0))
                grad_here = jnp.where(mine, grad, bf16(0))
                scores = jnp.where(same, dot_nt(keys, query_here), NEGATIVE)
                weights = jnp.exp(scores - r.log_totals[pl.ds(head, 1), here])
                grad_weights = dot_nt(values, grad_here)
                along = jnp.sum(weights * grad_weights, axis=0, keepdims=True)
                grad_scores = (weights * (grad_weights - along)).astype(bf16)
                grad_keys[:, lanes] += dot(grad_scores, query_here)
                grad_values[:, lanes] += dot(weights.astype(bf16), grad_here)
                outs.append(dot(r.key_turned[head_rows(head), :], grad_scores))
            grad_query = jnp.concatenate(outs, axis=0).T * HEAD**-0.5
            r.projected_low[here, lanes] = grad_query.astype(bf16)

    @pl.loop(0, 4)
    def _(turn):
        @pl.when(turn == 1)
        def _():
            gathers[3].wait_near()

        @pl.when(turn == 2)
        def _():
            for half in range(HALVES):
                gathers[3].wait_across(half)

        @pl.when(turn == 3)
        def _():
            for half in range(HALVES):
                gathers[3].wait_far(half)
            r.grad_output[...] = dot_tn(r.mixed[...], r.branch_all[...]).astype(bf16)
            output_sum.start()

        attend_back(tensor ^ turn)

        @pl.when(turn == 0)
        def _():
            down_sum.relay(1)

        @pl.when(turn == 1)
        def _():
            up_sum.relay(3)

        @pl.when(turn == 2)
        def _():
            down_sum.relay(2)
            rest_sum.turn(down_rest)

    up_sum.relay(2)
    up_sum.relay(1)
    r.projected_low[:, local : 2 * local] = grad_keys[...].astype(bf16)
    r.projected_low[:, 2 * local :] = grad_values[...].astype(bf16)
    r.held_totals[0] = jnp.zeros(r.held_totals.shape[1:], f32)
    r.held_totals[0, 2:8, :] = r.sums[0:6, :]
    r.held_totals[0, pl.ds(8 + tensor, 1), :] = r.sums[6:7, :]
    shifts = dot(jnp.ones((CHUNK, length), bf16), r.projected_low[...])
    for row, at in ((0, 0), (1, 2)):
        r.held_totals[0, row : row + 1, columns] = shifts[:1, at * local : (at + 1) * local]
    total.start()

    @pl.loop(0, r.gathered.shape[1] // rows)
    def _(index):
        lanes = block(index)
        product = dot_tn(r.gathered[:, lanes], r.projected_low[...]).astype(bf16)
        for at in range(3):
            r.grad_project[at, lanes, :] = product[:, at * local : (at + 1) * local]

    project_sum.start()

    def token_part(rank, lanes):
        product = 0
        for part in range(3):
            left = r.projected_low[block(rank), part * local : (part + 1) * local]
            product += dot_nt(left, r.triple[part, lanes, :])
        return product

    @pl.loop(0, 2)
    def _(at):
        give_halves(scatters[3].give_far, at, token_part(far, column_pair(at)))
        give_halves(scatters[3].give_across, at, token_part(across, column_pair(at)))
        keep_near(scatters[3], at, token_part)

    total.step(0)
    output_sum.relay(3)
    project_sum.relay(3)
    down_sum.finish(down_top)
    rest_sum.finish(down_rest)
    save(r.down_sum, r.down_out)

    def take_tokens(at):
        part, lanes = part_of(at % HALVES), column_pair(at // HALVES)
        r.grad_rows[part, lanes] += scatters[3].take(at, r.kept[part, lanes])

    take_tokens(0)
    take_tokens(1)
    output_sum.relay(2)
    take_tokens(2)
    total.step(1)
    take_tokens(3)
    save(r.grad_rows, r.grad_tokens)
    gathers[3].finish()
    for each in lines + [rest_line]:
        each.finish()
    project_sum.relay(2)
    project_sum.relay(1)
    scatters[3].finish()
    up_sum.finish(r.up_sum)
    save(r.up_sum, r.up_out)
    total.step(2)
    output_sum.relay(1)
    total.step(3)
    project_sum.finish(r.project_sum)
    save(r.project_sum, r.project_out)
    total.step(4)
    r.bias_sum[...] = r.held_totals[5, 0:6, :]
    r.gains_sum[...] = r.held_totals[5, 6:8, :]
    for at in range(4):
        r.hidden_sum[at * hidden : (at + 1) * hidden] = r.held_totals[5, 8 + at, :]
    save(r.bias_sum, r.bias_out)
    save(r.gains_sum, r.gains_out)
    save(r.hidden_sum, r.hidden_out)
    output_sum.finish(r.output_sum)
    save(r.output_sum, r.output_out)
    total.finish()
    for each in saves:
        each.wait()


def copy_kernel(count, *refs):
    sources, targets, held, sem = refs[:count], refs[count : 2 * count], refs[2 * count : -1], refs[-1]
    copies_in = [pltpu.make_async_copy(*pair, sem.at[at]) for at, pair in enumerate(zip(sources, held))]
    copies_out = [
        pltpu.make_async_copy(*pair, sem.at[count + at]) for at, pair in enumerate(zip(held, targets))
    ]
    for copy in copies_in:
        copy.start()
    for arrived, copy in zip(copies_in, copies_out):
        arrived.wait()
        copy.start()
    for copy in copies_out:
        copy.wait()


def per_device_kernel(
    tokens,
    segments,
    cotangent,
    project_weight,
    output_weight,
    up_weight,
    down_weight,
    norm_gains,
    bias_rows,
    hidden_bias,
):
    rows, width = tokens.shape
    length = segments.shape[1]
    local_hidden = up_weight.shape[1]
    local = output_weight.shape[0]
    piece = project_weight.shape[0]
    bf16, f32 = jnp.bfloat16, jnp.float32
    inputs = dict(
        tokens=tokens,
        triple_own=project_weight.transpose(1, 0, 2),
        output_own=output_weight,
        up_own=up_weight,
        down_own=down_weight,
        segments=segments,
        cotangent_from=cotangent,
        gains_from=norm_gains,
        bias_from=bias_rows,
        hidden_from=hidden_bias,
    )
    shapes = dict(
        project=(3, piece, local),
        output=(local, piece),
        up=(piece, local_hidden),
        down=(local_hidden, piece),
    )
    outputs = dict(layer_out=((rows, width), bf16), grad_tokens=((rows, width), f32))
    outputs |= {name + "_out": (shape, f32) for name, shape in shapes.items()}
    outputs |= dict(
        gains_out=((2, width), f32),
        bias_out=((6, width), f32),
        hidden_out=(hidden_bias.shape, f32),
    )
    scratch = dict(
        segment_row=((1, length), jnp.int32),
        segment_row_f32=((1, length), f32),
        segment_column=((length, 1), f32),
        cotangent=((rows, width), bf16),
        norm_gains=(norm_gains.shape, f32),
        bias_rows=(bias_rows.shape, f32),
        hidden_bias=((local_hidden,), f32),
        layer_low=((rows, width), bf16),
        bias_sum=(bias_rows.shape, f32),
        gains_sum=(norm_gains.shape, f32),
        hidden_sum=(hidden_bias.shape, f32),
        partial=((rows, width), f32),
        gathered=((length, width), bf16),
        triple=((3, width, local), bf16),
        output=((local, width), bf16),
        up=((width, local_hidden), bf16),
        down=((local_hidden, width), bf16),
        queries=((length, local), bf16),
        key_rows=((length, local), bf16),
        value_rows=((length, local), bf16),
        key_turned=((local, length), bf16),
        value_turned=((local, length), bf16),
        mixed=((length, local), bf16),
        log_totals=((local // HEAD, length), f32),
        normed_one=((rows, width), f32),
        inverse_one=((rows, 1), f32),
        first_all=((length, width), bf16),
        hidden=((length, local_hidden), bf16),
        slope=((length, local_hidden), f32),
        second_all=((length, width), bf16),
        upper_low=((length, local_hidden), bf16),
        upper=((rows, local_hidden), f32),
        kept=((rows, width), f32),
        held=((rows // HALVES, width), f32),
        grad_rows=((rows, width), f32),
        sums=((8, width), f32),
        branch_all=((length, width), bf16),
        mixed_low=((rows, local), bf16),
        projected_low=((length, 3 * local), bf16),
        grad_project=((3, width, local), bf16),
        grad_output=((local, width), bf16),
        grad_up=((width, local_hidden), bf16),
        grad_down=((local_hidden, width), bf16),
        held_totals=((6, 16, width), f32),
        arrived_totals=((5, 16, width), f32),
    )
    for name, shape in shapes.items():
        scratch[name + "_sum"] = (shape, f32)
        moved = (local_hidden // 2, piece) if name == "down" else shape
        scratch[name + "_side"] = ((LINES,) + moved, bf16)
        scratch[name + "_line"] = ((LINES - 1,) + moved, bf16)
    scratch |= dict(
        rest_line=((LINES - 1, local_hidden // 2, 2 * piece), bf16),
        rest_out=((local_hidden // 2, piece), bf16),
        rest_in=((local_hidden // 2, piece), bf16),
    )
    for name in ("near_out_", "near_in_"):
        scratch[name + "a"] = ((2 * HALVES, rows // HALVES, width), bf16)
        scratch[name + "b"] = ((2 * LINES, rows // HALVES, 4 * piece), bf16)
    for name in ("across_out_", "across_in_"):
        scratch[name + "a"] = ((rows, width), bf16)
        scratch[name + "b"] = ((LINES, rows // HALVES, 4 * piece), bf16)
    semaphores = dict(
        line_send=(5, 3 * LINES - 2),
        line_recv=(5, 2 * LINES),
        line_local=(5,),
        part_send=(4, 2 * LINES),
        part_recv=(4, 2 * LINES),
        pair_send=(2 * LINES - 1,),
        pair_recv=(LINES + 1,),
        pair_local=(),
        rest_send=(1, LINES),
        rest_recv=(1, LINES),
        row_send=(1 + 2 * HALVES,),
        row_recv=(1 + 2 * HALVES,),
        row_sum_send=(3 * HALVES,),
        row_sum_recv=(3 * HALVES,),
        column_sum_send=(3 * LINES,),
        column_sum_recv=(3 * LINES,),
        total_send=(5,),
        total_recv=(5,),
        load_sem=(6,),
        save_sem=(9,),
    )
    names = [*inputs, *outputs, *scratch, *semaphores]
    hbm = pl.BlockSpec(memory_space=pltpu.HBM)
    results = pl.pallas_call(
        functools.partial(layer_kernel, names, rows),
        out_shape=[jax.ShapeDtypeStruct(*leaf) for leaf in outputs.values()],
        in_specs=[hbm] * len(inputs),
        out_specs=[hbm] * len(outputs),
        scratch_shapes=[pltpu.VMEM(*leaf) for leaf in scratch.values()]
        + [pltpu.SemaphoreType.DMA(shape) for shape in semaphores.values()],
        compiler_params=pltpu.CompilerParams(
            collective_id=0, has_side_effects=True, vmem_limit_bytes=VMEM_BYTES
        ),
        name="layer",
    )(*inputs.values())
    results = pl.pallas_call(
        functools.partial(copy_kernel, len(outputs)),
        out_shape=[jax.ShapeDtypeStruct(*leaf) for leaf in outputs.values()],
        in_specs=[hbm] * len(outputs),
        out_specs=[hbm] * len(outputs),
        scratch_shapes=[pltpu.VMEM(*leaf) for leaf in outputs.values()]
        + [pltpu.SemaphoreType.DMA((2 * len(outputs),))],
        name="copy",
    )(*results)
    result = dict(zip(outputs, results))
    return (
        result["layer_out"],
        result["grad_tokens"],
        result["project_out"].transpose(1, 0, 2),
        result["output_out"],
        result["up_out"],
        result["down_out"],
        result["gains_out"],
        result["bias_out"],
        result["hidden_out"],
    )


def gelu_exact(values):
    return jax.nn.gelu(values, approximate=False)


def layer_norm(token_rows, gain, shift):
    average = jnp.mean(token_rows, axis=-1, keepdims=True)
    centred = token_rows - average
    variance = jnp.mean(centred * centred, axis=-1, keepdims=True)
    inverse = lax.rsqrt(variance + EPSILON)
    normed = centred * inverse
    return (normed * gain + shift, (normed, inverse))


def norm_back_saved(grad_rows, saved, gain):
    normed, inverse = saved
    grad_gain = jnp.sum(grad_rows * normed, axis=0)
    grad_shift = jnp.sum(grad_rows, axis=0)
    grad_normed = grad_rows * gain
    grad_input = inverse * (
        grad_normed
        - jnp.mean(grad_normed, axis=-1, keepdims=True)
        - normed * jnp.mean(grad_normed * normed, axis=-1, keepdims=True)
    )
    return (grad_input, grad_gain, grad_shift)


def split_heads(token_rows):
    return token_rows.reshape(token_rows.shape[0], token_rows.shape[1] // HEAD, HEAD)


def scatter_sum(partial_sum, axis_name, dimension):
    return lax.psum_scatter(
        partial_sum.astype(jnp.bfloat16), axis_name, scatter_dimension=dimension, tiled=True
    ).astype(jnp.float32)


def place_columns(partial_sum, column_block, total_width):
    full_rows = jnp.zeros(partial_sum.shape[:-1] + (total_width,), jnp.float32)
    return lax.dynamic_update_slice_in_dim(
        full_rows, partial_sum, column_block * partial_sum.shape[-1], partial_sum.ndim - 1
    )


def per_device(
    tokens,
    segments,
    cotangent,
    project_weight,
    output_weight,
    up_weight,
    down_weight,
    norm_gains,
    bias_rows,
    hidden_bias,
):
    tensor_rank = lax.axis_index("tensor")
    local_rows, model_width = tokens.shape
    seq_count, seq_length = segments.shape
    group_rows = seq_count * seq_length
    local_width = project_weight.shape[2]
    score_scale = HEAD ** (-0.5)
    block_rows = min(512, seq_length)
    per_sequence = seq_length // block_rows
    count_blocks = group_rows // block_rows
    block_ids = jnp.arange(count_blocks, dtype=jnp.int32)
    triple_full, output_full, upward_full, downward_full = (
        lax.all_gather(project_weight, "dp", axis=0, tiled=True),
        lax.all_gather(output_weight, "dp", axis=1, tiled=True),
        lax.all_gather(up_weight, "dp", axis=0, tiled=True),
        lax.all_gather(down_weight, "dp", axis=1, tiled=True),
    )
    local_hidden = upward_full.shape[1]
    triple_matrix = triple_full.reshape(model_width, 3 * local_width)
    gathered = lax.all_gather(tokens, "tensor", axis=0, tiled=True)
    head_bias = lax.dynamic_slice_in_dim(bias_rows, tensor_rank * local_width, local_width, 1)
    projected = jnp.dot(gathered, triple_matrix, preferred_element_type=jnp.float32).reshape(
        group_rows, 3, local_width
    )
    queries = (projected[:, 0] + head_bias[0]).astype(jnp.bfloat16)
    key_rows = projected[:, 1].astype(jnp.bfloat16)
    value_rows = (projected[:, 2] + head_bias[1]).astype(jnp.bfloat16)

    def block_parts(block_index):
        sequence = block_index // per_sequence
        row_start = block_index * block_rows
        seq_start = sequence * seq_length
        query_block = split_heads(lax.dynamic_slice_in_dim(queries, row_start, block_rows, 0))
        key_block = split_heads(key_rows)
        value_block = split_heads(value_rows)
        seq_ids = lax.dynamic_index_in_dim(segments, sequence, 0, keepdims=False)
        query_ids = lax.dynamic_slice_in_dim(seq_ids, row_start - seq_start, block_rows, 0)
        products = (
            jnp.einsum("qhd,khd->hqk", query_block, key_block, preferred_element_type=jnp.float32)
            * score_scale
        )
        scores = jnp.where((query_ids[:, None] == seq_ids[None, :])[None], products, NEGATIVE)
        return (row_start, query_block, key_block, value_block, scores)

    def forward_block(block_index):
        row_start, query_block, key_block, value_block, scores = block_parts(block_index)
        row_max = jnp.max(scores, axis=-1, keepdims=True)
        exponent = jnp.exp(scores - row_max)
        row_sum = jnp.sum(exponent, axis=-1, keepdims=True)
        weights_low = (exponent / row_sum).astype(jnp.bfloat16)
        mixed_block = jnp.einsum(
            "hqk,khd->qhd", weights_low, value_block, preferred_element_type=jnp.float32
        )
        log_total = row_max[:, :, 0] + jnp.log(row_sum[:, :, 0])
        return (mixed_block.reshape(block_rows, local_width).astype(jnp.bfloat16), log_total)

    mixed_blocks, log_totals = lax.map(forward_block, block_ids)
    mixed_rows = mixed_blocks.reshape(group_rows, local_width)
    branch_out = (
        scatter_sum(
            jnp.dot(mixed_rows, output_full, preferred_element_type=jnp.float32), "tensor", 0
        )
        + bias_rows[2]
    )
    first_out, first_saved = layer_norm(
        tokens.astype(jnp.float32) + branch_out, norm_gains[0], bias_rows[3]
    )
    first_gathered = lax.all_gather(first_out.astype(jnp.bfloat16), "tensor", axis=0, tiled=True)
    local_bias = lax.dynamic_slice_in_dim(hidden_bias, tensor_rank * local_hidden, local_hidden, 0)
    upper_rows = (
        jnp.dot(first_gathered, upward_full, preferred_element_type=jnp.float32) + local_bias
    )
    hidden_full, gelu_back = jax.vjp(gelu_exact, upper_rows)
    hidden_rows = hidden_full.astype(jnp.bfloat16)
    second_out = (
        scatter_sum(
            jnp.dot(hidden_rows, downward_full, preferred_element_type=jnp.float32), "tensor", 0
        )
        + bias_rows[4]
    )
    layer_out, second_saved = layer_norm(first_out + second_out, norm_gains[1], bias_rows[5])
    reloaded = (
        lax.all_gather(project_weight, "dp", axis=0, tiled=True),
        lax.all_gather(output_weight, "dp", axis=1, tiled=True),
        lax.all_gather(up_weight, "dp", axis=0, tiled=True),
        lax.all_gather(down_weight, "dp", axis=1, tiled=True),
    )
    back_triple = reloaded[0].reshape(model_width, 3 * local_width)
    back_output, back_upward, back_downward = (reloaded[1], reloaded[2], reloaded[3])
    grad_layer = cotangent.astype(jnp.float32)
    grad_second_in, grad_gain_two, grad_shift_two = norm_back_saved(
        grad_layer, second_saved, norm_gains[1]
    )
    grad_second = grad_second_in.astype(jnp.bfloat16)
    grad_second_all = lax.all_gather(grad_second, "tensor", axis=0, tiled=True)
    grad_down_part = jnp.einsum(
        "tf,td->fd", hidden_rows, grad_second_all, preferred_element_type=jnp.float32
    )
    grad_hidden = jnp.einsum(
        "td,fd->tf", grad_second_all, back_downward, preferred_element_type=jnp.float32
    )
    grad_upper = gelu_back(grad_hidden)[0].astype(jnp.bfloat16)
    grad_up_part = jnp.einsum(
        "td,tf->df", first_gathered, grad_upper, preferred_element_type=jnp.float32
    )
    grad_first = (
        scatter_sum(
            jnp.einsum("tf,df->td", grad_upper, back_upward, preferred_element_type=jnp.float32),
            "tensor",
            0,
        )
        + grad_second_in
    )
    grad_first_in, grad_gain_one, grad_shift_one = norm_back_saved(grad_first, first_saved, norm_gains[0])
    grad_branch = grad_first_in.astype(jnp.bfloat16)
    grad_branch_all = lax.all_gather(grad_branch, "tensor", axis=0, tiled=True)
    grad_output_part = jnp.einsum(
        "tc,td->cd", mixed_rows, grad_branch_all, preferred_element_type=jnp.float32
    )
    grad_mixed = jnp.einsum(
        "td,cd->tc", grad_branch_all, back_output, preferred_element_type=jnp.float32
    ).astype(jnp.bfloat16)

    def backward_block(block_index):
        row_start, query_block, key_block, value_block, scores = block_parts(block_index)
        weights_full = jnp.exp(scores - log_totals[block_index][:, :, None])
        grad_mixed_block = split_heads(
            lax.dynamic_slice_in_dim(grad_mixed, row_start, block_rows, 0)
        )
        grad_weights = jnp.einsum(
            "qhd,khd->hqk", grad_mixed_block, value_block, preferred_element_type=jnp.float32
        )
        row_dot = jnp.sum(weights_full * grad_weights, axis=-1, keepdims=True)
        grad_scores = (weights_full * (grad_weights - row_dot)).astype(jnp.bfloat16)
        grad_query = (
            jnp.einsum("hqk,khd->qhd", grad_scores, key_block, preferred_element_type=jnp.float32)
            * score_scale
        )
        grad_key = (
            jnp.einsum("hqk,qhd->khd", grad_scores, query_block, preferred_element_type=jnp.float32)
            * score_scale
        )
        grad_value = jnp.einsum(
            "hqk,qhd->khd",
            weights_full.astype(jnp.bfloat16),
            grad_mixed_block,
            preferred_element_type=jnp.float32,
        )
        return (
            grad_query.reshape(block_rows, local_width),
            grad_key.reshape(seq_length, local_width),
            grad_value.reshape(seq_length, local_width),
        )

    query_blocks, key_blocks, value_blocks = lax.map(backward_block, block_ids)
    grad_queries = query_blocks.reshape(group_rows, local_width)
    grad_keys = (
        key_blocks.reshape(seq_count, per_sequence, seq_length, local_width)
        .sum(axis=1)
        .reshape(group_rows, local_width)
    )
    grad_values = (
        value_blocks.reshape(seq_count, per_sequence, seq_length, local_width)
        .sum(axis=1)
        .reshape(group_rows, local_width)
    )
    grad_projected = jnp.stack((grad_queries, grad_keys, grad_values), axis=1).astype(jnp.bfloat16)
    grad_project_part = jnp.einsum(
        "te,tsc->esc", gathered, grad_projected, preferred_element_type=jnp.float32
    )
    grad_matrix = grad_projected.reshape(group_rows, 3 * local_width)
    grad_tokens = (
        lax.psum_scatter(
            jnp.einsum(
                "tc,ec->te", grad_matrix, back_triple, preferred_element_type=jnp.float32
            ).astype(jnp.bfloat16),
            "tensor",
            scatter_dimension=0,
            tiled=True,
        ).astype(jnp.float32)
        + grad_first_in
    )
    grad_project, grad_output, grad_up, grad_down = (
        scatter_sum(grad_project_part, "dp", 0),
        scatter_sum(grad_output_part, "dp", 1),
        scatter_sum(grad_up_part, "dp", 0),
        scatter_sum(grad_down_part, "dp", 1),
    )
    head_terms = place_columns(
        jnp.stack(
            (
                jnp.sum(grad_projected[:, 0], axis=0, dtype=jnp.float32),
                jnp.sum(grad_projected[:, 2], axis=0, dtype=jnp.float32),
            )
        ),
        tensor_rank,
        model_width,
    )
    shared_terms = jnp.stack(
        (
            jnp.sum(grad_branch, axis=0, dtype=jnp.float32),
            grad_shift_one,
            jnp.sum(grad_second, axis=0, dtype=jnp.float32),
            grad_shift_two,
        )
    )
    bias_terms = jnp.concatenate((head_terms, shared_terms), axis=0)
    gain_terms = jnp.stack((grad_gain_one, grad_gain_two))
    hidden_terms = place_columns(
        jnp.sum(grad_upper, axis=0, dtype=jnp.float32), tensor_rank, hidden_bias.shape[0]
    )
    grad_gains, grad_bias_rows, grad_hidden_bias = lax.psum(
        (gain_terms, bias_terms, hidden_terms), ("dp", "tensor")
    )
    return (
        layer_out.astype(jnp.bfloat16),
        grad_tokens,
        grad_project,
        grad_output,
        grad_up,
        grad_down,
        grad_gains,
        grad_bias_rows,
        grad_hidden_bias,
    )


def solution(mesh):
    fits = mesh.shape["dp"] == 2 * LINES and mesh.shape["tensor"] == 4
    placed = (
        P(("dp", "tensor"), None),
        P("dp", None),
        P(("dp", "tensor"), None),
        P("dp", None, "tensor"),
        P("tensor", "dp"),
        P("dp", "tensor"),
        P("tensor", "dp"),
        P(),
        P(),
        P(),
    )
    return jax.shard_map(
        per_device_kernel if fits else per_device,
        mesh=mesh,
        in_specs=placed,
        out_specs=(
            P(("dp", "tensor"), None),
            P(("dp", "tensor"), None),
            P("dp", None, "tensor"),
            P("tensor", "dp"),
            P("dp", "tensor"),
            P("tensor", "dp"),
            P(),
            P(),
            P(),
        ),
        check_vma=False,
    )
```

```python
import functools
import types

import jax
import jax.numpy as jnp
from jax import lax
from jax.experimental import pallas as pl
from jax.experimental.pallas import tpu as pltpu
from jax.sharding import PartitionSpec as P

HEAD = 64
EPSILON = 1e-05
NEGATIVE = -1e30
MESH = pl.DeviceIdType.MESH
LINES = 4
CORE, ACROSS, FAR = 1, 2, 3
HALVES = 2
CHUNK = 16
NORM = 64
ORDER = (3, 2, 1, 0)
VMEM_BYTES = 60 << 20


def remote(src, dst, send_sem, recv_sem, target):
    return pltpu.make_async_remote_copy(
        src_ref=src,
        dst_ref=dst,
        send_sem=send_sem,
        recv_sem=recv_sem,
        device_id=target,
        device_id_type=MESH,
    )


def position():
    return lax.axis_index("dp"), lax.axis_index("tensor")


def greet():
    dp, tensor = position()
    barrier = pltpu.get_barrier_semaphore()
    others = [(dp ^ step, tensor) for step in (1, 2, 4, 6)]
    others += [(dp, tensor ^ step) for step in (CORE, ACROSS)]
    for target in others:
        pl.semaphore_signal(barrier, inc=1, device_id=target, device_id_type=MESH)
    pl.semaphore_wait(barrier, len(others))


def row_piece(ref, index, size):
    return ref.at[pl.ds(pl.multiple_of(index * size, size), size), :]


def column_piece(ref, index, size):
    return ref.at[:, pl.ds(pl.multiple_of(index * size, size), size)]


class LineGather:
    def __init__(self, own, full, piece, send_sem, recv_sem, local_sem):
        self.own, self.full, self.piece = own, full, piece
        self.send_sem, self.recv_sem, self.local_sem = send_sem, recv_sem, local_sem
        self.dp, self.tensor = position()
        self.line, self.side = self.dp // 2, self.dp % 2
        up = self.dp + jnp.where(self.line < LINES - 1, 2, -2)
        down = self.dp + jnp.where(self.line > 0, -2, 2)
        self.targets = (
            (up, self.tensor),
            (down, self.tensor),
            (self.dp ^ 1, self.tensor),
        )

    def copy(self, index, way, src=None):
        view = self.piece(self.full, index)
        return remote(
            view if src is None else src,
            view,
            self.send_sem.at[(LINES - 1) * way - way % 2 + index // 2],
            self.recv_sem.at[index],
            self.targets[way],
        )

    def local(self):
        return pltpu.make_async_copy(self.own, self.piece(self.full, self.dp), self.local_sem)

    def start_along(self):
        self.local().start()

        @pl.when(self.line < LINES - 1)
        def _():
            self.copy(self.dp, 0, self.own).start()

        @pl.when(self.line > 0)
        def _():
            self.copy(self.dp, 1, self.own).start()

    def start_across(self):
        self.copy(self.dp, 2, self.own).start()

    def step_along(self, distance):
        @pl.when(self.line >= distance)
        def _():
            self.copy(self.dp - 2 * distance, 0).wait_recv()

            @pl.when(self.line < LINES - 1)
            def _():
                self.copy(self.dp - 2 * distance, 0).start()

        @pl.when(self.line + distance < LINES)
        def _():
            self.copy(self.dp + 2 * distance, 1).wait_recv()

            @pl.when(self.line > 0)
            def _():
                self.copy(self.dp + 2 * distance, 1).start()

    def step_across(self, distance):
        @pl.when(self.line >= distance)
        def _():
            self.copy(self.dp - 2 * distance, 2).start()

        @pl.when(self.line + distance < LINES)
        def _():
            self.copy(self.dp + 2 * distance, 2).start()

    def step(self, distance):
        self.step_along(distance)
        self.step_across(distance)

    def arrive_block(self, at):
        self.copy(self.dp ^ (2 * at) ^ 1, 2).wait_recv()

    def arrive(self):
        self.local().wait()
        for line in range(LINES):
            self.copy(2 * line + 1 - self.side, 2).wait_recv()

    def finish(self):
        for line in range(LINES):
            index = 2 * line + self.side
            self.copy(index, 2).wait_send()

            @pl.when((self.line < LINES - 1) & (line <= self.line))
            def _():
                self.copy(index, 0).wait_send()

            @pl.when((self.line > 0) & (line >= self.line))
            def _():
                self.copy(index, 1).wait_send()


class RowGather:
    def __init__(self, full, rows, send_sem, recv_sem):
        self.full, self.rows = full, rows
        self.send_sem, self.recv_sem = send_sem, recv_sem
        self.dp, self.tensor = position()

    def view(self, rank, half=None):
        if half is None:
            return row_piece(self.full, rank, self.rows)
        return row_piece(self.full, rank * HALVES + half, self.rows // HALVES)

    def near(self, rank):
        view = self.view(rank)
        target = (self.dp, self.tensor ^ CORE)
        return remote(view, view, self.send_sem.at[0], self.recv_sem.at[0], target)

    def across(self, rank, half):
        view, slot = self.view(rank, half), 1 + half
        target = (self.dp, self.tensor ^ ACROSS)
        return remote(view, view, self.send_sem.at[slot], self.recv_sem.at[slot], target)

    def far(self, rank, half):
        view, slot = self.view(rank, half), 1 + HALVES + half
        target = (self.dp, self.tensor ^ CORE)
        return remote(view, view, self.send_sem.at[slot], self.recv_sem.at[slot], target)

    def start_half(self, half):
        self.across(self.tensor, half).start()

    def start_near(self):
        self.near(self.tensor).start()

    def start(self):
        for half in range(HALVES):
            self.start_half(half)
        self.start_near()

    def wait_near(self):
        self.near(self.tensor ^ CORE).wait_recv()

    def wait_across(self, half):
        self.across(self.tensor ^ ACROSS, half).wait_recv()
        self.far(self.tensor ^ ACROSS, half).start()

    def wait_far(self, half):
        self.far(self.tensor ^ FAR, half).wait_recv()

    def finish(self):
        self.near(self.tensor).wait_send()
        for half in range(HALVES):
            self.across(self.tensor, half).wait_send()
            self.far(self.tensor ^ ACROSS, half).wait_send()


class RowScatter:
    def __init__(self, near_out, near_in, across_out, across_in, send_sem, recv_sem):
        self.near_out, self.near_in = near_out, near_in
        self.across_out, self.across_in = across_out, across_in
        self.send_sem, self.recv_sem = send_sem, recv_sem
        self.dp, self.tensor = position()

    def near(self, slot):
        return remote(
            self.near_out.at[slot],
            self.near_in.at[slot],
            self.send_sem.at[slot],
            self.recv_sem.at[slot],
            (self.dp, self.tensor ^ CORE),
        )

    def across(self, half):
        rows = self.across_in.shape[0] // HALVES
        return remote(
            row_piece(self.across_out, half, rows),
            row_piece(self.across_in, half, rows),
            self.send_sem.at[2 * HALVES + half],
            self.recv_sem.at[2 * HALVES + half],
            (self.dp, self.tensor ^ ACROSS),
        )

    def give_far(self, half, partial):
        self.near_out[half] = partial.astype(jnp.bfloat16)
        self.near(half).start()

    def give_across(self, half, partial):
        self.near(half).wait_recv()
        rows = partial.shape[0]
        total = partial + self.near_in[half].astype(jnp.float32)
        row_piece(self.across_out, half, rows)[...] = total.astype(jnp.bfloat16)
        self.across(half).start()

    def give_near(self, half, partial):
        self.near_out[HALVES + half] = partial.astype(jnp.bfloat16)
        self.near(HALVES + half).start()

    def take(self, half, partial):
        self.near(HALVES + half).wait_recv()
        rows = partial.shape[0]
        total = partial + self.near_in[HALVES + half].astype(jnp.float32)
        self.across(half).wait_recv()
        return total + row_piece(self.across_in, half, rows)[...].astype(jnp.float32)

    def finish(self):
        for slot in range(2 * HALVES):
            self.near(slot).wait_send()
        for half in range(HALVES):
            self.across(half).wait_send()


def dot(left, right):
    return jnp.dot(left, right, preferred_element_type=jnp.float32)


def dot_nt(left, right):
    return lax.dot_general(left, right, (((1,), (1,)), ((), ())), preferred_element_type=jnp.float32)


def dot_tn(left, right):
    return lax.dot_general(left, right, (((0,), (0,)), ((), ())), preferred_element_type=jnp.float32)


def normalize(rows):
    centred = rows - jnp.mean(rows, axis=-1, keepdims=True)
    inverse = lax.rsqrt(jnp.mean(centred * centred, axis=-1, keepdims=True) + EPSILON)
    return centred * inverse, inverse


def norm_back(grad, normed, inverse):
    average = jnp.mean(grad, axis=-1, keepdims=True)
    along = jnp.mean(grad * normed, axis=-1, keepdims=True)
    return inverse * (grad - average - normed * along)


class PairGather:
    def __init__(self, own, full, piece, pair, send_sem, recv_sem, local_sem):
        self.own, self.full, self.piece, self.pair = own, full, piece, pair
        self.send_sem, self.recv_sem, self.local_sem = send_sem, recv_sem, local_sem
        self.dp, self.tensor = position()
        self.line = self.dp // 2
        self.up = jnp.where(self.line < LINES - 1, 2, -2)
        self.down = jnp.where(self.line > 0, -2, 2)

    def local(self):
        return pltpu.make_async_copy(self.own, self.piece(self.full, self.dp), self.local_sem)

    def across(self):
        return remote(
            self.own,
            self.piece(self.full, self.dp),
            self.send_sem.at[0],
            self.recv_sem.at[LINES],
            (self.dp ^ 1, self.tensor),
        )

    def along(self, line, way):
        view = self.pair(self.full, line)
        return remote(
            view,
            view,
            self.send_sem.at[1 + way * 2 + line],
            self.recv_sem.at[line],
            (self.dp + (self.up if way == 0 else self.down), self.tensor),
        )

    def start(self):
        self.local().start()
        self.across().start()

    def begin(self):
        self.local().wait()
        self.across().wait_recv()

        @pl.when(self.line < LINES - 1)
        def _():
            self.along(self.line, 0).start()

        @pl.when(self.line > 0)
        def _():
            self.along(self.line, 1).start()

    def step(self, distance):
        @pl.when(self.line >= distance)
        def _():
            self.along(self.line - distance, 0).wait_recv()

            @pl.when(self.line < LINES - 1)
            def _():
                self.along(self.line - distance, 0).start()

        @pl.when(self.line + distance < LINES)
        def _():
            self.along(self.line + distance, 1).wait_recv()

            @pl.when(self.line > 0)
            def _():
                self.along(self.line + distance, 1).start()

    def finish(self):
        self.across().wait_send()
        for line in range(LINES):

            @pl.when((self.line < LINES - 1) & (line <= self.line))
            def _():
                self.along(line, 0).wait_send()

            @pl.when((self.line > 0) & (line >= self.line))
            def _():
                self.along(line, 1).wait_send()


class LineFirstScatter:
    def __init__(self, partial, piece, line_in, across_out, across_in, send_sem, recv_sem):
        self.partial, self.piece, self.line_in = partial, piece, line_in
        self.across_out, self.across_in = across_out, across_in
        self.send_sem, self.recv_sem = send_sem, recv_sem
        self.dp, self.tensor = position()

    def view(self, step):
        return self.piece(self.partial, (self.dp // 2) ^ step)

    def along(self, step):
        return remote(
            self.view(step),
            self.line_in.at[step // 2 if step != 2 else 2],
            self.send_sem.at[step],
            self.recv_sem.at[step],
            (self.dp ^ (2 if step != 2 else 4), self.tensor),
        )

    def across(self):
        return remote(
            self.across_out,
            self.across_in,
            self.send_sem.at[0],
            self.recv_sem.at[0],
            (self.dp ^ 1, self.tensor),
        )

    def start(self):
        self.along(3).start()

    def relay(self):
        self.along(3).wait_recv()
        total = self.view(2)[...].astype(jnp.float32) + self.line_in[1].astype(jnp.float32)
        self.view(2)[...] = total.astype(jnp.bfloat16)
        self.along(2).start()
        self.along(1).start()

    def turn(self, result):
        total = self.view(0)[...].astype(jnp.float32)
        for step, slot in ((1, 0), (2, 2)):
            self.along(step).wait_recv()
            total = total + self.line_in[slot].astype(jnp.float32)
        first, second = jnp.split(total, 2, 0 if result.shape[1] == total.shape[1] else 1)
        even = self.dp % 2 == 0
        result[...] = jnp.where(even, first, second)
        self.across_out[...] = jnp.where(even, second, first).astype(jnp.bfloat16)
        self.across().start()

    def finish(self, result):
        self.across().wait_recv()
        result[...] += self.across_in[...].astype(jnp.float32)
        self.across().wait_send()
        for step in range(1, LINES):
            self.along(step).wait_send()


class DirectGather:
    def __init__(self, own, full, piece, send_sem, recv_sem, local_sem):
        self.own, self.full, self.piece = own, full, piece
        self.send_sem, self.recv_sem, self.local_sem = send_sem, recv_sem, local_sem
        self.dp, self.tensor = position()

    def along(self, step):
        there = self.dp ^ (2 * step)
        return remote(
            self.own,
            self.piece(self.full, self.dp),
            self.send_sem.at[step],
            self.recv_sem.at[step],
            (there, self.tensor),
        )

    def across(self, step, source=None):
        view = self.piece(self.full, self.dp ^ (2 * step))
        return remote(
            view if source is None else source,
            view,
            self.send_sem.at[LINES + step],
            self.recv_sem.at[LINES + step],
            (self.dp ^ 1, self.tensor),
        )

    def local(self):
        return pltpu.make_async_copy(self.own, self.piece(self.full, self.dp), self.local_sem)

    def start_along(self):
        self.local().start()
        for step in range(1, LINES):
            self.along(step).start()

    def start_across(self):
        self.across(0, self.own).start()

    def step(self, step):
        self.along(step).wait_recv()
        self.across(step).start()

    def arrive(self, step):
        self.across(step).wait_recv()

    def finish(self):
        for step in range(LINES):
            self.across(step).wait_send()
        for step in range(1, LINES):
            self.along(step).wait_send()


class ColumnScatter:
    def __init__(self, near_out, near_in, across_out, across_in, send_sem, recv_sem):
        self.near_out, self.near_in = near_out, near_in
        self.across_out, self.across_in = across_out, across_in
        self.send_sem, self.recv_sem = send_sem, recv_sem
        self.dp, self.tensor = position()

    def near(self, slot):
        return remote(
            self.near_out.at[slot],
            self.near_in.at[slot],
            self.send_sem.at[slot],
            self.recv_sem.at[slot],
            (self.dp, self.tensor ^ CORE),
        )

    def across(self, at):
        return remote(
            self.across_out.at[at],
            self.across_in.at[at],
            self.send_sem.at[2 * LINES + at],
            self.recv_sem.at[2 * LINES + at],
            (self.dp, self.tensor ^ ACROSS),
        )

    def give_far(self, at, partial):
        self.near_out[at] = partial.astype(jnp.bfloat16)
        self.near(at).start()

    def give_near(self, at, partial):
        self.near_out[LINES + at] = partial.astype(jnp.bfloat16)
        self.near(LINES + at).start()

    def give_across(self, at, partial):
        self.near(at).wait_recv()
        total = partial + self.near_in[at].astype(jnp.float32)
        self.across_out[at] = total.astype(jnp.bfloat16)
        self.across(at).start()

    def take(self, at, partial):
        self.near(LINES + at).wait_recv()
        total = partial + self.near_in[LINES + at].astype(jnp.float32)
        self.across(at).wait_recv()
        return total + self.across_in[at].astype(jnp.float32)

    def finish(self):
        for slot in range(2 * LINES):
            self.near(slot).wait_send()
        for at in range(LINES):
            self.across(at).wait_send()


class LineScatter:
    def __init__(self, partial, piece, side_in, line_in, send_sem, recv_sem):
        self.partial, self.piece, self.side_in, self.line_in = partial, piece, side_in, line_in
        self.send_sem, self.recv_sem = send_sem, recv_sem
        self.dp, self.tensor = position()

    def view(self, step):
        return self.piece(self.partial, self.dp ^ (2 * step))

    def across(self, step):
        return remote(
            self.piece(self.partial, self.dp ^ (2 * step) ^ 1),
            self.side_in.at[step],
            self.send_sem.at[step],
            self.recv_sem.at[step],
            (self.dp ^ 1, self.tensor),
        )

    def along(self, step):
        return remote(
            self.view(step),
            self.line_in.at[step // 2 if step != 2 else 2],
            self.send_sem.at[LINES + step],
            self.recv_sem.at[LINES + step],
            (self.dp ^ (2 if step != 2 else 4), self.tensor),
        )

    def start(self, order=ORDER):
        for step in order:
            self.across(step).start()

    def total(self, step):
        self.across(step).wait_recv()
        return self.view(step)[...].astype(jnp.float32) + self.side_in[step].astype(jnp.float32)

    def relay(self, step):
        total = self.total(step)
        if step == 2:
            self.along(3).wait_recv()
            total = total + self.line_in[1].astype(jnp.float32)
        self.view(step)[...] = total.astype(jnp.bfloat16)
        self.along(step).start()

    def finish(self, result):
        total = self.total(0)
        self.along(1).wait_recv()
        total = total + self.line_in[0].astype(jnp.float32)
        self.along(2).wait_recv()
        result[...] = total + self.line_in[2].astype(jnp.float32)
        for step in range(LINES):
            self.across(step).wait_send()
        for step in range(1, LINES):
            self.along(step).wait_send()


class Total:
    def __init__(self, held, arrived, send_sem, recv_sem):
        self.held, self.arrived, self.send_sem, self.recv_sem = held, arrived, send_sem, recv_sem
        dp, tensor = position()
        self.targets = (
            (dp ^ 1, tensor),
            (dp ^ 2, tensor),
            (dp ^ 4, tensor),
            (dp, tensor ^ ACROSS),
            (dp, tensor ^ CORE),
        )

    def copy(self, step):
        return remote(
            self.part(self.held, step),
            self.part(self.arrived, step),
            self.send_sem.at[step],
            self.recv_sem.at[step],
            self.targets[step],
        )

    def start(self):
        self.copy(0).start()

    def part(self, ref, step):
        return ref.at[step, :8] if step < 3 else ref.at[step]

    def step(self, step, spread=None):
        self.copy(step).wait_recv()
        total = self.part(self.held, step)[...] + self.part(self.arrived, step)[...]
        if spread is None:
            self.held[step + 1, : total.shape[0]] = total
        else:
            spread(total)
        if step + 1 < len(self.targets):
            self.copy(step + 1).start()

    def finish(self):
        for step in range(len(self.targets)):
            self.copy(step).wait_send()


def layer_kernel(names, rows, *refs):
    r = types.SimpleNamespace(**dict(zip(names, refs)))
    dp, tensor = position()
    bf16, f32 = jnp.bfloat16, jnp.float32
    half_rows = rows // HALVES
    local = r.queries.shape[1]
    piece = r.triple_own.shape[1]
    pairs = local // (2 * HEAD)
    length, hidden = r.hidden.shape
    near, across, far = tensor ^ CORE, tensor ^ ACROSS, tensor ^ FAR

    def of_rows(ref, index):
        return row_piece(ref, index, piece)

    def of_columns(ref, index):
        return column_piece(ref, index, piece)

    def of_stack(ref, index):
        return ref.at[:, pl.ds(pl.multiple_of(index * piece, piece), piece), :]

    def of_half_stack(half):
        size = piece // HALVES

        def view(ref, index):
            return ref.at[:, pl.ds(pl.multiple_of(index * piece + half * size, size), size), :]

        return view, r.triple_own.at[:, half * size : (half + 1) * size, :]

    def block(rank, size=rows):
        return pl.ds(pl.multiple_of(rank * size, size), size)

    def split(partial):
        return [partial[half * half_rows : (half + 1) * half_rows] for half in range(HALVES)]

    def part_of(half):
        return slice(half * half_rows, (half + 1) * half_rows)

    (view_a, own_a), (view_b, own_b) = of_half_stack(0), of_half_stack(1)
    lines = [
        kind(own, full, view, r.line_send.at[at], r.line_recv.at[at], r.line_local.at[at])
        for at, (kind, own, full, view) in enumerate(
            (
                (LineGather, own_a, r.triple, view_a),
                (LineGather, own_b, r.triple, view_b),
                (DirectGather, r.output_own, r.output, of_columns),
                (LineGather, r.up_own, r.up, of_rows),
                (LineGather, r.down_own.at[: hidden // 2, :], r.down.at[: hidden // 2, :], of_columns),
            )
        )
    ]
    *triple_lines, output_line, up_line, down_line = lines

    def of_both(ref, index):
        return column_piece(ref, index, 2 * piece)

    rest_line = PairGather(
        r.down_own.at[hidden // 2 :, :],
        r.down.at[hidden // 2 :, :],
        of_columns,
        of_both,
        r.pair_send,
        r.pair_recv,
        r.pair_local,
    )
    sums = [
        LineScatter(partial, view, side, along, r.part_send.at[at], r.part_recv.at[at])
        for at, (partial, view, side, along) in enumerate(
            (
                (r.grad_project, of_stack, r.project_side, r.project_line),
                (r.grad_output, of_columns, r.output_side, r.output_line),
                (r.grad_up, of_rows, r.up_side, r.up_line),
                (r.grad_down.at[: hidden // 2, :], of_columns, r.down_side, r.down_line),
            )
        )
    ]
    project_sum, output_sum, up_sum, down_sum = sums

    rest_sum = LineFirstScatter(
        r.grad_down.at[hidden // 2 :, :],
        of_both,
        r.rest_line,
        r.rest_out,
        r.rest_in,
        r.rest_send.at[0],
        r.rest_recv.at[0],
    )
    down_top, down_rest = r.down_sum.at[: hidden // 2, :], r.down_sum.at[hidden // 2 :, :]
    gathers = [
        RowGather(full, rows, r.row_send, r.row_recv)
        for full in (r.gathered, r.first_all, r.second_all, r.branch_all)
    ]
    row_buffers = r.near_out_a, r.near_in_a, r.across_out_a, r.across_in_a
    column_buffers = r.near_out_b, r.near_in_b, r.across_out_b, r.across_in_b
    scatters = [
        RowScatter(*row_buffers, r.row_sum_send, r.row_sum_recv),
        ColumnScatter(*column_buffers, r.column_sum_send, r.column_sum_recv),
    ] * 2
    total = Total(r.held_totals, r.arrived_totals, r.total_send, r.total_recv)

    def column_pair(at):
        return block((dp // 4) ^ at, 4 * piece)

    def give_halves(method, at, partial):
        for half in range(HALVES):
            method(at * HALVES + half, partial[part_of(half)])

    def keep_near(scatter, at, product):
        give_halves(scatter.give_near, at, product(near, column_pair(at)))
        r.kept[:, column_pair(at)] = product(tensor, column_pair(at))

    def take_columns(scatter, result, at):
        part, lanes = block(at % HALVES, half_rows), column_pair(at // HALVES)
        result[part, lanes] = scatter.take(at, r.kept[part, lanes])

    def chunks(size, start, body, step=CHUNK):
        @pl.loop(0, size // step)
        def _(chunk):
            offset = chunk * step
            body(
                pl.ds(pl.multiple_of(offset, step), step),
                pl.ds(pl.multiple_of(start + offset, step), step),
            )

    loads = [
        pltpu.make_async_copy(source, target, r.load_sem.at[at])
        for at, (source, target) in enumerate(
            (
                (r.tokens, gathers[0].view(tensor)),
                (r.segments, r.segment_row),
                (r.bias_from, r.bias_rows),
                (r.gains_from, r.norm_gains),
                (r.hidden_from.at[pl.ds(pl.multiple_of(tensor * hidden, hidden), hidden)], r.hidden_bias),
                (r.cotangent_from, r.cotangent),
            )
        )
    ]
    for load in loads:
        load.start()
    greet()
    for line in triple_lines:
        line.start_along()
        line.start_across()
    loads[0].wait()
    gathers[0].start()
    for line in triple_lines:
        line.step(1)
    loads[1].wait()
    numbers = r.segment_row[...].astype(f32)
    r.segment_column[...] = jnp.broadcast_to(numbers, (8, numbers.shape[1])).T[:, :1]
    r.segment_row_f32[...] = numbers
    for line in triple_lines:
        line.step(2)
    gathers[0].wait_near()
    for half in range(HALVES):
        gathers[0].wait_across(half)
    for line in triple_lines:
        line.step(3)
    output_line.start_along()
    output_line.start_across()
    rest_line.start()
    up_line.start_along()
    down_line.start_along()
    for half in range(HALVES):
        gathers[0].wait_far(half)
    for line in triple_lines:
        line.arrive()
    for load in loads[2:]:
        load.wait()
    columns = pl.ds(pl.multiple_of(tensor * local, local), local)
    query_bias = r.bias_rows[0:1, columns]
    value_bias = r.bias_rows[1:2, columns]

    @pl.loop(0, 4)
    def _(index):
        here = block(index)
        left = r.gathered[here, :]
        query = (dot(left, r.triple[0]) + query_bias).astype(bf16)
        r.queries[here, :] = query * bf16(HEAD**-0.5)
        key = dot(left, r.triple[1])
        r.key_rows[here, :] = key.astype(bf16)
        r.key_turned[:, here] = key.T.astype(bf16)
        value = dot(left, r.triple[2]) + value_bias
        r.value_rows[here, :] = value.astype(bf16)
        r.value_turned[:, here] = value.T.astype(bf16)

    for step in range(1, LINES):
        output_line.step(step)
    up_line.start_across()

    def head_rows(head):
        return pl.ds(pl.multiple_of(head * HEAD, HEAD), HEAD)

    def attend(here, pair):
        lanes = block(pair, 2 * HEAD)
        query = r.queries[here, lanes]
        keys = r.key_rows[:, lanes]
        same = r.segment_column[...] == r.segment_row_f32[:, here]
        lane = lax.broadcasted_iota(jnp.int32, query.shape, 1)
        outs = []
        for side in range(2):
            scores = dot_nt(keys, jnp.where(lane // HEAD == side, query, bf16(0)))
            scores = jnp.where(same, scores, NEGATIVE)
            top = jnp.max(scores, axis=0, keepdims=True)
            exponent = jnp.exp(scores - top)
            mass = jnp.sum(exponent, axis=0, keepdims=True)
            weights = (exponent * (1.0 / mass)).astype(bf16)
            head = pair * 2 + side
            outs.append(dot(r.value_turned[head_rows(head), :], weights))
            r.log_totals[pl.ds(head, 1), here] = top + jnp.log(mass)
        r.mixed[here, lanes] = jnp.concatenate(outs, axis=0).T.astype(bf16)

    @pl.loop(0, 4 * pairs)
    def _(turn):
        rank, pair = tensor ^ (FAR - turn // pairs), turn % pairs
        here = block(rank)
        attend(here, pair)

        def give(rank, method):
            r.partial[...] = dot(r.mixed[block(rank), :], r.output[...])
            for half in range(HALVES):
                method(half, r.partial[part_of(half), :])

        def after(index):
            return pl.when(turn == index)

        @after(0)
        def _():
            up_line.step(1)

        @after(1)
        def _():
            rest_line.begin()

        @after(3)
        def _():
            output_line.local().wait()
            for step in range(LINES):
                output_line.arrive(step)
            give(far, scatters[0].give_far)
            give(across, scatters[0].give_across)

        @after(4)
        def _():
            up_line.step(2)
            down_line.step_along(1)

        @after(5)
        def _():
            give(near, scatters[0].give_near)

        @after(7)
        def _():
            rest_line.step(1)
            up_line.step(3)
            down_line.start_across()
            down_line.step_across(1)

    r.partial[...] = dot(r.mixed[block(tensor), :], r.output[...])
    gathers[0].finish()
    for half in range(HALVES):
        part = part_of(half)
        r.kept[part, :] = scatters[0].take(half, r.partial[part, :])

        def first_norm(_, here):
            own_rows = r.gathered[pl.ds(pl.multiple_of(tensor * rows + here.start, NORM), NORM), :]
            normed, inverse = normalize(own_rows.astype(f32) + r.kept[here, :] + r.bias_rows[2:3, :])
            r.normed_one[here, :] = normed
            r.inverse_one[here, :] = inverse
            first = normed * r.norm_gains[0:1, :] + r.bias_rows[3:4, :]
            into = pl.ds(pl.multiple_of(tensor * rows + here.start, NORM), NORM)
            r.first_all[into, :] = first.astype(bf16)

        chunks(half_rows, half * half_rows, first_norm, NORM)
        gathers[1].start_half(half)
    scatters[0].finish()

    gathers[1].start_near()
    r.sums[...] = jnp.zeros_like(r.sums)

    def extent(rank, half):
        size = rows if half is None else half_rows
        start = rank * rows + (0 if half is None else half * half_rows)
        return start, size, pl.ds(pl.multiple_of(start, size), size)

    def up_part(rank, half=None):
        start, size, here = extent(rank, half)
        r.upper[:size, :] = dot(r.first_all[here, :], r.up[...]) + r.hidden_bias[...].reshape(1, hidden)

        def body(part, into):
            value = r.upper[part, :]
            share = 0.5 + 0.5 * lax.erf(value * (0.5**0.5))
            r.hidden[into, :] = (value * share).astype(bf16)
            bell = jnp.exp(value * value * -0.5) * (2 * jnp.pi) ** -0.5
            r.slope[into, :] = share + value * bell

        chunks(size, start, body)

    def back_part(rank, half=None):
        start, size, here = extent(rank, half)
        r.upper[:size, :] = dot_nt(r.second_all[here, :], r.down[...])

        def body(part, into):
            low = (r.upper[part, :] * r.slope[into, :]).astype(bf16)
            r.upper_low[into, :] = low
            r.sums[6:7, :] += jnp.sum(low.astype(f32), axis=0, keepdims=True)

        chunks(size, start, body)
        r.partial[:size, :] = dot_nt(r.upper_low[here, :], r.up[...])

    down_line.step(2)
    up_line.arrive()

    @pl.loop(0, 2)
    def _(turn):
        @pl.when(turn == 1)
        def _():
            gathers[1].wait_near()
            down_line.step(3)
            rest_line.step(2)

        up_part(tensor ^ turn)

    def other_chip(gather, body):
        @pl.loop(0, 2 * HALVES)
        def _(turn):
            half, side = turn // 2, turn % 2

            @pl.when(turn == 0)
            def _():
                gather.wait_across(0)

            body(half, side)

    def up_other(half, side):
        @pl.when(side == 1)
        def _():
            gathers[1].wait_far(half)

        up_part(tensor ^ (ACROSS + side), half)

    def down_part(rank, lanes):
        return dot(r.hidden[block(rank), :], r.down[:, lanes])

    def send_unit(at, half):
        def product(rank):
            return dot(r.hidden[extent(rank, half)[2], :], r.down[:, column_pair(at)])

        scatters[1].give_far(at * HALVES + half, product(far))
        scatters[1].give_across(at * HALVES + half, product(across))

    def up_and_send(half, side):
        up_other(half, side)

        @pl.when((side == 1) & (half == 0))
        def _():
            gathers[1].wait_across(1)
            down_line.local().wait()
            down_line.arrive_block(0)
            down_line.arrive_block(1)
            send_unit(0, 0)

    other_chip(gathers[1], up_and_send)

    send_unit(0, 1)
    keep_near(scatters[1], 0, down_part)
    rest_line.step(3)
    down_line.arrive_block(2)
    down_line.arrive_block(3)
    send_unit(1, 0)
    send_unit(1, 1)
    keep_near(scatters[1], 1, down_part)

    def add_to(row, value):
        r.sums[row : row + 1, :] += jnp.sum(value, axis=0, keepdims=True)

    def second_norm(_, here):
        first = r.normed_one[here, :] * r.norm_gains[0:1, :] + r.bias_rows[3:4, :]
        normed, inverse = normalize(first + r.kept[here, :] + r.bias_rows[4:5, :])
        shifted = normed * r.norm_gains[1:2, :] + r.bias_rows[5:6, :]
        r.layer_low[here, :] = shifted.astype(bf16)
        grad = r.cotangent[here, :].astype(f32)
        add_to(5, grad * normed)
        add_to(3, grad)
        grad = norm_back(grad * r.norm_gains[1:2, :], normed, inverse)
        r.grad_rows[here, :] = grad
        low = grad.astype(bf16)
        add_to(2, low.astype(f32))
        r.second_all[pl.ds(pl.multiple_of(tensor * rows + here.start, NORM), NORM), :] = low

    gathers[1].finish()
    for half in range(HALVES):
        for at in range(2):
            take_columns(scatters[1], r.kept, at * HALVES + half)
        chunks(half_rows, half * half_rows, second_norm, NORM)
        gathers[2].start_half(half)
    saves = []

    def save(source, target):
        saves.append(pltpu.make_async_copy(source, target, r.save_sem.at[len(saves)]))
        saves[-1].start()

    save(r.layer_low, r.layer_out)
    scatters[1].finish()

    gathers[2].start_near()

    @pl.loop(0, 2)
    def _(turn):
        @pl.when(turn == 1)
        def _():
            gathers[2].wait_near()

        back_part(tensor ^ turn)

        @pl.when(turn == 0)
        def _():
            r.kept[...] = r.partial[...]

        @pl.when(turn == 1)
        def _():
            for half in range(HALVES):
                scatters[2].give_near(half, r.partial[part_of(half), :])

    def weight_grad(left, right, result, chip=None, add=False):
        depth = slice(None) if chip is None else block(chip, 2 * rows)

        @pl.loop(0, left.shape[1] // rows)
        def _(index):
            lanes = block(index)
            product = dot_tn(left[depth, lanes], right[depth, :])
            if add:
                product += result[lanes, :].astype(f32)
            result[lanes, :] = product.astype(bf16)

    weight_grad(r.hidden, r.second_all, r.grad_down, tensor // 2)

    def back_other(half, side):
        @pl.when((side == 1) & (half < HALVES - 1))
        def _():
            gathers[2].wait_far(half)

        @pl.when((side == 0) & (half == HALVES - 1))
        def _():
            gathers[2].wait_far(half)
            weight_grad(r.hidden, r.second_all, r.grad_down, 1 - tensor // 2, True)
            rest_sum.start()
            down_sum.start()

        back_part(tensor ^ (ACROSS + side), half)

        @pl.when(side == 0)
        def _():
            r.held[...] = r.partial[:half_rows, :]

        @pl.when(side == 1)
        def _():
            scatters[2].give_far(half, r.partial[:half_rows, :])

            @pl.when(half == 0)
            def _():
                gathers[2].wait_across(1)

            scatters[2].give_across(half, r.held[...])

    other_chip(gathers[2], back_other)

    weight_grad(r.first_all, r.upper_low, r.grad_up)
    up_sum.start()

    def first_back(_, here):
        grad = r.grad_rows[here, :] + r.kept[here, :]
        normed = r.normed_one[here, :]
        add_to(4, grad * normed)
        add_to(1, grad)
        grad = norm_back(grad * r.norm_gains[0:1, :], normed, r.inverse_one[here, :])
        r.grad_rows[here, :] = grad
        low = grad.astype(bf16)
        add_to(0, low.astype(f32))
        r.branch_all[pl.ds(pl.multiple_of(tensor * rows + here.start, NORM), NORM), :] = low

    gathers[2].finish()
    for half in range(HALVES):
        part = part_of(half)
        r.kept[part, :] = scatters[2].take(half, r.kept[part, :])
        chunks(half_rows, half * half_rows, first_back, NORM)
        gathers[3].start_half(half)
        if half == 0:
            rest_sum.relay()
            down_sum.relay(3)
    scatters[2].finish()

    gathers[3].start_near()
    grad_keys, grad_values = r.slope.at[:, :local], r.slope.at[:, local : 2 * local]
    r.slope[:, : 2 * local] = jnp.zeros((r.slope.shape[0], 2 * local), f32)

    def attend_back(rank):
        here = block(rank)
        r.mixed_low[...] = dot_nt(r.branch_all[here, :], r.output[...]).astype(bf16)

        @pl.loop(0, pairs)
        def _(pair):
            lanes = block(pair, 2 * HEAD)
            query = r.queries[here, lanes]
            grad = r.mixed_low[:, lanes]
            keys = r.key_rows[:, lanes]
            values = r.value_rows[:, lanes]
            same = r.segment_column[...] == r.segment_row_f32[:, here]
            lane = lax.broadcasted_iota(jnp.int32, query.shape, 1)
            outs = []
            for side in range(2):
                mine = lane // HEAD == side
                head = pair * 2 + side
                query_here = jnp.where(mine, query, bf16(0))
                grad_here = jnp.where(mine, grad, bf16(0))
                scores = jnp.where(same, dot_nt(keys, query_here), NEGATIVE)
                weights = jnp.exp(scores - r.log_totals[pl.ds(head, 1), here])
                grad_weights = dot_nt(values, grad_here)
                along = jnp.sum(weights * grad_weights, axis=0, keepdims=True)
                grad_scores = (weights * (grad_weights - along)).astype(bf16)
                grad_keys[:, lanes] += dot(grad_scores, query_here)
                grad_values[:, lanes] += dot(weights.astype(bf16), grad_here)
                outs.append(dot(r.key_turned[head_rows(head), :], grad_scores))
            grad_query = jnp.concatenate(outs, axis=0).T * HEAD**-0.5
            r.projected_low[here, lanes] = grad_query.astype(bf16)

    @pl.loop(0, 4)
    def _(turn):
        @pl.when(turn == 1)
        def _():
            gathers[3].wait_near()

        @pl.when(turn == 2)
        def _():
            for half in range(HALVES):
                gathers[3].wait_across(half)

        @pl.when(turn == 3)
        def _():
            for half in range(HALVES):
                gathers[3].wait_far(half)
            r.grad_output[...] = dot_tn(r.mixed[...], r.branch_all[...]).astype(bf16)
            output_sum.start()

        attend_back(tensor ^ turn)

        @pl.when(turn == 0)
        def _():
            down_sum.relay(1)

        @pl.when(turn == 1)
        def _():
            up_sum.relay(3)

        @pl.when(turn == 2)
        def _():
            down_sum.relay(2)
            rest_sum.turn(down_rest)

    up_sum.relay(2)
    up_sum.relay(1)
    r.projected_low[:, local : 2 * local] = grad_keys[...].astype(bf16)
    r.projected_low[:, 2 * local :] = grad_values[...].astype(bf16)
    r.held_totals[0, :8] = jnp.zeros((8,) + r.held_totals.shape[2:], f32)
    r.held_totals[0, 1:2, :] = r.sums[6:7, :]
    r.held_totals[0, 2:8, :] = r.sums[0:6, :]
    shifts = dot(jnp.ones((CHUNK, length), bf16), r.projected_low[...])
    for row, at in ((0, 0), (1, 2)):
        r.held_totals[0, 0:1, row * local : (row + 1) * local] = shifts[:1, at * local : (at + 1) * local]

    def spread(sums):
        r.held_totals[3] = jnp.zeros(r.held_totals.shape[1:], f32)
        r.held_totals[3, 2:8, :] = sums[2:8]
        r.held_totals[3, pl.ds(8 + tensor, 1), :] = sums[1:2]
        for row in range(2):
            r.held_totals[3, row : row + 1, columns] = sums[:1, row * local : (row + 1) * local]

    total.start()

    @pl.loop(0, r.gathered.shape[1] // rows)
    def _(index):
        lanes = block(index)
        product = dot_tn(r.gathered[:, lanes], r.projected_low[...]).astype(bf16)
        for at in range(3):
            r.grad_project[at, lanes, :] = product[:, at * local : (at + 1) * local]

    project_sum.start()

    def token_part(rank, lanes):
        product = 0
        for part in range(3):
            left = r.projected_low[block(rank), part * local : (part + 1) * local]
            product += dot_nt(left, r.triple[part, lanes, :])
        return product

    @pl.loop(0, 2)
    def _(at):
        give_halves(scatters[3].give_far, at, token_part(far, column_pair(at)))
        give_halves(scatters[3].give_across, at, token_part(across, column_pair(at)))
        keep_near(scatters[3], at, token_part)

    total.step(0)
    output_sum.relay(3)
    project_sum.relay(3)
    down_sum.finish(down_top)
    rest_sum.finish(down_rest)
    save(r.down_sum, r.down_out)

    def take_tokens(at):
        part, lanes = part_of(at % HALVES), column_pair(at // HALVES)
        r.grad_rows[part, lanes] += scatters[3].take(at, r.kept[part, lanes])

    take_tokens(0)
    take_tokens(1)
    output_sum.relay(2)
    take_tokens(2)
    total.step(1)
    take_tokens(3)
    save(r.grad_rows, r.grad_tokens)
    gathers[3].finish()
    for each in lines + [rest_line]:
        each.finish()
    project_sum.relay(2)
    project_sum.relay(1)
    scatters[3].finish()
    up_sum.finish(r.up_sum)
    save(r.up_sum, r.up_out)
    total.step(2, spread)
    output_sum.relay(1)
    total.step(3)
    project_sum.finish(r.project_sum)
    save(r.project_sum, r.project_out)
    total.step(4)
    r.bias_sum[...] = r.held_totals[5, 0:6, :]
    r.gains_sum[...] = r.held_totals[5, 6:8, :]
    for at in range(4):
        r.hidden_sum[at * hidden : (at + 1) * hidden] = r.held_totals[5, 8 + at, :]
    save(r.bias_sum, r.bias_out)
    save(r.gains_sum, r.gains_out)
    save(r.hidden_sum, r.hidden_out)
    output_sum.finish(r.output_sum)
    save(r.output_sum, r.output_out)
    total.finish()
    for each in saves:
        each.wait()


def copy_kernel(count, *refs):
    sources, targets, held, sem = refs[:count], refs[count : 2 * count], refs[2 * count : -1], refs[-1]
    copies_in = [pltpu.make_async_copy(*pair, sem.at[at]) for at, pair in enumerate(zip(sources, held))]
    copies_out = [
        pltpu.make_async_copy(*pair, sem.at[count + at]) for at, pair in enumerate(zip(held, targets))
    ]
    for copy in copies_in:
        copy.start()
    for arrived, copy in zip(copies_in, copies_out):
        arrived.wait()
        copy.start()
    for copy in copies_out:
        copy.wait()


def per_device_kernel(
    tokens,
    segments,
    cotangent,
    project_weight,
    output_weight,
    up_weight,
    down_weight,
    norm_gains,
    bias_rows,
    hidden_bias,
):
    rows, width = tokens.shape
    length = segments.shape[1]
    local_hidden = up_weight.shape[1]
    local = output_weight.shape[0]
    piece = project_weight.shape[0]
    bf16, f32 = jnp.bfloat16, jnp.float32
    inputs = dict(
        tokens=tokens,
        triple_own=project_weight.transpose(1, 0, 2),
        output_own=output_weight,
        up_own=up_weight,
        down_own=down_weight,
        segments=segments,
        cotangent_from=cotangent,
        gains_from=norm_gains,
        bias_from=bias_rows,
        hidden_from=hidden_bias,
    )
    shapes = dict(
        project=(3, piece, local),
        output=(local, piece),
        up=(piece, local_hidden),
        down=(local_hidden, piece),
    )
    outputs = dict(layer_out=((rows, width), bf16), grad_tokens=((rows, width), f32))
    outputs |= {name + "_out": (shape, f32) for name, shape in shapes.items()}
    outputs |= dict(
        gains_out=((2, width), f32),
        bias_out=((6, width), f32),
        hidden_out=(hidden_bias.shape, f32),
    )
    scratch = dict(
        segment_row=((1, length), jnp.int32),
        segment_row_f32=((1, length), f32),
        segment_column=((length, 1), f32),
        cotangent=((rows, width), bf16),
        norm_gains=(norm_gains.shape, f32),
        bias_rows=(bias_rows.shape, f32),
        hidden_bias=((local_hidden,), f32),
        layer_low=((rows, width), bf16),
        bias_sum=(bias_rows.shape, f32),
        gains_sum=(norm_gains.shape, f32),
        hidden_sum=(hidden_bias.shape, f32),
        partial=((rows, width), f32),
        gathered=((length, width), bf16),
        triple=((3, width, local), bf16),
        output=((local, width), bf16),
        up=((width, local_hidden), bf16),
        down=((local_hidden, width), bf16),
        queries=((length, local), bf16),
        key_rows=((length, local), bf16),
        value_rows=((length, local), bf16),
        key_turned=((local, length), bf16),
        value_turned=((local, length), bf16),
        mixed=((length, local), bf16),
        log_totals=((local // HEAD, length), f32),
        normed_one=((rows, width), f32),
        inverse_one=((rows, 1), f32),
        first_all=((length, width), bf16),
        hidden=((length, local_hidden), bf16),
        slope=((length, local_hidden), f32),
        second_all=((length, width), bf16),
        upper_low=((length, local_hidden), bf16),
        upper=((rows, local_hidden), f32),
        kept=((rows, width), f32),
        held=((rows // HALVES, width), f32),
        grad_rows=((rows, width), f32),
        sums=((8, width), f32),
        branch_all=((length, width), bf16),
        mixed_low=((rows, local), bf16),
        projected_low=((length, 3 * local), bf16),
        grad_project=((3, width, local), bf16),
        grad_output=((local, width), bf16),
        grad_up=((width, local_hidden), bf16),
        grad_down=((local_hidden, width), bf16),
        held_totals=((6, 16, width), f32),
        arrived_totals=((5, 16, width), f32),
    )
    for name, shape in shapes.items():
        scratch[name + "_sum"] = (shape, f32)
        moved = (local_hidden // 2, piece) if name == "down" else shape
        scratch[name + "_side"] = ((LINES,) + moved, bf16)
        scratch[name + "_line"] = ((LINES - 1,) + moved, bf16)
    scratch |= dict(
        rest_line=((LINES - 1, local_hidden // 2, 2 * piece), bf16),
        rest_out=((local_hidden // 2, piece), bf16),
        rest_in=((local_hidden // 2, piece), bf16),
    )
    for name in ("near_out_", "near_in_"):
        scratch[name + "a"] = ((2 * HALVES, rows // HALVES, width), bf16)
        scratch[name + "b"] = ((2 * LINES, rows // HALVES, 4 * piece), bf16)
    for name in ("across_out_", "across_in_"):
        scratch[name + "a"] = ((rows, width), bf16)
        scratch[name + "b"] = ((LINES, rows // HALVES, 4 * piece), bf16)
    semaphores = dict(
        line_send=(5, 3 * LINES - 2),
        line_recv=(5, 2 * LINES),
        line_local=(5,),
        part_send=(4, 2 * LINES),
        part_recv=(4, 2 * LINES),
        pair_send=(2 * LINES - 1,),
        pair_recv=(LINES + 1,),
        pair_local=(),
        rest_send=(1, LINES),
        rest_recv=(1, LINES),
        row_send=(1 + 2 * HALVES,),
        row_recv=(1 + 2 * HALVES,),
        row_sum_send=(3 * HALVES,),
        row_sum_recv=(3 * HALVES,),
        column_sum_send=(3 * LINES,),
        column_sum_recv=(3 * LINES,),
        total_send=(5,),
        total_recv=(5,),
        load_sem=(6,),
        save_sem=(9,),
    )
    names = [*inputs, *outputs, *scratch, *semaphores]
    hbm = pl.BlockSpec(memory_space=pltpu.HBM)
    results = pl.pallas_call(
        functools.partial(layer_kernel, names, rows),
        out_shape=[jax.ShapeDtypeStruct(*leaf) for leaf in outputs.values()],
        in_specs=[hbm] * len(inputs),
        out_specs=[hbm] * len(outputs),
        scratch_shapes=[pltpu.VMEM(*leaf) for leaf in scratch.values()]
        + [pltpu.SemaphoreType.DMA(shape) for shape in semaphores.values()],
        compiler_params=pltpu.CompilerParams(
            collective_id=0, has_side_effects=True, vmem_limit_bytes=VMEM_BYTES
        ),
        name="layer",
    )(*inputs.values())
    results = pl.pallas_call(
        functools.partial(copy_kernel, len(outputs)),
        out_shape=[jax.ShapeDtypeStruct(*leaf) for leaf in outputs.values()],
        in_specs=[hbm] * len(outputs),
        out_specs=[hbm] * len(outputs),
        scratch_shapes=[pltpu.VMEM(*leaf) for leaf in outputs.values()]
        + [pltpu.SemaphoreType.DMA((2 * len(outputs),))],
        name="copy",
    )(*results)
    result = dict(zip(outputs, results))
    return (
        result["layer_out"],
        result["grad_tokens"],
        result["project_out"].transpose(1, 0, 2),
        result["output_out"],
        result["up_out"],
        result["down_out"],
        result["gains_out"],
        result["bias_out"],
        result["hidden_out"],
    )


def gelu_exact(values):
    return jax.nn.gelu(values, approximate=False)


def layer_norm(token_rows, gain, shift):
    average = jnp.mean(token_rows, axis=-1, keepdims=True)
    centred = token_rows - average
    variance = jnp.mean(centred * centred, axis=-1, keepdims=True)
    inverse = lax.rsqrt(variance + EPSILON)
    normed = centred * inverse
    return (normed * gain + shift, (normed, inverse))


def norm_back_saved(grad_rows, saved, gain):
    normed, inverse = saved
    grad_gain = jnp.sum(grad_rows * normed, axis=0)
    grad_shift = jnp.sum(grad_rows, axis=0)
    grad_normed = grad_rows * gain
    grad_input = inverse * (
        grad_normed
        - jnp.mean(grad_normed, axis=-1, keepdims=True)
        - normed * jnp.mean(grad_normed * normed, axis=-1, keepdims=True)
    )
    return (grad_input, grad_gain, grad_shift)


def split_heads(token_rows):
    return token_rows.reshape(token_rows.shape[0], token_rows.shape[1] // HEAD, HEAD)


def scatter_sum(partial_sum, axis_name, dimension):
    return lax.psum_scatter(
        partial_sum.astype(jnp.bfloat16), axis_name, scatter_dimension=dimension, tiled=True
    ).astype(jnp.float32)


def place_columns(partial_sum, column_block, total_width):
    full_rows = jnp.zeros(partial_sum.shape[:-1] + (total_width,), jnp.float32)
    return lax.dynamic_update_slice_in_dim(
        full_rows, partial_sum, column_block * partial_sum.shape[-1], partial_sum.ndim - 1
    )


def per_device(
    tokens,
    segments,
    cotangent,
    project_weight,
    output_weight,
    up_weight,
    down_weight,
    norm_gains,
    bias_rows,
    hidden_bias,
):
    tensor_rank = lax.axis_index("tensor")
    local_rows, model_width = tokens.shape
    seq_count, seq_length = segments.shape
    group_rows = seq_count * seq_length
    local_width = project_weight.shape[2]
    score_scale = HEAD ** (-0.5)
    block_rows = min(512, seq_length)
    per_sequence = seq_length // block_rows
    count_blocks = group_rows // block_rows
    block_ids = jnp.arange(count_blocks, dtype=jnp.int32)
    triple_full, output_full, upward_full, downward_full = (
        lax.all_gather(project_weight, "dp", axis=0, tiled=True),
        lax.all_gather(output_weight, "dp", axis=1, tiled=True),
        lax.all_gather(up_weight, "dp", axis=0, tiled=True),
        lax.all_gather(down_weight, "dp", axis=1, tiled=True),
    )
    local_hidden = upward_full.shape[1]
    triple_matrix = triple_full.reshape(model_width, 3 * local_width)
    gathered = lax.all_gather(tokens, "tensor", axis=0, tiled=True)
    head_bias = lax.dynamic_slice_in_dim(bias_rows, tensor_rank * local_width, local_width, 1)
    projected = jnp.dot(gathered, triple_matrix, preferred_element_type=jnp.float32).reshape(
        group_rows, 3, local_width
    )
    queries = (projected[:, 0] + head_bias[0]).astype(jnp.bfloat16)
    key_rows = projected[:, 1].astype(jnp.bfloat16)
    value_rows = (projected[:, 2] + head_bias[1]).astype(jnp.bfloat16)

    def block_parts(block_index):
        sequence = block_index // per_sequence
        row_start = block_index * block_rows
        seq_start = sequence * seq_length
        query_block = split_heads(lax.dynamic_slice_in_dim(queries, row_start, block_rows, 0))
        key_block = split_heads(key_rows)
        value_block = split_heads(value_rows)
        seq_ids = lax.dynamic_index_in_dim(segments, sequence, 0, keepdims=False)
        query_ids = lax.dynamic_slice_in_dim(seq_ids, row_start - seq_start, block_rows, 0)
        products = (
            jnp.einsum("qhd,khd->hqk", query_block, key_block, preferred_element_type=jnp.float32)
            * score_scale
        )
        scores = jnp.where((query_ids[:, None] == seq_ids[None, :])[None], products, NEGATIVE)
        return (row_start, query_block, key_block, value_block, scores)

    def forward_block(block_index):
        row_start, query_block, key_block, value_block, scores = block_parts(block_index)
        row_max = jnp.max(scores, axis=-1, keepdims=True)
        exponent = jnp.exp(scores - row_max)
        row_sum = jnp.sum(exponent, axis=-1, keepdims=True)
        weights_low = (exponent / row_sum).astype(jnp.bfloat16)
        mixed_block = jnp.einsum(
            "hqk,khd->qhd", weights_low, value_block, preferred_element_type=jnp.float32
        )
        log_total = row_max[:, :, 0] + jnp.log(row_sum[:, :, 0])
        return (mixed_block.reshape(block_rows, local_width).astype(jnp.bfloat16), log_total)

    mixed_blocks, log_totals = lax.map(forward_block, block_ids)
    mixed_rows = mixed_blocks.reshape(group_rows, local_width)
    branch_out = (
        scatter_sum(
            jnp.dot(mixed_rows, output_full, preferred_element_type=jnp.float32), "tensor", 0
        )
        + bias_rows[2]
    )
    first_out, first_saved = layer_norm(
        tokens.astype(jnp.float32) + branch_out, norm_gains[0], bias_rows[3]
    )
    first_gathered = lax.all_gather(first_out.astype(jnp.bfloat16), "tensor", axis=0, tiled=True)
    local_bias = lax.dynamic_slice_in_dim(hidden_bias, tensor_rank * local_hidden, local_hidden, 0)
    upper_rows = (
        jnp.dot(first_gathered, upward_full, preferred_element_type=jnp.float32) + local_bias
    )
    hidden_full, gelu_back = jax.vjp(gelu_exact, upper_rows)
    hidden_rows = hidden_full.astype(jnp.bfloat16)
    second_out = (
        scatter_sum(
            jnp.dot(hidden_rows, downward_full, preferred_element_type=jnp.float32), "tensor", 0
        )
        + bias_rows[4]
    )
    layer_out, second_saved = layer_norm(first_out + second_out, norm_gains[1], bias_rows[5])
    reloaded = (
        lax.all_gather(project_weight, "dp", axis=0, tiled=True),
        lax.all_gather(output_weight, "dp", axis=1, tiled=True),
        lax.all_gather(up_weight, "dp", axis=0, tiled=True),
        lax.all_gather(down_weight, "dp", axis=1, tiled=True),
    )
    back_triple = reloaded[0].reshape(model_width, 3 * local_width)
    back_output, back_upward, back_downward = (reloaded[1], reloaded[2], reloaded[3])
    grad_layer = cotangent.astype(jnp.float32)
    grad_second_in, grad_gain_two, grad_shift_two = norm_back_saved(
        grad_layer, second_saved, norm_gains[1]
    )
    grad_second = grad_second_in.astype(jnp.bfloat16)
    grad_second_all = lax.all_gather(grad_second, "tensor", axis=0, tiled=True)
    grad_down_part = jnp.einsum(
        "tf,td->fd", hidden_rows, grad_second_all, preferred_element_type=jnp.float32
    )
    grad_hidden = jnp.einsum(
        "td,fd->tf", grad_second_all, back_downward, preferred_element_type=jnp.float32
    )
    grad_upper = gelu_back(grad_hidden)[0].astype(jnp.bfloat16)
    grad_up_part = jnp.einsum(
        "td,tf->df", first_gathered, grad_upper, preferred_element_type=jnp.float32
    )
    grad_first = (
        scatter_sum(
            jnp.einsum("tf,df->td", grad_upper, back_upward, preferred_element_type=jnp.float32),
            "tensor",
            0,
        )
        + grad_second_in
    )
    grad_first_in, grad_gain_one, grad_shift_one = norm_back_saved(grad_first, first_saved, norm_gains[0])
    grad_branch = grad_first_in.astype(jnp.bfloat16)
    grad_branch_all = lax.all_gather(grad_branch, "tensor", axis=0, tiled=True)
    grad_output_part = jnp.einsum(
        "tc,td->cd", mixed_rows, grad_branch_all, preferred_element_type=jnp.float32
    )
    grad_mixed = jnp.einsum(
        "td,cd->tc", grad_branch_all, back_output, preferred_element_type=jnp.float32
    ).astype(jnp.bfloat16)

    def backward_block(block_index):
        row_start, query_block, key_block, value_block, scores = block_parts(block_index)
        weights_full = jnp.exp(scores - log_totals[block_index][:, :, None])
        grad_mixed_block = split_heads(
            lax.dynamic_slice_in_dim(grad_mixed, row_start, block_rows, 0)
        )
        grad_weights = jnp.einsum(
            "qhd,khd->hqk", grad_mixed_block, value_block, preferred_element_type=jnp.float32
        )
        row_dot = jnp.sum(weights_full * grad_weights, axis=-1, keepdims=True)
        grad_scores = (weights_full * (grad_weights - row_dot)).astype(jnp.bfloat16)
        grad_query = (
            jnp.einsum("hqk,khd->qhd", grad_scores, key_block, preferred_element_type=jnp.float32)
            * score_scale
        )
        grad_key = (
            jnp.einsum("hqk,qhd->khd", grad_scores, query_block, preferred_element_type=jnp.float32)
            * score_scale
        )
        grad_value = jnp.einsum(
            "hqk,qhd->khd",
            weights_full.astype(jnp.bfloat16),
            grad_mixed_block,
            preferred_element_type=jnp.float32,
        )
        return (
            grad_query.reshape(block_rows, local_width),
            grad_key.reshape(seq_length, local_width),
            grad_value.reshape(seq_length, local_width),
        )

    query_blocks, key_blocks, value_blocks = lax.map(backward_block, block_ids)
    grad_queries = query_blocks.reshape(group_rows, local_width)
    grad_keys = (
        key_blocks.reshape(seq_count, per_sequence, seq_length, local_width)
        .sum(axis=1)
        .reshape(group_rows, local_width)
    )
    grad_values = (
        value_blocks.reshape(seq_count, per_sequence, seq_length, local_width)
        .sum(axis=1)
        .reshape(group_rows, local_width)
    )
    grad_projected = jnp.stack((grad_queries, grad_keys, grad_values), axis=1).astype(jnp.bfloat16)
    grad_project_part = jnp.einsum(
        "te,tsc->esc", gathered, grad_projected, preferred_element_type=jnp.float32
    )
    grad_matrix = grad_projected.reshape(group_rows, 3 * local_width)
    grad_tokens = (
        lax.psum_scatter(
            jnp.einsum(
                "tc,ec->te", grad_matrix, back_triple, preferred_element_type=jnp.float32
            ).astype(jnp.bfloat16),
            "tensor",
            scatter_dimension=0,
            tiled=True,
        ).astype(jnp.float32)
        + grad_first_in
    )
    grad_project, grad_output, grad_up, grad_down = (
        scatter_sum(grad_project_part, "dp", 0),
        scatter_sum(grad_output_part, "dp", 1),
        scatter_sum(grad_up_part, "dp", 0),
        scatter_sum(grad_down_part, "dp", 1),
    )
    head_terms = place_columns(
        jnp.stack(
            (
                jnp.sum(grad_projected[:, 0], axis=0, dtype=jnp.float32),
                jnp.sum(grad_projected[:, 2], axis=0, dtype=jnp.float32),
            )
        ),
        tensor_rank,
        model_width,
    )
    shared_terms = jnp.stack(
        (
            jnp.sum(grad_branch, axis=0, dtype=jnp.float32),
            grad_shift_one,
            jnp.sum(grad_second, axis=0, dtype=jnp.float32),
            grad_shift_two,
        )
    )
    bias_terms = jnp.concatenate((head_terms, shared_terms), axis=0)
    gain_terms = jnp.stack((grad_gain_one, grad_gain_two))
    hidden_terms = place_columns(
        jnp.sum(grad_upper, axis=0, dtype=jnp.float32), tensor_rank, hidden_bias.shape[0]
    )
    grad_gains, grad_bias_rows, grad_hidden_bias = lax.psum(
        (gain_terms, bias_terms, hidden_terms), ("dp", "tensor")
    )
    return (
        layer_out.astype(jnp.bfloat16),
        grad_tokens,
        grad_project,
        grad_output,
        grad_up,
        grad_down,
        grad_gains,
        grad_bias_rows,
        grad_hidden_bias,
    )


def solution(mesh):
    fits = mesh.shape["dp"] == 2 * LINES and mesh.shape["tensor"] == 4
    placed = (
        P(("dp", "tensor"), None),
        P("dp", None),
        P(("dp", "tensor"), None),
        P("dp", None, "tensor"),
        P("tensor", "dp"),
        P("dp", "tensor"),
        P("tensor", "dp"),
        P(),
        P(),
        P(),
    )
    return jax.shard_map(
        per_device_kernel if fits else per_device,
        mesh=mesh,
        in_specs=placed,
        out_specs=(
            P(("dp", "tensor"), None),
            P(("dp", "tensor"), None),
            P("dp", None, "tensor"),
            P("tensor", "dp"),
            P("dp", "tensor"),
            P("tensor", "dp"),
            P(),
            P(),
            P(),
        ),
        check_vma=False,
    )
```
